32 devices in a mesh: items: 8 (over z, y), stream: 2 (over x), heads: 2 (over core).
Axes of the slice: x: 2, y: 2, z: 4, core: 2. Of those that a mesh axis runs over, the one named last changes fastest.
Arguments:
- hidden: bfloat16 [128, 2, 32, 768], P('items', 'stream'), may hold values from -6 to 6
- features: bfloat16 [128, 257, 1408], P('items'), may hold values from -6 to 6
- segments: int32 [128, 32], P('items'), may hold values from 0 to 2, never falling along the last dimension, each value on 1 to 16 neighbouring positions
- modes: int32 [128], P('items'), may hold values from 0 to 2
- w_qkv: bfloat16 [3, 768, 768], P(None, ('items', 'stream'), 'heads'), may hold values from -0.21875 to 0.21875
- self_bias: float32 [3, 768], replicated, may hold values from -1.5 to 1.5
- self_out: bfloat16 [768, 768], P('heads', ('items', 'stream')), may hold values from -0.625 to 0.625
- cross_q: bfloat16 [768, 768], P(('items', 'stream'), 'heads'), may hold values from -0.21875 to 0.21875
- cross_kv: bfloat16 [2, 1408, 768], P(None, ('items', 'stream'), 'heads'), may hold values from -0.15625 to 0.15625
- cross_bias: float32 [3, 768], replicated, may hold values from -1.5 to 1.5
- cross_out: bfloat16 [768, 768], P('heads', ('items', 'stream')), may hold values from -1.75 to 1.75
- gains: float32 [4, 768], replicated, may hold values from 0.25 to 1.75
- shifts: float32 [4, 768], replicated, may hold values from -1.5 to 1.5
- feat_gain: float32 [1408], replicated, may hold values from 0.25 to 1.75
- feat_shift: float32 [1408], replicated, may hold values from -1.5 to 1.5
- ffn_in: bfloat16 [2, 768, 3072], P('stream', 'items', 'heads'), may hold values from -0.21875 to 0.21875
- ffn_bias_in: float32 [2, 3072], replicated, may hold values from -1.5 to 1.5
- ffn_out: bfloat16 [2, 3072, 768], P('stream', 'heads', 'items'), may hold values from -0.15625 to 0.15625
- ffn_bias_out: float32 [2, 768], replicated, may hold values from -1.5 to 1.5
- cotangent: float32 [128, 2, 32, 768], P('items', 'stream'), may hold values from -6 to 6
Outputs:
- output: bfloat16 [128, 2, 32, 768], P('items', 'stream')
- grad_hidden: float32 [128, 2, 32, 768], P('items', 'stream')
- grad_qkv: float32 [3, 768, 768], P(None, ('items', 'stream'), 'heads')
- grad_self_bias: float32 [3, 768], replicated
- grad_self_out: float32 [768, 768], P('heads', ('items', 'stream'))
- grad_cross_q: float32 [768, 768], P(('items', 'stream'), 'heads')
- grad_cross_kv: float32 [2, 1408, 768], P(None, ('items', 'stream'), 'heads')
- grad_cross_bias: float32 [3, 768], replicated
- grad_cross_out: float32 [768, 768], P('heads', ('items', 'stream'))
- grad_gains: float32 [4, 768], replicated
- grad_shifts: float32 [4, 768], replicated
- grad_feat_gain: float32 [1408], replicated
- grad_feat_shift: float32 [1408], replicated
- grad_ffn_in: float32 [2, 768, 3072], P('stream', 'items', 'heads')
- grad_ffn_bias_in: float32 [2, 3072], replicated
- grad_ffn_out: float32 [2, 3072, 768], P('stream', 'heads', 'items')
- grad_ffn_bias_out: float32 [2, 768], replicated
The draws below stay inside these ranges and needn't reach their ends.
Inputs may be any that keep to these rules, and one draw needn't show every extreme that they name: `segments`: each item's text row is 3 captions of consecutive tokens, each of 1 to 16 tokens. `modes`: 0: queries and text see only themselves; 1: text also sees the queries; 2: all rows see all rows.
All inputs are finite; a program needn't handle non-finite values.
Results may differ from the reference program's by a relative error of at most 0.017.
Values may be sent and summed in bfloat16 or wider, within the bound.
No kernel may reach another device: no remote copies, remote signals or barrier semaphores. Data moves between devices by JAX's collectives and lax.ppermute only.
A program may use at most 256 MiB of HBM per device.

```python
import math
import jax
import jax.numpy as jnp
import numpy as np
from jax import lax

D = 768
HEAD_DIM = 64
FF = 3072
DV = 1408
PATCHES = 257
ROW_LEN = 32
CAPTIONS = 3
CAPTION_MOST = 16
ITEMS_DEV = 16
ITEMS = 128


def plant(values, own_key, least, top_value):
    longest = values.shape.index(max(values.shape))
    spots = []
    for shift in (0, 1):
        where = [jax.random.randint(jax.random.fold_in(own_key, axis), (), 0, length) for axis, length in enumerate(values.shape)]
        where[longest] = (where[longest] + shift) % values.shape[longest]
        spots.append(tuple(where))
    return values.at[spots[0]].set(least).at[spots[1]].set(top_value)


def steps_of(key, shape, pieces, low, largest):
    level, own = 1.0, jax.random.fold_in(key, 6)
    for dim, parts in pieces:
        draws = jnp.exp(jax.random.uniform(jax.random.fold_in(own, dim), (parts,), jnp.float32, low / len(pieces), largest / len(pieces)))
        level = level * jnp.repeat(draws, shape[dim] // parts).reshape([-1 if axis == dim else 1 for axis in range(len(shape))])
    return level


def profile(count, total, most, lean):
    loads = [(1 << 20) // math.isqrt(grade ** lean) + 1 for grade in range(2, count + 1)]
    surplus, counts = total - most - (count - 1), [1] * (count - 1)
    while surplus > 0:
        movable = [i for i in range(count - 1) if counts[i] < most]
        pool, remaining = sum([loads[i] for i in movable]), surplus
        for i in movable:
            more = min(most - counts[i], max(1, remaining * loads[i] // pool), surplus)
            counts[i] = counts[i] + more
            surplus = surplus - more
    return np.array([most] + counts)


def ragged(own_key, amount, total, bound, lean):
    if amount == 2:
        one = jax.random.randint(own_key, (), max(1, total - bound), min(bound, total - 1) + 1)
        return jnp.stack([one, total - one])
    lengths = jnp.asarray(profile(amount, total, bound, lean), jnp.int32)
    pairs = (amount - 1) // 2
    giver, receiver = lengths[1:1 + 2 * pairs:2], lengths[2:2 + 2 * pairs:2]
    margin = jnp.minimum(giver - 1, bound - receiver)
    passed = jax.random.randint(jax.random.fold_in(own_key, 1), (pairs,), 0, 1 << 20) % (margin + 1)
    lengths = lengths.at[1:1 + 2 * pairs:2].set(giver - passed).at[2:2 + 2 * pairs:2].set(receiver + passed)
    return lengths[jax.random.permutation(jax.random.fold_in(own_key, 2), amount)]


def scatter_about(stream_key, dims, scale, most, split=(), kind=jnp.bfloat16):
    factor_of = steps_of(stream_key, dims, split, -0.22, 0.18) if split else 1.0
    entries = jax.random.normal(stream_key, dims, jnp.float32) * scale * factor_of
    return jnp.minimum(jnp.maximum(entries, -most), most).astype(kind)


def setup_inputs(seed: int = 0) -> dict:
    keys = jax.random.split(jax.random.key(seed), 21)
    return {
        "hidden": scatter_about(keys[0], (ITEMS, 2, ROW_LEN, D), 1.0, 6.0, ((0, 8), (1, 2))),
        "features": scatter_about(keys[1], (ITEMS, PATCHES, DV), 1.0, 6.0, ((0, 8),)),
        "segments": jax.vmap(lambda own: jnp.searchsorted(jnp.cumsum(ragged(own, CAPTIONS, ROW_LEN, CAPTION_MOST, 0)), jnp.arange(ROW_LEN), side="right"))(jax.random.split(keys[2], ITEMS)).reshape((ITEMS, ROW_LEN)).astype(jnp.int32),
        "modes": plant(jax.random.randint(keys[3], (ITEMS,), 0, 3), jax.random.fold_in(keys[3], 1), 0, 2).astype(jnp.int32),
        "w_qkv": scatter_about(keys[4], (3, D, D), D ** -0.5, 0.21875, ((1, 16), (2, 2))),
        "self_bias": scatter_about(keys[5], (3, D), 0.3, 1.5, (), jnp.float32),
        "self_out": scatter_about(keys[6], (D, D), (D // 8) ** -0.5, 0.625, ((0, 2), (1, 16))),
        "cross_q": scatter_about(keys[7], (D, D), D ** -0.5, 0.21875, ((0, 16), (1, 2))),
        "cross_kv": scatter_about(keys[8], (2, DV, D), DV ** -0.5, 0.15625, ((1, 16), (2, 2))),
        "cross_bias": scatter_about(keys[9], (3, D), 0.3, 1.5, (), jnp.float32),
        "cross_out": scatter_about(keys[10], (D, D), (D // 64) ** -0.5, 1.75, ((0, 2), (1, 16))),
        "gains": jnp.clip(1.0 + 0.15 * jax.random.normal(keys[11], (4, D), jnp.float32), 0.25, 1.75),
        "shifts": scatter_about(keys[12], (4, D), 0.3, 1.5, (), jnp.float32),
        "feat_gain": jnp.clip(1.0 + 0.15 * jax.random.normal(keys[13], (DV,), jnp.float32), 0.25, 1.75),
        "feat_shift": scatter_about(keys[14], (DV,), 0.3, 1.5, (), jnp.float32),
        "ffn_in": scatter_about(keys[15], (2, D, FF), D ** -0.5, 0.21875, ((0, 2), (1, 8), (2, 2))),
        "ffn_bias_in": scatter_about(keys[16], (2, FF), 0.3, 1.5, (), jnp.float32),
        "ffn_out": scatter_about(keys[17], (2, FF, D), (FF // 2) ** -0.5, 0.15625, ((0, 2), (1, 2), (2, 8))),
        "ffn_bias_out": scatter_about(keys[18], (2, D), 0.3, 1.5, (), jnp.float32),
        "cotangent": scatter_about(keys[19], (ITEMS, 2, ROW_LEN, D), 1.0, 6.0, ((0, 8), (1, 2)), jnp.float32),
    }


EPS = 1e-06
NEG = -1e+30
HIGH = lax.Precision.HIGHEST

@jax.custom_vjp
def low(v):
    return lax.optimization_barrier(v.astype(jnp.bfloat16)).astype(jnp.float32)

@jax.custom_vjp
def low_back(v):
    return v

def low_keep(v):
    return (low(v), None)

def low_pass(kept, grad):
    return (grad,)

def back_keep(v):
    return (v, None)

def back_low(kept, grad):
    return (low(grad),)
low.defvjp(low_keep, low_pass)
low_back.defvjp(back_keep, back_low)

def standard(inputs):
    center = inputs - lax.optimization_barrier(jnp.mean(inputs, axis=-1, keepdims=True))
    return center * lax.rsqrt(lax.optimization_barrier(jnp.mean(center * center, axis=-1, keepdims=True)) + EPS)

def normed(inputs, gain, shift):
    return standard(inputs) * gain + shift

def rounded(inputs):
    return low_back(low(inputs))

def project(inputs, weight):
    return jnp.dot(inputs, weight, precision=HIGH)

def split_heads(inputs):
    return inputs.reshape(inputs.shape[:-1] + (inputs.shape[-1] // HEAD_DIM, HEAD_DIM))

def attention(queries, key_rows, values, allowed):
    scores = jnp.einsum('gqhd,gkhd->ghqk', split_heads(queries), split_heads(key_rows), precision=HIGH)
    scores = low_back(scores * HEAD_DIM ** (-0.5))
    if allowed is not None:
        scores = jnp.where(allowed[:, None], scores, NEG)
    weights = jax.nn.softmax(scores, axis=-1)
    attended = jnp.einsum('ghqk,gkhd->gqhd', low(weights), split_heads(values), precision=HIGH)
    return rounded(attended.reshape(queries.shape))

def feed(inputs, w_in, b_in, w_out, b_out, gain, shift):
    pre_act = low_back(project(low(inputs), w_in) + b_in)
    activated = low(jax.nn.gelu(pre_act, approximate=False))
    branch = low_back(project(activated, w_out) + b_out)
    return normed(inputs + branch, gain, shift)

def visible_all(segments, modes):
    same = segments[:, :, None] == segments[:, None, :]
    later = jnp.broadcast_to((modes >= 1)[:, None, None], same.shape)
    every = jnp.broadcast_to((modes == 2)[:, None, None], same.shape)
    full = jnp.ones(same.shape, dtype=bool)
    upper = jnp.concatenate([full, every], axis=2)
    lower = jnp.concatenate([later, same], axis=2)
    return jnp.concatenate([upper, lower], axis=1)

def layer(params, hidden, features, allowed):
    w_qkv, self_bias, self_out, cross_q, cross_kv, cross_bias, cross_out, gains, shifts, feat_gain, feat_shift, ffn_in, ffn_bias_in, ffn_out, ffn_bias_out = params
    row_count = hidden.shape[2]
    tokens = jnp.concatenate([hidden[:, 0], hidden[:, 1]], axis=1)
    queries = rounded(project(tokens, w_qkv[0]) + self_bias[0])
    key_rows = rounded(project(tokens, w_qkv[1]))
    values = rounded(project(tokens, w_qkv[2]) + self_bias[1])
    mixed = low_back(project(attention(queries, key_rows, values, allowed), self_out) + self_bias[2])
    after_self = normed(tokens + mixed, gains[0], shifts[0])
    query_rows = after_self[:, :row_count]
    text_rows = after_self[:, row_count:]
    feat_norm = low(normed(features, feat_gain, feat_shift))
    query_c = rounded(project(low(query_rows), cross_q) + cross_bias[0])
    key_c = rounded(project(feat_norm, cross_kv[0]))
    value_c = rounded(project(feat_norm, cross_kv[1]) + cross_bias[1])
    mixed_c = low_back(project(attention(query_c, key_c, value_c, None), cross_out) + cross_bias[2])
    after_cross = normed(query_rows + mixed_c, gains[1], shifts[1])
    out_query = feed(after_cross, ffn_in[0], ffn_bias_in[0], ffn_out[0], ffn_bias_out[0], gains[2], shifts[2])
    out_text = feed(text_rows, ffn_in[1], ffn_bias_in[1], ffn_out[1], ffn_bias_out[1], gains[3], shifts[3])
    return jnp.stack([out_query, out_text], axis=1)

def reference(hidden, features, segments, modes, w_qkv, self_bias, self_out, cross_q, cross_kv, cross_bias, cross_out, gains, shifts, feat_gain, feat_shift, ffn_in, ffn_bias_in, ffn_out, ffn_bias_out, cotangent):
    params = tuple((weight.astype(jnp.float32) for weight in (w_qkv, self_bias, self_out, cross_q, cross_kv, cross_bias, cross_out, gains, shifts, feat_gain, feat_shift, ffn_in, ffn_bias_in, ffn_out, ffn_bias_out)))
    groups = ITEMS // ITEMS_DEV

    def regroup(source):
        return source.reshape((groups, ITEMS_DEV) + source.shape[1:])
    blocks = (regroup(hidden.astype(jnp.float32)), regroup(features.astype(jnp.float32)), regroup(segments), regroup(modes), regroup(cotangent.astype(jnp.float32)))
    zeros = tuple((jnp.zeros_like(weight) for weight in params))

    def step(running, block):
        hid_block, feat_block, seg_block, mode_block, cot_block = block
        allowed = visible_all(seg_block, mode_block)
        result, backward = jax.vjp(lambda weights, inputs: layer(weights, inputs, feat_block, allowed), params, hid_block)
        grad_params, grad_inputs = backward(cot_block)
        running = tuple((left + right for left, right in zip(running, grad_params)))
        return (running, (result.astype(jnp.bfloat16), grad_inputs))
    totals, (results, grad_inputs) = lax.scan(step, zeros, blocks)
    return (results.reshape(hidden.shape), grad_inputs.reshape(hidden.shape), totals[0], totals[1], totals[2], totals[3], totals[4], totals[5], totals[6], totals[7], totals[8], totals[9], totals[10], totals[11], totals[12], totals[13], totals[14])
```

```python
import math
from functools import partial

import jax
import jax.numpy as jnp
from jax import lax
from jax.sharding import PartitionSpec as P

HEAD_DIM = 64


EPS = 1e-06
NEG = -1e30


def partner(shard, axis, distance):
    return lax.ppermute(shard, axis, [(i, i ^ 1 << distance) for i in range(lax.axis_size(axis))])


def standard(inputs):
    center = inputs - jnp.mean(inputs, axis=-1, keepdims=True)
    return center * lax.rsqrt(jnp.mean(center * center, axis=-1, keepdims=True) + EPS)


def normed(inputs, gain, shift):
    return standard(inputs) * gain + shift


def linear(left, weight):
    return jnp.dot(left, weight, preferred_element_type=jnp.float32)


def linear_back(gradient, weight):
    return lax.dot_general(
        gradient,
        weight,
        (((gradient.ndim - 1,), (1,)), ((), ())),
        preferred_element_type=jnp.float32,
    )


def outer_sum(left, right):
    flat_left = left.reshape(-1, left.shape[-1])
    flat_right = right.reshape(-1, right.shape[-1])
    return lax.dot_general(
        flat_left, flat_right, (((0,), (0,)), ((), ())), preferred_element_type=jnp.float32
    )


def column_sum(gradient):
    return jnp.sum(gradient, axis=(0, 1), dtype=jnp.float32)


def heads_total(partial_sum):
    return partial_sum + partner(partial_sum, "heads", 0)


def ring_of(count):
    return list(range(0, count, 2)) + list(range(1, count, 2))[::-1]


def ring_place(count):
    order = ring_of(count)
    places = [order.index(i) for i in range(count)]
    place = jnp.asarray(places, jnp.int32)[lax.axis_index("items")]
    return order, place


def shift_ring(shard, order, step):
    count = len(order)
    return lax.ppermute(
        shard, "items", [(order[i], order[(i + step) % count]) for i in range(count)]
    )


def gather_items(shard):
    count = lax.axis_size("items")
    order, place = ring_place(count)
    table = jnp.asarray(order, jnp.int32)
    rows = shard.shape[0]
    whole = jnp.zeros((count * rows,) + shard.shape[1:], shard.dtype)

    def put(whole, piece, distance):
        start = table[(place + distance) % count] * rows
        return lax.dynamic_update_slice_in_dim(whole, piece, start, 0)

    whole = put(whole, shard, 0)
    up = down = shard
    for hop in range(1, count // 2 + 1):
        up = shift_ring(up, order, 1)
        whole = put(whole, up, count - hop)
        if hop <= (count - 1) // 2:
            down = shift_ring(down, order, -1)
            whole = put(whole, down, hop)
    return whole


def pair_streams(shard):
    other = partner(shard, "stream", 0)
    first = lax.axis_index("stream") == 0
    return jnp.where(
        first, jnp.concatenate([shard, other], axis=0), jnp.concatenate([other, shard], axis=0)
    )


def scatter_items(total):
    count = lax.axis_size("items")
    order, place = ring_place(count)
    table = jnp.asarray(order, jnp.int32)
    rows = total.shape[0] // count

    def piece(distance):
        start = table[(place + distance) % count] * rows
        return lax.dynamic_slice_in_dim(total, start, rows, 0)

    far_up, far_down = count // 2, (count - 1) // 2
    result = piece(0)
    up = down = None
    for hop in range(far_up, 0, -1):
        own = piece(hop)
        up = shift_ring((own if up is None else own + up).astype(jnp.bfloat16), order, 1).astype(jnp.float32)
        if hop <= far_down:
            own = piece(count - hop)
            down = shift_ring((own if down is None else own + down).astype(jnp.bfloat16), order, -1).astype(jnp.float32)
    return result + up + down


def scatter_both(total):
    count = lax.axis_size("items")
    rows = total.shape[0] // (2 * count)
    parts = total.reshape((count, 2, rows, total.shape[1]))
    stream = lax.axis_index("stream")
    keep = lax.dynamic_index_in_dim(parts, stream, 1, keepdims=False)
    away = lax.dynamic_index_in_dim(parts, 1 - stream, 1, keepdims=False)
    arrived = partner(away.astype(jnp.bfloat16), "stream", 0).astype(jnp.float32)
    return scatter_items((keep + arrived).reshape(count * rows, total.shape[1]))


def all_total(vector):
    vector = heads_total(vector)
    vector = vector + partner(vector, "stream", 0)
    count = lax.axis_size("items")
    bit = 0
    while (1 << bit) < count:
        vector = vector + partner(vector, "items", bit)
        bit += 1
    return vector


def all_totals(arrays):
    sizes = [math.prod(one.shape) for one in arrays]
    packed = jnp.concatenate([one.reshape(-1) for one in arrays]).reshape(-1, 128)
    total = all_total(packed).reshape(-1)
    results, start = [], 0
    for one, size in zip(arrays, sizes):
        results.append(total[start : start + size].reshape(one.shape))
        start += size
    return tuple(results)


def split_heads(inputs):
    return inputs.reshape(inputs.shape[:-1] + (inputs.shape[-1] // HEAD_DIM, HEAD_DIM))


def merge_heads(inputs):
    return inputs.reshape(inputs.shape[:-2] + (inputs.shape[-2] * inputs.shape[-1],))


def scores_of(queries, key_rows, allowed):
    scores = jnp.einsum(
        "bqhd,bkhd->bhqk",
        split_heads(queries),
        split_heads(key_rows),
        preferred_element_type=jnp.float32,
    ) * HEAD_DIM ** (-0.5)
    if allowed is not None:
        scores = jnp.where(allowed[:, None], scores, NEG)
    return scores


def attend(queries, key_rows, values, allowed):
    scores = scores_of(queries, key_rows, allowed)
    row_max = jnp.max(scores, axis=-1, keepdims=True)
    log_total = row_max + jnp.log(jnp.sum(jnp.exp(scores - row_max), axis=-1, keepdims=True))
    weights = jnp.exp(scores - log_total).astype(jnp.bfloat16)
    attended = jnp.einsum(
        "bhqk,bkhd->bqhd", weights, split_heads(values), preferred_element_type=jnp.float32
    )
    return (merge_heads(attended).astype(jnp.bfloat16), log_total)


def attend_back(queries, key_rows, values, allowed, log_total, grad_out):
    weights = jnp.exp(scores_of(queries, key_rows, allowed) - log_total)
    grad_heads = split_heads(grad_out)
    grad_weights = jnp.einsum(
        "bqhd,bkhd->bhqk", grad_heads, split_heads(values), preferred_element_type=jnp.float32
    )
    grad_values = jnp.einsum(
        "bhqk,bqhd->bkhd",
        weights.astype(jnp.bfloat16),
        grad_heads,
        preferred_element_type=jnp.float32,
    )
    row_delta = jnp.sum(grad_weights * weights, axis=-1, keepdims=True)
    grad_scores = (weights * (grad_weights - row_delta)).astype(jnp.bfloat16)
    score_scale = HEAD_DIM ** (-0.5)
    grad_queries = (
        jnp.einsum(
            "bhqk,bkhd->bqhd",
            grad_scores,
            split_heads(key_rows),
            preferred_element_type=jnp.float32,
        )
        * score_scale
    )
    grad_keys = (
        jnp.einsum(
            "bhqk,bqhd->bkhd", grad_scores, split_heads(queries), preferred_element_type=jnp.float32
        )
        * score_scale
    )
    return (merge_heads(grad_queries), merge_heads(grad_keys), merge_heads(grad_values))


def visible(stream, segments, modes):
    same_caption = segments[:, :, None] == segments[:, None, :]
    query_cols = jnp.where(stream == 0, True, modes >= 1)[:, None, None]
    text_cols = jnp.where(stream == 0, (modes == 2)[:, None, None], same_caption)
    return jnp.concatenate([jnp.broadcast_to(query_cols, same_caption.shape), text_cols], axis=2)


def feature_keys(feats, key_weight, value_weight, value_bias, feat_gain, feat_shift):
    feat_norm = normed(feats.astype(jnp.float32), feat_gain, feat_shift).astype(jnp.bfloat16)
    key_c = linear(feat_norm, key_weight).astype(jnp.bfloat16)
    value_c = (linear(feat_norm, value_weight) + value_bias).astype(jnp.bfloat16)
    return (feat_norm, key_c, value_c)


def feature_grads(feats, feat_norm, grad_keys, grad_values, key_weight, value_weight):
    key_grad = outer_sum(feat_norm, grad_keys)
    value_grad = outer_sum(feat_norm, grad_values)
    grad_norm = linear_back(grad_keys, key_weight) + linear_back(grad_values, value_weight)
    base_norm = standard(feats.astype(jnp.float32))
    gain_grad = jnp.sum(grad_norm * base_norm, axis=(0, 1))
    shift_grad = jnp.sum(grad_norm, axis=(0, 1))
    return (jnp.concatenate([key_grad, value_grad], axis=1), gain_grad, shift_grad, column_sum(grad_values))


def spread(piece, start, full_len):
    return lax.dynamic_update_slice_in_dim(jnp.zeros((full_len,), jnp.float32), piece, start, 0)


def body(
    hidden,
    features,
    segments,
    modes,
    w_qkv,
    self_bias,
    self_out,
    cross_q,
    cross_kv,
    cross_bias,
    cross_out,
    gains,
    shifts,
    feat_gain,
    feat_shift,
    ffn_in,
    ffn_bias_in,
    ffn_out,
    ffn_bias_out,
    cotangent,
):
    stream = lax.axis_index("stream")
    head_index = lax.axis_index("heads")
    query_side = stream == 0
    query_mask = query_side.astype(jnp.float32)
    text_mask = 1.0 - query_mask
    lead_mask = (head_index == 0).astype(jnp.float32)
    head_cols = w_qkv.shape[2]
    three = [slice(i * head_cols, (i + 1) * head_cols) for i in range(3)]
    qkv_all = gather_items(pair_streams(jnp.concatenate([w_qkv[0], w_qkv[1], w_qkv[2]], axis=1)))
    qkv_full = [qkv_all[:, cols] for cols in three]
    kv_all = gather_items(pair_streams(jnp.concatenate([cross_kv[0], cross_kv[1]], axis=1)))
    cross_kv_full = [kv_all[:, cols] for cols in three[:2]]
    rest_all = gather_items(
        pair_streams(jnp.concatenate([self_out.T, cross_q, cross_out.T], axis=1))
    )
    self_out_full = rest_all[:, three[0]].T
    cross_q_full = rest_all[:, three[1]]
    cross_out_full = rest_all[:, three[2]].T
    ffn_all = lax.all_gather(
        jnp.concatenate([ffn_in[0], ffn_out[0].T], axis=1), "items", axis=0, tiled=True
    )
    ffn_in_full = [ffn_all[:, : ffn_in.shape[2]]]
    ffn_out_full = [ffn_all[:, ffn_in.shape[2] :].T]
    inner_weight = ffn_in_full[0]
    outer_weight = ffn_out_full[0]
    own_rows = hidden[:, 0]
    item_count, row_count, width = own_rows.shape
    head_count = head_cols // HEAD_DIM
    col_start = head_index * head_cols
    hidden_cols = inner_weight.shape[1]
    hidden_start = head_index * hidden_cols
    patch_count = features.shape[1]
    feat_width = features.shape[2]

    def my_cols(vector):
        return lax.dynamic_slice_in_dim(vector, col_start, head_cols, 0)

    bias_q = my_cols(self_bias[0])
    bias_v = my_cols(self_bias[1])
    bias_o = self_bias[2]
    bias_qc = my_cols(cross_bias[0])
    bias_vc = my_cols(cross_bias[1])
    bias_oc = cross_bias[2]
    gain_ffn = lax.dynamic_index_in_dim(gains, 2 + stream, 0, keepdims=False)
    shift_ffn = lax.dynamic_index_in_dim(shifts, 2 + stream, 0, keepdims=False)
    bias_in = lax.dynamic_slice_in_dim(
        lax.dynamic_index_in_dim(ffn_bias_in, stream, 0, keepdims=False),
        hidden_start,
        hidden_cols,
        0,
    )
    bias_out = lax.dynamic_index_in_dim(ffn_bias_out, stream, 0, keepdims=False)
    queries = (linear(own_rows, qkv_full[0]) + bias_q).astype(jnp.bfloat16)
    key_rows = linear(own_rows, qkv_full[1]).astype(jnp.bfloat16)
    values = (linear(own_rows, qkv_full[2]) + bias_v).astype(jnp.bfloat16)
    key_far, value_far = partner((key_rows, values), "stream", 0)
    all_keys = jnp.where(
        query_side,
        jnp.concatenate([key_rows, key_far], axis=1),
        jnp.concatenate([key_far, key_rows], axis=1),
    )
    all_values = jnp.where(
        query_side,
        jnp.concatenate([values, value_far], axis=1),
        jnp.concatenate([value_far, values], axis=1),
    )
    allowed = visible(stream, segments, modes)
    attended, log_total = attend(queries, all_keys, all_values, allowed)
    residual_one = (
        own_rows.astype(jnp.float32) + heads_total(linear(attended, self_out_full)) + bias_o
    )
    after_self = normed(residual_one, gains[0], shifts[0])
    after_low = after_self.astype(jnp.bfloat16)
    empty_rows = jnp.zeros((item_count, row_count, head_cols), jnp.bfloat16)
    empty_total = jnp.zeros((item_count, head_count, row_count, 1), jnp.float32)
    empty_mix = jnp.zeros((item_count, row_count, width), jnp.float32)

    def cross_front(cross_keys, cross_values):
        query_c = (linear(after_low, cross_q_full) + bias_qc).astype(jnp.bfloat16)
        attended_c, total_c = attend(query_c, cross_keys, cross_values, None)
        return (query_c, attended_c, total_c, linear(attended_c, cross_out_full))

    def front_run():
        norm_all, keys_all, values_all = feature_keys(
            features, cross_kv_full[0], cross_kv_full[1], bias_vc, feat_gain, feat_shift
        )
        return (norm_all, keys_all, values_all) + cross_front(keys_all, values_all)

    def front_skip():
        empty_feats = jnp.zeros((item_count, patch_count, feat_width), jnp.bfloat16)
        empty_keys = jnp.zeros((item_count, patch_count, head_cols), jnp.bfloat16)
        return (empty_feats, empty_keys, empty_keys, empty_rows, empty_rows, empty_total, empty_mix)

    norm_all, cross_keys, cross_values, query_c, attended_c, total_c, cross_part = lax.cond(
        query_side, front_run, front_skip
    )
    residual_two = after_self + heads_total(cross_part) + bias_oc
    after_cross = normed(residual_two, gains[1], shifts[1])
    ffn_input = jnp.where(query_side, after_cross, after_self)
    ffn_low = jnp.where(query_side, after_cross.astype(jnp.bfloat16), after_low)
    pre_act = linear(ffn_low, inner_weight) + bias_in
    activated = jax.nn.gelu(pre_act, approximate=False).astype(jnp.bfloat16)
    residual_three = ffn_input + heads_total(linear(activated, outer_weight)) + bias_out
    result_rows = normed(residual_three, gain_ffn, shift_ffn)
    output = result_rows.astype(jnp.bfloat16)[:, None]
    unused_three, norm_three_back = jax.vjp(normed, residual_three, gain_ffn, shift_ffn)
    grad_three, gain_three, shift_three = norm_three_back(cotangent[:, 0])
    grad_branch = grad_three.astype(jnp.bfloat16)
    grad_outer = outer_sum(grad_branch, activated)
    bias_out_grad = column_sum(grad_branch)
    unused_pre, gelu_back = jax.vjp(partial(jax.nn.gelu, approximate=False), pre_act)
    grad_pre = gelu_back(linear_back(grad_branch, outer_weight))[0].astype(jnp.bfloat16)
    grad_inner = outer_sum(ffn_low, grad_pre)
    bias_in_grad = column_sum(grad_pre)
    ffn_red = lax.psum_scatter(
        jnp.concatenate([grad_inner.astype(jnp.bfloat16), grad_outer.astype(jnp.bfloat16)], axis=1),
        "items",
        scatter_dimension=0,
        tiled=True,
    ).astype(jnp.float32)
    ffn_in_red = ffn_red[:, :hidden_cols][None]
    ffn_out_red = ffn_red[:, hidden_cols:].T[None]
    grad_ffn_input = grad_three + heads_total(linear_back(grad_pre, inner_weight))
    unused_two, norm_two_back = jax.vjp(normed, residual_two, gains[1], shifts[1])
    grad_two, gain_two, shift_two = norm_two_back(grad_ffn_input * query_mask)

    def cross_back():
        grad_mix = grad_two.astype(jnp.bfloat16)
        out_grad = outer_sum(grad_mix, attended_c)
        grad_att = linear_back(grad_mix, cross_out_full).astype(jnp.bfloat16)
        grad_qc, grad_kc, grad_vc = attend_back(
            query_c, cross_keys, cross_values, None, total_c, grad_att
        )
        grad_qc = grad_qc.astype(jnp.bfloat16)
        return (
            out_grad,
            column_sum(grad_mix),
            column_sum(grad_qc),
            outer_sum(after_low, grad_qc),
            linear_back(grad_qc, cross_q_full),
            grad_kc.astype(jnp.bfloat16),
            grad_vc.astype(jnp.bfloat16),
        )

    def back_empty():
        empty_keys = jnp.zeros((item_count, patch_count, head_cols), jnp.bfloat16)
        return (
            jnp.zeros((width, head_cols), jnp.float32),
            jnp.zeros((width,), jnp.float32),
            jnp.zeros((head_cols,), jnp.float32),
            jnp.zeros((width, head_cols), jnp.float32),
            empty_mix,
            empty_keys,
            empty_keys,
        )

    def back_run():
        pieces = cross_back()
        return pieces[:5] + feature_grads(
            features, norm_all, pieces[5], pieces[6], cross_kv_full[0], cross_kv_full[1]
        )

    def back_skip():
        pieces = back_empty()
        return pieces[:5] + (
            jnp.zeros((feat_width, 2 * head_cols), jnp.float32),
            jnp.zeros((feat_width,), jnp.float32),
            jnp.zeros((feat_width,), jnp.float32),
            jnp.zeros((head_cols,), jnp.float32),
        )

    (
        cross_out_grad,
        bias_oc_grad,
        bias_qc_grad,
        cross_q_grad,
        cross_part_grad,
        cross_kv_grad,
        feat_gain_grad,
        feat_shift_grad,
        bias_vc_grad,
    ) = lax.cond(query_side, back_run, back_skip)
    grad_after_self = jnp.where(query_side, grad_two + heads_total(cross_part_grad), grad_ffn_input)
    unused_one, norm_one_back = jax.vjp(normed, residual_one, gains[0], shifts[0])
    grad_one, gain_one, shift_one = norm_one_back(grad_after_self)
    grad_mix_self = grad_one.astype(jnp.bfloat16)
    self_out_grad = outer_sum(grad_mix_self, attended)
    bias_o_grad = column_sum(grad_mix_self)
    grad_attended = linear_back(grad_mix_self, self_out_full).astype(jnp.bfloat16)
    grad_q, grad_keys, grad_values = attend_back(
        queries, all_keys, all_values, allowed, log_total, grad_attended
    )
    keys_first = grad_keys[:, :row_count]
    keys_second = grad_keys[:, row_count:]
    values_first = grad_values[:, :row_count]
    values_second = grad_values[:, row_count:]
    keys_own = jnp.where(query_side, keys_first, keys_second)
    keys_away = jnp.where(query_side, keys_second, keys_first)
    values_own = jnp.where(query_side, values_first, values_second)
    values_away = jnp.where(query_side, values_second, values_first)
    keys_home, values_home = (
        partner(keys_away.astype(jnp.bfloat16), "stream", 0).astype(keys_away.dtype),
        partner(values_away.astype(jnp.bfloat16), "stream", 0).astype(values_away.dtype),
    )
    grad_kb = (keys_own + keys_home).astype(jnp.bfloat16)
    grad_vb = (values_own + values_home).astype(jnp.bfloat16)
    grad_qb = grad_q.astype(jnp.bfloat16)
    qkv_grad = jnp.concatenate(
        [
            outer_sum(own_rows, grad_qb),
            outer_sum(own_rows, grad_kb),
            outer_sum(own_rows, grad_vb),
            self_out_grad,
        ],
        axis=1,
    )
    grad_input = grad_one + heads_total(
        linear_back(grad_qb, qkv_full[0])
        + linear_back(grad_kb, qkv_full[1])
        + linear_back(grad_vb, qkv_full[2])
    )
    cross_red = scatter_both(jnp.concatenate([cross_q_grad, cross_out_grad], axis=1))
    cross_q_red = cross_red[:, three[0]]
    cross_out_red = cross_red[:, three[1]].T
    kv_red = scatter_both(cross_kv_grad)
    cross_kv_red = jnp.stack([kv_red[:, cols] for cols in three[:2]])
    self_red = scatter_both(qkv_grad)
    qkv_red = jnp.stack([self_red[:, cols] for cols in three])
    self_out_red = self_red[:, 3 * head_cols :].T
    self_bias_grad = jnp.stack(
        [
            spread(column_sum(grad_qb), col_start, width),
            spread(column_sum(grad_vb), col_start, width),
            lead_mask * bias_o_grad,
        ]
    )
    cross_bias_grad = jnp.stack(
        [
            spread(bias_qc_grad, col_start, width),
            spread(bias_vc_grad, col_start, width),
            lead_mask * bias_oc_grad,
        ]
    )
    gains_grad = lead_mask * jnp.stack(
        [gain_one, gain_two, query_mask * gain_three, text_mask * gain_three]
    )
    shifts_grad = lead_mask * jnp.stack(
        [shift_one, shift_two, query_mask * shift_three, text_mask * shift_three]
    )
    bias_in_full = spread(bias_in_grad, hidden_start, ffn_bias_in.shape[1])
    ffn_bias_in_grad = jnp.stack([query_mask * bias_in_full, text_mask * bias_in_full])
    ffn_bias_out_grad = lead_mask * jnp.stack(
        [query_mask * bias_out_grad, text_mask * bias_out_grad]
    )
    (
        self_bias_sum,
        cross_bias_sum,
        gains_sum,
        shifts_sum,
        feat_gain_sum,
        feat_shift_sum,
        bias_in_sum,
        bias_out_sum,
    ) = all_totals(
        (
            self_bias_grad,
            cross_bias_grad,
            gains_grad,
            shifts_grad,
            feat_gain_grad,
            feat_shift_grad,
            ffn_bias_in_grad,
            ffn_bias_out_grad,
        )
    )
    return (
        output,
        grad_input[:, None],
        qkv_red,
        self_bias_sum,
        self_out_red,
        cross_q_red,
        cross_kv_red,
        cross_bias_sum,
        cross_out_red,
        gains_sum,
        shifts_sum,
        feat_gain_sum,
        feat_shift_sum,
        ffn_in_red,
        bias_in_sum,
        ffn_out_red,
        bias_out_sum,
    )


def solution(mesh):
    placed = (
        P("items", "stream", None, None),
        P("items", None, None),
        P("items", None),
        P("items"),
        P(None, ("items", "stream"), "heads"),
        P(),
        P("heads", ("items", "stream")),
        P(("items", "stream"), "heads"),
        P(None, ("items", "stream"), "heads"),
        P(),
        P("heads", ("items", "stream")),
        P(),
        P(),
        P(),
        P(),
        P("stream", "items", "heads"),
        P(),
        P("stream", "heads", "items"),
        P(),
        P("items", "stream", None, None),
    )
    return jax.shard_map(
        body,
        mesh=mesh,
        in_specs=placed,
        out_specs=(
            P("items", "stream", None, None),
            P("items", "stream", None, None),
            P(None, ("items", "stream"), "heads"),
            P(),
            P("heads", ("items", "stream")),
            P(("items", "stream"), "heads"),
            P(None, ("items", "stream"), "heads"),
            P(),
            P("heads", ("items", "stream")),
            P(),
            P(),
            P(),
            P(),
            P("stream", "items", "heads"),
            P(),
            P("stream", "heads", "items"),
            P(),
        ),
        check_vma=False,
    )
```

```python
import math

import jax
import jax.numpy as jnp
from jax import lax
from jax.experimental import pallas as pl
from jax.experimental.pallas import tpu as pltpu
from jax.sharding import PartitionSpec as P

HEAD_DIM = 64
EPS = 1e-06
NEG = -1e30
BF = jnp.bfloat16
F32 = jnp.float32


def partner(shard, axis, distance):
    return lax.ppermute(shard, axis, [(i, i ^ 1 << distance) for i in range(lax.axis_size(axis))])


def ring_of(count):
    return list(range(0, count, 2)) + list(range(1, count, 2))[::-1]


def ring_place(count):
    order = ring_of(count)
    places = [order.index(i) for i in range(count)]
    return order, jnp.asarray(places, jnp.int32)[lax.axis_index("items")]


def shift_ring(shard, order, step):
    count = len(order)
    return lax.ppermute(
        shard, "items", [(order[i], order[(i + step) % count]) for i in range(count)]
    )


def gather_items(shard):
    count = lax.axis_size("items")
    order, place = ring_place(count)
    table = jnp.asarray(order, jnp.int32)
    rows = shard.shape[0]
    whole = jnp.zeros((count * rows,) + shard.shape[1:], shard.dtype)

    def put(whole, piece, distance):
        start = table[(place + distance) % count] * rows
        return lax.dynamic_update_slice_in_dim(whole, piece, start, 0)

    whole = put(whole, shard, 0)
    up = down = shard
    for hop in range(1, count // 2 + 1):
        up = shift_ring(up, order, 1)
        whole = put(whole, up, count - hop)
        if hop <= (count - 1) // 2:
            down = shift_ring(down, order, -1)
            whole = put(whole, down, hop)
    return whole


def pair_streams(shard):
    other = partner(shard, "stream", 0)
    first = lax.axis_index("stream") == 0
    return jnp.where(
        first, jnp.concatenate([shard, other], axis=0), jnp.concatenate([other, shard], axis=0)
    )


def scatter_items(total):
    count = lax.axis_size("items")
    order, place = ring_place(count)
    table = jnp.asarray(order, jnp.int32)
    rows = total.shape[0] // count

    def piece(distance):
        start = table[(place + distance) % count] * rows
        return lax.dynamic_slice_in_dim(total, start, rows, 0).astype(F32)

    far_up, far_down = count // 2, (count - 1) // 2
    result = piece(0)
    up = down = None
    for hop in range(far_up, 0, -1):
        own = piece(hop)
        up = shift_ring((own if up is None else own + up).astype(BF), order, 1).astype(F32)
        if hop <= far_down:
            own = piece(count - hop)
            down = shift_ring((own if down is None else own + down).astype(BF), order, -1).astype(F32)
    return result + up + down


def scatter_both(total):
    count = lax.axis_size("items")
    rows = total.shape[0] // (2 * count)
    parts = total.reshape((count, 2, rows, total.shape[1]))
    stream = lax.axis_index("stream")
    keep = lax.dynamic_index_in_dim(parts, stream, 1, keepdims=False)
    away = lax.dynamic_index_in_dim(parts, 1 - stream, 1, keepdims=False)
    arrived = partner(away, "stream", 0)
    both = keep.astype(F32) + arrived.astype(F32)
    return scatter_items(both.reshape(count * rows, total.shape[1]))


def all_total(vector):
    vector = vector + partner(vector, "heads", 0)
    vector = vector + partner(vector, "stream", 0)
    bit = 0
    while (1 << bit) < lax.axis_size("items"):
        vector = vector + partner(vector, "items", bit)
        bit += 1
    return vector


def all_totals(arrays):
    sizes = [math.prod(one.shape) for one in arrays]
    packed = jnp.concatenate([one.reshape(-1) for one in arrays]).reshape(-1, 128)
    total = all_total(packed).reshape(-1)
    results, start = [], 0
    for one, size in zip(arrays, sizes):
        results.append(total[start : start + size].reshape(one.shape))
        start += size
    return tuple(results)


def spread(piece, start, full_len):
    return lax.dynamic_update_slice_in_dim(jnp.zeros((full_len,), F32), piece, start, 0)


def mul(left, right):
    return jnp.dot(left, right, preferred_element_type=F32)


def mul_t(left, right):
    return lax.dot_general(left, right, (((1,), (1,)), ((), ())), preferred_element_type=F32)


def t_mul(left, right):
    return lax.dot_general(left, right, (((0,), (0,)), ((), ())), preferred_element_type=F32)


def standard(rows):
    center = rows - jnp.mean(rows, axis=-1, keepdims=True)
    scale = lax.rsqrt(jnp.mean(center * center, axis=-1, keepdims=True) + EPS)
    return center * scale, scale


def norm_back(grad, unit, scale, gain):
    inner = grad * gain
    return scale * (
        inner
        - jnp.mean(inner, axis=-1, keepdims=True)
        - unit * jnp.mean(inner * unit, axis=-1, keepdims=True)
    )


def total_rows(rows):
    return jnp.sum(rows, axis=0, keepdims=True)


def head_mask(rows, heads, value, dtype):
    row = lax.broadcasted_iota(jnp.int32, (heads * rows, heads * HEAD_DIM), 0) // rows
    col = lax.broadcasted_iota(jnp.int32, (heads * rows, heads * HEAD_DIM), 1) // HEAD_DIM
    return jnp.where(row == col, value, 0.0).astype(dtype)


def stack_heads(rows, heads, mask):
    return jnp.concatenate([rows] * heads, axis=0) * mask


def fold_heads(stacked, heads, mask):
    rows = stacked.shape[0] // heads
    stacked = stacked * mask
    result = stacked[:rows]
    for head in range(1, heads):
        result = result + stacked[head * rows : (head + 1) * rows]
    return result


def softmax(scores):
    power = jnp.exp(scores - jnp.max(scores, axis=-1, keepdims=True))
    return power * (1.0 / jnp.sum(power, axis=-1, keepdims=True))


def attend(queries, keys, values, hide, heads, scaled_mask, out_mask):
    scores = hide(mul_t(stack_heads(queries, heads, scaled_mask), keys))
    weights = softmax(scores).astype(BF)
    return fold_heads(mul(weights, values), heads, out_mask).astype(BF)


def attend_back(queries, keys, values, grad, hide, heads, scaled_mask, plain_mask, out_mask):
    queries = stack_heads(queries, heads, scaled_mask)
    grad = stack_heads(grad, heads, plain_mask)
    weights = softmax(hide(mul_t(queries, keys)))
    grad_weights = mul_t(grad, values)
    grad_values = t_mul(weights.astype(BF), grad)
    delta = jnp.sum(grad_weights * weights, axis=-1, keepdims=True)
    grad_scores = (weights * (grad_weights - delta)).astype(BF)
    grad_queries = fold_heads(mul(grad_scores, keys), heads, out_mask) * HEAD_DIM ** (-0.5)
    return grad_queries, t_mul(grad_scores, queries), grad_values


def whole(shape):
    return pl.BlockSpec(shape, lambda i: (0,) * len(shape))


def block(shape):
    return pl.BlockSpec(shape, lambda i: (i,) + (0,) * (len(shape) - 1))


def column(shape):
    return pl.BlockSpec(shape, lambda i: (0, i))


def shaped(shape, dtype):
    return jax.ShapeDtypeStruct(shape, dtype)


def call(kernel, grid, in_specs, out_specs, out_shape, scratch=(), flops=0, moved=0):
    return pl.pallas_call(
        kernel,
        grid=(grid,),
        in_specs=in_specs,
        out_specs=out_specs,
        out_shape=out_shape,
        scratch_shapes=list(scratch),
        compiler_params=pltpu.CompilerParams(
            dimension_semantics=("arbitrary",), vmem_limit_bytes=56 << 20
        ),
        cost_estimate=pl.CostEstimate(flops=flops, bytes_accessed=moved, transcendentals=0),
    )


def feature_norm(features, gain, shift, padded):
    items, patches, width = features.shape

    def kernel(feat, gain, shift, out):
        unit, _ = standard(feat[0].astype(F32))
        out[0, :patches] = (unit * gain[...] + shift[...]).astype(BF)
        out[0, patches:] = jnp.zeros((padded - patches, width), BF)

    return call(
        kernel,
        items,
        [block((1, patches, width)), whole((1, width)), whole((1, width))],
        block((1, padded, width)),
        shaped((items, padded, width), BF),
        moved=4 * items * patches * width,
    )(features, gain, shift)


def project(own, far, weight, bias):
    rows, width = own.shape
    cols = weight.shape[1]
    head_cols = cols // 3
    step = rows // 4

    def kernel(own, far, weight, bias, q, kv, kv_far):
        near = mul(own[...], weight[...]) + bias[...]
        q[...] = near[:, :head_cols].astype(BF)
        kv[...] = near[:, head_cols:].astype(BF)
        kv_far[...] = (mul(far[...], weight[:, head_cols:]) + bias[:, head_cols:]).astype(BF)

    return call(
        kernel,
        4,
        [block((step, width)), block((step, width)), whole((width, cols)), whole((1, cols))],
        [block((step, head_cols)), block((step, 2 * head_cols)), block((step, 2 * head_cols))],
        [shaped((rows, head_cols), BF)] + [shaped((rows, 2 * head_cols), BF)] * 2,
        flops=10 * rows * width * head_cols,
        moved=4 * rows * width + 2 * width * cols,
    )(own, far, weight, bias)


def self_attention(q, kv, kv_far, allowed, weight, items, batch):
    rows, cols = q.shape
    heads, each = cols // HEAD_DIM, rows // items
    width = weight.shape[0]

    def kernel(q, kv, kv_far, allowed, weight, attended, out):
        index = pl.program_id(0)
        scaled = head_mask(each, heads, HEAD_DIM ** (-0.5), BF)
        ones = head_mask(each, heads, 1.0, F32)
        for item in range(batch):
            span = slice(item * each, (item + 1) * each)
            keys = jnp.concatenate([kv[span, :cols], kv_far[span, :cols]], axis=0)
            values = jnp.concatenate([kv[span, cols:], kv_far[span, cols:]], axis=0)
            seen = jnp.concatenate([allowed[item]] * heads, axis=0) > 0
            result = attend(
                q[span], keys, values, lambda s: jnp.where(seen, s, NEG), heads, scaled, ones
            )
            start = pl.multiple_of((index * batch + item) * each, each)
            attended[pl.ds(start, each), :] = result

        @pl.when(index == pl.num_programs(0) - 1)
        def _():
            out[...] = mul_t(attended[...], weight[...])

    part = batch * each
    return call(
        kernel,
        items // batch,
        [
            block((part, cols)),
            block((part, 2 * cols)),
            block((part, 2 * cols)),
            block((batch, each, 2 * each)),
            whole((width, cols)),
        ],
        [whole((rows, cols)), whole((rows, width))],
        [shaped((rows, cols), BF), shaped((rows, width), F32)],
        flops=2 * rows * cols * width * 3,
        moved=rows * cols * 14 + rows * width * 4,
    )(q, kv, kv_far, allowed, weight)


def cross_attention(own, near, away, rows_in, cq, keys_values, weight, items, batch, patches):
    rows, width = own.shape
    cols = weight.shape[1]
    heads, each = cols // HEAD_DIM, rows // items
    padded = keys_values.shape[1]

    def kernel(own, near, away, bias, gain, shift, bias_q, cq, kv, weight, unit, scale, low, qc, attended, out):
        index = pl.program_id(0)

        @pl.when(index == 0)
        def _():
            one, size = standard(own[...].astype(F32) + near[...] + away[...] + bias[...])
            unit[...] = one
            scale[...] = size
            low[...] = (one * gain[...] + shift[...]).astype(BF)
            qc[...] = (mul(low[...], cq[...]) + bias_q[...]).astype(BF)

        scaled = head_mask(each, heads, HEAD_DIM ** (-0.5), BF)
        ones = head_mask(each, heads, 1.0, F32)
        real = lax.broadcasted_iota(jnp.int32, (heads * each, padded), 1) < patches
        for item in range(batch):
            start = pl.multiple_of((index * batch + item) * each, each)
            attended[pl.ds(start, each), :] = attend(
                qc[pl.ds(start, each), :],
                kv[item, :, :cols],
                kv[item, :, cols:],
                lambda s: jnp.where(real, s, NEG),
                heads,
                scaled,
                ones,
            )

        @pl.when(index == pl.num_programs(0) - 1)
        def _():
            out[...] = mul_t(attended[...], weight[...])

    bias, gain, shift, bias_q = rows_in
    return call(
        kernel,
        items // batch,
        [whole((rows, width))] * 3
        + [whole((1, width))] * 3
        + [whole((1, cols)), whole((width, cols)), block((batch, padded, 2 * cols)), whole((width, cols))],
        [
            whole((rows, width)),
            whole((rows, 1)),
            whole((rows, width)),
            whole((rows, cols)),
            whole((rows, cols)),
            whole((rows, width)),
        ],
        [
            shaped((rows, width), F32),
            shaped((rows, 1), F32),
            shaped((rows, width), BF),
            shaped((rows, cols), BF),
            shaped((rows, cols), BF),
            shaped((rows, width), F32),
        ],
        flops=2 * rows * cols * padded * heads * 2,
        moved=rows * width * 20 + 4 * items * padded * cols,
    )(own, near, away, bias, gain, shift, bias_q, cq, keys_values, weight)


def feed_forward(flag, unit, near, away, rows_in, w_in, b_in, w_out, chunk):
    rows, width = unit.shape
    hidden = w_in.shape[1]

    def kernel(flag, unit, near, away, gain0, shift0, bias, gain1, shift1, w_in, b_in, w_out, z, z_low, unit2, scale2, act, slope, out):
        @pl.when(pl.program_id(0) == 0)
        def _():
            after = unit[...] * gain0[...] + shift0[...]
            one, size = standard(after + near[...] + away[...] + bias[...])
            unit2[...] = one
            scale2[...] = size
            z[...] = jnp.where(flag[0] == 0, one * gain1[...] + shift1[...], after)
            z_low[...] = z[...].astype(BF)
            out[...] = jnp.zeros_like(out)

        for half in range(2):
            span = slice(half * rows // 2, (half + 1) * rows // 2)
            u = mul(z_low[span], w_in[...]) + b_in[...]
            share = 0.5 + 0.5 * lax.erf(u * math.sqrt(0.5))
            act_half = (u * share).astype(BF)
            act[span] = act_half
            slope[span] = share + u * (jnp.exp(-0.5 * u * u) * (1.0 / math.sqrt(2.0 * math.pi)))
            out[span] += mul_t(act_half, w_out[...])

    row = whole((1, width))
    return call(
        kernel,
        hidden // chunk,
        [pl.BlockSpec(memory_space=pltpu.SMEM)]
        + [whole((rows, width))] * 3
        + [row] * 5
        + [column((width, chunk)), column((1, chunk)), column((width, chunk))],
        [
            whole((rows, width)),
            whole((rows, width)),
            whole((rows, width)),
            whole((rows, 1)),
            column((rows, chunk)),
            column((rows, chunk)),
            whole((rows, width)),
        ],
        [
            shaped((rows, width), F32),
            shaped((rows, width), BF),
            shaped((rows, width), F32),
            shaped((rows, 1), F32),
            shaped((rows, hidden), BF),
            shaped((rows, hidden), F32),
            shaped((rows, width), F32),
        ],
        flops=4 * rows * hidden * width,
        moved=rows * width * 26 + rows * hidden * 6 + width * hidden * 4,
    )(flag, unit, near, away, *rows_in, w_in, b_in, w_out)


def feed_back(z, near, away, cotangent, rows_in, slope, w_in, w_out, chunk):
    rows, width = z.shape
    hidden = w_in.shape[1]

    def kernel(z, near, away, cot, bias, gain, shift, slope, w_in, w_out, result, grad_v, grad_u, grad_pre, out, sums, sum_pre):
        @pl.when(pl.program_id(0) == 0)
        def _():
            one, size = standard(z[...] + near[...] + away[...] + bias[...])
            dy = cot[...]
            result[...] = (one * gain[...] + shift[...]).astype(BF)
            grad_v[...] = norm_back(dy, one, size, gain[...])
            grad_u[...] = grad_v[...].astype(BF)
            sums[0:1] = total_rows(dy * one)
            sums[1:2] = total_rows(dy)
            sums[2:3] = total_rows(grad_u[...].astype(F32))
            out[...] = jnp.zeros_like(out)

        for half in range(2):
            span = slice(half * rows // 2, (half + 1) * rows // 2)
            pre = (mul(grad_u[span], w_out[...]) * slope[span]).astype(BF)
            grad_pre[span] = pre
            out[span] += mul_t(pre, w_in[...])
        sum_pre[...] = total_rows(grad_pre[...].astype(F32))

    row = whole((1, width))
    return call(
        kernel,
        hidden // chunk,
        [whole((rows, width))] * 4
        + [row] * 3
        + [column((rows, chunk)), column((width, chunk)), column((width, chunk))],
        [
            whole((rows, width)),
            whole((rows, width)),
            whole((rows, width)),
            column((rows, chunk)),
            whole((rows, width)),
            whole((8, width)),
            column((1, chunk)),
        ],
        [
            shaped((rows, width), BF),
            shaped((rows, width), F32),
            shaped((rows, width), BF),
            shaped((rows, hidden), BF),
            shaped((rows, width), F32),
            shaped((8, width), F32),
            shaped((1, hidden), F32),
        ],
        flops=4 * rows * hidden * width,
        moved=rows * width * 28 + rows * hidden * 6 + width * hidden * 4,
    )(z, near, away, cotangent, *rows_in, slope, w_in, w_out)


def cross_back(flag, grad_v, near, away, unit2, scale2, gain, qc, keys_values, weight, cq, items, batch, patches):
    rows, width = grad_v.shape
    cols = weight.shape[1]
    heads, each = cols // HEAD_DIM, rows // items
    padded = keys_values.shape[1]

    def kernel(flag, grad_v, near, away, unit2, scale2, gain, qc, kv, weight, cq, after, mix, grad_qc, grad_kv, out, sums, sums_c, grad_att):
        index = pl.program_id(0)

        @pl.when(index == 0)
        def _():
            dz = grad_v[...] + near[...] + away[...]
            mine = flag[0] == 0
            used = jnp.where(mine, dz, 0.0)
            two = norm_back(used, unit2[...], scale2[...], gain[...])
            after[...] = jnp.where(mine, two, dz)
            mix[...] = two.astype(BF)
            grad_att[...] = mul(mix[...], weight[...]).astype(BF)
            sums[0:1] = total_rows(used * unit2[...])
            sums[1:2] = total_rows(used)
            sums[2:3] = total_rows(mix[...].astype(F32))
            sums_c[...] = jnp.zeros_like(sums_c)

        root = HEAD_DIM ** (-0.5)
        scaled = head_mask(each, heads, root, BF)
        plain = head_mask(each, heads, 1.0, BF)
        ones = head_mask(each, heads, 1.0, F32)
        real = lax.broadcasted_iota(jnp.int32, (heads * each, padded), 1) < patches
        for item in range(batch):
            start = pl.multiple_of((index * batch + item) * each, each)
            dq, dk, dv = attend_back(
                qc[pl.ds(start, each), :],
                kv[item, :, :cols],
                kv[item, :, cols:],
                grad_att[pl.ds(start, each), :],
                lambda s: jnp.where(real, s, NEG),
                heads,
                scaled,
                plain,
                ones,
            )
            grad_qc[pl.ds(start, each), :] = dq.astype(BF)
            dk, dv = dk.astype(BF), dv.astype(BF)
            grad_kv[item, :, :cols] = dk
            grad_kv[item, :, cols:] = dv
            sums_c[1:2] += total_rows(dk.astype(F32))
            sums_c[2:3] += total_rows(dv.astype(F32))

        @pl.when(index == pl.num_programs(0) - 1)
        def _():
            out[...] = mul_t(grad_qc[...], cq[...])
            sums_c[0:1] = total_rows(grad_qc[...].astype(F32))

    return call(
        kernel,
        items // batch,
        [pl.BlockSpec(memory_space=pltpu.SMEM)]
        + [whole((rows, width))] * 4
        + [
            whole((rows, 1)),
            whole((1, width)),
            whole((rows, cols)),
            block((batch, padded, 2 * cols)),
            whole((width, cols)),
            whole((width, cols)),
        ],
        [
            whole((rows, width)),
            whole((rows, width)),
            whole((rows, cols)),
            block((batch, padded, 2 * cols)),
            whole((rows, width)),
            whole((8, width)),
            whole((8, cols)),
        ],
        [
            shaped((rows, width), F32),
            shaped((rows, width), BF),
            shaped((rows, cols), BF),
            shaped((items, padded, 2 * cols), BF),
            shaped((rows, width), F32),
            shaped((8, width), F32),
            shaped((8, cols), F32),
        ],
        scratch=[pltpu.VMEM((rows, cols), BF)],
        flops=2 * rows * cols * padded * heads * 5,
        moved=rows * width * 26 + 8 * items * padded * cols,
    )(flag, grad_v, near, away, unit2, scale2, gain, qc, keys_values, weight, cq)


def self_back(after, near, away, unit, scale, gain, q, kv, kv_far, allowed, weight, w_qkv, items, batch):
    rows, width = after.shape
    cols = weight.shape[1]
    heads, each = cols // HEAD_DIM, rows // items

    def kernel(after, near, away, unit, scale, gain, q, kv, kv_far, allowed, weight, w_qkv, grad_one, mix, grad_near, grad_away, out, out_far, sums, sums_c, grad_att):
        index = pl.program_id(0)

        @pl.when(index == 0)
        def _():
            grad = after[...] + near[...] + away[...]
            grad_one[...] = norm_back(grad, unit[...], scale[...], gain[...])
            mix[...] = grad_one[...].astype(BF)
            grad_att[...] = mul(mix[...], weight[...]).astype(BF)
            sums[0:1] = total_rows(grad * unit[...])
            sums[1:2] = total_rows(grad)
            sums[2:3] = total_rows(mix[...].astype(F32))

        scaled = head_mask(each, heads, HEAD_DIM ** (-0.5), BF)
        plain = head_mask(each, heads, 1.0, BF)
        ones = head_mask(each, heads, 1.0, F32)
        for item in range(batch):
            span = slice(item * each, (item + 1) * each)
            start = pl.multiple_of((index * batch + item) * each, each)
            keys = jnp.concatenate([kv[span, :cols], kv_far[span, :cols]], axis=0)
            values = jnp.concatenate([kv[span, cols:], kv_far[span, cols:]], axis=0)
            seen = jnp.concatenate([allowed[item]] * heads, axis=0) > 0
            dq, dk, dv = attend_back(
                q[span],
                keys,
                values,
                grad_att[pl.ds(start, each), :],
                lambda s: jnp.where(seen, s, NEG),
                heads,
                scaled,
                plain,
                ones,
            )
            grad_near[pl.ds(start, each), :cols] = dq.astype(BF)
            grad_near[pl.ds(start, each), cols : 2 * cols] = dk[:each].astype(BF)
            grad_near[pl.ds(start, each), 2 * cols :] = dv[:each].astype(BF)
            grad_away[pl.ds(start, each), :cols] = dk[each:].astype(BF)
            grad_away[pl.ds(start, each), cols:] = dv[each:].astype(BF)

        @pl.when(index == pl.num_programs(0) - 1)
        def _():
            out[...] = mul_t(grad_near[...], w_qkv[...])
            out_far[...] = mul_t(grad_away[...], w_qkv[:, cols:])
            sums_c[0:1] = total_rows(grad_near[...].astype(F32))
            sums_c[1:2, cols:] = total_rows(grad_away[...].astype(F32))

    part = batch * each
    return call(
        kernel,
        items // batch,
        [whole((rows, width))] * 4
        + [
            whole((rows, 1)),
            whole((1, width)),
            block((part, cols)),
            block((part, 2 * cols)),
            block((part, 2 * cols)),
            block((batch, each, 2 * each)),
            whole((width, cols)),
            whole((width, 3 * cols)),
        ],
        [
            whole((rows, width)),
            whole((rows, width)),
            whole((rows, 3 * cols)),
            whole((rows, 2 * cols)),
            whole((rows, width)),
            whole((rows, width)),
            whole((8, width)),
            whole((8, 3 * cols)),
        ],
        [
            shaped((rows, width), F32),
            shaped((rows, width), BF),
            shaped((rows, 3 * cols), BF),
            shaped((rows, 2 * cols), BF),
            shaped((rows, width), F32),
            shaped((rows, width), F32),
            shaped((8, width), F32),
            shaped((8, 3 * cols), F32),
        ],
        scratch=[pltpu.VMEM((rows, cols), BF)],
        flops=2 * rows * cols * width * 9,
        moved=rows * width * 32 + rows * cols * 20,
    )(after, near, away, unit, scale, gain, q, kv, kv_far, allowed, weight, w_qkv)


def visible(stream, segments, modes):
    same_caption = segments[:, :, None] == segments[:, None, :]
    own = jnp.logical_or(stream == 0, same_caption)
    far = jnp.where(stream == 0, modes == 2, modes >= 1)[:, None, None]
    return jnp.concatenate([own, jnp.broadcast_to(far, own.shape)], axis=2).astype(F32)


def body(
    hidden,
    features,
    segments,
    modes,
    w_qkv,
    self_bias,
    self_out,
    cross_q,
    cross_kv,
    cross_bias,
    cross_out,
    gains,
    shifts,
    feat_gain,
    feat_shift,
    ffn_in,
    ffn_bias_in,
    ffn_out,
    ffn_bias_out,
    cotangent,
):
    stream = lax.axis_index("stream")
    head_index = lax.axis_index("heads")
    query_mask = (stream == 0).astype(F32)
    text_mask = 1.0 - query_mask
    lead_mask = (head_index == 0).astype(F32)
    items, _, each, width = hidden.shape
    rows = items * each
    half = rows // 2
    cols = w_qkv.shape[2]
    hidden_cols = ffn_in.shape[2]
    patches, feat_width = features.shape[1:]
    padded = (patches + 7) // 8 * 8
    col_start = head_index * cols
    hidden_start = head_index * hidden_cols
    flag = stream.astype(jnp.int32).reshape(1)

    three = [slice(i * cols, (i + 1) * cols) for i in range(3)]
    qkv_all = gather_items(pair_streams(jnp.concatenate([w_qkv[0], w_qkv[1], w_qkv[2]], axis=1)))
    own = hidden.reshape(rows, width)
    my_half = lax.dynamic_slice_in_dim(own, head_index * half, half, 0)
    far_half = partner(my_half, "stream", 0)
    far_other = partner(far_half, "heads", 0)
    far = jnp.where(
        head_index == 0,
        jnp.concatenate([far_half, far_other], axis=0),
        jnp.concatenate([far_other, far_half], axis=0),
    )
    kv_all = gather_items(pair_streams(jnp.concatenate([cross_kv[0], cross_kv[1]], axis=1)))
    rest_all = gather_items(
        pair_streams(jnp.concatenate([self_out.T, cross_q, cross_out.T], axis=1))
    )
    self_out_t, cross_q_all, cross_out_t = (rest_all[:, one] for one in three)
    ffn_all = lax.all_gather(
        jnp.concatenate([ffn_in[0], ffn_out[0].T], axis=1), "items", axis=0, tiled=True
    )
    inner, outer_t = ffn_all[:, :hidden_cols], ffn_all[:, hidden_cols:]

    def my_cols(vector):
        return lax.dynamic_slice_in_dim(vector, col_start, cols, 0)

    def row(vector):
        return vector.reshape(1, -1)

    none = jnp.zeros((cols,), F32)
    bias_qkv = row(jnp.concatenate([my_cols(self_bias[0]), none, my_cols(self_bias[1])]))
    bias_kv = row(jnp.concatenate([none, my_cols(cross_bias[1])]))
    gain_ffn = row(lax.dynamic_index_in_dim(gains, 2 + stream, 0, keepdims=False))
    shift_ffn = row(lax.dynamic_index_in_dim(shifts, 2 + stream, 0, keepdims=False))
    bias_in = row(
        lax.dynamic_slice_in_dim(
            lax.dynamic_index_in_dim(ffn_bias_in, stream, 0, keepdims=False),
            hidden_start,
            hidden_cols,
            0,
        )
    )
    bias_out = row(lax.dynamic_index_in_dim(ffn_bias_out, stream, 0, keepdims=False))

    def swap(part):
        return partner(part, "heads", 0)

    feat_norm = feature_norm(features, row(feat_gain), row(feat_shift), padded)
    feat_rows = feat_norm.reshape(items * padded, feat_width)
    q, kv, kv_far = project(own, far, qkv_all, bias_qkv)
    allowed = visible(stream, segments, modes)
    attended, part = self_attention(q, kv, kv_far, allowed, self_out_t, items, 4)
    keys_values = (mul(feat_rows, kv_all) + bias_kv).astype(BF).reshape(items, padded, 2 * cols)
    unit_one, scale_one, after_low, qc, attended_c, part_c = cross_attention(
        own,
        part,
        swap(part),
        (row(self_bias[2]), row(gains[0]), row(shifts[0]), row(my_cols(cross_bias[0]))),
        cross_q_all,
        keys_values,
        cross_out_t,
        items,
        2,
        patches,
    )
    z, z_low, unit_two, scale_two, activated, slope, part_f = feed_forward(
        flag,
        unit_one,
        part_c,
        swap(part_c),
        (row(gains[0]), row(shifts[0]), row(cross_bias[2]), row(gains[1]), row(shifts[1])),
        inner,
        bias_in,
        outer_t,
        256,
    )

    output, grad_three, grad_u, grad_pre, part_z, sums_three, sum_pre = feed_back(
        z,
        part_f,
        swap(part_f),
        cotangent.reshape(rows, width),
        (bias_out, gain_ffn, shift_ffn),
        slope,
        inner,
        outer_t,
        256,
    )
    away_z = swap(part_z)
    ffn_grad = jnp.concatenate(
        [t_mul(z_low, grad_pre).astype(BF), t_mul(grad_u, activated).astype(BF)], axis=1
    )
    ffn_red = lax.psum_scatter(ffn_grad, "items", scatter_dimension=0, tiled=True).astype(F32)
    grad_after, mix_c, grad_qc, grad_kv, part_a, sums_two, sums_cross = cross_back(
        flag,
        grad_three,
        part_z,
        away_z,
        unit_two,
        scale_two,
        row(gains[1]),
        qc,
        keys_values,
        cross_out_t,
        cross_q_all,
        items,
        2,
        patches,
    )
    away_a = swap(part_a)
    cross_grad = jnp.concatenate(
        [t_mul(after_low, grad_qc).astype(BF), t_mul(mix_c, attended_c).astype(BF)], axis=1
    )
    kv_grad = t_mul(feat_rows, grad_kv.reshape(items * padded, 2 * cols))
    grad_one, mix, grad_near, grad_away, part_h, part_far, sums_one, sums_self = self_back(
        grad_after,
        part_a,
        away_a,
        unit_one,
        scale_one,
        row(gains[0]),
        q,
        kv,
        kv_far,
        allowed,
        self_out_t,
        qkv_all,
        items,
        4,
    )
    self_grad = jnp.concatenate(
        [
            t_mul(own, grad_near[:, :cols]).astype(BF),
            (t_mul(own, grad_near[:, cols:]) + t_mul(far, grad_away)).astype(BF),
            t_mul(mix, attended).astype(BF),
        ],
        axis=1,
    )

    def mine(part):
        return lax.dynamic_slice_in_dim(part, head_index * half, half, 0)

    def theirs(part):
        return lax.dynamic_slice_in_dim(part, (1 - head_index) * half, half, 0)

    far_sum = mine(part_far) + swap(theirs(part_far))
    from_far = partner(far_sum.astype(BF), "stream", 0).astype(F32)
    in_half = mine(grad_one) + (mine(part_h) + swap(theirs(part_h))) + from_far
    in_other = swap(in_half)
    grad_input = jnp.where(
        head_index == 0,
        jnp.concatenate([in_half, in_other], axis=0),
        jnp.concatenate([in_other, in_half], axis=0),
    )

    cross_red = scatter_both(cross_grad)
    kv_red = scatter_both(kv_grad.astype(BF))
    self_red = scatter_both(self_grad)

    dot_w = jnp.sum(kv_grad * kv_all.astype(F32), axis=1)
    feat_shift_grad = jnp.sum(
        kv_all.astype(F32) * jnp.concatenate([sums_cross[1], sums_cross[2]])[None], axis=1
    )
    feat_gain_grad = (dot_w - feat_shift * feat_shift_grad) / feat_gain

    bias_q_sum, _, bias_v_sum = (sums_self[0, one] for one in three)
    bias_v_sum = bias_v_sum + sums_self[1, three[2]]
    self_bias_grad = jnp.stack(
        [
            spread(bias_q_sum, col_start, width),
            spread(bias_v_sum, col_start, width),
            lead_mask * sums_one[2],
        ]
    )
    cross_bias_grad = jnp.stack(
        [
            spread(sums_cross[0], col_start, width),
            spread(sums_cross[2], col_start, width),
            lead_mask * sums_two[2],
        ]
    )
    gains_grad = lead_mask * jnp.stack(
        [sums_one[0], sums_two[0], query_mask * sums_three[0], text_mask * sums_three[0]]
    )
    shifts_grad = lead_mask * jnp.stack(
        [sums_one[1], sums_two[1], query_mask * sums_three[1], text_mask * sums_three[1]]
    )
    bias_in_full = spread(sum_pre[0], hidden_start, ffn_bias_in.shape[1])
    ffn_bias_in_grad = jnp.stack([query_mask * bias_in_full, text_mask * bias_in_full])
    ffn_bias_out_grad = lead_mask * jnp.stack(
        [query_mask * sums_three[2], text_mask * sums_three[2]]
    )
    (
        self_bias_sum,
        cross_bias_sum,
        gains_sum,
        shifts_sum,
        feat_gain_sum,
        feat_shift_sum,
        bias_in_sum,
        bias_out_sum,
    ) = all_totals(
        (
            self_bias_grad,
            cross_bias_grad,
            gains_grad,
            shifts_grad,
            feat_gain_grad,
            feat_shift_grad,
            ffn_bias_in_grad,
            ffn_bias_out_grad,
        )
    )
    return (
        output.reshape(items, 1, each, width),
        grad_input.reshape(items, 1, each, width),
        jnp.stack([self_red[:, one] for one in three]),
        self_bias_sum,
        self_red[:, 3 * cols :].T,
        cross_red[:, three[0]],
        jnp.stack([kv_red[:, one] for one in three[:2]]),
        cross_bias_sum,
        cross_red[:, three[1]].T,
        gains_sum,
        shifts_sum,
        feat_gain_sum,
        feat_shift_sum,
        ffn_red[:, :hidden_cols][None],
        bias_in_sum,
        ffn_red[:, hidden_cols:].T[None],
        bias_out_sum,
    )

def solution(mesh):
    placed = (
        P("items", "stream", None, None),
        P("items", None, None),
        P("items", None),
        P("items"),
        P(None, ("items", "stream"), "heads"),
        P(),
        P("heads", ("items", "stream")),
        P(("items", "stream"), "heads"),
        P(None, ("items", "stream"), "heads"),
        P(),
        P("heads", ("items", "stream")),
        P(),
        P(),
        P(),
        P(),
        P("stream", "items", "heads"),
        P(),
        P("stream", "heads", "items"),
        P(),
        P("items", "stream", None, None),
    )
    return jax.shard_map(
        body,
        mesh=mesh,
        in_specs=placed,
        out_specs=(
            P("items", "stream", None, None),
            P("items", "stream", None, None),
            P(None, ("items", "stream"), "heads"),
            P(),
            P("heads", ("items", "stream")),
            P(("items", "stream"), "heads"),
            P(None, ("items", "stream"), "heads"),
            P(),
            P("heads", ("items", "stream")),
            P(),
            P(),
            P(),
            P(),
            P("stream", "items", "heads"),
            P(),
            P("stream", "heads", "items"),
            P(),
        ),
        check_vma=False,
    )
```

```python
import math

import jax
import jax.numpy as jnp
from jax import lax
from jax.experimental import pallas as pl
from jax.experimental.pallas import tpu as pltpu
from jax.sharding import PartitionSpec as P

HEAD_DIM = 64
EPS = 1e-06
NEG = -1e30
BF = jnp.bfloat16
F32 = jnp.float32


def partner(shard, axis, distance):
    return lax.ppermute(shard, axis, [(i, i ^ 1 << distance) for i in range(lax.axis_size(axis))])


def after(value, *earlier):
    return lax.optimization_barrier((value,) + earlier)[0]


def ring_of(count):
    return list(range(0, count, 2)) + list(range(1, count, 2))[::-1]


def ring_place(count):
    order = ring_of(count)
    places = [order.index(i) for i in range(count)]
    return order, jnp.asarray(places, jnp.int32)[lax.axis_index("items")]


def shift_ring(shard, order, step):
    count = len(order)
    return lax.ppermute(
        shard, "items", [(order[i], order[(i + step) % count]) for i in range(count)]
    )


def gather_items(shard):
    count = lax.axis_size("items")
    order, place = ring_place(count)
    table = jnp.asarray(order, jnp.int32)
    whole = jnp.zeros((count,) + shard.shape, shard.dtype)

    def put(whole, piece, distance):
        return lax.dynamic_update_index_in_dim(whole, piece, table[(place + distance) % count], 0)

    whole = put(whole, shard, 0)
    up = down = shard
    arrived = []
    for hop in range(1, count // 2 + 1):
        up = shift_ring(up, order, 1)
        arrived.append(up)
        whole = put(whole, up, count - hop)
        if hop <= (count - 1) // 2:
            down = shift_ring(down, order, -1)
            whole = put(whole, down, hop)
    return whole, arrived


def by_stream(own, other, axis):
    first = lax.axis_index("stream") == 0
    return jnp.where(
        first, jnp.stack([own, other], axis=axis), jnp.stack([other, own], axis=axis)
    )


def gather_streams(pieces, *earlier):
    if earlier:
        pieces = after(pieces, *earlier)
    other = partner(pieces, "stream", 0)
    both = by_stream(pieces, other, 1)
    return both.reshape((both.shape[0] * both.shape[1] * both.shape[2], both.shape[3])), other


def together(sends):
    values = lax.optimization_barrier(tuple(value for value, _ in sends))
    return lax.optimization_barrier(tuple(move(one) for one, (_, move) in zip(values, sends)))


def at(pieces):
    return lambda which: lax.dynamic_index_in_dim(pieces, which, 0, keepdims=False)


def at_stream(pieces, outer):
    stream = lax.axis_index("stream")

    def read(which):
        start = (stream, which) if outer else (which, stream)
        found = lax.dynamic_slice(pieces, start + (0, 0), (1, 1) + pieces.shape[2:])
        return found.reshape(pieces.shape[2:])

    return read


class Scatter:
    def __init__(self, groups, axis):
        self.groups, self.axis = groups, axis
        self.count = lax.axis_size("items")
        self.order, self.place = ring_place(self.count)
        self.hop = self.count // 2
        self.up = self.down = None

    def piece(self, distance, gate=None):
        which = jnp.asarray(self.order, jnp.int32)[(self.place + distance) % self.count]
        if gate is not None:
            which = after(which, gate)
        parts = [sum(read(which).astype(F32) for read in group) for group in self.groups]
        return jnp.concatenate(parts, axis=self.axis)

    def sends(self, gate=None):
        own = self.piece(self.hop, gate)
        own = own if self.up is None else own + self.up.astype(F32)
        result = [(own.astype(BF), lambda one: shift_ring(one, self.order, 1))]
        if self.hop <= (self.count - 1) // 2:
            own = self.piece(self.count - self.hop, gate)
            own = own if self.down is None else own + self.down.astype(F32)
            result.append((own.astype(BF), lambda one: shift_ring(one, self.order, -1)))
        return result

    def take(self, arrivals):
        self.up = arrivals[0]
        if len(arrivals) > 1:
            self.down = arrivals[1]
        self.hop -= 1
        return arrivals[0]

    def step(self, gate=None):
        return self.take(together(self.sends(gate)))

    def result(self):
        return self.piece(0) + self.up.astype(F32) + self.down.astype(F32)


def halves(total):
    count = lax.axis_size("items")
    rows = total.shape[0] // (2 * count)
    parts = total.reshape((count, 2, rows, total.shape[1]))
    stream = lax.axis_index("stream")
    away = lax.dynamic_index_in_dim(parts, 1 - stream, 1, keepdims=False)
    return parts, away


def over(axis, distance=0):
    return lambda one: partner(one, axis, distance)


def mul(left, right):
    return jnp.dot(left, right, preferred_element_type=F32)


def mul_t(left, right):
    return lax.dot_general(left, right, (((1,), (1,)), ((), ())), preferred_element_type=F32)


def t_mul(left, right):
    return lax.dot_general(left, right, (((0,), (0,)), ((), ())), preferred_element_type=F32)


def standard(rows):
    center = rows - jnp.mean(rows, axis=-1, keepdims=True)
    scale = lax.rsqrt(jnp.mean(center * center, axis=-1, keepdims=True) + EPS)
    return center * scale, scale


def norm_back(grad, unit, scale, gain):
    inner = grad * gain
    return scale * (
        inner
        - jnp.mean(inner, axis=-1, keepdims=True)
        - unit * jnp.mean(inner * unit, axis=-1, keepdims=True)
    )


def pair_sum(near, away):
    return near[...].astype(F32) + away[...].astype(F32)


def total_rows(rows):
    return jnp.sum(rows, axis=0, keepdims=True)


def head_mask(rows, heads, value, dtype):
    row = lax.broadcasted_iota(jnp.int32, (heads * rows, heads * HEAD_DIM), 0) // rows
    col = lax.broadcasted_iota(jnp.int32, (heads * rows, heads * HEAD_DIM), 1) // HEAD_DIM
    return jnp.where(row == col, value, 0.0).astype(dtype)


def stack_heads(rows, heads, mask):
    return jnp.concatenate([rows] * heads, axis=0) * mask


def fold_heads(stacked, heads, mask):
    rows = stacked.shape[0] // heads
    stacked = stacked * mask
    result = stacked[:rows]
    for head in range(1, heads):
        result = result + stacked[head * rows : (head + 1) * rows]
    return result


def softmax(scores):
    power = jnp.exp(scores - jnp.max(scores, axis=-1, keepdims=True))
    return power * (1.0 / jnp.sum(power, axis=-1, keepdims=True))


def attend(queries, keys, values, hide, heads, scaled_mask, out_mask):
    scores = hide(mul_t(stack_heads(queries, heads, scaled_mask), keys))
    weights = softmax(scores).astype(BF)
    return fold_heads(mul(weights, values), heads, out_mask).astype(BF)


def attend_back(queries, keys, values, grad, hide, heads, scaled_mask, plain_mask, out_mask):
    queries = stack_heads(queries, heads, scaled_mask)
    grad = stack_heads(grad, heads, plain_mask)
    weights = softmax(hide(mul_t(queries, keys)))
    grad_weights = mul_t(grad, values)
    grad_values = t_mul(weights.astype(BF), grad)
    delta = jnp.sum(grad_weights * weights, axis=-1, keepdims=True)
    grad_scores = (weights * (grad_weights - delta)).astype(BF)
    grad_queries = fold_heads(mul(grad_scores, keys), heads, out_mask) * HEAD_DIM ** (-0.5)
    return grad_queries, t_mul(grad_scores, queries), grad_values


def whole(shape):
    return pl.BlockSpec(shape, lambda i: (0,) * len(shape))


def block(shape):
    return pl.BlockSpec(shape, lambda i: (i,) + (0,) * (len(shape) - 1))


def column(shape, first=0):
    return pl.BlockSpec(shape, lambda i: (0, i + first))


def shaped(shape, dtype):
    return jax.ShapeDtypeStruct(shape, dtype)


def call(kernel, grid, in_specs, out_specs, out_shape, scratch=(), flops=0, moved=0):
    return pl.pallas_call(
        kernel,
        grid=(grid,),
        in_specs=in_specs,
        out_specs=out_specs,
        out_shape=out_shape,
        scratch_shapes=list(scratch),
        compiler_params=pltpu.CompilerParams(
            dimension_semantics=("arbitrary",), vmem_limit_bytes=56 << 20
        ),
        cost_estimate=pl.CostEstimate(flops=flops, bytes_accessed=moved, transcendentals=0),
    )


def feature_norm(features, gain, shift, padded, gates):
    items, patches, width = features.shape
    each = items // len(gates)
    result = None

    def kernel(feat, gain, shift, *refs):
        out = refs[-1]
        unit, _ = standard(feat[0].astype(F32))
        out[0, :patches] = (unit * gain[...] + shift[...]).astype(BF)
        out[0, patches:] = jnp.zeros((padded - patches, width), BF)

    for number, gate in enumerate(gates):
        begin = number * each

        def at(i, begin=begin):
            return (i + begin, 0, 0)

        prior = [] if result is None else [result]
        result = pl.pallas_call(
            kernel,
            grid=(each,),
            in_specs=[pl.BlockSpec((1, patches, width), at), whole((1, width)), whole((1, width))]
            + [pl.BlockSpec(memory_space=pl.ANY)] * len(prior),
            out_specs=pl.BlockSpec((1, padded, width), at),
            out_shape=shaped((items, padded, width), BF),
            input_output_aliases={3: 0} if prior else {},
            compiler_params=pltpu.CompilerParams(
                dimension_semantics=("arbitrary",), vmem_limit_bytes=56 << 20
            ),
            cost_estimate=pl.CostEstimate(
                flops=0, bytes_accessed=4 * each * patches * width, transcendentals=0
            ),
        )(features, after(gain, gate) if gate is not None else gain, shift, *prior)
    return result


def project(own, far, weight, bias):
    rows, width = own.shape
    cols = weight.shape[1]
    head_cols = cols // 3
    step = rows // 4

    def kernel(own, far, weight, bias, q, kv, kv_far):
        near = mul(own[...], weight[...]) + bias[...]
        q[...] = near[:, :head_cols].astype(BF)
        kv[...] = near[:, head_cols:].astype(BF)
        kv_far[...] = (mul(far[...], weight[:, head_cols:]) + bias[:, head_cols:]).astype(BF)

    return call(
        kernel,
        4,
        [block((step, width)), block((step, width)), whole((width, cols)), whole((1, cols))],
        [block((step, head_cols)), block((step, 2 * head_cols)), block((step, 2 * head_cols))],
        [shaped((rows, head_cols), BF)] + [shaped((rows, 2 * head_cols), BF)] * 2,
        flops=10 * rows * width * head_cols,
        moved=4 * rows * width + 2 * width * cols,
    )(own, far, weight, bias)


def self_attention(q, kv, kv_far, allowed, weight, items, batch):
    rows, cols = q.shape
    heads, each = cols // HEAD_DIM, rows // items
    width = weight.shape[0]

    def kernel(q, kv, kv_far, allowed, weight, attended, out):
        index = pl.program_id(0)
        scaled = head_mask(each, heads, HEAD_DIM ** (-0.5), BF)
        ones = head_mask(each, heads, 1.0, F32)
        for item in range(batch):
            span = slice(item * each, (item + 1) * each)
            keys = jnp.concatenate([kv[span, :cols], kv_far[span, :cols]], axis=0)
            values = jnp.concatenate([kv[span, cols:], kv_far[span, cols:]], axis=0)
            seen = jnp.concatenate([allowed[item]] * heads, axis=0) > 0
            result = attend(
                q[span], keys, values, lambda s: jnp.where(seen, s, NEG), heads, scaled, ones
            )
            start = pl.multiple_of((index * batch + item) * each, each)
            attended[pl.ds(start, each), :] = result

        @pl.when(index == pl.num_programs(0) - 1)
        def _():
            out[...] = mul_t(attended[...], weight[...]).astype(BF)

    part = batch * each
    return call(
        kernel,
        items // batch,
        [
            block((part, cols)),
            block((part, 2 * cols)),
            block((part, 2 * cols)),
            block((batch, each, 2 * each)),
            whole((width, cols)),
        ],
        [whole((rows, cols)), whole((rows, width))],
        [shaped((rows, cols), BF), shaped((rows, width), BF)],
        flops=2 * rows * cols * width * 3,
        moved=rows * cols * 14 + rows * width * 4,
    )(q, kv, kv_far, allowed, weight)


def cross_attention(own, near, away, rows_in, cq, keys_values, weight, items, batch, patches):
    rows, width = own.shape
    cols = weight.shape[1]
    heads, each = cols // HEAD_DIM, rows // items
    padded = keys_values.shape[1]

    def kernel(own, near, away, bias, gain, shift, bias_q, cq, kv, weight, unit, scale, low, qc, attended, out):
        index = pl.program_id(0)

        @pl.when(index == 0)
        def _():
            one, size = standard(own[...].astype(F32) + pair_sum(near, away) + bias[...])
            unit[...] = one
            scale[...] = size
            low[...] = (one * gain[...] + shift[...]).astype(BF)
            qc[...] = (mul(low[...], cq[...]) + bias_q[...]).astype(BF)

        scaled = head_mask(each, heads, HEAD_DIM ** (-0.5), BF)
        ones = head_mask(each, heads, 1.0, F32)
        real = lax.broadcasted_iota(jnp.int32, (heads * each, padded), 1) < patches
        for item in range(batch):
            start = pl.multiple_of((index * batch + item) * each, each)
            attended[pl.ds(start, each), :] = attend(
                qc[pl.ds(start, each), :],
                kv[item, :, :cols],
                kv[item, :, cols:],
                lambda s: jnp.where(real, s, NEG),
                heads,
                scaled,
                ones,
            )

        @pl.when(index == pl.num_programs(0) - 1)
        def _():
            out[...] = mul_t(attended[...], weight[...]).astype(BF)

    bias, gain, shift, bias_q = rows_in
    return call(
        kernel,
        items // batch,
        [whole((rows, width))] * 3
        + [whole((1, width))] * 3
        + [whole((1, cols)), whole((width, cols)), block((batch, padded, 2 * cols)), whole((width, cols))],
        [
            whole((rows, width)),
            whole((rows, 1)),
            whole((rows, width)),
            whole((rows, cols)),
            whole((rows, cols)),
            whole((rows, width)),
        ],
        [
            shaped((rows, width), F32),
            shaped((rows, 1), F32),
            shaped((rows, width), BF),
            shaped((rows, cols), BF),
            shaped((rows, cols), BF),
            shaped((rows, width), BF),
        ],
        flops=2 * rows * cols * padded * heads * 2,
        moved=rows * width * 20 + 4 * items * padded * cols,
    )(own, near, away, bias, gain, shift, bias_q, cq, keys_values, weight)


def feed_forward(flag, unit, near, away, rows_in, w_both, b_in, chunk):
    rows, width = unit.shape
    hidden = w_both.shape[1] // 2
    steps = hidden // chunk

    def kernel(flag, unit, near, away, gain0, shift0, bias, gain1, shift1, w_in, b_in, w_out, z, z_low, unit2, scale2, act, slope, part, out):
        @pl.when(pl.program_id(0) == 0)
        def _():
            after = unit[...] * gain0[...] + shift0[...]
            one, size = standard(after + pair_sum(near, away) + bias[...])
            unit2[...] = one
            scale2[...] = size
            z[...] = jnp.where(flag[0] == 0, one * gain1[...] + shift1[...], after)
            z_low[...] = z[...].astype(BF)
            out[...] = jnp.zeros_like(out)

        for half in range(2):
            span = slice(half * rows // 2, (half + 1) * rows // 2)
            u = mul(z_low[span], w_in[...]) + b_in[...]
            share = 0.5 + 0.5 * lax.erf(u * math.sqrt(0.5))
            act_half = (u * share).astype(BF)
            act[span] = act_half
            slope[span] = share + u * (jnp.exp(-0.5 * u * u) * (1.0 / math.sqrt(2.0 * math.pi)))
            out[span] += mul_t(act_half, w_out[...])

        @pl.when(pl.program_id(0) == steps - 1)
        def _():
            part[...] = out[...].astype(BF)

    row = whole((1, width))
    return call(
        kernel,
        steps,
        [pl.BlockSpec(memory_space=pltpu.SMEM)]
        + [whole((rows, width))] * 3
        + [row] * 5
        + [column((width, chunk)), column((1, chunk)), column((width, chunk), steps)],
        [
            whole((rows, width)),
            whole((rows, width)),
            whole((rows, width)),
            whole((rows, 1)),
            column((rows, chunk)),
            column((rows, chunk)),
            whole((rows, width)),
        ],
        [
            shaped((rows, width), F32),
            shaped((rows, width), BF),
            shaped((rows, width), F32),
            shaped((rows, 1), F32),
            shaped((rows, hidden), BF),
            shaped((rows, hidden), F32),
            shaped((rows, width), BF),
        ],
        scratch=[pltpu.VMEM((rows, width), F32)],
        flops=4 * rows * hidden * width,
        moved=rows * width * 26 + rows * hidden * 6 + width * hidden * 4,
    )(flag, unit, near, away, *rows_in, w_both, b_in, w_both)


def feed_back(z, near, away, cotangent, rows_in, slope, w_both, chunk):
    rows, width = z.shape
    hidden = w_both.shape[1] // 2
    steps = hidden // chunk

    def kernel(z, near, away, cot, bias, gain, shift, slope, w_in, w_out, result, grad_v, grad_u, grad_pre, part, sums, sum_pre, out):
        @pl.when(pl.program_id(0) == 0)
        def _():
            one, size = standard(z[...] + pair_sum(near, away) + bias[...])
            dy = cot[...]
            result[...] = (one * gain[...] + shift[...]).astype(BF)
            grad_v[...] = norm_back(dy, one, size, gain[...])
            grad_u[...] = grad_v[...].astype(BF)
            sums[0:1] = total_rows(dy * one)
            sums[1:2] = total_rows(dy)
            sums[2:3] = total_rows(grad_u[...].astype(F32))
            out[...] = jnp.zeros_like(out)

        for half in range(2):
            span = slice(half * rows // 2, (half + 1) * rows // 2)
            pre = (mul(grad_u[span], w_out[...]) * slope[span]).astype(BF)
            grad_pre[span] = pre
            out[span] += mul_t(pre, w_in[...])
        sum_pre[...] = total_rows(grad_pre[...].astype(F32))

        @pl.when(pl.program_id(0) == steps - 1)
        def _():
            part[...] = out[...].astype(BF)

    row = whole((1, width))
    return call(
        kernel,
        steps,
        [whole((rows, width))] * 4
        + [row] * 3
        + [column((rows, chunk)), column((width, chunk)), column((width, chunk), steps)],
        [
            whole((rows, width)),
            whole((rows, width)),
            whole((rows, width)),
            column((rows, chunk)),
            whole((rows, width)),
            whole((8, width)),
            column((1, chunk)),
        ],
        [
            shaped((rows, width), BF),
            shaped((rows, width), F32),
            shaped((rows, width), BF),
            shaped((rows, hidden), BF),
            shaped((rows, width), BF),
            shaped((8, width), F32),
            shaped((1, hidden), F32),
        ],
        scratch=[pltpu.VMEM((rows, width), F32)],
        flops=4 * rows * hidden * width,
        moved=rows * width * 28 + rows * hidden * 6 + width * hidden * 4,
    )(z, near, away, cotangent, *rows_in, slope, w_both, w_both)


def cross_back(flag, grad_v, near, away, unit2, scale2, gain, qc, keys_values, weight, cq, items, batch, patches):
    rows, width = grad_v.shape
    cols = weight.shape[1]
    heads, each = cols // HEAD_DIM, rows // items
    padded = keys_values.shape[1]

    def kernel(flag, grad_v, near, away, unit2, scale2, gain, qc, kv, weight, cq, after, mix, grad_qc, grad_kv, out, sums, sums_c, grad_att):
        index = pl.program_id(0)

        @pl.when(index == 0)
        def _():
            dz = grad_v[...] + pair_sum(near, away)
            mine = flag[0] == 0
            used = jnp.where(mine, dz, 0.0)
            two = norm_back(used, unit2[...], scale2[...], gain[...])
            after[...] = jnp.where(mine, two, dz)
            mix[...] = two.astype(BF)
            grad_att[...] = mul(mix[...], weight[...]).astype(BF)
            sums[0:1] = total_rows(used * unit2[...])
            sums[1:2] = total_rows(used)
            sums[2:3] = total_rows(mix[...].astype(F32))
            sums_c[...] = jnp.zeros_like(sums_c)

        root = HEAD_DIM ** (-0.5)
        scaled = head_mask(each, heads, root, BF)
        plain = head_mask(each, heads, 1.0, BF)
        ones = head_mask(each, heads, 1.0, F32)
        real = lax.broadcasted_iota(jnp.int32, (heads * each, padded), 1) < patches
        for item in range(batch):
            start = pl.multiple_of((index * batch + item) * each, each)
            dq, dk, dv = attend_back(
                qc[pl.ds(start, each), :],
                kv[item, :, :cols],
                kv[item, :, cols:],
                grad_att[pl.ds(start, each), :],
                lambda s: jnp.where(real, s, NEG),
                heads,
                scaled,
                plain,
                ones,
            )
            grad_qc[pl.ds(start, each), :] = dq.astype(BF)
            dk, dv = dk.astype(BF), dv.astype(BF)
            grad_kv[item, :, :cols] = dk
            grad_kv[item, :, cols:] = dv
            sums_c[1:2] += total_rows(dk.astype(F32))
            sums_c[2:3] += total_rows(dv.astype(F32))

        @pl.when(index == pl.num_programs(0) - 1)
        def _():
            out[...] = mul_t(grad_qc[...], cq[...]).astype(BF)
            sums_c[0:1] = total_rows(grad_qc[...].astype(F32))

    return call(
        kernel,
        items // batch,
        [pl.BlockSpec(memory_space=pltpu.SMEM)]
        + [whole((rows, width))] * 4
        + [
            whole((rows, 1)),
            whole((1, width)),
            whole((rows, cols)),
            block((batch, padded, 2 * cols)),
            whole((width, cols)),
            whole((width, cols)),
        ],
        [
            whole((rows, width)),
            whole((rows, width)),
            whole((rows, cols)),
            block((batch, padded, 2 * cols)),
            whole((rows, width)),
            whole((8, width)),
            whole((8, cols)),
        ],
        [
            shaped((rows, width), F32),
            shaped((rows, width), BF),
            shaped((rows, cols), BF),
            shaped((items, padded, 2 * cols), BF),
            shaped((rows, width), BF),
            shaped((8, width), F32),
            shaped((8, cols), F32),
        ],
        scratch=[pltpu.VMEM((rows, cols), BF)],
        flops=2 * rows * cols * padded * heads * 5,
        moved=rows * width * 26 + 8 * items * padded * cols,
    )(flag, grad_v, near, away, unit2, scale2, gain, qc, keys_values, weight, cq)


def self_back(after, near, away, unit, scale, gain, q, kv, kv_far, allowed, weight, w_qkv, own, far, attended, items, batch, shards):
    rows, width = after.shape
    cols = weight.shape[1]
    heads, each = cols // HEAD_DIM, rows // items
    piece = width // shards

    def kernel(after, near, away, unit, scale, gain, q, kv, kv_far, allowed, weight, w_qkv, own, far, attended, grad_one, mix, grad_near, grad_away, both, sums, sums_c, grad_w, grad_att):
        index = pl.program_id(0)

        @pl.when(index == 0)
        def _():
            grad = after[...] + pair_sum(near, away)
            grad_one[...] = norm_back(grad, unit[...], scale[...], gain[...])
            mix[...] = grad_one[...].astype(BF)
            grad_att[...] = mul(mix[...], weight[...]).astype(BF)
            sums[0:1] = total_rows(grad * unit[...])
            sums[1:2] = total_rows(grad)
            sums[2:3] = total_rows(mix[...].astype(F32))

        scaled = head_mask(each, heads, HEAD_DIM ** (-0.5), BF)
        plain = head_mask(each, heads, 1.0, BF)
        ones = head_mask(each, heads, 1.0, F32)
        for item in range(batch):
            span = slice(item * each, (item + 1) * each)
            start = pl.multiple_of((index * batch + item) * each, each)
            keys = jnp.concatenate([kv[span, :cols], kv_far[span, :cols]], axis=0)
            values = jnp.concatenate([kv[span, cols:], kv_far[span, cols:]], axis=0)
            seen = jnp.concatenate([allowed[item]] * heads, axis=0) > 0
            dq, dk, dv = attend_back(
                q[span],
                keys,
                values,
                grad_att[pl.ds(start, each), :],
                lambda s: jnp.where(seen, s, NEG),
                heads,
                scaled,
                plain,
                ones,
            )
            grad_near[pl.ds(start, each), :cols] = dq.astype(BF)
            grad_near[pl.ds(start, each), cols : 2 * cols] = dk[:each].astype(BF)
            grad_near[pl.ds(start, each), 2 * cols :] = dv[:each].astype(BF)
            grad_away[pl.ds(start, each), :cols] = dk[each:].astype(BF)
            grad_away[pl.ds(start, each), cols:] = dv[each:].astype(BF)

        @pl.when(index == pl.num_programs(0) - 1)
        def _():
            both[:, :width] = mul_t(grad_near[...], w_qkv[...]).astype(BF)
            both[:, width:] = mul_t(grad_away[...], w_qkv[:, cols:]).astype(BF)
            for place in range(4):
                span = slice(place * cols, (place + 1) * cols)
                if place == 3:
                    total = t_mul(mix[...], attended[...])
                else:
                    total = t_mul(own[...], grad_near[:, span])
                if place in (1, 2):
                    total = total + t_mul(far[...], grad_away[:, (place - 1) * cols : place * cols])
                total = total.astype(BF)
                for one in range(shards):
                    grad_w[one % 2, one // 2, :, span] = total[one * piece : (one + 1) * piece]
            sums_c[0:1] = total_rows(grad_near[...].astype(F32))
            sums_c[1:2, cols:] = total_rows(grad_away[...].astype(F32))

    part = batch * each
    return call(
        kernel,
        items // batch,
        [whole((rows, width))] * 4
        + [
            whole((rows, 1)),
            whole((1, width)),
            block((part, cols)),
            block((part, 2 * cols)),
            block((part, 2 * cols)),
            block((batch, each, 2 * each)),
            whole((width, cols)),
            whole((width, 3 * cols)),
            whole((rows, width)),
            whole((rows, width)),
            whole((rows, cols)),
        ],
        [
            whole((rows, width)),
            whole((rows, width)),
            whole((rows, 3 * cols)),
            whole((rows, 2 * cols)),
            whole((rows, 2 * width)),
            whole((8, width)),
            whole((8, 3 * cols)),
            whole((2, shards // 2, piece, 4 * cols)),
        ],
        [
            shaped((rows, width), F32),
            shaped((rows, width), BF),
            shaped((rows, 3 * cols), BF),
            shaped((rows, 2 * cols), BF),
            shaped((rows, 2 * width), BF),
            shaped((8, width), F32),
            shaped((8, 3 * cols), F32),
            shaped((2, shards // 2, piece, 4 * cols), BF),
        ],
        scratch=[pltpu.VMEM((rows, cols), BF)],
        flops=2 * rows * cols * width * 9,
        moved=rows * width * 32 + rows * cols * 20,
    )(after, near, away, unit, scale, gain, q, kv, kv_far, allowed, weight, w_qkv, own, far, attended)


def visible(stream, segments, modes):
    same_caption = segments[:, :, None] == segments[:, None, :]
    own = jnp.logical_or(stream == 0, same_caption)
    far = jnp.where(stream == 0, modes == 2, modes >= 1)[:, None, None]
    return jnp.concatenate([own, jnp.broadcast_to(far, own.shape)], axis=2).astype(F32)


def body(
    hidden,
    features,
    segments,
    modes,
    w_qkv,
    self_bias,
    self_out,
    cross_q,
    cross_kv,
    cross_bias,
    cross_out,
    gains,
    shifts,
    feat_gain,
    feat_shift,
    ffn_in,
    ffn_bias_in,
    ffn_out,
    ffn_bias_out,
    cotangent,
):
    stream = lax.axis_index("stream")
    head_index = lax.axis_index("heads")
    items, _, each, width = hidden.shape
    rows = items * each
    half = rows // 2
    cols = w_qkv.shape[2]
    hidden_cols = ffn_in.shape[2]
    patches, feat_width = features.shape[1:]
    padded = (patches + 7) // 8 * 8
    col_start = head_index * cols
    hidden_start = head_index * hidden_cols
    flag = stream.astype(jnp.int32).reshape(1)
    shards = 2 * lax.axis_size("items")
    three = [slice(i * cols, (i + 1) * cols) for i in range(3)]

    part_qkv = jnp.concatenate([w_qkv[0], w_qkv[1], w_qkv[2]], axis=1)
    pair_qkv = by_stream(part_qkv, partner(part_qkv, "stream", 0), 0)
    qkv_all, arrived_qkv = gather_items(pair_qkv)
    qkv_all = qkv_all.reshape(width, 3 * cols)
    own = hidden.reshape(rows, width)
    my_half = lax.dynamic_slice_in_dim(own, head_index * half, half, 0)
    far_half = partner(my_half, "stream", 0)
    far_other = partner(far_half, "heads", 0)
    far = jnp.where(
        head_index == 0,
        jnp.concatenate([far_half, far_other], axis=0),
        jnp.concatenate([far_other, far_half], axis=0),
    )
    later_out = after(self_out, part_qkv)
    rest, _ = gather_items(
        jnp.concatenate([later_out.T, cross_q, cross_out.T, cross_kv[0], cross_kv[1]], axis=0)
    )
    piece = cross_q.shape[0]
    kv_piece = cross_kv.shape[1]
    self_out_t, arrived = gather_streams(rest[:, :piece])
    kv_rest = jnp.concatenate(
        [rest[:, 3 * piece : 3 * piece + kv_piece], rest[:, 3 * piece + kv_piece :]], axis=2
    )
    kv_all, arrived = gather_streams(kv_rest, arrived)
    mid_all, _ = gather_streams(
        jnp.concatenate([rest[:, piece : 2 * piece], rest[:, 2 * piece : 3 * piece]], axis=2),
        arrived,
    )
    cross_q_all, cross_out_t = mid_all[:, :cols], mid_all[:, cols:]
    ffn_part = jnp.concatenate([ffn_in[0], ffn_out[0].T], axis=1)
    ffn_all, _ = gather_items(after(ffn_part, arrived_qkv[min(1, len(arrived_qkv) - 1)]))
    ffn_all = ffn_all.reshape(width, 2 * hidden_cols)

    def my_cols(vector):
        return lax.dynamic_slice_in_dim(vector, col_start, cols, 0)

    def row(vector):
        return vector.reshape(1, -1)

    none = jnp.zeros((cols,), F32)
    bias_qkv = row(jnp.concatenate([my_cols(self_bias[0]), none, my_cols(self_bias[1])]))
    bias_kv = row(jnp.concatenate([none, my_cols(cross_bias[1])]))
    gain_ffn = row(lax.dynamic_index_in_dim(gains, 2 + stream, 0, keepdims=False))
    shift_ffn = row(lax.dynamic_index_in_dim(shifts, 2 + stream, 0, keepdims=False))
    bias_in = row(
        lax.dynamic_slice_in_dim(
            lax.dynamic_index_in_dim(ffn_bias_in, stream, 0, keepdims=False),
            hidden_start,
            hidden_cols,
            0,
        )
    )
    bias_out = row(lax.dynamic_index_in_dim(ffn_bias_out, stream, 0, keepdims=False))

    def swap(part):
        return partner(part, "heads", 0)

    feat_norm = feature_norm(
        features, row(feat_gain), row(feat_shift), padded, [None] + arrived_qkv[:3]
    )
    feat_rows = feat_norm.reshape(items * padded, feat_width)
    q, kv, kv_far = project(own, far, qkv_all, bias_qkv)
    allowed = visible(stream, segments, modes)
    attended, part = self_attention(q, kv, kv_far, allowed, self_out_t, items, 4)
    keys_values = (mul(feat_rows, kv_all) + bias_kv).astype(BF).reshape(items, padded, 2 * cols)
    unit_one, scale_one, after_low, qc, attended_c, part_c = cross_attention(
        own,
        part,
        swap(part),
        (row(self_bias[2]), row(gains[0]), row(shifts[0]), row(my_cols(cross_bias[0]))),
        cross_q_all,
        keys_values,
        cross_out_t,
        items,
        2,
        patches,
    )
    z, z_low, unit_two, scale_two, activated, slope, part_f = feed_forward(
        flag,
        unit_one,
        part_c,
        swap(part_c),
        (row(gains[0]), row(shifts[0]), row(cross_bias[2]), row(gains[1]), row(shifts[1])),
        ffn_all,
        bias_in,
        256,
    )

    output, grad_three, grad_u, grad_pre, part_z, sums_three, sum_pre = feed_back(
        z,
        part_f,
        swap(part_f),
        cotangent.reshape(rows, width),
        (bias_out, gain_ffn, shift_ffn),
        slope,
        ffn_all,
        256,
    )
    away_z = swap(part_z)
    in_grad = t_mul(z_low, grad_pre).astype(BF)
    out_grad = t_mul(grad_u, activated).astype(BF)
    count = shards // 2
    ffn_ring = Scatter(
        [
            [at(in_grad.reshape(count, -1, hidden_cols))],
            [at(out_grad.reshape(count, -1, hidden_cols))],
        ],
        1,
    )
    first = ffn_ring.step()
    grad_after, mix_c, grad_qc, grad_kv, part_a, sums_two, sums_cross = cross_back(
        flag,
        grad_three,
        part_z,
        after(away_z, in_grad, out_grad),
        unit_two,
        scale_two,
        row(gains[1]),
        qc,
        keys_values,
        cross_out_t,
        cross_q_all,
        items,
        2,
        patches,
    )
    grad_after, mix_c, grad_qc, grad_kv, part_a, sums_two, sums_cross, first = (
        lax.optimization_barrier(
            (grad_after, mix_c, grad_qc, grad_kv, part_a, sums_two, sums_cross, first)
        )
    )
    ffn_ring.up = first
    away_a = swap(part_a)
    keep_q, away_q = halves(t_mul(after_low, grad_qc).astype(BF))
    keep_o, away_o = halves(t_mul(mix_c, attended_c).astype(BF))
    away_c = jnp.concatenate([away_q, away_o], axis=2)
    kv_grad = t_mul(
        feat_rows, after(grad_kv, away_c).reshape(items * padded, 2 * cols)
    )
    ffn_ring.step()
    kv_grad_low = kv_grad.astype(BF)
    arrived_c = partner(away_c, "stream", 0)
    kv_grad, kv_grad_low, arrived_c, ffn_ring.up, ffn_ring.down = lax.optimization_barrier(
        (kv_grad, kv_grad_low, arrived_c, ffn_ring.up, ffn_ring.down)
    )
    keep_kv, away_kv = halves(kv_grad_low)
    ffn_ring.step()
    arrived_kv = partner(away_kv, "stream", 0)
    grad_one, mix, grad_near, grad_away, both, sums_one, sums_self, self_grad = self_back(
        grad_after,
        part_a,
        after(away_a, kv_grad_low, away_kv),
        unit_one,
        scale_one,
        row(gains[0]),
        q,
        kv,
        kv_far,
        allowed,
        self_out_t,
        qkv_all,
        own,
        far,
        attended,
        items,
        4,
        shards,
    )

    results = (grad_one, both, sums_one, sums_self, self_grad, arrived_kv)
    grad_one, both, sums_one, sums_self, self_grad, arrived_kv, ffn_ring.up, ffn_ring.down = (
        lax.optimization_barrier(results + (ffn_ring.up, ffn_ring.down))
    )

    rest_ring = Scatter(
        [
            [at_stream(keep_q, False), at(arrived_c[:, :, :cols])],
            [at_stream(keep_o, False), at(arrived_c[:, :, cols:])],
            [at_stream(keep_kv[..., :cols], False), at(arrived_kv[:, :, :cols])],
            [at_stream(keep_kv[..., cols:], False), at(arrived_kv[:, :, cols:])],
        ],
        0,
    )
    away_self = lax.dynamic_index_in_dim(self_grad, 1 - stream, 0, keepdims=False)
    theirs = lax.dynamic_slice_in_dim(both, (1 - head_index) * half, half, 0)
    theirs, away_self = lax.optimization_barrier((theirs, away_self))
    arrived_self = partner(away_self, "stream", 0)
    mine = lax.dynamic_slice_in_dim(both, head_index * half, half, 0)

    def ring_steps(rings, rider=None):
        sends = [ring.sends(away_self) for ring in rings]
        flat = [one for part in sends for one in part]
        arrivals = together(flat + ([rider] if rider else []))
        for ring, part in zip(rings, sends):
            ring.take(arrivals[: len(part)])
            arrivals = arrivals[len(part) :]
        return arrivals[0] if rider else None

    from_swap = swap(theirs)
    ring_steps([ffn_ring, rest_ring])
    total = mine.astype(F32) + from_swap.astype(F32)
    from_far = partner(total[:, width:].astype(BF), "stream", 0)
    small = (sums_one, sums_two, sums_three, sums_self, sums_cross, sum_pre, kv_grad, kv_all)
    small = lax.optimization_barrier(small + (rest_ring.up,))
    sums_one, sums_two, sums_three, sums_self, sums_cross, sum_pre, kv_grad, kv_late, _ = small

    dot_w = jnp.sum(kv_grad * kv_late.astype(F32), axis=1)
    feat_shift_grad = jnp.sum(
        kv_late.astype(F32) * jnp.concatenate([sums_cross[1], sums_cross[2]])[None], axis=1
    )
    feat_gain_grad = (dot_w - feat_shift * feat_shift_grad) / feat_gain

    def pair_row(left, right):
        return jnp.concatenate([left, right]).reshape(1, width)

    def fold(vector):
        length = (vector.shape[0] + width - 1) // width * width
        return jnp.pad(vector, (0, length - vector.shape[0])).reshape(-1, width)

    on_query, on_text = (stream == 0).astype(F32), (stream == 1).astype(F32)
    pre_rows = sum_pre.reshape(-1, width)
    full = [sums_one[:3], sums_two[:3], on_query * sums_three[:3], on_text * sums_three[:3]]
    own_half = [
        pair_row(sums_self[0, three[0]], sums_self[0, three[2]] + sums_self[1, three[2]]),
        pair_row(sums_cross[0], sums_cross[2]),
        on_query * pre_rows,
        on_text * pre_rows,
    ]
    feats = [fold(feat_gain_grad), fold(feat_shift_grad)]
    packed = jnp.concatenate(full + own_half + feats, axis=0)
    moves = [over("stream")] + [over("items", bit) for bit in range((count - 1).bit_length())]

    ring_steps(([ffn_ring] if ffn_ring.hop else []) + [rest_ring])
    while rest_ring.hop or ffn_ring.hop:
        rings = [ring for ring in (ffn_ring, rest_ring) if ring.hop]
        if moves:
            packed = packed + ring_steps(rings, (packed, moves.pop(0)))
        else:
            ring_steps(rings)
    in_half = (
        lax.dynamic_slice_in_dim(grad_one, head_index * half, half, 0)
        + total[:, :width]
        + from_far.astype(F32)
    )
    self_ring = Scatter([[at_stream(self_grad, True), at(after(arrived_self, rest_ring.up))]], 0)
    while self_ring.hop:
        if moves:
            packed = packed + ring_steps([self_ring], (packed, moves.pop(0)))
        else:
            ring_steps([self_ring])
        if self_ring.hop == count // 2 - 1:
            in_other = swap(after(in_half, self_ring.up))
    while moves:
        packed = packed + moves.pop(0)(packed)
    grad_input = jnp.where(
        head_index == 0,
        jnp.concatenate([in_half, in_other], axis=0),
        jnp.concatenate([in_other, in_half], axis=0),
    )
    ffn_red, rest_red, self_red = ffn_ring.result(), rest_ring.result(), self_ring.result()
    tail = packed[12:]
    other = swap(tail)
    low_rows = jnp.where(head_index == 0, tail, other)
    high_rows = jnp.where(head_index == 0, other, tail)
    pres = pre_rows.shape[0]

    def side(one):
        return jnp.concatenate([low_rows[one, :cols], high_rows[one, :cols]]), jnp.concatenate(
            [low_rows[one, cols:], high_rows[one, cols:]]
        )

    self_q, self_v = side(0)
    cross_qb, cross_vb = side(1)

    def hidden_bias(start):
        return jnp.concatenate(
            [low_rows[start : start + pres].reshape(-1), high_rows[start : start + pres].reshape(-1)]
        )

    feat_sums = (tail + other)[2 + 2 * pres :]
    folds = feat_sums.shape[0] // 2
    return (
        output.reshape(items, 1, each, width),
        grad_input.reshape(items, 1, each, width),
        jnp.stack([self_red[:, one] for one in three]),
        jnp.stack([self_q, self_v, packed[2]]),
        self_red[:, 3 * cols :].T,
        rest_red[:piece],
        jnp.stack([rest_red[2 * piece : 2 * piece + kv_piece], rest_red[2 * piece + kv_piece :]]),
        jnp.stack([cross_qb, cross_vb, packed[5]]),
        rest_red[piece : 2 * piece].T,
        jnp.stack([packed[0], packed[3], packed[6], packed[9]]),
        jnp.stack([packed[1], packed[4], packed[7], packed[10]]),
        feat_sums[:folds].reshape(-1)[:feat_width],
        feat_sums[folds:].reshape(-1)[:feat_width],
        ffn_red[:, :hidden_cols][None],
        jnp.stack([hidden_bias(2), hidden_bias(2 + pres)]),
        ffn_red[:, hidden_cols:].T[None],
        jnp.stack([packed[8], packed[11]]),
    )


def solution(mesh):
    placed = (
        P("items", "stream", None, None),
        P("items", None, None),
        P("items", None),
        P("items"),
        P(None, ("items", "stream"), "heads"),
        P(),
        P("heads", ("items", "stream")),
        P(("items", "stream"), "heads"),
        P(None, ("items", "stream"), "heads"),
        P(),
        P("heads", ("items", "stream")),
        P(),
        P(),
        P(),
        P(),
        P("stream", "items", "heads"),
        P(),
        P("stream", "heads", "items"),
        P(),
        P("items", "stream", None, None),
    )
    return jax.shard_map(
        body,
        mesh=mesh,
        in_specs=placed,
        out_specs=(
            P("items", "stream", None, None),
            P("items", "stream", None, None),
            P(None, ("items", "stream"), "heads"),
            P(),
            P("heads", ("items", "stream")),
            P(("items", "stream"), "heads"),
            P(None, ("items", "stream"), "heads"),
            P(),
            P("heads", ("items", "stream")),
            P(),
            P(),
            P(),
            P(),
            P("stream", "items", "heads"),
            P(),
            P("stream", "heads", "items"),
            P(),
        ),
        check_vma=False,
    )
```

```python
import math

import jax
import jax.numpy as jnp
import numpy as np
from jax import lax
from jax.experimental import pallas as pl
from jax.experimental.pallas import tpu as pltpu
from jax.sharding import PartitionSpec as P

HEAD_DIM = 64
EPS = 1e-06
NEG = -1e30
BF = jnp.bfloat16
F32 = jnp.float32


def partner(shard, axis, distance):
    return lax.ppermute(shard, axis, [(i, i ^ 1 << distance) for i in range(lax.axis_size(axis))])


def joined(*values):
    return lax.optimization_barrier(values)


def ring_of(count):
    return list(range(0, count, 2)) + list(range(1, count, 2))[::-1]


def ring_places():
    count = lax.axis_size("items")
    order = ring_of(count)
    table = np.zeros((count, count), np.uint32)
    for place, index in enumerate(order):
        table[index] = [order[(place + far) % count] for far in range(count)]
    row = lax.axis_index("items").astype(jnp.uint32)
    found = lax.dynamic_slice(jnp.asarray(table), (row, jnp.uint32(0)), (1, count))
    return found.reshape(count)


def arrival_order(count):
    order = [0]
    for hop in range(1, count // 2 + 1):
        order.append(count - hop)
        if hop <= (count - 1) // 2:
            order.append(hop)
    return order


def shift_ring(shard, order, step):
    count = len(order)
    return lax.ppermute(
        shard, "items", [(order[i], order[(i + step) % count]) for i in range(count)]
    )


def together(sends):
    values = lax.optimization_barrier(tuple(value for value, _ in sends))
    return lax.optimization_barrier(tuple(move(one) for one, (_, move) in zip(values, sends)))


class Gather:
    def __init__(self, shard):
        self.count = lax.axis_size("items")
        self.order = ring_of(self.count)
        self.up = self.down = shard
        self.pieces = [shard]
        self.hop = 1

    def sends(self):
        result = [(self.up, lambda one: shift_ring(one, self.order, 1))]
        if self.hop <= (self.count - 1) // 2:
            result.append((self.down, lambda one: shift_ring(one, self.order, -1)))
        return result

    def take(self, arrivals):
        self.pieces += arrivals
        self.up = arrivals[0]
        self.down = arrivals[-1]
        self.hop += 1

    def replace(self, up, down):
        self.pieces[-1] = down
        if self.hop - 1 <= (self.count - 1) // 2:
            self.pieces[-2] = up
        self.up, self.down = up, down

    @property
    def left(self):
        return self.hop <= self.count // 2


def gather_step(rings):
    sends = [ring.sends() for ring in rings]
    arrivals = together([one for part in sends for one in part])
    for ring, part in zip(rings, sends):
        ring.take(list(arrivals[: len(part)]))
        arrivals = arrivals[len(part) :]


def place_items(pieces, places):
    whole = jnp.zeros((len(pieces),) + pieces[0].shape, pieces[0].dtype)
    for far, piece in zip(arrival_order(len(pieces)), pieces):
        whole = lax.dynamic_update_index_in_dim(whole, piece, places[far], 0)
    return whole


def by_stream(own, other, axis):
    first = lax.axis_index("stream") == 0
    return jnp.where(
        first, jnp.stack([own, other], axis=axis), jnp.stack([other, own], axis=axis)
    )


def whole_rows(own, other):
    both = by_stream(own, other, 1)
    return both.reshape((both.shape[0] * both.shape[1] * both.shape[2], both.shape[3]))


def at(pieces):
    return lambda which: lax.dynamic_index_in_dim(pieces, which, 0, keepdims=False)


def at_stream(pieces, outer):
    stream = lax.axis_index("stream").astype(jnp.uint32)
    zero = jnp.uint32(0)

    def read(which):
        start = (stream, which) if outer else (which, stream)
        found = lax.dynamic_slice(pieces, start + (zero, zero), (1, 1) + pieces.shape[2:])
        return found.reshape(pieces.shape[2:])

    return read


class Scatter:
    def __init__(self, groups, axis, places):
        self.groups, self.axis = groups, axis
        self.count = lax.axis_size("items")
        self.order, self.places = ring_of(self.count), places
        self.hop = self.count // 2
        self.up = self.down = None

    def piece(self, distance):
        which = self.places[distance % self.count]
        parts = [sum(read(which).astype(F32) for read in group) for group in self.groups]
        return jnp.concatenate(parts, axis=self.axis)

    def sends(self):
        own = self.piece(self.hop)
        own = own if self.up is None else own + self.up.astype(F32)
        result = [(own.astype(BF), lambda one: shift_ring(one, self.order, 1))]
        if self.hop <= (self.count - 1) // 2:
            own = self.piece(self.count - self.hop)
            own = own if self.down is None else own + self.down.astype(F32)
            result.append((own.astype(BF), lambda one: shift_ring(one, self.order, -1)))
        return result

    def take(self, arrivals):
        self.up = arrivals[0]
        if len(arrivals) > 1:
            self.down = arrivals[1]
        self.hop -= 1
        return arrivals[0]

    def step(self):
        return self.take(together(self.sends()))

    def result(self):
        return self.piece(0) + self.up.astype(F32) + self.down.astype(F32)


def halves(total):
    count = lax.axis_size("items")
    rows = total.shape[0] // (2 * count)
    parts = total.reshape((count, 2, rows, total.shape[1]))
    stream = lax.axis_index("stream").astype(jnp.uint32)
    away = lax.dynamic_index_in_dim(parts, 1 - stream, 1, keepdims=False)
    return parts, away


def over(axis, distance=0):
    return lambda one: partner(one, axis, distance)


def mul(left, right):
    return jnp.dot(left, right, preferred_element_type=F32)


def mul_t(left, right):
    return lax.dot_general(left, right, (((1,), (1,)), ((), ())), preferred_element_type=F32)


def t_mul(left, right):
    return lax.dot_general(left, right, (((0,), (0,)), ((), ())), preferred_element_type=F32)


def standard(rows):
    center = rows - jnp.mean(rows, axis=-1, keepdims=True)
    scale = lax.rsqrt(jnp.mean(center * center, axis=-1, keepdims=True) + EPS)
    return center * scale, scale


def norm_back(grad, unit, scale, gain):
    inner = grad * gain
    return scale * (
        inner
        - jnp.mean(inner, axis=-1, keepdims=True)
        - unit * jnp.mean(inner * unit, axis=-1, keepdims=True)
    )


def pair_sum(near, away):
    return near[...].astype(F32) + away[...].astype(F32)


def total_rows(rows):
    return jnp.sum(rows, axis=0, keepdims=True)


def head_mask(rows, heads, value, dtype):
    row = lax.broadcasted_iota(jnp.int32, (heads * rows, heads * HEAD_DIM), 0) // rows
    col = lax.broadcasted_iota(jnp.int32, (heads * rows, heads * HEAD_DIM), 1) // HEAD_DIM
    return jnp.where(row == col, value, 0.0).astype(dtype)


def stack_heads(rows, heads, mask):
    return jnp.concatenate([rows] * heads, axis=0) * mask


def fold_heads(stacked, heads, mask):
    rows = stacked.shape[0] // heads
    stacked = stacked * mask
    result = stacked[:rows]
    for head in range(1, heads):
        result = result + stacked[head * rows : (head + 1) * rows]
    return result


def softmax(scores):
    power = jnp.exp(scores - jnp.max(scores, axis=-1, keepdims=True))
    return power * (1.0 / jnp.sum(power, axis=-1, keepdims=True))


def attend(queries, keys, values, hide, heads, scaled_mask, out_mask):
    scores = hide(mul_t(stack_heads(queries, heads, scaled_mask), keys))
    weights = softmax(scores).astype(BF)
    return fold_heads(mul(weights, values), heads, out_mask).astype(BF)


def attend_back(queries, keys, values, grad, hide, heads, scaled_mask, plain_mask, out_mask):
    queries = stack_heads(queries, heads, scaled_mask)
    grad = stack_heads(grad, heads, plain_mask)
    weights = softmax(hide(mul_t(queries, keys)))
    grad_weights = mul_t(grad, values)
    grad_values = t_mul(weights.astype(BF), grad)
    delta = jnp.sum(grad_weights * weights, axis=-1, keepdims=True)
    grad_scores = (weights * (grad_weights - delta)).astype(BF)
    grad_queries = fold_heads(mul(grad_scores, keys), heads, out_mask) * HEAD_DIM ** (-0.5)
    return grad_queries, t_mul(grad_scores, queries), grad_values


def whole(shape):
    return pl.BlockSpec(shape, lambda i: (0,) * len(shape))


def block(shape):
    return pl.BlockSpec(shape, lambda i: (i,) + (0,) * (len(shape) - 1))


def column(shape, first=0):
    return pl.BlockSpec(shape, lambda i: (0, i + first))


def shaped(shape, dtype):
    return jax.ShapeDtypeStruct(shape, dtype)


def call(kernel, grid, in_specs, out_specs, out_shape, scratch=(), flops=0, moved=0):
    return pl.pallas_call(
        kernel,
        grid=(grid,),
        in_specs=in_specs,
        out_specs=out_specs,
        out_shape=out_shape,
        scratch_shapes=list(scratch),
        compiler_params=pltpu.CompilerParams(
            dimension_semantics=("arbitrary",), vmem_limit_bytes=56 << 20
        ),
        cost_estimate=pl.CostEstimate(flops=flops, bytes_accessed=moved, transcendentals=0),
    )


def feature_norm(features, gain, shift, padded, begin, each, prior):
    items, patches, width = features.shape

    def kernel(feat, gain, shift, *refs):
        out, token = refs[-2:]
        unit, _ = standard(feat[0].astype(F32))
        out[0, :patches] = (unit * gain[...] + shift[...]).astype(BF)
        out[0, patches:] = jnp.zeros((padded - patches, width), BF)
        token[...] = jnp.zeros_like(token)

    def at_item(i):
        return (i + begin, 0, 0)

    return pl.pallas_call(
        kernel,
        grid=(each,),
        in_specs=[pl.BlockSpec((1, patches, width), at_item), whole((1, width)), whole((1, width))]
        + [pl.BlockSpec(memory_space=pl.ANY)] * len(prior),
        out_specs=[pl.BlockSpec((1, padded, width), at_item), whole((8, 128))],
        out_shape=[shaped((items, padded, width), BF), shaped((8, 128), F32)],
        input_output_aliases={3: 0} if prior else {},
        compiler_params=pltpu.CompilerParams(
            dimension_semantics=("arbitrary",), vmem_limit_bytes=56 << 20
        ),
        cost_estimate=pl.CostEstimate(
            flops=0, bytes_accessed=4 * each * patches * width, transcendentals=0
        ),
    )(features, gain, shift, *prior)


def project(places, own, far, pieces, bias):
    rows, width = own.shape
    count = len(pieces)
    cols = pieces[0].shape[1]
    head_cols = cols // 3
    step = rows // 4
    spots = arrival_order(count)

    def kernel(places, own, far, bias, *refs):
        q, kv, kv_far, weight, laid = refs[count:]

        @pl.when(pl.program_id(0) == 0)
        def _():
            for far_off, one in zip(spots, refs[:count]):
                laid[places[far_off]] = one[...]
            weight[...] = laid[...].reshape(width, cols)

        near = mul(own[...], weight[...]) + bias[...]
        q[...] = near[:, :head_cols].astype(BF)
        kv[...] = near[:, head_cols:].astype(BF)
        kv_far[...] = (mul(far[...], weight[:, head_cols:]) + bias[:, head_cols:]).astype(BF)

    return call(
        kernel,
        4,
        [pl.BlockSpec(memory_space=pltpu.SMEM)]
        + [block((step, width)), block((step, width)), whole((1, cols))]
        + [whole((width // count, cols))] * count,
        [block((step, head_cols)), block((step, 2 * head_cols)), block((step, 2 * head_cols))]
        + [whole((width, cols))],
        [shaped((rows, head_cols), BF)]
        + [shaped((rows, 2 * head_cols), BF)] * 2
        + [shaped((width, cols), BF)],
        scratch=[pltpu.VMEM((count, width // count, cols), BF)],
        flops=10 * rows * width * head_cols,
        moved=4 * rows * width + 4 * width * cols,
    )(places, own, far, bias, *pieces)


def self_attention(q, kv, kv_far, allowed, weight, items, batch):
    rows, cols = q.shape
    heads, each = cols // HEAD_DIM, rows // items
    width = weight.shape[0]

    def kernel(q, kv, kv_far, allowed, weight, attended, out):
        index = pl.program_id(0)
        scaled = head_mask(each, heads, HEAD_DIM ** (-0.5), BF)
        ones = head_mask(each, heads, 1.0, F32)
        for item in range(batch):
            span = slice(item * each, (item + 1) * each)
            keys = jnp.concatenate([kv[span, :cols], kv_far[span, :cols]], axis=0)
            values = jnp.concatenate([kv[span, cols:], kv_far[span, cols:]], axis=0)
            seen = jnp.concatenate([allowed[item]] * heads, axis=0) > 0
            result = attend(
                q[span], keys, values, lambda s: jnp.where(seen, s, NEG), heads, scaled, ones
            )
            start = pl.multiple_of((index * batch + item) * each, each)
            attended[pl.ds(start, each), :] = result

        @pl.when(index == pl.num_programs(0) - 1)
        def _():
            out[...] = mul_t(attended[...], weight[...]).astype(BF)

    part = batch * each
    return call(
        kernel,
        items // batch,
        [
            block((part, cols)),
            block((part, 2 * cols)),
            block((part, 2 * cols)),
            block((batch, each, 2 * each)),
            whole((width, cols)),
        ],
        [whole((rows, cols)), whole((rows, width))],
        [shaped((rows, cols), BF), shaped((rows, width), BF)],
        flops=2 * rows * cols * width * 3,
        moved=rows * cols * 14 + rows * width * 4,
    )(q, kv, kv_far, allowed, weight)


def cross_attention(own, near, away, rows_in, cq, keys_values, weight, items, batch, patches):
    rows, width = own.shape
    cols = weight.shape[1]
    heads, each = cols // HEAD_DIM, rows // items
    padded = keys_values.shape[1]

    def kernel(own, near, away, bias, gain, shift, bias_q, cq, kv, weight, unit, scale, low, qc, attended, out):
        index = pl.program_id(0)

        @pl.when(index == 0)
        def _():
            one, size = standard(own[...].astype(F32) + pair_sum(near, away) + bias[...])
            unit[...] = one
            scale[...] = size
            low[...] = (one * gain[...] + shift[...]).astype(BF)
            qc[...] = (mul(low[...], cq[...]) + bias_q[...]).astype(BF)

        scaled = head_mask(each, heads, HEAD_DIM ** (-0.5), BF)
        ones = head_mask(each, heads, 1.0, F32)
        real = lax.broadcasted_iota(jnp.int32, (heads * each, padded), 1) < patches
        for item in range(batch):
            start = pl.multiple_of((index * batch + item) * each, each)
            attended[pl.ds(start, each), :] = attend(
                qc[pl.ds(start, each), :],
                kv[item, :, :cols],
                kv[item, :, cols:],
                lambda s: jnp.where(real, s, NEG),
                heads,
                scaled,
                ones,
            )

        @pl.when(index == pl.num_programs(0) - 1)
        def _():
            out[...] = mul_t(attended[...], weight[...]).astype(BF)

    bias, gain, shift, bias_q = rows_in
    return call(
        kernel,
        items // batch,
        [whole((rows, width))] * 3
        + [whole((1, width))] * 3
        + [whole((1, cols)), whole((width, cols)), block((batch, padded, 2 * cols)), whole((width, cols))],
        [
            whole((rows, width)),
            whole((rows, 1)),
            whole((rows, width)),
            whole((rows, cols)),
            whole((rows, cols)),
            whole((rows, width)),
        ],
        [
            shaped((rows, width), F32),
            shaped((rows, 1), F32),
            shaped((rows, width), BF),
            shaped((rows, cols), BF),
            shaped((rows, cols), BF),
            shaped((rows, width), BF),
        ],
        flops=2 * rows * cols * padded * heads * 2,
        moved=rows * width * 20 + 4 * items * padded * cols,
    )(own, near, away, bias, gain, shift, bias_q, cq, keys_values, weight)


def lay_pieces(places, spots, refs, laid):
    count, rows, cols = laid.shape[1:]
    for far_off, w_in, w_out in zip(spots, refs[:count], refs[count:]):
        laid[0, places[far_off]] = w_in[...]
        laid[1, places[far_off]] = w_out[...]
    return laid[0].reshape(count * rows, cols), laid[1].reshape(count * rows, cols)


def feed_forward(flag, places, unit, near, away, rows_in, pieces, b_in, chunk):
    rows, width = unit.shape
    hidden = pieces[0].shape[1] // 2
    steps = hidden // chunk
    count = len(pieces)
    spots = arrival_order(count)

    def kernel(flag, places, unit, near, away, gain0, shift0, bias, gain1, shift1, b_in, *refs):
        z, z_low, unit2, scale2, act, slope, part, out, laid = refs[2 * count :]
        w_in, w_out = lay_pieces(places, spots, refs[: 2 * count], laid)

        @pl.when(pl.program_id(0) == 0)
        def _():
            after = unit[...] * gain0[...] + shift0[...]
            one, size = standard(after + pair_sum(near, away) + bias[...])
            unit2[...] = one
            scale2[...] = size
            z[...] = jnp.where(flag[0] == 0, one * gain1[...] + shift1[...], after)
            z_low[...] = z[...].astype(BF)
            out[...] = jnp.zeros_like(out)

        for half in range(2):
            span = slice(half * rows // 2, (half + 1) * rows // 2)
            u = mul(z_low[span], w_in) + b_in[...]
            share = 0.5 + 0.5 * lax.erf(u * math.sqrt(0.5))
            act_half = (u * share).astype(BF)
            act[span] = act_half
            slope[span] = share + u * (jnp.exp(-0.5 * u * u) * (1.0 / math.sqrt(2.0 * math.pi)))
            out[span] += mul_t(act_half, w_out)

        @pl.when(pl.program_id(0) == steps - 1)
        def _():
            part[...] = out[...].astype(BF)

    row = whole((1, width))
    return call(
        kernel,
        steps,
        [pl.BlockSpec(memory_space=pltpu.SMEM)] * 2
        + [whole((rows, width))] * 3
        + [row] * 5
        + [column((1, chunk))]
        + [column((width // count, chunk))] * count
        + [column((width // count, chunk), steps)] * count,
        [
            whole((rows, width)),
            whole((rows, width)),
            whole((rows, width)),
            whole((rows, 1)),
            column((rows, chunk)),
            column((rows, chunk)),
            whole((rows, width)),
        ],
        [
            shaped((rows, width), F32),
            shaped((rows, width), BF),
            shaped((rows, width), F32),
            shaped((rows, 1), F32),
            shaped((rows, hidden), BF),
            shaped((rows, hidden), F32),
            shaped((rows, width), BF),
        ],
        scratch=[pltpu.VMEM((rows, width), F32), pltpu.VMEM((2, count, width // count, chunk), BF)],
        flops=4 * rows * hidden * width,
        moved=rows * width * 26 + rows * hidden * 6 + width * hidden * 4,
    )(flag, places, unit, near, away, *rows_in, b_in, *pieces, *pieces)


def feed_back(places, z, near, away, cotangent, rows_in, slope, pieces, chunk):
    rows, width = z.shape
    hidden = pieces[0].shape[1] // 2
    steps = hidden // chunk
    count = len(pieces)
    spots = arrival_order(count)

    def kernel(places, z, near, away, cot, bias, gain, shift, slope, *refs):
        result, grad_v, grad_u, grad_pre, part, sums, sum_pre, out, laid = refs[2 * count :]
        w_in, w_out = lay_pieces(places, spots, refs[: 2 * count], laid)

        @pl.when(pl.program_id(0) == 0)
        def _():
            one, size = standard(z[...] + pair_sum(near, away) + bias[...])
            dy = cot[...]
            result[...] = (one * gain[...] + shift[...]).astype(BF)
            grad_v[...] = norm_back(dy, one, size, gain[...])
            grad_u[...] = grad_v[...].astype(BF)
            sums[0:1] = total_rows(dy * one)
            sums[1:2] = total_rows(dy)
            sums[2:3] = total_rows(grad_u[...].astype(F32))
            out[...] = jnp.zeros_like(out)

        for half in range(2):
            span = slice(half * rows // 2, (half + 1) * rows // 2)
            pre = (mul(grad_u[span], w_out) * slope[span]).astype(BF)
            grad_pre[span] = pre
            out[span] += mul_t(pre, w_in)
        sum_pre[...] = total_rows(grad_pre[...].astype(F32))

        @pl.when(pl.program_id(0) == steps - 1)
        def _():
            part[...] = out[...].astype(BF)

    row = whole((1, width))
    return call(
        kernel,
        steps,
        [pl.BlockSpec(memory_space=pltpu.SMEM)]
        + [whole((rows, width))] * 4
        + [row] * 3
        + [column((rows, chunk))]
        + [column((width // count, chunk))] * count
        + [column((width // count, chunk), steps)] * count,
        [
            whole((rows, width)),
            whole((rows, width)),
            whole((rows, width)),
            column((rows, chunk)),
            whole((rows, width)),
            whole((8, width)),
            column((1, chunk)),
        ],
        [
            shaped((rows, width), BF),
            shaped((rows, width), F32),
            shaped((rows, width), BF),
            shaped((rows, hidden), BF),
            shaped((rows, width), BF),
            shaped((8, width), F32),
            shaped((1, hidden), F32),
        ],
        scratch=[pltpu.VMEM((rows, width), F32), pltpu.VMEM((2, count, width // count, chunk), BF)],
        flops=4 * rows * hidden * width,
        moved=rows * width * 28 + rows * hidden * 6 + width * hidden * 4,
    )(places, z, near, away, cotangent, *rows_in, slope, *pieces, *pieces)


def cross_back(flag, grad_v, near, away, unit2, scale2, gain, qc, keys_values, weight, cq, items, batch, patches):
    rows, width = grad_v.shape
    cols = weight.shape[1]
    heads, each = cols // HEAD_DIM, rows // items
    padded = keys_values.shape[1]

    def kernel(flag, grad_v, near, away, unit2, scale2, gain, qc, kv, weight, cq, after, mix, grad_qc, grad_kv, out, sums, sums_c, grad_att):
        index = pl.program_id(0)

        @pl.when(index == 0)
        def _():
            dz = grad_v[...] + pair_sum(near, away)
            mine = flag[0] == 0
            used = jnp.where(mine, dz, 0.0)
            two = norm_back(used, unit2[...], scale2[...], gain[...])
            after[...] = jnp.where(mine, two, dz)
            mix[...] = two.astype(BF)
            grad_att[...] = mul(mix[...], weight[...]).astype(BF)
            sums[0:1] = total_rows(used * unit2[...])
            sums[1:2] = total_rows(used)
            sums[2:3] = total_rows(mix[...].astype(F32))
            sums_c[...] = jnp.zeros_like(sums_c)

        root = HEAD_DIM ** (-0.5)
        scaled = head_mask(each, heads, root, BF)
        plain = head_mask(each, heads, 1.0, BF)
        ones = head_mask(each, heads, 1.0, F32)
        real = lax.broadcasted_iota(jnp.int32, (heads * each, padded), 1) < patches
        for item in range(batch):
            start = pl.multiple_of((index * batch + item) * each, each)
            dq, dk, dv = attend_back(
                qc[pl.ds(start, each), :],
                kv[item, :, :cols],
                kv[item, :, cols:],
                grad_att[pl.ds(start, each), :],
                lambda s: jnp.where(real, s, NEG),
                heads,
                scaled,
                plain,
                ones,
            )
            grad_qc[pl.ds(start, each), :] = dq.astype(BF)
            dk, dv = dk.astype(BF), dv.astype(BF)
            grad_kv[item, :, :cols] = dk
            grad_kv[item, :, cols:] = dv
            sums_c[1:2] += total_rows(dk.astype(F32))
            sums_c[2:3] += total_rows(dv.astype(F32))

        @pl.when(index == pl.num_programs(0) - 1)
        def _():
            out[...] = mul_t(grad_qc[...], cq[...]).astype(BF)
            sums_c[0:1] = total_rows(grad_qc[...].astype(F32))

    return call(
        kernel,
        items // batch,
        [pl.BlockSpec(memory_space=pltpu.SMEM)]
        + [whole((rows, width))] * 4
        + [
            whole((rows, 1)),
            whole((1, width)),
            whole((rows, cols)),
            block((batch, padded, 2 * cols)),
            whole((width, cols)),
            whole((width, cols)),
        ],
        [
            whole((rows, width)),
            whole((rows, width)),
            whole((rows, cols)),
            block((batch, padded, 2 * cols)),
            whole((rows, width)),
            whole((8, width)),
            whole((8, cols)),
        ],
        [
            shaped((rows, width), F32),
            shaped((rows, width), BF),
            shaped((rows, cols), BF),
            shaped((items, padded, 2 * cols), BF),
            shaped((rows, width), BF),
            shaped((8, width), F32),
            shaped((8, cols), F32),
        ],
        scratch=[pltpu.VMEM((rows, cols), BF)],
        flops=2 * rows * cols * padded * heads * 5,
        moved=rows * width * 26 + 8 * items * padded * cols,
    )(flag, grad_v, near, away, unit2, scale2, gain, qc, keys_values, weight, cq)


def self_back(flag, after, near, away, unit, scale, gain, q, kv, kv_far, allowed, weight, w_qkv, own, far, attended, items, batch, shards):
    rows, width = after.shape
    cols = weight.shape[1]
    heads, each = cols // HEAD_DIM, rows // items
    piece = width // shards

    def kernel(flag, after, near, away, unit, scale, gain, q, kv, kv_far, allowed, weight, w_qkv, own, far, attended, grad_one, mix, grad_near, grad_away, both, sums, sums_c, grad_keep, grad_sent, grad_att):
        index = pl.program_id(0)

        @pl.when(index == 0)
        def _():
            grad = after[...] + pair_sum(near, away)
            grad_one[...] = norm_back(grad, unit[...], scale[...], gain[...])
            mix[...] = grad_one[...].astype(BF)
            grad_att[...] = mul(mix[...], weight[...]).astype(BF)
            sums[0:1] = total_rows(grad * unit[...])
            sums[1:2] = total_rows(grad)
            sums[2:3] = total_rows(mix[...].astype(F32))

        scaled = head_mask(each, heads, HEAD_DIM ** (-0.5), BF)
        plain = head_mask(each, heads, 1.0, BF)
        ones = head_mask(each, heads, 1.0, F32)
        for item in range(batch):
            span = slice(item * each, (item + 1) * each)
            start = pl.multiple_of((index * batch + item) * each, each)
            keys = jnp.concatenate([kv[span, :cols], kv_far[span, :cols]], axis=0)
            values = jnp.concatenate([kv[span, cols:], kv_far[span, cols:]], axis=0)
            seen = jnp.concatenate([allowed[item]] * heads, axis=0) > 0
            dq, dk, dv = attend_back(
                q[span],
                keys,
                values,
                grad_att[pl.ds(start, each), :],
                lambda s: jnp.where(seen, s, NEG),
                heads,
                scaled,
                plain,
                ones,
            )
            grad_near[pl.ds(start, each), :cols] = dq.astype(BF)
            grad_near[pl.ds(start, each), cols : 2 * cols] = dk[:each].astype(BF)
            grad_near[pl.ds(start, each), 2 * cols :] = dv[:each].astype(BF)
            grad_away[pl.ds(start, each), :cols] = dk[each:].astype(BF)
            grad_away[pl.ds(start, each), cols:] = dv[each:].astype(BF)

        @pl.when(index == pl.num_programs(0) - 1)
        def _():
            both[:, :width] = mul_t(grad_near[...], w_qkv[...]).astype(BF)
            both[:, width:] = mul_t(grad_away[...], w_qkv[:, cols:]).astype(BF)
            for place in range(4):
                span = slice(place * cols, (place + 1) * cols)
                if place == 3:
                    total = t_mul(mix[...], attended[...])
                else:
                    total = t_mul(own[...], grad_near[:, span])
                if place in (1, 2):
                    total = total + t_mul(far[...], grad_away[:, (place - 1) * cols : place * cols])
                total = total.astype(BF)
                for side in range(2):
                    pieces = [
                        total[one * piece : (one + 1) * piece] for one in range(side, shards, 2)
                    ]

                    @pl.when(flag[0] == side)
                    def _():
                        for one, value in enumerate(pieces):
                            grad_keep[one, :, span] = value

                    @pl.when(flag[0] != side)
                    def _():
                        for one, value in enumerate(pieces):
                            grad_sent[one, :, span] = value
            sums_c[0:1] = total_rows(grad_near[...].astype(F32))
            sums_c[1:2, cols:] = total_rows(grad_away[...].astype(F32))

    part = batch * each
    return call(
        kernel,
        items // batch,
        [pl.BlockSpec(memory_space=pltpu.SMEM)]
        + [whole((rows, width))] * 4
        + [
            whole((rows, 1)),
            whole((1, width)),
            block((part, cols)),
            block((part, 2 * cols)),
            block((part, 2 * cols)),
            block((batch, each, 2 * each)),
            whole((width, cols)),
            whole((width, 3 * cols)),
            whole((rows, width)),
            whole((rows, width)),
            whole((rows, cols)),
        ],
        [
            whole((rows, width)),
            whole((rows, width)),
            whole((rows, 3 * cols)),
            whole((rows, 2 * cols)),
            whole((rows, 2 * width)),
            whole((8, width)),
            whole((8, 3 * cols)),
            whole((shards // 2, piece, 4 * cols)),
            whole((shards // 2, piece, 4 * cols)),
        ],
        [
            shaped((rows, width), F32),
            shaped((rows, width), BF),
            shaped((rows, 3 * cols), BF),
            shaped((rows, 2 * cols), BF),
            shaped((rows, 2 * width), BF),
            shaped((8, width), F32),
            shaped((8, 3 * cols), F32),
            shaped((shards // 2, piece, 4 * cols), BF),
            shaped((shards // 2, piece, 4 * cols), BF),
        ],
        scratch=[pltpu.VMEM((rows, cols), BF)],
        flops=2 * rows * cols * width * 9,
        moved=rows * width * 32 + rows * cols * 20,
    )(flag, after, near, away, unit, scale, gain, q, kv, kv_far, allowed, weight, w_qkv, own, far, attended)


def visible(stream, segments, modes):
    same_caption = segments[:, :, None] == segments[:, None, :]
    own = jnp.logical_or(stream == 0, same_caption)
    far = jnp.where(stream == 0, modes == 2, modes >= 1)[:, None, None]
    return jnp.concatenate([own, jnp.broadcast_to(far, own.shape)], axis=2).astype(F32)


def body(
    hidden,
    features,
    segments,
    modes,
    w_qkv,
    self_bias,
    self_out,
    cross_q,
    cross_kv,
    cross_bias,
    cross_out,
    gains,
    shifts,
    feat_gain,
    feat_shift,
    ffn_in,
    ffn_bias_in,
    ffn_out,
    ffn_bias_out,
    cotangent,
):
    stream = lax.axis_index("stream")
    stream_u = stream.astype(jnp.uint32)
    head_index = lax.axis_index("heads")
    items, _, each, width = hidden.shape
    rows = items * each
    half = rows // 2
    cols = w_qkv.shape[2]
    hidden_cols = ffn_in.shape[2]
    patches, feat_width = features.shape[1:]
    padded = (patches + 7) // 8 * 8
    col_start = head_index.astype(jnp.uint32) * cols
    hidden_start = head_index.astype(jnp.uint32) * hidden_cols
    flag = stream.astype(jnp.int32).reshape(1)
    shards = 2 * lax.axis_size("items")
    three = [slice(i * cols, (i + 1) * cols) for i in range(3)]

    part_qkv = jnp.concatenate([w_qkv[0], w_qkv[1], w_qkv[2]], axis=1)
    pair_qkv = by_stream(part_qkv, partner(part_qkv, "stream", 0), 0)
    places = ring_places()
    spots = places.astype(jnp.int32)
    qkv_ring = Gather(pair_qkv.reshape(width // (shards // 2), 3 * cols))
    own = hidden.reshape(rows, width)
    heads_u = head_index.astype(jnp.uint32)
    my_half = lax.dynamic_slice_in_dim(own, heads_u * half, half, 0)
    far_half = partner(my_half, "stream", 0)
    far_other = partner(far_half, "heads", 0)
    far = jnp.where(
        head_index == 0,
        jnp.concatenate([far_half, far_other], axis=0),
        jnp.concatenate([far_other, far_half], axis=0),
    )
    later_out, part_qkv = joined(self_out, part_qkv)
    rest_ring = Gather(
        jnp.concatenate([later_out.T, cross_q, cross_out.T, cross_kv[0], cross_kv[1]], axis=0)
    )

    def row(vector):
        return vector.reshape(1, -1)

    kept, chunk = [], items // 4
    for number in range(max(4, shards // 4)):
        if qkv_ring.left:
            gather_step([qkv_ring, rest_ring])
        if number < 4:
            *kept, token = list(
                feature_norm(
                    features, row(feat_gain), row(feat_shift), padded, number * chunk, chunk, kept
                )
            )
            ends = joined(qkv_ring.up, qkv_ring.down, rest_ring.up, rest_ring.down, token)
            qkv_ring.replace(*ends[:2])
            rest_ring.replace(*ends[2:4])
            kept = [kept[0], ends[4]]
    feat_norm = kept[0]
    feat_rows = feat_norm.reshape(items * padded, feat_width)
    qkv_pieces = qkv_ring.pieces
    rest = place_items(rest_ring.pieces, places)
    piece = cross_q.shape[0]
    kv_piece = cross_kv.shape[1]
    out_rest = rest[:, :piece]
    mid_rest = jnp.concatenate(
        [rest[:, piece : 2 * piece], rest[:, 2 * piece : 3 * piece]], axis=2
    )
    kv_rest = jnp.concatenate(
        [rest[:, 3 * piece : 3 * piece + kv_piece], rest[:, 3 * piece + kv_piece :]], axis=2
    )
    out_other, kv_rest = joined(partner(out_rest, "stream", 0), kv_rest)
    kv_other, mid_rest = joined(partner(kv_rest, "stream", 0), mid_rest)
    self_out_t = whole_rows(out_rest, out_other)
    kv_all = whole_rows(kv_rest, kv_other)
    mid_all = whole_rows(mid_rest, partner(mid_rest, "stream", 0))
    cross_q_all, cross_out_t = mid_all[:, :cols], mid_all[:, cols:]
    ffn_part = jnp.concatenate([ffn_in[0], ffn_out[0].T], axis=1)
    ffn_part, last = joined(ffn_part, qkv_ring.up)
    qkv_ring.replace(last, last)
    ffn_gather = Gather(ffn_part)
    while ffn_gather.left:
        gather_step([ffn_gather])
    ffn_pieces = ffn_gather.pieces

    def my_cols(vector):
        return lax.dynamic_slice_in_dim(vector, col_start, cols, 0)

    none = jnp.zeros((cols,), F32)
    bias_qkv = row(jnp.concatenate([my_cols(self_bias[0]), none, my_cols(self_bias[1])]))
    bias_kv = row(jnp.concatenate([none, my_cols(cross_bias[1])]))
    gain_ffn = row(lax.dynamic_index_in_dim(gains, 2 + stream_u, 0, keepdims=False))
    shift_ffn = row(lax.dynamic_index_in_dim(shifts, 2 + stream_u, 0, keepdims=False))
    bias_in = row(
        lax.dynamic_slice_in_dim(
            lax.dynamic_index_in_dim(ffn_bias_in, stream_u, 0, keepdims=False),
            hidden_start,
            hidden_cols,
            0,
        )
    )
    bias_out = row(lax.dynamic_index_in_dim(ffn_bias_out, stream_u, 0, keepdims=False))

    def swap(part):
        return partner(part, "heads", 0)

    q, kv, kv_far, qkv_all = project(spots, own, far, qkv_pieces, bias_qkv)
    allowed = visible(stream, segments, modes)
    attended, part = self_attention(q, kv, kv_far, allowed, self_out_t, items, 4)
    keys_values = (mul(feat_rows, kv_all) + bias_kv).astype(BF).reshape(items, padded, 2 * cols)
    unit_one, scale_one, after_low, qc, attended_c, part_c = cross_attention(
        own,
        part,
        swap(part),
        (row(self_bias[2]), row(gains[0]), row(shifts[0]), row(my_cols(cross_bias[0]))),
        cross_q_all,
        keys_values,
        cross_out_t,
        items,
        2,
        patches,
    )
    z, z_low, unit_two, scale_two, activated, slope, part_f = feed_forward(
        flag,
        spots,
        unit_one,
        part_c,
        swap(part_c),
        (row(gains[0]), row(shifts[0]), row(cross_bias[2]), row(gains[1]), row(shifts[1])),
        ffn_pieces,
        bias_in,
        256,
    )

    output, grad_three, grad_u, grad_pre, part_z, sums_three, sum_pre = feed_back(
        spots,
        z,
        part_f,
        swap(part_f),
        cotangent.reshape(rows, width),
        (bias_out, gain_ffn, shift_ffn),
        slope,
        ffn_pieces,
        256,
    )
    away_z = swap(part_z)
    in_grad = t_mul(z_low, grad_pre).astype(BF)
    out_grad = t_mul(grad_u, activated).astype(BF)
    count = shards // 2
    ffn_ring = Scatter(
        [
            [at(in_grad.reshape(count, -1, hidden_cols))],
            [at(out_grad.reshape(count, -1, hidden_cols))],
        ],
        1,
        places,
    )
    first = ffn_ring.step()
    grad_after, mix_c, grad_qc, grad_kv, part_a, sums_two, sums_cross = cross_back(
        flag,
        grad_three,
        part_z,
        away_z,
        unit_two,
        scale_two,
        row(gains[1]),
        qc,
        keys_values,
        cross_out_t,
        cross_q_all,
        items,
        2,
        patches,
    )
    grad_after, mix_c, grad_qc, grad_kv, part_a, sums_two, sums_cross, first = (
        lax.optimization_barrier(
            (grad_after, mix_c, grad_qc, grad_kv, part_a, sums_two, sums_cross, first)
        )
    )
    ffn_ring.up = first
    away_a = swap(part_a)
    keep_q, away_q = halves(t_mul(after_low, grad_qc).astype(BF))
    keep_o, away_o = halves(t_mul(mix_c, attended_c).astype(BF))
    away_c = jnp.concatenate([away_q, away_o], axis=2)
    grad_kv, away_c = joined(grad_kv, away_c)
    kv_grad = t_mul(feat_rows, grad_kv.reshape(items * padded, 2 * cols))
    ffn_ring.step()
    kv_grad_low = kv_grad.astype(BF)
    arrived_c = partner(away_c, "stream", 0)
    kv_grad, kv_grad_low, arrived_c, ffn_ring.up, ffn_ring.down = lax.optimization_barrier(
        (kv_grad, kv_grad_low, arrived_c, ffn_ring.up, ffn_ring.down)
    )
    keep_kv, away_kv = halves(kv_grad_low)
    ffn_ring.step()
    away_a, away_kv = joined(away_a, away_kv)
    arrived_kv = partner(away_kv, "stream", 0)
    grad_one, mix, grad_near, grad_away, both, sums_one, sums_self, keep_self, away_self = self_back(
        flag,
        grad_after,
        part_a,
        away_a,
        unit_one,
        scale_one,
        row(gains[0]),
        q,
        kv,
        kv_far,
        allowed,
        self_out_t,
        qkv_all,
        own,
        far,
        attended,
        items,
        4,
        shards,
    )

    results = (grad_one, both, sums_one, sums_self, keep_self, away_self, arrived_kv)
    results = lax.optimization_barrier(results + (ffn_ring.up, ffn_ring.down))
    grad_one, both, sums_one, sums_self, keep_self, away_self, arrived_kv = results[:-2]
    ffn_ring.up, ffn_ring.down = results[-2:]

    rest_ring = Scatter(
        [
            [at_stream(keep_q, False), at(arrived_c[:, :, :cols])],
            [at_stream(keep_o, False), at(arrived_c[:, :, cols:])],
            [at_stream(keep_kv[..., :cols], False), at(arrived_kv[:, :, :cols])],
            [at_stream(keep_kv[..., cols:], False), at(arrived_kv[:, :, cols:])],
        ],
        0,
        places,
    )
    theirs = lax.dynamic_slice_in_dim(both, (1 - heads_u) * half, half, 0)
    mine = lax.dynamic_slice_in_dim(both, heads_u * half, half, 0)

    def ring_steps(rings, *riders):
        sends = [ring.sends() for ring in rings]
        flat = [one for part in sends for one in part]
        arrivals = together(list(riders) + flat)
        rest = arrivals[len(riders) :]
        for ring, part in zip(rings, sends):
            ring.take(rest[: len(part)])
            rest = rest[len(part) :]
        return arrivals[: len(riders)]

    arrived_self, from_swap = ring_steps(
        [ffn_ring, rest_ring], (away_self, over("stream")), (theirs, over("heads"))
    )
    self_ring = Scatter([[at(keep_self), at(arrived_self)]], 0, places)
    total = mine.astype(F32) + from_swap.astype(F32)
    from_far = partner(total[:, width:].astype(BF), "stream", 0)
    small = (sums_one, sums_two, sums_three, sums_self, sums_cross, sum_pre, kv_grad, kv_all)
    sums_one, sums_two, sums_three, sums_self, sums_cross, sum_pre, kv_grad, kv_late = (
        lax.optimization_barrier(small)
    )

    dot_w = jnp.sum(kv_grad * kv_late.astype(F32), axis=1)
    feat_shift_grad = jnp.sum(
        kv_late.astype(F32) * jnp.concatenate([sums_cross[1], sums_cross[2]])[None], axis=1
    )
    feat_gain_grad = (dot_w - feat_shift * feat_shift_grad) / feat_gain

    def pair_row(left, right):
        return jnp.concatenate([left, right]).reshape(1, width)

    def fold(vector):
        length = (vector.shape[0] + width - 1) // width * width
        return jnp.pad(vector, (0, length - vector.shape[0])).reshape(-1, width)

    on_query, on_text = (stream == 0).astype(F32), (stream == 1).astype(F32)
    pre_rows = sum_pre.reshape(-1, width)
    full = [
        one[place : place + 1]
        for place in range(3)
        for one in (sums_one, sums_two, on_query * sums_three, on_text * sums_three)
    ]
    own_half = [
        pair_row(sums_self[0, three[0]], sums_self[0, three[2]] + sums_self[1, three[2]]),
        pair_row(sums_cross[0], sums_cross[2]),
        on_query * pre_rows,
        on_text * pre_rows,
    ]
    feats = [fold(feat_gain_grad), fold(feat_shift_grad)]
    packed = jnp.concatenate(full + own_half + feats, axis=0)
    moves = [over("stream")] + [over("items", bit) for bit in range((count - 1).bit_length())]

    in_half = (
        lax.dynamic_slice_in_dim(grad_one, heads_u * half, half, 0)
        + total[:, :width]
        + from_far.astype(F32)
    )
    (arrived,) = ring_steps(
        [ring for ring in (ffn_ring, rest_ring, self_ring) if ring.hop], (packed, moves.pop(0))
    )
    packed = packed + arrived
    in_other = swap(in_half)
    while self_ring.hop or ffn_ring.hop:
        rings = [ring for ring in (ffn_ring, rest_ring, self_ring) if ring.hop]
        riders = [(packed, moves.pop(0))] if moves else []
        for arrived in ring_steps(rings, *riders):
            packed = packed + arrived
    while moves:
        packed = packed + moves.pop(0)(packed)
    grad_input = jnp.where(
        head_index == 0,
        jnp.concatenate([in_half, in_other], axis=0),
        jnp.concatenate([in_other, in_half], axis=0),
    )
    ffn_red, rest_red, self_red = ffn_ring.result(), rest_ring.result(), self_ring.result()
    tail = packed[12:]
    other = swap(tail)
    low_rows = jnp.where(head_index == 0, tail, other)
    high_rows = jnp.where(head_index == 0, other, tail)
    pres = pre_rows.shape[0]

    def side(one):
        return jnp.concatenate([low_rows[one, :cols], high_rows[one, :cols]]), jnp.concatenate(
            [low_rows[one, cols:], high_rows[one, cols:]]
        )

    self_q, self_v = side(0)
    cross_qb, cross_vb = side(1)

    def hidden_bias(start):
        return jnp.concatenate(
            [low_rows[start : start + pres].reshape(-1), high_rows[start : start + pres].reshape(-1)]
        )

    feat_sums = (tail + other)[2 + 2 * pres :]
    folds = feat_sums.shape[0] // 2
    return (
        output.reshape(items, 1, each, width),
        grad_input.reshape(items, 1, each, width),
        jnp.stack([self_red[:, one] for one in three]),
        jnp.stack([self_q, self_v, packed[8]]),
        self_red[:, 3 * cols :].T,
        rest_red[:piece],
        jnp.stack([rest_red[2 * piece : 2 * piece + kv_piece], rest_red[2 * piece + kv_piece :]]),
        jnp.stack([cross_qb, cross_vb, packed[9]]),
        rest_red[piece : 2 * piece].T,
        packed[0:4],
        packed[4:8],
        feat_sums[:folds].reshape(-1)[:feat_width],
        feat_sums[folds:].reshape(-1)[:feat_width],
        ffn_red[:, :hidden_cols][None],
        jnp.stack([hidden_bias(2), hidden_bias(2 + pres)]),
        ffn_red[:, hidden_cols:].T[None],
        packed[10:12],
    )


def solution(mesh):
    placed = (
        P("items", "stream", None, None),
        P("items", None, None),
        P("items", None),
        P("items"),
        P(None, ("items", "stream"), "heads"),
        P(),
        P("heads", ("items", "stream")),
        P(("items", "stream"), "heads"),
        P(None, ("items", "stream"), "heads"),
        P(),
        P("heads", ("items", "stream")),
        P(),
        P(),
        P(),
        P(),
        P("stream", "items", "heads"),
        P(),
        P("stream", "heads", "items"),
        P(),
        P("items", "stream", None, None),
    )
    return jax.shard_map(
        body,
        mesh=mesh,
        in_specs=placed,
        out_specs=(
            P("items", "stream", None, None),
            P("items", "stream", None, None),
            P(None, ("items", "stream"), "heads"),
            P(),
            P("heads", ("items", "stream")),
            P(("items", "stream"), "heads"),
            P(None, ("items", "stream"), "heads"),
            P(),
            P("heads", ("items", "stream")),
            P(),
            P(),
            P(),
            P(),
            P("stream", "items", "heads"),
            P(),
            P("stream", "heads", "items"),
            P(),
        ),
        check_vma=False,
    )
```

```python
import math

import jax
import jax.numpy as jnp
import numpy as np
from jax import lax
from jax.experimental import pallas as pl
from jax.experimental.pallas import tpu as pltpu
from jax.sharding import PartitionSpec as P

HEAD_DIM = 64
EPS = 1e-06
NEG = -1e30
BF = jnp.bfloat16
F32 = jnp.float32


def partner(shard, axis, distance):
    return lax.ppermute(shard, axis, [(i, i ^ 1 << distance) for i in range(lax.axis_size(axis))])


def joined(*values):
    return lax.optimization_barrier(values)


def ring_of(count):
    return list(range(0, count, 2)) + list(range(1, count, 2))[::-1]


def ring_table():
    count = lax.axis_size("items")
    order = ring_of(count)
    table = np.zeros((count, count), np.uint32)
    for place, index in enumerate(order):
        table[index] = [order[(place + far) % count] for far in range(count)]
    return table


def ring_row():
    row = lax.axis_index("items").astype(jnp.uint32)
    table = jnp.asarray(ring_table().astype(np.int32))
    found = lax.dynamic_slice(table, (row, jnp.uint32(0)), (1, table.shape[1]))
    return found.reshape(table.shape[1])


def ring_places():
    table = ring_table()
    count = table.shape[0]
    bits = max(1, (count - 1).bit_length())
    per_word = 32 // bits
    index = lax.axis_index("items").astype(jnp.uint32)
    places = []
    for begin in range(0, count, per_word):
        part = table[:, begin : begin + per_word]
        words = [sum(int(one) << (bits * k) for k, one in enumerate(line)) for line in part]
        word = jnp.uint32(words[0])
        for item in range(1, count):
            word = jnp.where(index == jnp.uint32(item), jnp.uint32(words[item]), word)
        for k in range(part.shape[1]):
            places.append((word >> jnp.uint32(bits * k)) & jnp.uint32((1 << bits) - 1))
    return places


def arrival_order(count):
    order = [0]
    for hop in range(1, count // 2 + 1):
        order.append(count - hop)
        if hop <= (count - 1) // 2:
            order.append(hop)
    return order


def shift_ring(shard, order, step):
    count = len(order)
    return lax.ppermute(
        shard, "items", [(order[i], order[(i + step) % count]) for i in range(count)]
    )


def together(sends):
    values = lax.optimization_barrier(tuple(value for value, _ in sends))
    return lax.optimization_barrier(tuple(move(one) for one, (_, move) in zip(values, sends)))


class Gather:
    def __init__(self, shard):
        self.count = lax.axis_size("items")
        self.order = ring_of(self.count)
        self.up = self.down = shard
        self.pieces = [shard]
        self.hop = 1

    def sends(self):
        result = [(self.up, lambda one: shift_ring(one, self.order, 1))]
        if self.hop <= (self.count - 1) // 2:
            result.append((self.down, lambda one: shift_ring(one, self.order, -1)))
        return result

    def take(self, arrivals):
        self.pieces += arrivals
        self.up = arrivals[0]
        self.down = arrivals[-1]
        self.hop += 1

    def replace(self, up, down):
        self.pieces[-1] = down
        if self.hop - 1 <= (self.count - 1) // 2:
            self.pieces[-2] = up
        self.up, self.down = up, down

    @property
    def left(self):
        return self.hop <= self.count // 2


def gather_step(rings, *riders):
    sends = [ring.sends() for ring in rings]
    arrivals = together(list(riders) + [one for part in sends for one in part])
    ridden, arrivals = arrivals[: len(riders)], arrivals[len(riders) :]
    for ring, part in zip(rings, sends):
        ring.take(list(arrivals[: len(part)]))
        arrivals = arrivals[len(part) :]
    return ridden


def place_items(pieces, places):
    whole = jnp.zeros((len(pieces),) + pieces[0].shape, pieces[0].dtype)
    for far, piece in zip(arrival_order(len(pieces)), pieces):
        whole = lax.dynamic_update_index_in_dim(whole, piece, places[far], 0)
    return whole


def by_stream(own, other, axis):
    first = lax.axis_index("stream") == 0
    return jnp.where(
        first, jnp.stack([own, other], axis=axis), jnp.stack([other, own], axis=axis)
    )


def whole_rows(own, other):
    both = by_stream(own, other, 1)
    return both.reshape((both.shape[0] * both.shape[1] * both.shape[2], both.shape[3]))


def at(pieces, span=slice(None)):
    return lambda which: lax.dynamic_index_in_dim(pieces, which, 0, keepdims=False)[:, span]


def at_stream(pieces, span=slice(None)):
    stream = lax.axis_index("stream").astype(jnp.uint32)
    zero = jnp.uint32(0)

    def read(which):
        start = (which, stream, zero, zero)
        found = lax.dynamic_slice(pieces, start, (1, 1) + pieces.shape[2:])
        return found.reshape(pieces.shape[2:])[:, span]

    return read


class Scatter:
    def __init__(self, groups, axis, places):
        self.groups, self.axis = groups, axis
        self.count = lax.axis_size("items")
        self.order, self.places = ring_of(self.count), places
        self.hop = self.count // 2
        self.up = self.down = None

    def piece(self, distance):
        which = self.places[distance % self.count]
        parts = [sum(read(which).astype(F32) for read in group) for group in self.groups]
        return jnp.concatenate(parts, axis=self.axis)

    def sends(self):
        own = self.piece(self.hop)
        own = own if self.up is None else own + self.up.astype(F32)
        result = [(own.astype(BF), lambda one: shift_ring(one, self.order, 1))]
        if self.hop <= (self.count - 1) // 2:
            own = self.piece(self.count - self.hop)
            own = own if self.down is None else own + self.down.astype(F32)
            result.append((own.astype(BF), lambda one: shift_ring(one, self.order, -1)))
        return result

    def take(self, arrivals):
        self.up = arrivals[0]
        if len(arrivals) > 1:
            self.down = arrivals[1]
        self.hop -= 1
        return arrivals[0]

    def step(self):
        return self.take(together(self.sends()))

    def result(self):
        return self.piece(0) + self.up.astype(F32) + self.down.astype(F32)


def halves(total):
    count = lax.axis_size("items")
    rows = total.shape[0] // (2 * count)
    parts = total.reshape((count, 2, rows, total.shape[1]))
    stream = lax.axis_index("stream").astype(jnp.uint32)
    away = lax.dynamic_index_in_dim(parts, 1 - stream, 1, keepdims=False)
    return parts, away


def over(axis, distance=0):
    return lambda one: partner(one, axis, distance)


def mul(left, right):
    return jnp.dot(left, right, preferred_element_type=F32)


def mul_t(left, right):
    return lax.dot_general(left, right, (((1,), (1,)), ((), ())), preferred_element_type=F32)


def t_mul(left, right):
    return lax.dot_general(left, right, (((0,), (0,)), ((), ())), preferred_element_type=F32)


def standard(rows):
    center = rows - jnp.mean(rows, axis=-1, keepdims=True)
    scale = lax.rsqrt(jnp.mean(center * center, axis=-1, keepdims=True) + EPS)
    return center * scale, scale


def norm_back(grad, unit, scale, gain):
    inner = grad * gain
    return scale * (
        inner
        - jnp.mean(inner, axis=-1, keepdims=True)
        - unit * jnp.mean(inner * unit, axis=-1, keepdims=True)
    )


def pair_sum(near, away):
    return near[...].astype(F32) + away[...].astype(F32)


def total_rows(rows):
    return jnp.sum(rows, axis=0, keepdims=True)


def head_mask(rows, heads, value, dtype):
    row = lax.broadcasted_iota(jnp.int32, (heads * rows, heads * HEAD_DIM), 0) // rows
    col = lax.broadcasted_iota(jnp.int32, (heads * rows, heads * HEAD_DIM), 1) // HEAD_DIM
    return jnp.where(row == col, value, 0.0).astype(dtype)


def stack_heads(rows, heads, mask):
    return jnp.concatenate([rows] * heads, axis=0) * mask


def fold_heads(stacked, heads, mask):
    rows = stacked.shape[0] // heads
    stacked = stacked * mask
    result = stacked[:rows]
    for head in range(1, heads):
        result = result + stacked[head * rows : (head + 1) * rows]
    return result


def softmax(scores):
    power = jnp.exp(scores - jnp.max(scores, axis=-1, keepdims=True))
    return power * (1.0 / jnp.sum(power, axis=-1, keepdims=True))


def attend(queries, keys, values, hide, heads, scaled_mask, out_mask):
    scores = hide(mul_t(stack_heads(queries, heads, scaled_mask), keys))
    weights = softmax(scores).astype(BF)
    return fold_heads(mul(weights, values), heads, out_mask).astype(BF)


def attend_back(queries, keys, values, grad, hide, heads, scaled_mask, plain_mask, out_mask):
    queries = stack_heads(queries, heads, scaled_mask)
    grad = stack_heads(grad, heads, plain_mask)
    weights = softmax(hide(mul_t(queries, keys)))
    grad_weights = mul_t(grad, values)
    grad_values = t_mul(weights.astype(BF), grad)
    delta = jnp.sum(grad_weights * weights, axis=-1, keepdims=True)
    grad_scores = (weights * (grad_weights - delta)).astype(BF)
    grad_queries = fold_heads(mul(grad_scores, keys), heads, out_mask) * HEAD_DIM ** (-0.5)
    return grad_queries, t_mul(grad_scores, queries), grad_values


def whole(shape):
    return pl.BlockSpec(shape, lambda i: (0,) * len(shape))


def block(shape):
    return pl.BlockSpec(shape, lambda i: (i,) + (0,) * (len(shape) - 1))


def column(shape, first=0):
    return pl.BlockSpec(shape, lambda i: (0, i + first))


def shaped(shape, dtype):
    return jax.ShapeDtypeStruct(shape, dtype)


def call(kernel, grid, in_specs, out_specs, out_shape, scratch=(), flops=0, moved=0):
    return pl.pallas_call(
        kernel,
        grid=(grid,),
        in_specs=in_specs,
        out_specs=out_specs,
        out_shape=out_shape,
        scratch_shapes=list(scratch),
        compiler_params=pltpu.CompilerParams(
            dimension_semantics=("arbitrary",), vmem_limit_bytes=56 << 20
        ),
        cost_estimate=pl.CostEstimate(flops=flops, bytes_accessed=moved, transcendentals=0),
    )


def feature_norm(features, gain, shift, padded, begin, each, prior):
    items, patches, width = features.shape

    def kernel(feat, gain, shift, *refs):
        out, token = refs[-2:]
        unit, _ = standard(feat[0].astype(F32))
        out[0, :patches] = (unit * gain[...] + shift[...]).astype(BF)
        out[0, patches:] = jnp.zeros((padded - patches, width), BF)
        token[...] = jnp.zeros_like(token)

    def at_item(i):
        return (i + begin, 0, 0)

    return pl.pallas_call(
        kernel,
        grid=(each,),
        in_specs=[pl.BlockSpec((1, patches, width), at_item), whole((1, width)), whole((1, width))]
        + [pl.BlockSpec(memory_space=pl.ANY)] * len(prior),
        out_specs=[pl.BlockSpec((1, padded, width), at_item), whole((8, 128))],
        out_shape=[shaped((items, padded, width), BF), shaped((8, 128), F32)],
        input_output_aliases={3: 0} if prior else {},
        compiler_params=pltpu.CompilerParams(
            dimension_semantics=("arbitrary",), vmem_limit_bytes=56 << 20
        ),
        cost_estimate=pl.CostEstimate(
            flops=0, bytes_accessed=4 * each * patches * width, transcendentals=0
        ),
    )(features, gain, shift, *prior)


def project(places, own, far, pieces, bias):
    rows, width = own.shape
    count = len(pieces)
    cols = pieces[0].shape[1]
    head_cols = cols // 3
    step = rows // 4
    spots = arrival_order(count)

    def kernel(places, own, far, bias, *refs):
        q, kv, kv_far, weight, laid = refs[count:]

        @pl.when(pl.program_id(0) == 0)
        def _():
            for far_off, one in zip(spots, refs[:count]):
                laid[places[far_off]] = one[...]
            weight[...] = laid[...].reshape(width, cols)

        near = mul(own[...], weight[...]) + bias[...]
        q[...] = near[:, :head_cols].astype(BF)
        kv[...] = near[:, head_cols:].astype(BF)
        kv_far[...] = (mul(far[...], weight[:, head_cols:]) + bias[:, head_cols:]).astype(BF)

    return call(
        kernel,
        4,
        [pl.BlockSpec(memory_space=pltpu.SMEM)]
        + [block((step, width)), block((step, width)), whole((1, cols))]
        + [whole((width // count, cols))] * count,
        [block((step, head_cols)), block((step, 2 * head_cols)), block((step, 2 * head_cols))]
        + [whole((width, cols))],
        [shaped((rows, head_cols), BF)]
        + [shaped((rows, 2 * head_cols), BF)] * 2
        + [shaped((width, cols), BF)],
        scratch=[pltpu.VMEM((count, width // count, cols), BF)],
        flops=10 * rows * width * head_cols,
        moved=4 * rows * width + 4 * width * cols,
    )(places, own, far, bias, *pieces)


def self_attention(q, kv, kv_far, allowed, weight, items, batch):
    rows, cols = q.shape
    heads, each = cols // HEAD_DIM, rows // items
    width = weight.shape[0]

    def kernel(q, kv, kv_far, allowed, weight, attended, out):
        index = pl.program_id(0)
        scaled = head_mask(each, heads, HEAD_DIM ** (-0.5), BF)
        ones = head_mask(each, heads, 1.0, F32)
        for item in range(batch):
            span = slice(item * each, (item + 1) * each)
            keys = jnp.concatenate([kv[span, :cols], kv_far[span, :cols]], axis=0)
            values = jnp.concatenate([kv[span, cols:], kv_far[span, cols:]], axis=0)
            seen = jnp.concatenate([allowed[item]] * heads, axis=0) > 0
            result = attend(
                q[span], keys, values, lambda s: jnp.where(seen, s, NEG), heads, scaled, ones
            )
            start = pl.multiple_of((index * batch + item) * each, each)
            attended[pl.ds(start, each), :] = result

        @pl.when(index == pl.num_programs(0) - 1)
        def _():
            out[...] = mul_t(attended[...], weight[...]).astype(BF)

    part = batch * each
    return call(
        kernel,
        items // batch,
        [
            block((part, cols)),
            block((part, 2 * cols)),
            block((part, 2 * cols)),
            block((batch, each, 2 * each)),
            whole((width, cols)),
        ],
        [whole((rows, cols)), whole((rows, width))],
        [shaped((rows, cols), BF), shaped((rows, width), BF)],
        flops=2 * rows * cols * width * 3,
        moved=rows * cols * 14 + rows * width * 4,
    )(q, kv, kv_far, allowed, weight)


def cross_attention(own, near, away, rows_in, cq, keys_values, weight, items, batch, patches):
    rows, width = own.shape
    cols = weight.shape[1]
    heads, each = cols // HEAD_DIM, rows // items
    padded = keys_values.shape[1]

    def kernel(own, near, away, bias, gain, shift, bias_q, cq, kv, weight, unit, scale, low, qc, attended, out):
        index = pl.program_id(0)

        @pl.when(index == 0)
        def _():
            one, size = standard(own[...].astype(F32) + pair_sum(near, away) + bias[...])
            unit[...] = one
            scale[...] = size
            low[...] = (one * gain[...] + shift[...]).astype(BF)
            qc[...] = (mul(low[...], cq[...]) + bias_q[...]).astype(BF)

        scaled = head_mask(each, heads, HEAD_DIM ** (-0.5), BF)
        ones = head_mask(each, heads, 1.0, F32)
        real = lax.broadcasted_iota(jnp.int32, (heads * each, padded), 1) < patches
        for item in range(batch):
            start = pl.multiple_of((index * batch + item) * each, each)
            attended[pl.ds(start, each), :] = attend(
                qc[pl.ds(start, each), :],
                kv[item, :, :cols],
                kv[item, :, cols:],
                lambda s: jnp.where(real, s, NEG),
                heads,
                scaled,
                ones,
            )

        @pl.when(index == pl.num_programs(0) - 1)
        def _():
            out[...] = mul_t(attended[...], weight[...]).astype(BF)

    bias, gain, shift, bias_q = rows_in
    return call(
        kernel,
        items // batch,
        [whole((rows, width))] * 3
        + [whole((1, width))] * 3
        + [whole((1, cols)), whole((width, cols)), block((batch, padded, 2 * cols)), whole((width, cols))],
        [
            whole((rows, width)),
            whole((rows, 1)),
            whole((rows, width)),
            whole((rows, cols)),
            whole((rows, cols)),
            whole((rows, width)),
        ],
        [
            shaped((rows, width), F32),
            shaped((rows, 1), F32),
            shaped((rows, width), BF),
            shaped((rows, cols), BF),
            shaped((rows, cols), BF),
            shaped((rows, width), BF),
        ],
        flops=2 * rows * cols * padded * heads * 2,
        moved=rows * width * 20 + 4 * items * padded * cols,
    )(own, near, away, bias, gain, shift, bias_q, cq, keys_values, weight)


def lay_pieces(places, spots, refs, laid):
    count, rows, cols = laid.shape[1:]
    for far_off, w_in, w_out in zip(spots, refs[:count], refs[count:]):
        laid[0, places[far_off]] = w_in[...]
        laid[1, places[far_off]] = w_out[...]
    return laid[0].reshape(count * rows, cols), laid[1].reshape(count * rows, cols)


def feed_forward(flag, places, unit, near, away, rows_in, pieces, b_in, chunk):
    rows, width = unit.shape
    hidden = pieces[0].shape[1] // 2
    steps = hidden // chunk
    count = len(pieces)
    spots = arrival_order(count)

    def kernel(flag, places, unit, near, away, gain0, shift0, bias, gain1, shift1, b_in, *refs):
        z, z_low, unit2, scale2, act, slope, part, out, laid = refs[2 * count :]
        w_in, w_out = lay_pieces(places, spots, refs[: 2 * count], laid)

        @pl.when(pl.program_id(0) == 0)
        def _():
            after = unit[...] * gain0[...] + shift0[...]
            one, size = standard(after + pair_sum(near, away) + bias[...])
            unit2[...] = one
            scale2[...] = size
            z[...] = jnp.where(flag[0] == 0, one * gain1[...] + shift1[...], after)
            z_low[...] = z[...].astype(BF)
            out[...] = jnp.zeros_like(out)

        for half in range(2):
            span = slice(half * rows // 2, (half + 1) * rows // 2)
            u = mul(z_low[span], w_in) + b_in[...]
            share = 0.5 + 0.5 * lax.erf(u * math.sqrt(0.5))
            act_half = (u * share).astype(BF)
            act[span] = act_half
            slope[span] = share + u * (jnp.exp(-0.5 * u * u) * (1.0 / math.sqrt(2.0 * math.pi)))
            out[span] += mul_t(act_half, w_out)

        @pl.when(pl.program_id(0) == steps - 1)
        def _():
            part[...] = out[...].astype(BF)

    row = whole((1, width))
    return call(
        kernel,
        steps,
        [pl.BlockSpec(memory_space=pltpu.SMEM)] * 2
        + [whole((rows, width))] * 3
        + [row] * 5
        + [column((1, chunk))]
        + [column((width // count, chunk))] * count
        + [column((width // count, chunk), steps)] * count,
        [
            whole((rows, width)),
            whole((rows, width)),
            whole((rows, width)),
            whole((rows, 1)),
            column((rows, chunk)),
            column((rows, chunk)),
            whole((rows, width)),
        ],
        [
            shaped((rows, width), F32),
            shaped((rows, width), BF),
            shaped((rows, width), F32),
            shaped((rows, 1), F32),
            shaped((rows, hidden), BF),
            shaped((rows, hidden), F32),
            shaped((rows, width), BF),
        ],
        scratch=[pltpu.VMEM((rows, width), F32), pltpu.VMEM((2, count, width // count, chunk), BF)],
        flops=4 * rows * hidden * width,
        moved=rows * width * 26 + rows * hidden * 6 + width * hidden * 4,
    )(flag, places, unit, near, away, *rows_in, b_in, *pieces, *pieces)


def feed_back(places, z, near, away, cotangent, rows_in, slope, pieces, chunk):
    rows, width = z.shape
    hidden = pieces[0].shape[1] // 2
    steps = hidden // chunk
    count = len(pieces)
    spots = arrival_order(count)

    def kernel(places, z, near, away, cot, bias, gain, shift, slope, *refs):
        result, grad_v, grad_u, grad_pre, part, sums, sum_pre, out, laid = refs[2 * count :]
        w_in, w_out = lay_pieces(places, spots, refs[: 2 * count], laid)

        @pl.when(pl.program_id(0) == 0)
        def _():
            one, size = standard(z[...] + pair_sum(near, away) + bias[...])
            dy = cot[...]
            result[...] = (one * gain[...] + shift[...]).astype(BF)
            grad_v[...] = norm_back(dy, one, size, gain[...])
            grad_u[...] = grad_v[...].astype(BF)
            sums[0:1] = total_rows(dy * one)
            sums[1:2] = total_rows(dy)
            sums[2:3] = total_rows(grad_u[...].astype(F32))
            out[...] = jnp.zeros_like(out)

        for half in range(2):
            span = slice(half * rows // 2, (half + 1) * rows // 2)
            pre = (mul(grad_u[span], w_out) * slope[span]).astype(BF)
            grad_pre[span] = pre
            out[span] += mul_t(pre, w_in)
        sum_pre[...] = total_rows(grad_pre[...].astype(F32))

        @pl.when(pl.program_id(0) == steps - 1)
        def _():
            part[...] = out[...].astype(BF)

    row = whole((1, width))
    return call(
        kernel,
        steps,
        [pl.BlockSpec(memory_space=pltpu.SMEM)]
        + [whole((rows, width))] * 4
        + [row] * 3
        + [column((rows, chunk))]
        + [column((width // count, chunk))] * count
        + [column((width // count, chunk), steps)] * count,
        [
            whole((rows, width)),
            whole((rows, width)),
            whole((rows, width)),
            column((rows, chunk)),
            whole((rows, width)),
            whole((8, width)),
            column((1, chunk)),
        ],
        [
            shaped((rows, width), BF),
            shaped((rows, width), F32),
            shaped((rows, width), BF),
            shaped((rows, hidden), BF),
            shaped((rows, width), BF),
            shaped((8, width), F32),
            shaped((1, hidden), F32),
        ],
        scratch=[pltpu.VMEM((rows, width), F32), pltpu.VMEM((2, count, width // count, chunk), BF)],
        flops=4 * rows * hidden * width,
        moved=rows * width * 28 + rows * hidden * 6 + width * hidden * 4,
    )(places, z, near, away, cotangent, *rows_in, slope, *pieces, *pieces)


def cross_back(flag, grad_v, near, away, unit2, scale2, gain, qc, keys_values, weight, cq, items, batch, patches):
    rows, width = grad_v.shape
    cols = weight.shape[1]
    heads, each = cols // HEAD_DIM, rows // items
    padded = keys_values.shape[1]

    def kernel(flag, grad_v, near, away, unit2, scale2, gain, qc, kv, weight, cq, after, mix, grad_qc, grad_kv, out, sums, sums_c, grad_att):
        index = pl.program_id(0)

        @pl.when(index == 0)
        def _():
            dz = grad_v[...] + pair_sum(near, away)
            mine = flag[0] == 0
            used = jnp.where(mine, dz, 0.0)
            two = norm_back(used, unit2[...], scale2[...], gain[...])
            after[...] = jnp.where(mine, two, dz)
            mix[...] = two.astype(BF)
            grad_att[...] = mul(mix[...], weight[...]).astype(BF)
            sums[0:1] = total_rows(used * unit2[...])
            sums[1:2] = total_rows(used)
            sums[2:3] = total_rows(mix[...].astype(F32))
            sums_c[...] = jnp.zeros_like(sums_c)

        root = HEAD_DIM ** (-0.5)
        scaled = head_mask(each, heads, root, BF)
        plain = head_mask(each, heads, 1.0, BF)
        ones = head_mask(each, heads, 1.0, F32)
        real = lax.broadcasted_iota(jnp.int32, (heads * each, padded), 1) < patches
        for item in range(batch):
            start = pl.multiple_of((index * batch + item) * each, each)
            dq, dk, dv = attend_back(
                qc[pl.ds(start, each), :],
                kv[item, :, :cols],
                kv[item, :, cols:],
                grad_att[pl.ds(start, each), :],
                lambda s: jnp.where(real, s, NEG),
                heads,
                scaled,
                plain,
                ones,
            )
            grad_qc[pl.ds(start, each), :] = dq.astype(BF)
            dk, dv = dk.astype(BF), dv.astype(BF)
            grad_kv[item, :, :cols] = dk
            grad_kv[item, :, cols:] = dv
            sums_c[1:2] += total_rows(dk.astype(F32))
            sums_c[2:3] += total_rows(dv.astype(F32))

        @pl.when(index == pl.num_programs(0) - 1)
        def _():
            out[...] = mul_t(grad_qc[...], cq[...]).astype(BF)
            sums_c[0:1] = total_rows(grad_qc[...].astype(F32))

    return call(
        kernel,
        items // batch,
        [pl.BlockSpec(memory_space=pltpu.SMEM)]
        + [whole((rows, width))] * 4
        + [
            whole((rows, 1)),
            whole((1, width)),
            whole((rows, cols)),
            block((batch, padded, 2 * cols)),
            whole((width, cols)),
            whole((width, cols)),
        ],
        [
            whole((rows, width)),
            whole((rows, width)),
            whole((rows, cols)),
            block((batch, padded, 2 * cols)),
            whole((rows, width)),
            whole((8, width)),
            whole((8, cols)),
        ],
        [
            shaped((rows, width), F32),
            shaped((rows, width), BF),
            shaped((rows, cols), BF),
            shaped((items, padded, 2 * cols), BF),
            shaped((rows, width), BF),
            shaped((8, width), F32),
            shaped((8, cols), F32),
        ],
        scratch=[pltpu.VMEM((rows, cols), BF)],
        flops=2 * rows * cols * padded * heads * 5,
        moved=rows * width * 26 + 8 * items * padded * cols,
    )(flag, grad_v, near, away, unit2, scale2, gain, qc, keys_values, weight, cq)


def self_back(flag, after, near, away, unit, scale, gain, q, kv, kv_far, allowed, weight, w_qkv, own, far, attended, items, batch, shards):
    rows, width = after.shape
    cols = weight.shape[1]
    heads, each = cols // HEAD_DIM, rows // items
    piece = width // shards

    def kernel(flag, after, near, away, unit, scale, gain, q, kv, kv_far, allowed, weight, w_qkv, own, far, attended, grad_one, mix, grad_near, grad_away, both, sums, sums_c, grad_keep, grad_sent, grad_att):
        index = pl.program_id(0)

        @pl.when(index == 0)
        def _():
            grad = after[...] + pair_sum(near, away)
            grad_one[...] = norm_back(grad, unit[...], scale[...], gain[...])
            mix[...] = grad_one[...].astype(BF)
            grad_att[...] = mul(mix[...], weight[...]).astype(BF)
            sums[0:1] = total_rows(grad * unit[...])
            sums[1:2] = total_rows(grad)
            sums[2:3] = total_rows(mix[...].astype(F32))

        scaled = head_mask(each, heads, HEAD_DIM ** (-0.5), BF)
        plain = head_mask(each, heads, 1.0, BF)
        ones = head_mask(each, heads, 1.0, F32)
        for item in range(batch):
            span = slice(item * each, (item + 1) * each)
            start = pl.multiple_of((index * batch + item) * each, each)
            keys = jnp.concatenate([kv[span, :cols], kv_far[span, :cols]], axis=0)
            values = jnp.concatenate([kv[span, cols:], kv_far[span, cols:]], axis=0)
            seen = jnp.concatenate([allowed[item]] * heads, axis=0) > 0
            dq, dk, dv = attend_back(
                q[span],
                keys,
                values,
                grad_att[pl.ds(start, each), :],
                lambda s: jnp.where(seen, s, NEG),
                heads,
                scaled,
                plain,
                ones,
            )
            grad_near[pl.ds(start, each), :cols] = dq.astype(BF)
            grad_near[pl.ds(start, each), cols : 2 * cols] = dk[:each].astype(BF)
            grad_near[pl.ds(start, each), 2 * cols :] = dv[:each].astype(BF)
            grad_away[pl.ds(start, each), :cols] = dk[each:].astype(BF)
            grad_away[pl.ds(start, each), cols:] = dv[each:].astype(BF)

        @pl.when(index == pl.num_programs(0) - 1)
        def _():
            both[:, :width] = mul_t(grad_near[...], w_qkv[...]).astype(BF)
            both[:, width:] = mul_t(grad_away[...], w_qkv[:, cols:]).astype(BF)
            for place in range(4):
                span = slice(place * cols, (place + 1) * cols)
                if place == 3:
                    total = t_mul(mix[...], attended[...])
                else:
                    total = t_mul(own[...], grad_near[:, span])
                if place in (1, 2):
                    total = total + t_mul(far[...], grad_away[:, (place - 1) * cols : place * cols])
                total = total.astype(BF)
                for side in range(2):
                    pieces = [
                        total[one * piece : (one + 1) * piece] for one in range(side, shards, 2)
                    ]

                    @pl.when(flag[0] == side)
                    def _():
                        for one, value in enumerate(pieces):
                            grad_keep[one, :, span] = value

                    @pl.when(flag[0] != side)
                    def _():
                        for one, value in enumerate(pieces):
                            grad_sent[one, :, span] = value
            sums_c[0:1] = total_rows(grad_near[...].astype(F32))
            sums_c[1:2, cols:] = total_rows(grad_away[...].astype(F32))

    part = batch * each
    return call(
        kernel,
        items // batch,
        [pl.BlockSpec(memory_space=pltpu.SMEM)]
        + [whole((rows, width))] * 4
        + [
            whole((rows, 1)),
            whole((1, width)),
            block((part, cols)),
            block((part, 2 * cols)),
            block((part, 2 * cols)),
            block((batch, each, 2 * each)),
            whole((width, cols)),
            whole((width, 3 * cols)),
            whole((rows, width)),
            whole((rows, width)),
            whole((rows, cols)),
        ],
        [
            whole((rows, width)),
            whole((rows, width)),
            whole((rows, 3 * cols)),
            whole((rows, 2 * cols)),
            whole((rows, 2 * width)),
            whole((8, width)),
            whole((8, 3 * cols)),
            whole((shards // 2, piece, 4 * cols)),
            whole((shards // 2, piece, 4 * cols)),
        ],
        [
            shaped((rows, width), F32),
            shaped((rows, width), BF),
            shaped((rows, 3 * cols), BF),
            shaped((rows, 2 * cols), BF),
            shaped((rows, 2 * width), BF),
            shaped((8, width), F32),
            shaped((8, 3 * cols), F32),
            shaped((shards // 2, piece, 4 * cols), BF),
            shaped((shards // 2, piece, 4 * cols), BF),
        ],
        scratch=[pltpu.VMEM((rows, cols), BF)],
        flops=2 * rows * cols * width * 9,
        moved=rows * width * 32 + rows * cols * 20,
    )(flag, after, near, away, unit, scale, gain, q, kv, kv_far, allowed, weight, w_qkv, own, far, attended)


def visible(stream, segments, modes):
    same_caption = segments[:, :, None] == segments[:, None, :]
    own = jnp.logical_or(stream == 0, same_caption)
    far = jnp.where(stream == 0, modes == 2, modes >= 1)[:, None, None]
    return jnp.concatenate([own, jnp.broadcast_to(far, own.shape)], axis=2).astype(F32)


def body(
    hidden,
    features,
    segments,
    modes,
    w_qkv,
    self_bias,
    self_out,
    cross_q,
    cross_kv,
    cross_bias,
    cross_out,
    gains,
    shifts,
    feat_gain,
    feat_shift,
    ffn_in,
    ffn_bias_in,
    ffn_out,
    ffn_bias_out,
    cotangent,
):
    stream = lax.axis_index("stream")
    stream_u = stream.astype(jnp.uint32)
    head_index = lax.axis_index("heads")
    items, _, each, width = hidden.shape
    rows = items * each
    half = rows // 2
    cols = w_qkv.shape[2]
    hidden_cols = ffn_in.shape[2]
    patches, feat_width = features.shape[1:]
    padded = (patches + 7) // 8 * 8
    col_start = head_index.astype(jnp.uint32) * cols
    hidden_start = head_index.astype(jnp.uint32) * hidden_cols
    flag = stream.astype(jnp.int32).reshape(1)
    shards = 2 * lax.axis_size("items")
    three = [slice(i * cols, (i + 1) * cols) for i in range(3)]

    part_qkv = jnp.concatenate([w_qkv[0], w_qkv[1], w_qkv[2]], axis=1)
    pair_qkv = by_stream(part_qkv, partner(part_qkv, "stream", 0), 0)
    places = ring_places()
    spots = ring_row()
    qkv_ring = Gather(pair_qkv.reshape(width // (shards // 2), 3 * cols))
    own = hidden.reshape(rows, width)
    heads_u = head_index.astype(jnp.uint32)
    my_half = lax.dynamic_slice_in_dim(own, heads_u * half, half, 0)
    far_half = partner(my_half, "stream", 0)
    later_out, part_qkv = joined(self_out, part_qkv)
    rest_ring = Gather(
        jnp.concatenate([later_out.T, cross_q, cross_out.T, cross_kv[0], cross_kv[1]], axis=0)
    )

    def row(vector):
        return vector.reshape(1, -1)

    kept, chunk = [], items // 4
    for number in range(max(4, shards // 4)):
        if number == 1:
            (far_other,) = gather_step([qkv_ring, rest_ring], (far_half, over("heads")))
        elif qkv_ring.left:
            gather_step([qkv_ring, rest_ring])
        if number < 4:
            *kept, token = list(
                feature_norm(
                    features, row(feat_gain), row(feat_shift), padded, number * chunk, chunk, kept
                )
            )
            ends = joined(qkv_ring.up, qkv_ring.down, rest_ring.up, rest_ring.down, token)
            qkv_ring.replace(*ends[:2])
            rest_ring.replace(*ends[2:4])
            kept = [kept[0], ends[4]]
    feat_norm = kept[0]
    far = jnp.where(
        head_index == 0,
        jnp.concatenate([far_half, far_other], axis=0),
        jnp.concatenate([far_other, far_half], axis=0),
    )
    feat_rows = feat_norm.reshape(items * padded, feat_width)
    qkv_pieces = qkv_ring.pieces
    rest = place_items(rest_ring.pieces, places)
    piece = cross_q.shape[0]
    kv_piece = cross_kv.shape[1]
    out_rest = rest[:, :piece]
    mid_rest = jnp.concatenate(
        [rest[:, piece : 2 * piece], rest[:, 2 * piece : 3 * piece]], axis=2
    )
    kv_rest = jnp.concatenate(
        [rest[:, 3 * piece : 3 * piece + kv_piece], rest[:, 3 * piece + kv_piece :]], axis=2
    )
    out_other, kv_rest = joined(partner(out_rest, "stream", 0), kv_rest)
    kv_other, mid_rest = joined(partner(kv_rest, "stream", 0), mid_rest)
    self_out_t = whole_rows(out_rest, out_other)
    kv_all = whole_rows(kv_rest, kv_other)
    mid_all = whole_rows(mid_rest, partner(mid_rest, "stream", 0))
    cross_q_all, cross_out_t = mid_all[:, :cols], mid_all[:, cols:]
    ffn_part = jnp.concatenate([ffn_in[0], ffn_out[0].T], axis=1)
    ffn_part, last = joined(ffn_part, qkv_ring.up)
    qkv_ring.replace(last, last)
    ffn_gather = Gather(ffn_part)

    def ffn_step(value, last=False):
        if not ffn_gather.left:
            return value
        gather_step([ffn_gather])
        while last and ffn_gather.left:
            gather_step([ffn_gather])
        value, up, down = joined(value, ffn_gather.up, ffn_gather.down)
        ffn_gather.replace(up, down)
        return value

    def my_cols(vector):
        return lax.dynamic_slice_in_dim(vector, col_start, cols, 0)

    none = jnp.zeros((cols,), F32)
    bias_qkv = row(jnp.concatenate([my_cols(self_bias[0]), none, my_cols(self_bias[1])]))
    bias_kv = row(jnp.concatenate([none, my_cols(cross_bias[1])]))
    gain_ffn = row(lax.dynamic_index_in_dim(gains, 2 + stream_u, 0, keepdims=False))
    shift_ffn = row(lax.dynamic_index_in_dim(shifts, 2 + stream_u, 0, keepdims=False))
    bias_in = row(
        lax.dynamic_slice_in_dim(
            lax.dynamic_index_in_dim(ffn_bias_in, stream_u, 0, keepdims=False),
            hidden_start,
            hidden_cols,
            0,
        )
    )
    bias_out = row(lax.dynamic_index_in_dim(ffn_bias_out, stream_u, 0, keepdims=False))

    def swap(part):
        return partner(part, "heads", 0)

    far = ffn_step(far)
    q, kv, kv_far, qkv_all = project(spots, own, far, qkv_pieces, bias_qkv)
    allowed = visible(stream, segments, modes)
    kv_far = ffn_step(kv_far)
    attended, part = self_attention(q, kv, kv_far, allowed, self_out_t, items, 4)
    kv_all = ffn_step(kv_all)
    away_one = ffn_step(swap(part), True)
    ffn_pieces = ffn_gather.pieces
    keys_values = (mul(feat_rows, kv_all) + bias_kv).astype(BF).reshape(items, padded, 2 * cols)
    unit_one, scale_one, after_low, qc, attended_c, part_c = cross_attention(
        own,
        part,
        away_one,
        (row(self_bias[2]), row(gains[0]), row(shifts[0]), row(my_cols(cross_bias[0]))),
        cross_q_all,
        keys_values,
        cross_out_t,
        items,
        2,
        patches,
    )
    z, z_low, unit_two, scale_two, activated, slope, part_f = feed_forward(
        flag,
        spots,
        unit_one,
        part_c,
        swap(part_c),
        (row(gains[0]), row(shifts[0]), row(cross_bias[2]), row(gains[1]), row(shifts[1])),
        ffn_pieces,
        bias_in,
        256,
    )

    output, grad_three, grad_u, grad_pre, part_z, sums_three, sum_pre = feed_back(
        spots,
        z,
        part_f,
        swap(part_f),
        cotangent.reshape(rows, width),
        (bias_out, gain_ffn, shift_ffn),
        slope,
        ffn_pieces,
        256,
    )
    away_z = swap(part_z)
    in_grad = t_mul(z_low, grad_pre).astype(BF)
    out_grad = t_mul(grad_u, activated).astype(BF)
    count = shards // 2
    ffn_ring = Scatter(
        [
            [at(in_grad.reshape(count, -1, hidden_cols))],
            [at(out_grad.reshape(count, -1, hidden_cols))],
        ],
        1,
        places,
    )
    first = ffn_ring.step()
    grad_after, mix_c, grad_qc, grad_kv, part_a, sums_two, sums_cross = cross_back(
        flag,
        grad_three,
        part_z,
        away_z,
        unit_two,
        scale_two,
        row(gains[1]),
        qc,
        keys_values,
        cross_out_t,
        cross_q_all,
        items,
        2,
        patches,
    )
    grad_after, mix_c, grad_qc, grad_kv, part_a, sums_two, sums_cross, first = (
        lax.optimization_barrier(
            (grad_after, mix_c, grad_qc, grad_kv, part_a, sums_two, sums_cross, first)
        )
    )
    ffn_ring.up = first
    away_a = swap(part_a)
    keep_q, away_q = halves(t_mul(after_low, grad_qc).astype(BF))
    keep_o, away_o = halves(t_mul(mix_c, attended_c).astype(BF))
    away_c = jnp.concatenate([away_q, away_o], axis=2)
    grad_kv, away_c = joined(grad_kv, away_c)
    kv_grad = t_mul(feat_rows, grad_kv.reshape(items * padded, 2 * cols))
    ffn_ring.step()
    kv_grad_low = kv_grad.astype(BF)
    arrived_c = partner(away_c, "stream", 0)
    kv_grad, kv_grad_low, arrived_c, ffn_ring.up, ffn_ring.down = lax.optimization_barrier(
        (kv_grad, kv_grad_low, arrived_c, ffn_ring.up, ffn_ring.down)
    )
    keep_kv, away_kv = halves(kv_grad_low)
    ffn_ring.step()
    away_a, away_kv = joined(away_a, away_kv)
    arrived_kv = partner(away_kv, "stream", 0)
    grad_one, mix, grad_near, grad_away, both, sums_one, sums_self, keep_self, away_self = self_back(
        flag,
        grad_after,
        part_a,
        away_a,
        unit_one,
        scale_one,
        row(gains[0]),
        q,
        kv,
        kv_far,
        allowed,
        self_out_t,
        qkv_all,
        own,
        far,
        attended,
        items,
        4,
        shards,
    )

    results = (grad_one, both, sums_one, sums_self, keep_self, away_self, arrived_kv)
    results = lax.optimization_barrier(results + (ffn_ring.up, ffn_ring.down))
    grad_one, both, sums_one, sums_self, keep_self, away_self, arrived_kv = results[:-2]
    ffn_ring.up, ffn_ring.down = results[-2:]

    theirs = lax.dynamic_slice_in_dim(both, (1 - heads_u) * half, half, 0)
    mine = lax.dynamic_slice_in_dim(both, heads_u * half, half, 0)

    def ring_steps(rings, *riders):
        sends = [ring.sends() for ring in rings]
        flat = [one for part in sends for one in part]
        arrivals = together(list(riders) + flat)
        rest = arrivals[len(riders) :]
        for ring, part in zip(rings, sends):
            ring.take(rest[: len(part)])
            rest = rest[len(part) :]
        return arrivals[: len(riders)]

    rest_ring = Scatter(
        [
            [at_stream(keep_q), at(arrived_c, three[0])],
            [at_stream(keep_o), at(arrived_c, three[1])],
            [at_stream(keep_kv, three[0]), at(arrived_kv, three[0])],
            [at_stream(keep_kv, three[1]), at(arrived_kv, three[1])],
        ],
        0,
        places,
    )
    arrived_self, from_swap = ring_steps(
        [ffn_ring, rest_ring], (away_self, over("stream")), (theirs, over("heads"))
    )
    self_ring = Scatter([[at(keep_self), at(arrived_self)]], 0, places)
    total = mine.astype(F32) + from_swap.astype(F32)
    from_far = partner(total[:, width:].astype(BF), "stream", 0)
    small = (sums_one, sums_two, sums_three, sums_self, sums_cross, sum_pre, kv_grad, kv_all)
    sums_one, sums_two, sums_three, sums_self, sums_cross, sum_pre, kv_grad, kv_late = (
        lax.optimization_barrier(small)
    )

    dot_w = jnp.sum(kv_grad * kv_late.astype(F32), axis=1)
    feat_shift_grad = jnp.sum(
        kv_late.astype(F32) * jnp.concatenate([sums_cross[1], sums_cross[2]])[None], axis=1
    )
    feat_gain_grad = (dot_w - feat_shift * feat_shift_grad) / feat_gain

    def pair_row(left, right):
        return jnp.concatenate([left, right]).reshape(1, width)

    def fold(vector):
        length = (vector.shape[0] + width - 1) // width * width
        return jnp.pad(vector, (0, length - vector.shape[0])).reshape(-1, width)

    on_query, on_text = (stream == 0).astype(F32), (stream == 1).astype(F32)
    pre_rows = sum_pre.reshape(-1, width)
    full = [
        one[place : place + 1]
        for place in range(3)
        for one in (sums_one, sums_two, on_query * sums_three, on_text * sums_three)
    ]
    own_half = [
        pair_row(sums_self[0, three[0]], sums_self[0, three[2]] + sums_self[1, three[2]]),
        pair_row(sums_cross[0], sums_cross[2]),
        on_query * pre_rows,
        on_text * pre_rows,
    ]
    feats = [fold(feat_gain_grad), fold(feat_shift_grad)]
    packed = jnp.concatenate(full + own_half + feats, axis=0)
    moves = [over("stream")] + [over("items", bit) for bit in range((count - 1).bit_length())]

    in_half = (
        lax.dynamic_slice_in_dim(grad_one, heads_u * half, half, 0)
        + total[:, :width]
        + from_far.astype(F32)
    )
    (arrived,) = ring_steps(
        [one for one in (ffn_ring, rest_ring, self_ring) if one.hop], (packed, moves.pop(0))
    )
    packed = packed + arrived
    in_other = swap(in_half)
    while self_ring.hop or ffn_ring.hop:
        rings = [one for one in (ffn_ring, rest_ring, self_ring) if one.hop]
        riders = [(packed, moves.pop(0))] if moves else []
        for arrived in ring_steps(rings, *riders):
            packed = packed + arrived
    while moves:
        packed = packed + moves.pop(0)(packed)
    grad_input = jnp.where(
        head_index == 0,
        jnp.concatenate([in_half, in_other], axis=0),
        jnp.concatenate([in_other, in_half], axis=0),
    )
    ffn_red, rest_red, self_red = ffn_ring.result(), rest_ring.result(), self_ring.result()
    tail = packed[12:]
    other = swap(tail)
    low_rows = jnp.where(head_index == 0, tail, other)
    high_rows = jnp.where(head_index == 0, other, tail)
    pres = pre_rows.shape[0]

    def side(one):
        return jnp.concatenate([low_rows[one, :cols], high_rows[one, :cols]]), jnp.concatenate(
            [low_rows[one, cols:], high_rows[one, cols:]]
        )

    self_q, self_v = side(0)
    cross_qb, cross_vb = side(1)

    def hidden_bias(start):
        return jnp.concatenate(
            [low_rows[start : start + pres].reshape(-1), high_rows[start : start + pres].reshape(-1)]
        )

    feat_sums = (tail + other)[2 + 2 * pres :]
    folds = feat_sums.shape[0] // 2
    return (
        output.reshape(items, 1, each, width),
        grad_input.reshape(items, 1, each, width),
        jnp.stack([self_red[:, one] for one in three]),
        jnp.stack([self_q, self_v, packed[8]]),
        self_red[:, 3 * cols :].T,
        rest_red[:piece],
        rest_red[2 * piece :].reshape(2, kv_piece, cols),
        jnp.stack([cross_qb, cross_vb, packed[9]]),
        rest_red[piece : 2 * piece].T,
        packed[0:4],
        packed[4:8],
        feat_sums[:folds].reshape(-1)[:feat_width],
        feat_sums[folds:].reshape(-1)[:feat_width],
        ffn_red[:, :hidden_cols][None],
        jnp.stack([hidden_bias(2), hidden_bias(2 + pres)]),
        ffn_red[:, hidden_cols:].T[None],
        packed[10:12],
    )


def solution(mesh):
    placed = (
        P("items", "stream", None, None),
        P("items", None, None),
        P("items", None),
        P("items"),
        P(None, ("items", "stream"), "heads"),
        P(),
        P("heads", ("items", "stream")),
        P(("items", "stream"), "heads"),
        P(None, ("items", "stream"), "heads"),
        P(),
        P("heads", ("items", "stream")),
        P(),
        P(),
        P(),
        P(),
        P("stream", "items", "heads"),
        P(),
        P("stream", "heads", "items"),
        P(),
        P("items", "stream", None, None),
    )
    return jax.shard_map(
        body,
        mesh=mesh,
        in_specs=placed,
        out_specs=(
            P("items", "stream", None, None),
            P("items", "stream", None, None),
            P(None, ("items", "stream"), "heads"),
            P(),
            P("heads", ("items", "stream")),
            P(("items", "stream"), "heads"),
            P(None, ("items", "stream"), "heads"),
            P(),
            P("heads", ("items", "stream")),
            P(),
            P(),
            P(),
            P(),
            P("stream", "items", "heads"),
            P(),
            P("stream", "heads", "items"),
            P(),
        ),
        check_vma=False,
    )
```

```python
import math

import jax
import jax.numpy as jnp
import numpy as np
from jax import lax
from jax.experimental import pallas as pl
from jax.experimental.pallas import tpu as pltpu
from jax.sharding import PartitionSpec as P

HEAD_DIM = 64
EPS = 1e-06
NEG = -1e30
BF = jnp.bfloat16
F32 = jnp.float32


def partner(shard, axis, distance):
    return lax.ppermute(shard, axis, [(i, i ^ 1 << distance) for i in range(lax.axis_size(axis))])


def joined(*values):
    return lax.optimization_barrier(values)


def ring_of(count):
    return list(range(0, count, 2)) + list(range(1, count, 2))[::-1]


def ring_table():
    count = lax.axis_size("items")
    order = ring_of(count)
    table = np.zeros((count, count), np.uint32)
    for place, index in enumerate(order):
        table[index] = [order[(place + far) % count] for far in range(count)]
    return table


def ring_row():
    row = lax.axis_index("items").astype(jnp.uint32)
    table = jnp.asarray(ring_table().astype(np.int32))
    found = lax.dynamic_slice(table, (row, jnp.uint32(0)), (1, table.shape[1]))
    return found.reshape(table.shape[1])


def ring_places():
    table = ring_table()
    count = table.shape[0]
    bits = max(1, (count - 1).bit_length())
    per_word = 32 // bits
    index = lax.axis_index("items").astype(jnp.uint32)
    places = []
    for begin in range(0, count, per_word):
        part = table[:, begin : begin + per_word]
        words = [sum(int(one) << (bits * k) for k, one in enumerate(line)) for line in part]
        word = jnp.uint32(words[0])
        for item in range(1, count):
            word = jnp.where(index == jnp.uint32(item), jnp.uint32(words[item]), word)
        for k in range(part.shape[1]):
            places.append((word >> jnp.uint32(bits * k)) & jnp.uint32((1 << bits) - 1))
    return places


def arrival_order(count):
    order = [0]
    for hop in range(1, count // 2 + 1):
        order.append(count - hop)
        if hop <= (count - 1) // 2:
            order.append(hop)
    return order


def shift_ring(shard, order, step):
    count = len(order)
    return lax.ppermute(
        shard, "items", [(order[i], order[(i + step) % count]) for i in range(count)]
    )


def together(sends):
    values = lax.optimization_barrier(tuple(value for value, _ in sends))
    return lax.optimization_barrier(tuple(move(one) for one, (_, move) in zip(values, sends)))


class Gather:
    def __init__(self, shard):
        self.count = lax.axis_size("items")
        self.order = ring_of(self.count)
        self.up = self.down = shard
        self.pieces = [shard]
        self.hop = 1

    def sends(self):
        result = [(self.up, lambda one: shift_ring(one, self.order, 1))]
        if self.hop <= (self.count - 1) // 2:
            result.append((self.down, lambda one: shift_ring(one, self.order, -1)))
        return result

    def take(self, arrivals):
        self.pieces += arrivals
        self.up = arrivals[0]
        self.down = arrivals[-1]
        self.hop += 1

    def replace(self, up, down):
        self.pieces[-1] = down
        if self.hop - 1 <= (self.count - 1) // 2:
            self.pieces[-2] = up
        self.up, self.down = up, down

    @property
    def left(self):
        return self.hop <= self.count // 2


def gather_step(rings, *riders):
    sends = [ring.sends() for ring in rings]
    arrivals = together(list(riders) + [one for part in sends for one in part])
    ridden, arrivals = arrivals[: len(riders)], arrivals[len(riders) :]
    for ring, part in zip(rings, sends):
        ring.take(list(arrivals[: len(part)]))
        arrivals = arrivals[len(part) :]
    return ridden


def place_items(pieces, places):
    whole = jnp.zeros((len(pieces),) + pieces[0].shape, pieces[0].dtype)
    for far, piece in zip(arrival_order(len(pieces)), pieces):
        whole = lax.dynamic_update_index_in_dim(whole, piece, places[far], 0)
    return whole


def by_stream(own, other, axis):
    first = lax.axis_index("stream") == 0
    return jnp.where(
        first, jnp.stack([own, other], axis=axis), jnp.stack([other, own], axis=axis)
    )


def whole_rows(own, other):
    both = by_stream(own, other, 1)
    return both.reshape((both.shape[0] * both.shape[1] * both.shape[2], both.shape[3]))


def at(pieces, span=slice(None)):
    return lambda which: lax.dynamic_index_in_dim(pieces, which, 0, keepdims=False)[:, span]


def at_stream(pieces, span=slice(None)):
    stream = lax.axis_index("stream").astype(jnp.uint32)
    zero = jnp.uint32(0)

    def read(which):
        start = (which, stream, zero, zero)
        found = lax.dynamic_slice(pieces, start, (1, 1) + pieces.shape[2:])
        return found.reshape(pieces.shape[2:])[:, span]

    return read


class Scatter:
    def __init__(self, groups, axis, places):
        self.groups, self.axis = groups, axis
        self.count = lax.axis_size("items")
        self.order, self.places = ring_of(self.count), places
        self.hop = self.count // 2
        self.up = self.down = None

    def piece(self, distance):
        which = self.places[distance % self.count]
        parts = [sum(read(which).astype(F32) for read in group) for group in self.groups]
        return jnp.concatenate(parts, axis=self.axis)

    def sends(self):
        own = self.piece(self.hop)
        own = own if self.up is None else own + self.up.astype(F32)
        result = [(own.astype(BF), lambda one: shift_ring(one, self.order, 1))]
        if self.hop <= (self.count - 1) // 2:
            own = self.piece(self.count - self.hop)
            own = own if self.down is None else own + self.down.astype(F32)
            result.append((own.astype(BF), lambda one: shift_ring(one, self.order, -1)))
        return result

    def take(self, arrivals):
        self.up = arrivals[0]
        if len(arrivals) > 1:
            self.down = arrivals[1]
        self.hop -= 1
        return arrivals[0]

    def step(self):
        return self.take(together(self.sends()))

    def result(self):
        return self.piece(0) + self.up.astype(F32) + self.down.astype(F32)


def halves(total):
    count = lax.axis_size("items")
    rows = total.shape[0] // (2 * count)
    parts = total.reshape((count, 2, rows, total.shape[1]))
    stream = lax.axis_index("stream").astype(jnp.uint32)
    away = lax.dynamic_index_in_dim(parts, 1 - stream, 1, keepdims=False)
    return parts, away


def over(axis, distance=0):
    return lambda one: partner(one, axis, distance)


def mul(left, right):
    return jnp.dot(left, right, preferred_element_type=F32)


def mul_t(left, right):
    return lax.dot_general(left, right, (((1,), (1,)), ((), ())), preferred_element_type=F32)


def t_mul(left, right):
    return lax.dot_general(left, right, (((0,), (0,)), ((), ())), preferred_element_type=F32)


def standard(rows):
    center = rows - jnp.mean(rows, axis=-1, keepdims=True)
    scale = lax.rsqrt(jnp.mean(center * center, axis=-1, keepdims=True) + EPS)
    return center * scale, scale


def norm_back(grad, unit, scale, gain):
    inner = grad * gain
    return scale * (
        inner
        - jnp.mean(inner, axis=-1, keepdims=True)
        - unit * jnp.mean(inner * unit, axis=-1, keepdims=True)
    )


def pair_sum(near, away):
    return near[...].astype(F32) + away[...].astype(F32)


def total_rows(rows):
    return jnp.sum(rows, axis=0, keepdims=True)


def head_mask(rows, heads, value, dtype):
    row = lax.broadcasted_iota(jnp.int32, (heads * rows, heads * HEAD_DIM), 0) // rows
    col = lax.broadcasted_iota(jnp.int32, (heads * rows, heads * HEAD_DIM), 1) // HEAD_DIM
    return jnp.where(row == col, value, 0.0).astype(dtype)


def stack_heads(rows, heads, mask):
    return jnp.concatenate([rows] * heads, axis=0) * mask


def fold_heads(stacked, heads, mask):
    rows = stacked.shape[0] // heads
    stacked = stacked * mask
    result = stacked[:rows]
    for head in range(1, heads):
        result = result + stacked[head * rows : (head + 1) * rows]
    return result


def softmax(scores):
    power = jnp.exp(scores - jnp.max(scores, axis=-1, keepdims=True))
    return power * (1.0 / jnp.sum(power, axis=-1, keepdims=True))


def attend(queries, keys, values, hide, heads, scaled_mask, out_mask):
    scores = hide(mul_t(stack_heads(queries, heads, scaled_mask), keys))
    weights = softmax(scores).astype(BF)
    return fold_heads(mul(weights, values), heads, out_mask).astype(BF)


def attend_back(queries, keys, values, grad, hide, heads, scaled_mask, plain_mask, out_mask):
    queries = stack_heads(queries, heads, scaled_mask)
    grad = stack_heads(grad, heads, plain_mask)
    weights = softmax(hide(mul_t(queries, keys)))
    grad_weights = mul_t(grad, values)
    grad_values = t_mul(weights.astype(BF), grad)
    delta = jnp.sum(grad_weights * weights, axis=-1, keepdims=True)
    grad_scores = (weights * (grad_weights - delta)).astype(BF)
    grad_queries = fold_heads(mul(grad_scores, keys), heads, out_mask) * HEAD_DIM ** (-0.5)
    return grad_queries, t_mul(grad_scores, queries), grad_values


def whole(shape):
    return pl.BlockSpec(shape, lambda i: (0,) * len(shape))


def block(shape):
    return pl.BlockSpec(shape, lambda i: (i,) + (0,) * (len(shape) - 1))


def column(shape, first=0):
    return pl.BlockSpec(shape, lambda i: (0, i + first))


def shaped(shape, dtype):
    return jax.ShapeDtypeStruct(shape, dtype)


def call(kernel, grid, in_specs, out_specs, out_shape, scratch=(), flops=0, moved=0):
    return pl.pallas_call(
        kernel,
        grid=(grid,),
        in_specs=in_specs,
        out_specs=out_specs,
        out_shape=out_shape,
        scratch_shapes=list(scratch),
        compiler_params=pltpu.CompilerParams(
            dimension_semantics=("arbitrary",), vmem_limit_bytes=56 << 20
        ),
        cost_estimate=pl.CostEstimate(flops=flops, bytes_accessed=moved, transcendentals=0),
    )


def feature_norm(features, gain, shift, padded, begin, each, prior):
    items, patches, width = features.shape

    def kernel(feat, gain, shift, *refs):
        out, token = refs[-2:]
        unit, _ = standard(feat[0].astype(F32))
        out[0, :patches] = (unit * gain[...] + shift[...]).astype(BF)
        out[0, patches:] = jnp.zeros((padded - patches, width), BF)
        token[...] = jnp.zeros_like(token)

    def at_item(i):
        return (i + begin, 0, 0)

    return pl.pallas_call(
        kernel,
        grid=(each,),
        in_specs=[pl.BlockSpec((1, patches, width), at_item), whole((1, width)), whole((1, width))]
        + [pl.BlockSpec(memory_space=pl.ANY)] * len(prior),
        out_specs=[pl.BlockSpec((1, padded, width), at_item), whole((8, 128))],
        out_shape=[shaped((items, padded, width), BF), shaped((8, 128), F32)],
        input_output_aliases={3: 0} if prior else {},
        compiler_params=pltpu.CompilerParams(
            dimension_semantics=("arbitrary",), vmem_limit_bytes=56 << 20
        ),
        cost_estimate=pl.CostEstimate(
            flops=0, bytes_accessed=4 * each * patches * width, transcendentals=0
        ),
    )(features, gain, shift, *prior)


def project(places, own, far, pieces, bias):
    rows, width = own.shape
    count = len(pieces)
    cols = pieces[0].shape[1]
    head_cols = cols // 3
    step = rows // 4
    spots = arrival_order(count)

    def kernel(places, own, far, bias, *refs):
        q, kv, kv_far, weight, laid = refs[count:]

        @pl.when(pl.program_id(0) == 0)
        def _():
            for far_off, one in zip(spots, refs[:count]):
                laid[places[far_off]] = one[...]
            weight[...] = laid[...].reshape(width, cols)

        near = mul(own[...], weight[...]) + bias[...]
        q[...] = near[:, :head_cols].astype(BF)
        kv[...] = near[:, head_cols:].astype(BF)
        kv_far[...] = (mul(far[...], weight[:, head_cols:]) + bias[:, head_cols:]).astype(BF)

    return call(
        kernel,
        4,
        [pl.BlockSpec(memory_space=pltpu.SMEM)]
        + [block((step, width)), block((step, width)), whole((1, cols))]
        + [whole((width // count, cols))] * count,
        [block((step, head_cols)), block((step, 2 * head_cols)), block((step, 2 * head_cols))]
        + [whole((width, cols))],
        [shaped((rows, head_cols), BF)]
        + [shaped((rows, 2 * head_cols), BF)] * 2
        + [shaped((width, cols), BF)],
        scratch=[pltpu.VMEM((count, width // count, cols), BF)],
        flops=10 * rows * width * head_cols,
        moved=4 * rows * width + 4 * width * cols,
    )(places, own, far, bias, *pieces)


def self_attention(q, kv, kv_far, allowed, weight, items, batch):
    rows, cols = q.shape
    heads, each = cols // HEAD_DIM, rows // items
    width = weight.shape[0]

    def kernel(q, kv, kv_far, allowed, weight, attended, out):
        index = pl.program_id(0)
        scaled = head_mask(each, heads, HEAD_DIM ** (-0.5), BF)
        ones = head_mask(each, heads, 1.0, F32)
        for item in range(batch):
            span = slice(item * each, (item + 1) * each)
            keys = jnp.concatenate([kv[span, :cols], kv_far[span, :cols]], axis=0)
            values = jnp.concatenate([kv[span, cols:], kv_far[span, cols:]], axis=0)
            seen = jnp.concatenate([allowed[item]] * heads, axis=0) > 0
            result = attend(
                q[span], keys, values, lambda s: jnp.where(seen, s, NEG), heads, scaled, ones
            )
            start = pl.multiple_of((index * batch + item) * each, each)
            attended[pl.ds(start, each), :] = result

        @pl.when(index == pl.num_programs(0) - 1)
        def _():
            out[...] = mul_t(attended[...], weight[...]).astype(BF)

    part = batch * each
    return call(
        kernel,
        items // batch,
        [
            block((part, cols)),
            block((part, 2 * cols)),
            block((part, 2 * cols)),
            block((batch, each, 2 * each)),
            whole((width, cols)),
        ],
        [whole((rows, cols)), whole((rows, width))],
        [shaped((rows, cols), BF), shaped((rows, width), BF)],
        flops=2 * rows * cols * width * 3,
        moved=rows * cols * 14 + rows * width * 4,
    )(q, kv, kv_far, allowed, weight)


def cross_attention(own, near, away, rows_in, cq, keys_values, weight, items, batch, patches):
    rows, width = own.shape
    cols = weight.shape[1]
    heads, each = cols // HEAD_DIM, rows // items
    padded = keys_values.shape[1]

    def kernel(own, near, away, bias, gain, shift, bias_q, cq, kv, weight, unit, scale, low, qc, attended, out):
        index = pl.program_id(0)

        @pl.when(index == 0)
        def _():
            one, size = standard(own[...].astype(F32) + pair_sum(near, away) + bias[...])
            unit[...] = one
            scale[...] = size
            low[...] = (one * gain[...] + shift[...]).astype(BF)
            qc[...] = (mul(low[...], cq[...]) + bias_q[...]).astype(BF)

        scaled = head_mask(each, heads, HEAD_DIM ** (-0.5), BF)
        ones = head_mask(each, heads, 1.0, F32)
        real = lax.broadcasted_iota(jnp.int32, (heads * each, padded), 1) < patches
        for item in range(batch):
            start = pl.multiple_of((index * batch + item) * each, each)
            attended[pl.ds(start, each), :] = attend(
                qc[pl.ds(start, each), :],
                kv[item, :, :cols],
                kv[item, :, cols:],
                lambda s: jnp.where(real, s, NEG),
                heads,
                scaled,
                ones,
            )

        @pl.when(index == pl.num_programs(0) - 1)
        def _():
            out[...] = mul_t(attended[...], weight[...]).astype(BF)

    bias, gain, shift, bias_q = rows_in
    return call(
        kernel,
        items // batch,
        [whole((rows, width))] * 3
        + [whole((1, width))] * 3
        + [whole((1, cols)), whole((width, cols)), block((batch, padded, 2 * cols)), whole((width, cols))],
        [
            whole((rows, width)),
            whole((rows, 1)),
            whole((rows, width)),
            whole((rows, cols)),
            whole((rows, cols)),
            whole((rows, width)),
        ],
        [
            shaped((rows, width), F32),
            shaped((rows, 1), F32),
            shaped((rows, width), BF),
            shaped((rows, cols), BF),
            shaped((rows, cols), BF),
            shaped((rows, width), BF),
        ],
        flops=2 * rows * cols * padded * heads * 2,
        moved=rows * width * 20 + 4 * items * padded * cols,
    )(own, near, away, bias, gain, shift, bias_q, cq, keys_values, weight)


def lay_pieces(places, spots, refs, laid):
    count, rows, cols = laid.shape[1:]
    for far_off, w_in, w_out in zip(spots, refs[:count], refs[count:]):
        laid[0, places[far_off]] = w_in[...]
        laid[1, places[far_off]] = w_out[...]
    return laid[0].reshape(count * rows, cols), laid[1].reshape(count * rows, cols)


def feed_forward(flag, places, unit, near, away, rows_in, pieces, b_in, chunk):
    rows, width = unit.shape
    hidden = pieces[0].shape[1] // 2
    steps = hidden // chunk
    count = len(pieces)
    spots = arrival_order(count)

    def kernel(flag, places, unit, near, away, gain0, shift0, bias, gain1, shift1, b_in, *refs):
        z, z_low, unit2, scale2, act, slope, part, out, laid = refs[2 * count :]
        w_in, w_out = lay_pieces(places, spots, refs[: 2 * count], laid)

        @pl.when(pl.program_id(0) == 0)
        def _():
            after = unit[...] * gain0[...] + shift0[...]
            one, size = standard(after + pair_sum(near, away) + bias[...])
            unit2[...] = one
            scale2[...] = size
            z[...] = jnp.where(flag[0] == 0, one * gain1[...] + shift1[...], after)
            z_low[...] = z[...].astype(BF)
            out[...] = jnp.zeros_like(out)

        for half in range(2):
            span = slice(half * rows // 2, (half + 1) * rows // 2)
            u = mul(z_low[span], w_in) + b_in[...]
            share = 0.5 + 0.5 * lax.erf(u * math.sqrt(0.5))
            act_half = (u * share).astype(BF)
            act[span] = act_half
            slope[0, span] = share + u * (jnp.exp(-0.5 * u * u) * (1.0 / math.sqrt(2.0 * math.pi)))
            out[span] += mul_t(act_half, w_out)

        @pl.when(pl.program_id(0) == steps - 1)
        def _():
            part[...] = out[...].astype(BF)

    row = whole((1, width))
    return call(
        kernel,
        steps,
        [pl.BlockSpec(memory_space=pltpu.SMEM)] * 2
        + [whole((rows, width))] * 3
        + [row] * 5
        + [column((1, chunk))]
        + [column((width // count, chunk))] * count
        + [column((width // count, chunk), steps)] * count,
        [
            whole((rows, width)),
            whole((rows, width)),
            whole((rows, width)),
            whole((rows, 1)),
            column((rows, chunk)),
            block((1, rows, chunk)),
            whole((rows, width)),
        ],
        [
            shaped((rows, width), F32),
            shaped((rows, width), BF),
            shaped((rows, width), F32),
            shaped((rows, 1), F32),
            shaped((rows, hidden), BF),
            shaped((steps, rows, chunk), F32),
            shaped((rows, width), BF),
        ],
        scratch=[pltpu.VMEM((rows, width), F32), pltpu.VMEM((2, count, width // count, chunk), BF)],
        flops=4 * rows * hidden * width,
        moved=rows * width * 26 + rows * hidden * 6 + width * hidden * 4,
    )(flag, places, unit, near, away, *rows_in, b_in, *pieces, *pieces)


def feed_back(places, z, near, away, cotangent, rows_in, slope, pieces, chunk):
    rows, width = z.shape
    hidden = pieces[0].shape[1] // 2
    steps = hidden // chunk
    count = len(pieces)
    spots = arrival_order(count)

    def kernel(places, z, near, away, cot, bias, gain, shift, slope, *refs):
        result, grad_v, grad_u, grad_pre, part, sums, sum_pre, out, laid = refs[2 * count :]
        w_in, w_out = lay_pieces(places, spots, refs[: 2 * count], laid)

        @pl.when(pl.program_id(0) == 0)
        def _():
            one, size = standard(z[...] + pair_sum(near, away) + bias[...])
            dy = cot[...]
            result[...] = (one * gain[...] + shift[...]).astype(BF)
            grad_v[...] = norm_back(dy, one, size, gain[...])
            grad_u[...] = grad_v[...].astype(BF)
            sums[0:1] = total_rows(dy * one)
            sums[1:2] = total_rows(dy)
            sums[2:3] = total_rows(grad_u[...].astype(F32))
            out[...] = jnp.zeros_like(out)

        for half in range(2):
            span = slice(half * rows // 2, (half + 1) * rows // 2)
            pre = (mul(grad_u[span], w_out) * slope[0, span]).astype(BF)
            grad_pre[span] = pre
            out[span] += mul_t(pre, w_in)
        sum_pre[...] = total_rows(grad_pre[...].astype(F32))

        @pl.when(pl.program_id(0) == steps - 1)
        def _():
            part[...] = out[...].astype(BF)

    row = whole((1, width))
    return call(
        kernel,
        steps,
        [pl.BlockSpec(memory_space=pltpu.SMEM)]
        + [whole((rows, width))] * 4
        + [row] * 3
        + [block((1, rows, chunk))]
        + [column((width // count, chunk))] * count
        + [column((width // count, chunk), steps)] * count,
        [
            whole((rows, width)),
            whole((rows, width)),
            whole((rows, width)),
            column((rows, chunk)),
            whole((rows, width)),
            whole((8, width)),
            column((1, chunk)),
        ],
        [
            shaped((rows, width), BF),
            shaped((rows, width), F32),
            shaped((rows, width), BF),
            shaped((rows, hidden), BF),
            shaped((rows, width), BF),
            shaped((8, width), F32),
            shaped((1, hidden), F32),
        ],
        scratch=[pltpu.VMEM((rows, width), F32), pltpu.VMEM((2, count, width // count, chunk), BF)],
        flops=4 * rows * hidden * width,
        moved=rows * width * 28 + rows * hidden * 6 + width * hidden * 4,
    )(places, z, near, away, cotangent, *rows_in, slope, *pieces, *pieces)


def cross_back(flag, grad_v, near, away, unit2, scale2, gain, qc, keys_values, weight, cq, items, batch, patches):
    rows, width = grad_v.shape
    cols = weight.shape[1]
    heads, each = cols // HEAD_DIM, rows // items
    padded = keys_values.shape[1]

    def kernel(flag, grad_v, near, away, unit2, scale2, gain, qc, kv, weight, cq, after, mix, grad_qc, grad_kv, out, sums, sums_c, grad_att):
        index = pl.program_id(0)

        @pl.when(index == 0)
        def _():
            dz = grad_v[...] + pair_sum(near, away)
            mine = flag[0] == 0
            used = jnp.where(mine, dz, 0.0)
            two = norm_back(used, unit2[...], scale2[...], gain[...])
            after[...] = jnp.where(mine, two, dz)
            mix[...] = two.astype(BF)
            grad_att[...] = mul(mix[...], weight[...]).astype(BF)
            sums[0:1] = total_rows(used * unit2[...])
            sums[1:2] = total_rows(used)
            sums[2:3] = total_rows(mix[...].astype(F32))
            sums_c[...] = jnp.zeros_like(sums_c)

        root = HEAD_DIM ** (-0.5)
        scaled = head_mask(each, heads, root, BF)
        plain = head_mask(each, heads, 1.0, BF)
        ones = head_mask(each, heads, 1.0, F32)
        real = lax.broadcasted_iota(jnp.int32, (heads * each, padded), 1) < patches
        for item in range(batch):
            start = pl.multiple_of((index * batch + item) * each, each)
            dq, dk, dv = attend_back(
                qc[pl.ds(start, each), :],
                kv[item, :, :cols],
                kv[item, :, cols:],
                grad_att[pl.ds(start, each), :],
                lambda s: jnp.where(real, s, NEG),
                heads,
                scaled,
                plain,
                ones,
            )
            grad_qc[pl.ds(start, each), :] = dq.astype(BF)
            dk, dv = dk.astype(BF), dv.astype(BF)
            grad_kv[item, :, :cols] = dk
            grad_kv[item, :, cols:] = dv
            sums_c[1:2] += total_rows(dk.astype(F32))
            sums_c[2:3] += total_rows(dv.astype(F32))

        @pl.when(index == pl.num_programs(0) - 1)
        def _():
            out[...] = mul_t(grad_qc[...], cq[...]).astype(BF)
            sums_c[0:1] = total_rows(grad_qc[...].astype(F32))

    return call(
        kernel,
        items // batch,
        [pl.BlockSpec(memory_space=pltpu.SMEM)]
        + [whole((rows, width))] * 4
        + [
            whole((rows, 1)),
            whole((1, width)),
            whole((rows, cols)),
            block((batch, padded, 2 * cols)),
            whole((width, cols)),
            whole((width, cols)),
        ],
        [
            whole((rows, width)),
            whole((rows, width)),
            whole((rows, cols)),
            block((batch, padded, 2 * cols)),
            whole((rows, width)),
            whole((8, width)),
            whole((8, cols)),
        ],
        [
            shaped((rows, width), F32),
            shaped((rows, width), BF),
            shaped((rows, cols), BF),
            shaped((items, padded, 2 * cols), BF),
            shaped((rows, width), BF),
            shaped((8, width), F32),
            shaped((8, cols), F32),
        ],
        scratch=[pltpu.VMEM((rows, cols), BF)],
        flops=2 * rows * cols * padded * heads * 5,
        moved=rows * width * 26 + 8 * items * padded * cols,
    )(flag, grad_v, near, away, unit2, scale2, gain, qc, keys_values, weight, cq)


def self_back(flag, after, near, away, unit, scale, gain, q, kv, kv_far, allowed, weight, w_qkv, own, far, attended, items, batch, shards):
    rows, width = after.shape
    cols = weight.shape[1]
    heads, each = cols // HEAD_DIM, rows // items
    piece = width // shards

    def kernel(flag, after, near, away, unit, scale, gain, q, kv, kv_far, allowed, weight, w_qkv, own, far, attended, grad_one, mix, grad_near, grad_away, both, sums, sums_c, grad_keep, grad_sent, grad_att):
        index = pl.program_id(0)

        @pl.when(index == 0)
        def _():
            grad = after[...] + pair_sum(near, away)
            grad_one[...] = norm_back(grad, unit[...], scale[...], gain[...])
            mix[...] = grad_one[...].astype(BF)
            grad_att[...] = mul(mix[...], weight[...]).astype(BF)
            sums[0:1] = total_rows(grad * unit[...])
            sums[1:2] = total_rows(grad)
            sums[2:3] = total_rows(mix[...].astype(F32))

        scaled = head_mask(each, heads, HEAD_DIM ** (-0.5), BF)
        plain = head_mask(each, heads, 1.0, BF)
        ones = head_mask(each, heads, 1.0, F32)
        for item in range(batch):
            span = slice(item * each, (item + 1) * each)
            start = pl.multiple_of((index * batch + item) * each, each)
            keys = jnp.concatenate([kv[span, :cols], kv_far[span, :cols]], axis=0)
            values = jnp.concatenate([kv[span, cols:], kv_far[span, cols:]], axis=0)
            seen = jnp.concatenate([allowed[item]] * heads, axis=0) > 0
            dq, dk, dv = attend_back(
                q[span],
                keys,
                values,
                grad_att[pl.ds(start, each), :],
                lambda s: jnp.where(seen, s, NEG),
                heads,
                scaled,
                plain,
                ones,
            )
            grad_near[pl.ds(start, each), :cols] = dq.astype(BF)
            grad_near[pl.ds(start, each), cols : 2 * cols] = dk[:each].astype(BF)
            grad_near[pl.ds(start, each), 2 * cols :] = dv[:each].astype(BF)
            grad_away[pl.ds(start, each), :cols] = dk[each:].astype(BF)
            grad_away[pl.ds(start, each), cols:] = dv[each:].astype(BF)

        @pl.when(index == pl.num_programs(0) - 1)
        def _():
            both[:, :width] = mul_t(grad_near[...], w_qkv[...]).astype(BF)
            both[:, width:] = mul_t(grad_away[...], w_qkv[:, cols:]).astype(BF)
            for place in range(4):
                span = slice(place * cols, (place + 1) * cols)
                if place == 3:
                    total = t_mul(mix[...], attended[...])
                else:
                    total = t_mul(own[...], grad_near[:, span])
                if place in (1, 2):
                    total = total + t_mul(far[...], grad_away[:, (place - 1) * cols : place * cols])
                total = total.astype(BF)
                for side in range(2):
                    pieces = [
                        total[one * piece : (one + 1) * piece] for one in range(side, shards, 2)
                    ]

                    @pl.when(flag[0] == side)
                    def _():
                        for one, value in enumerate(pieces):
                            grad_keep[one, :, span] = value

                    @pl.when(flag[0] != side)
                    def _():
                        for one, value in enumerate(pieces):
                            grad_sent[one, :, span] = value
            sums_c[0:1] = total_rows(grad_near[...].astype(F32))
            sums_c[1:2, cols:] = total_rows(grad_away[...].astype(F32))

    part = batch * each
    return call(
        kernel,
        items // batch,
        [pl.BlockSpec(memory_space=pltpu.SMEM)]
        + [whole((rows, width))] * 4
        + [
            whole((rows, 1)),
            whole((1, width)),
            block((part, cols)),
            block((part, 2 * cols)),
            block((part, 2 * cols)),
            block((batch, each, 2 * each)),
            whole((width, cols)),
            whole((width, 3 * cols)),
            whole((rows, width)),
            whole((rows, width)),
            whole((rows, cols)),
        ],
        [
            whole((rows, width)),
            whole((rows, width)),
            whole((rows, 3 * cols)),
            whole((rows, 2 * cols)),
            whole((rows, 2 * width)),
            whole((8, width)),
            whole((8, 3 * cols)),
            whole((shards // 2, piece, 4 * cols)),
            whole((shards // 2, piece, 4 * cols)),
        ],
        [
            shaped((rows, width), F32),
            shaped((rows, width), BF),
            shaped((rows, 3 * cols), BF),
            shaped((rows, 2 * cols), BF),
            shaped((rows, 2 * width), BF),
            shaped((8, width), F32),
            shaped((8, 3 * cols), F32),
            shaped((shards // 2, piece, 4 * cols), BF),
            shaped((shards // 2, piece, 4 * cols), BF),
        ],
        scratch=[pltpu.VMEM((rows, cols), BF)],
        flops=2 * rows * cols * width * 9,
        moved=rows * width * 32 + rows * cols * 20,
    )(flag, after, near, away, unit, scale, gain, q, kv, kv_far, allowed, weight, w_qkv, own, far, attended)


def pack_small(flag, one, two, three, own, cross, pre, kv_grad, kv_all, gain, shift):
    width = one.shape[1]
    cols = cross.shape[1]
    feat_width = kv_all.shape[0]
    pres = pre.shape[1] // width
    folds = (feat_width + width - 1) // width
    rows = (14 + 2 * pres + 2 * folds + 7) // 8 * 8

    def exact(left, right):
        return lax.dot_general(
            left,
            right,
            (((1,), (1,)), ((), ())),
            precision=lax.Precision.HIGHEST,
            preferred_element_type=F32,
        )

    def kernel(flag, one, two, three, own, cross, pre, kv_grad, kv_all, gain, shift, out):
        on_text = flag[0].astype(F32)
        on_query = 1.0 - on_text
        out[...] = jnp.zeros_like(out)
        for place in range(3):
            line = slice(place, place + 1)
            out[4 * place : 4 * place + 1] = one[line]
            out[4 * place + 1 : 4 * place + 2] = two[line]
            out[4 * place + 2 : 4 * place + 3] = on_query * three[line]
            out[4 * place + 3 : 4 * place + 4] = on_text * three[line]
        out[12:13, :cols] = own[0:1, :cols]
        out[12:13, cols:] = own[0:1, 2 * cols :] + own[1:2, 2 * cols :]
        out[13:14, :cols] = cross[0:1]
        out[13:14, cols:] = cross[2:3]
        for k in range(pres):
            line = pre[:, k * width : (k + 1) * width]
            out[14 + k : 15 + k] = on_query * line
            out[14 + pres + k : 15 + pres + k] = on_text * line
        weight = kv_all[...].astype(F32)
        column_sums = jnp.concatenate([cross[1:2], cross[2:3]], axis=1)
        d_shift = exact(jnp.broadcast_to(column_sums, (8, width)), weight)[0:1]
        dot = exact(jnp.ones((8, width), F32), kv_grad[...] * weight)[0:1]
        d_gain = (dot - shift[...] * d_shift) / gain[...]
        start = 14 + 2 * pres
        for k in range(folds):
            end = min(feat_width, (k + 1) * width)
            out[start + k : start + k + 1, : end - k * width] = d_gain[:, k * width : end]
            out[start + folds + k : start + folds + k + 1, : end - k * width] = d_shift[
                :, k * width : end
            ]

    arrays = (one, two, three, own, cross, pre, kv_grad, kv_all, gain, shift)
    return call(
        kernel,
        1,
        [pl.BlockSpec(memory_space=pltpu.SMEM)] + [whole(array.shape) for array in arrays],
        whole((rows, width)),
        shaped((rows, width), F32),
        moved=6 * feat_width * width,
    )(flag, *arrays)


def unpack_small(head, packed, other, pres, feat_width):
    width = packed.shape[1]
    half = width // 2
    folds = (feat_width + width - 1) // width

    def kernel(head, packed, other, own_bias, cross_bias, gains, shifts, d_gain, d_shift, pre, post):
        first = head[0] == 0
        near, away = packed[12:], other[...]
        low = jnp.where(first, near, away)
        high = jnp.where(first, away, near)
        for place, out in enumerate((own_bias, cross_bias)):
            for part in range(2):
                span = slice(part * half, (part + 1) * half)
                out[part : part + 1, :half] = low[place : place + 1, span]
                out[part : part + 1, half:] = high[place : place + 1, span]
        own_bias[2:3] = packed[8:9]
        cross_bias[2:3] = packed[9:10]
        gains[...] = packed[0:4]
        shifts[...] = packed[4:8]
        post[...] = packed[10:12]
        for side in range(2):
            for k in range(pres):
                line = slice(2 + side * pres + k, 3 + side * pres + k)
                pre[side : side + 1, k * width : (k + 1) * width] = low[line]
                pre[side : side + 1, (pres + k) * width : (pres + k + 1) * width] = high[line]
        both = near + away
        for place, out in enumerate((d_gain, d_shift)):
            for k in range(folds):
                end = min(feat_width, (k + 1) * width)
                line = 2 + 2 * pres + place * folds + k
                out[:, k * width : end] = both[line : line + 1, : end - k * width]

    shapes = [(3, width)] * 2 + [(4, width)] * 2 + [(1, feat_width)] * 2
    shapes = shapes + [(2, 2 * pres * width), (2, width)]
    return call(
        kernel,
        1,
        [pl.BlockSpec(memory_space=pltpu.SMEM), whole(packed.shape), whole(other.shape)],
        [whole(shape) for shape in shapes],
        [shaped(shape, F32) for shape in shapes],
        moved=200000,
    )(head, packed, other)


def visible(stream, segments, modes):
    same_caption = segments[:, :, None] == segments[:, None, :]
    own = jnp.logical_or(stream == 0, same_caption)
    far = jnp.where(stream == 0, modes == 2, modes >= 1)[:, None, None]
    return jnp.concatenate([own, jnp.broadcast_to(far, own.shape)], axis=2).astype(F32)


def body(
    hidden,
    features,
    segments,
    modes,
    w_qkv,
    self_bias,
    self_out,
    cross_q,
    cross_kv,
    cross_bias,
    cross_out,
    gains,
    shifts,
    feat_gain,
    feat_shift,
    ffn_in,
    ffn_bias_in,
    ffn_out,
    ffn_bias_out,
    cotangent,
):
    stream = lax.axis_index("stream")
    stream_u = stream.astype(jnp.uint32)
    head_index = lax.axis_index("heads")
    items, _, each, width = hidden.shape
    rows = items * each
    half = rows // 2
    cols = w_qkv.shape[2]
    hidden_cols = ffn_in.shape[2]
    patches, feat_width = features.shape[1:]
    padded = (patches + 7) // 8 * 8
    col_start = head_index.astype(jnp.uint32) * cols
    hidden_start = head_index.astype(jnp.uint32) * hidden_cols
    flag = stream.astype(jnp.int32).reshape(1)
    shards = 2 * lax.axis_size("items")
    three = [slice(i * cols, (i + 1) * cols) for i in range(3)]

    part_qkv = jnp.concatenate([w_qkv[0], w_qkv[1], w_qkv[2]], axis=1)
    pair_qkv = by_stream(part_qkv, partner(part_qkv, "stream", 0), 0)
    places = ring_places()
    spots = ring_row()
    qkv_ring = Gather(pair_qkv.reshape(width // (shards // 2), 3 * cols))
    own = hidden.reshape(rows, width)
    heads_u = head_index.astype(jnp.uint32)
    my_half = lax.dynamic_slice_in_dim(own, heads_u * half, half, 0)
    far_half = partner(my_half, "stream", 0)
    later_out, part_qkv = joined(self_out, part_qkv)
    rest_ring = Gather(
        jnp.concatenate([later_out.T, cross_q, cross_out.T, cross_kv[0], cross_kv[1]], axis=0)
    )

    def row(vector):
        return vector.reshape(1, -1)

    features, first_pair = joined(features, qkv_ring.up)
    qkv_ring = Gather(first_pair)

    kept, chunk = [], items // 4
    for number in range(max(4, shards // 4)):
        if number == 1:
            (far_other,) = gather_step([qkv_ring, rest_ring], (far_half, over("heads")))
        elif qkv_ring.left:
            gather_step([qkv_ring, rest_ring])
        if number < 4:
            *kept, token = list(
                feature_norm(
                    features, row(feat_gain), row(feat_shift), padded, number * chunk, chunk, kept
                )
            )
            ends = joined(qkv_ring.up, qkv_ring.down, rest_ring.up, rest_ring.down, token)
            qkv_ring.replace(*ends[:2])
            rest_ring.replace(*ends[2:4])
            kept = [kept[0], ends[4]]
    feat_norm = kept[0]
    far = jnp.where(
        head_index == 0,
        jnp.concatenate([far_half, far_other], axis=0),
        jnp.concatenate([far_other, far_half], axis=0),
    )
    feat_rows = feat_norm.reshape(items * padded, feat_width)
    qkv_pieces = qkv_ring.pieces
    rest = place_items(rest_ring.pieces, places)
    piece = cross_q.shape[0]
    kv_piece = cross_kv.shape[1]
    out_rest = rest[:, :piece]
    mid_rest = jnp.concatenate(
        [rest[:, piece : 2 * piece], rest[:, 2 * piece : 3 * piece]], axis=2
    )
    kv_rest = jnp.concatenate(
        [rest[:, 3 * piece : 3 * piece + kv_piece], rest[:, 3 * piece + kv_piece :]], axis=2
    )
    out_other, kv_rest = joined(partner(out_rest, "stream", 0), kv_rest)
    kv_other, mid_rest = joined(partner(kv_rest, "stream", 0), mid_rest)
    self_out_t = whole_rows(out_rest, out_other)
    kv_all = whole_rows(kv_rest, kv_other)
    mid_all = whole_rows(mid_rest, partner(mid_rest, "stream", 0))
    cross_q_all, cross_out_t = mid_all[:, :cols], mid_all[:, cols:]
    ffn_part = jnp.concatenate([ffn_in[0], ffn_out[0].T], axis=1)
    ffn_part, last = joined(ffn_part, qkv_ring.up)
    qkv_ring.replace(last, last)
    ffn_gather = Gather(ffn_part)

    def ffn_step(value, last=False):
        if not ffn_gather.left:
            return value
        gather_step([ffn_gather])
        while last and ffn_gather.left:
            gather_step([ffn_gather])
        value, up, down = joined(value, ffn_gather.up, ffn_gather.down)
        ffn_gather.replace(up, down)
        return value

    def my_cols(vector):
        return lax.dynamic_slice_in_dim(vector, col_start, cols, 0)

    none = jnp.zeros((cols,), F32)
    bias_qkv = row(jnp.concatenate([my_cols(self_bias[0]), none, my_cols(self_bias[1])]))
    bias_kv = row(jnp.concatenate([none, my_cols(cross_bias[1])]))
    gain_ffn = row(lax.dynamic_index_in_dim(gains, 2 + stream_u, 0, keepdims=False))
    shift_ffn = row(lax.dynamic_index_in_dim(shifts, 2 + stream_u, 0, keepdims=False))
    bias_in = row(
        lax.dynamic_slice_in_dim(
            lax.dynamic_index_in_dim(ffn_bias_in, stream_u, 0, keepdims=False),
            hidden_start,
            hidden_cols,
            0,
        )
    )
    bias_out = row(lax.dynamic_index_in_dim(ffn_bias_out, stream_u, 0, keepdims=False))

    def swap(part):
        return partner(part, "heads", 0)

    far = ffn_step(far)
    q, kv, kv_far, qkv_all = project(spots, own, far, qkv_pieces, bias_qkv)
    allowed = visible(stream, segments, modes)
    kv_far = ffn_step(kv_far)
    attended, part = self_attention(q, kv, kv_far, allowed, self_out_t, items, 4)
    kv_all = ffn_step(kv_all)
    away_one = ffn_step(swap(part), True)
    ffn_pieces = ffn_gather.pieces
    keys_values = (mul(feat_rows, kv_all) + bias_kv).astype(BF).reshape(items, padded, 2 * cols)
    unit_one, scale_one, after_low, qc, attended_c, part_c = cross_attention(
        own,
        part,
        away_one,
        (row(self_bias[2]), row(gains[0]), row(shifts[0]), row(my_cols(cross_bias[0]))),
        cross_q_all,
        keys_values,
        cross_out_t,
        items,
        2,
        patches,
    )
    z, z_low, unit_two, scale_two, activated, slope, part_f = feed_forward(
        flag,
        spots,
        unit_one,
        part_c,
        swap(part_c),
        (row(gains[0]), row(shifts[0]), row(cross_bias[2]), row(gains[1]), row(shifts[1])),
        ffn_pieces,
        bias_in,
        256,
    )

    output, grad_three, grad_u, grad_pre, part_z, sums_three, sum_pre = feed_back(
        spots,
        z,
        part_f,
        swap(part_f),
        cotangent.reshape(rows, width),
        (bias_out, gain_ffn, shift_ffn),
        slope,
        ffn_pieces,
        256,
    )
    away_z = swap(part_z)
    in_grad = t_mul(z_low, grad_pre).astype(BF)
    out_grad = t_mul(grad_u, activated).astype(BF)
    count = shards // 2
    grad_after, mix_c, grad_qc, grad_kv, part_a, sums_two, sums_cross = cross_back(
        flag,
        grad_three,
        part_z,
        away_z,
        unit_two,
        scale_two,
        row(gains[1]),
        qc,
        keys_values,
        cross_out_t,
        cross_q_all,
        items,
        2,
        patches,
    )
    in_grad, out_grad, sums_two = joined(in_grad, out_grad, sums_two)
    ffn_ring = Scatter(
        [
            [at(in_grad.reshape(count, -1, hidden_cols))],
            [at(out_grad.reshape(count, -1, hidden_cols))],
        ],
        1,
        places,
    )
    ffn_ring.step()
    away_a = swap(part_a)
    keep_q, away_q = halves(t_mul(after_low, grad_qc).astype(BF))
    keep_o, away_o = halves(t_mul(mix_c, attended_c).astype(BF))
    away_c = jnp.concatenate([away_q, away_o], axis=2)
    grad_kv, away_c = joined(grad_kv, away_c)
    kv_grad = t_mul(feat_rows, grad_kv.reshape(items * padded, 2 * cols))
    kv_grad_low = kv_grad.astype(BF)
    arrived_c = partner(away_c, "stream", 0)
    kv_grad, kv_grad_low, arrived_c, ffn_ring.up = joined(
        kv_grad, kv_grad_low, arrived_c, ffn_ring.up
    )
    keep_kv, away_kv = halves(kv_grad_low)
    ffn_ring.step()
    away_a, away_kv = joined(away_a, away_kv)
    arrived_kv = partner(away_kv, "stream", 0)
    grad_one, mix, grad_near, grad_away, both, sums_one, sums_self, keep_self, away_self = self_back(
        flag,
        grad_after,
        part_a,
        away_a,
        unit_one,
        scale_one,
        row(gains[0]),
        q,
        kv,
        kv_far,
        allowed,
        self_out_t,
        qkv_all,
        own,
        far,
        attended,
        items,
        4,
        shards,
    )

    results = (grad_one, both, sums_one, sums_self, keep_self, away_self, arrived_kv)
    results = lax.optimization_barrier(results + (ffn_ring.up, ffn_ring.down))
    grad_one, both, sums_one, sums_self, keep_self, away_self, arrived_kv = results[:-2]
    ffn_ring.up, ffn_ring.down = results[-2:]

    theirs = lax.dynamic_slice_in_dim(both, (1 - heads_u) * half, half, 0)
    mine = lax.dynamic_slice_in_dim(both, heads_u * half, half, 0)

    def ring_steps(rings, *riders):
        ridden = [move(value) for value, move in riders]
        sends = [ring.sends() for ring in rings]
        flat = [one for part in sends for one in part]
        arrivals = lax.optimization_barrier(tuple(ridden) + tuple(together(flat)))
        rest = arrivals[len(riders) :]
        for ring, part in zip(rings, sends):
            ring.take(rest[: len(part)])
            rest = rest[len(part) :]
        return arrivals[: len(riders)]

    rest_ring = Scatter(
        [
            [at_stream(keep_q), at(arrived_c, three[0])],
            [at_stream(keep_o), at(arrived_c, three[1])],
            [at_stream(keep_kv, three[0]), at(arrived_kv, three[0])],
            [at_stream(keep_kv, three[1]), at(arrived_kv, three[1])],
        ],
        0,
        places,
    )
    arrived_self, from_swap = ring_steps(
        [ffn_ring, rest_ring], (away_self, over("stream")), (theirs, over("heads"))
    )
    self_ring = Scatter([[at(keep_self), at(arrived_self)]], 0, places)
    total = mine.astype(F32) + from_swap.astype(F32)
    from_far = partner(total[:, width:].astype(BF), "stream", 0)
    packed = pack_small(
        flag,
        sums_one,
        sums_two,
        sums_three,
        sums_self,
        sums_cross,
        sum_pre,
        kv_grad,
        kv_all,
        row(feat_gain),
        row(feat_shift),
    )
    moves = [over("stream")] + [over("items", bit) for bit in range((count - 1).bit_length())]

    in_half = (
        lax.dynamic_slice_in_dim(grad_one, heads_u * half, half, 0)
        + total[:, :width]
        + from_far.astype(F32)
    )
    (arrived,) = ring_steps(
        [one for one in (ffn_ring, self_ring) if one.hop], (packed, moves.pop(0))
    )
    packed = packed + arrived
    in_other = swap(in_half)
    while self_ring.hop or ffn_ring.hop or rest_ring.hop:
        rings = [one for one in (ffn_ring, rest_ring, self_ring) if one.hop]
        riders = [(packed, moves.pop(0))] if moves else []
        for arrived in ring_steps(rings, *riders):
            packed = packed + arrived
    while moves:
        packed = packed + moves.pop(0)(packed)
    grad_input = jnp.where(
        head_index == 0,
        jnp.concatenate([in_half, in_other], axis=0),
        jnp.concatenate([in_other, in_half], axis=0),
    )
    ffn_red, rest_red, self_red = ffn_ring.result(), rest_ring.result(), self_ring.result()
    small = unpack_small(
        head_index.astype(jnp.int32).reshape(1),
        packed,
        swap(packed[12:]),
        hidden_cols // width,
        feat_width,
    )
    return (
        output.reshape(items, 1, each, width),
        grad_input.reshape(items, 1, each, width),
        jnp.stack([self_red[:, one] for one in three]),
        small[0],
        self_red[:, 3 * cols :].T,
        rest_red[:piece],
        rest_red[2 * piece :].reshape(2, kv_piece, cols),
        small[1],
        rest_red[piece : 2 * piece].T,
        small[2],
        small[3],
        small[4].reshape(feat_width),
        small[5].reshape(feat_width),
        ffn_red[:, :hidden_cols][None],
        small[6],
        ffn_red[:, hidden_cols:].T[None],
        small[7],
    )


def solution(mesh):
    placed = (
        P("items", "stream", None, None),
        P("items", None, None),
        P("items", None),
        P("items"),
        P(None, ("items", "stream"), "heads"),
        P(),
        P("heads", ("items", "stream")),
        P(("items", "stream"), "heads"),
        P(None, ("items", "stream"), "heads"),
        P(),
        P("heads", ("items", "stream")),
        P(),
        P(),
        P(),
        P(),
        P("stream", "items", "heads"),
        P(),
        P("stream", "heads", "items"),
        P(),
        P("items", "stream", None, None),
    )
    return jax.shard_map(
        body,
        mesh=mesh,
        in_specs=placed,
        out_specs=(
            P("items", "stream", None, None),
            P("items", "stream", None, None),
            P(None, ("items", "stream"), "heads"),
            P(),
            P("heads", ("items", "stream")),
            P(("items", "stream"), "heads"),
            P(None, ("items", "stream"), "heads"),
            P(),
            P("heads", ("items", "stream")),
            P(),
            P(),
            P(),
            P(),
            P("stream", "items", "heads"),
            P(),
            P("stream", "heads", "items"),
            P(),
        ),
        check_vma=False,
    )
```

```python
import math

import jax
import jax.numpy as jnp
import numpy as np
from jax import lax
from jax.experimental import pallas as pl
from jax.experimental.pallas import tpu as pltpu
from jax.sharding import PartitionSpec as P

HEAD_DIM = 64
EPS = 1e-06
NEG = -1e30
BF = jnp.bfloat16
F32 = jnp.float32


def partner(shard, axis, distance):
    return lax.ppermute(shard, axis, [(i, i ^ 1 << distance) for i in range(lax.axis_size(axis))])


def joined(*values):
    return lax.optimization_barrier(values)


def ring_of(count):
    return list(range(0, count, 2)) + list(range(1, count, 2))[::-1]


def ring_table():
    count = lax.axis_size("items")
    order = ring_of(count)
    table = np.zeros((count, count), np.uint32)
    for place, index in enumerate(order):
        table[index] = [order[(place + far) % count] for far in range(count)]
    return table


def ring_row():
    row = lax.axis_index("items").astype(jnp.uint32)
    table = jnp.asarray(ring_table().astype(np.int32))
    found = lax.dynamic_slice(table, (row, jnp.uint32(0)), (1, table.shape[1]))
    return found.reshape(table.shape[1])


def ring_places():
    table = ring_table()
    count = table.shape[0]
    bits = max(1, (count - 1).bit_length())
    per_word = 32 // bits
    index = lax.axis_index("items").astype(jnp.uint32)
    places = []
    for begin in range(0, count, per_word):
        part = table[:, begin : begin + per_word]
        words = [sum(int(one) << (bits * k) for k, one in enumerate(line)) for line in part]
        word = jnp.uint32(words[0])
        for item in range(1, count):
            word = jnp.where(index == jnp.uint32(item), jnp.uint32(words[item]), word)
        for k in range(part.shape[1]):
            places.append((word >> jnp.uint32(bits * k)) & jnp.uint32((1 << bits) - 1))
    return places


def arrival_order(count):
    order = [0]
    for hop in range(1, count // 2 + 1):
        order.append(count - hop)
        if hop <= (count - 1) // 2:
            order.append(hop)
    return order


def shift_ring(shard, order, step):
    count = len(order)
    return lax.ppermute(
        shard, "items", [(order[i], order[(i + step) % count]) for i in range(count)]
    )


def together(sends):
    values = lax.optimization_barrier(tuple(value for value, _ in sends))
    return lax.optimization_barrier(tuple(move(one) for one, (_, move) in zip(values, sends)))


class Gather:
    def __init__(self, shard):
        self.count = lax.axis_size("items")
        self.order = ring_of(self.count)
        self.up = self.down = shard
        self.pieces = [shard]
        self.hop = 1

    def sends(self):
        result = [(self.up, lambda one: shift_ring(one, self.order, 1))]
        if self.hop <= (self.count - 1) // 2:
            result.append((self.down, lambda one: shift_ring(one, self.order, -1)))
        return result

    def take(self, arrivals):
        self.pieces += arrivals
        self.up = arrivals[0]
        self.down = arrivals[-1]
        self.hop += 1

    def replace(self, up, down):
        self.pieces[-1] = down
        if self.hop - 1 <= (self.count - 1) // 2:
            self.pieces[-2] = up
        self.up, self.down = up, down

    @property
    def left(self):
        return self.hop <= self.count // 2


def gather_step(rings, *riders):
    sends = [ring.sends() for ring in rings]
    arrivals = together(list(riders) + [one for part in sends for one in part])
    ridden, arrivals = arrivals[: len(riders)], arrivals[len(riders) :]
    for ring, part in zip(rings, sends):
        ring.take(list(arrivals[: len(part)]))
        arrivals = arrivals[len(part) :]
    return ridden


def place_items(pieces, places):
    whole = jnp.zeros((len(pieces),) + pieces[0].shape, pieces[0].dtype)
    for far, piece in zip(arrival_order(len(pieces)), pieces):
        whole = lax.dynamic_update_index_in_dim(whole, piece, places[far], 0)
    return whole


def by_stream(own, other, axis):
    first = lax.axis_index("stream") == 0
    return jnp.where(
        first, jnp.stack([own, other], axis=axis), jnp.stack([other, own], axis=axis)
    )


def whole_rows(own, other):
    both = by_stream(own, other, 1)
    return both.reshape((both.shape[0] * both.shape[1] * both.shape[2], both.shape[3]))


def at(pieces, span=slice(None)):
    return lambda which: lax.dynamic_index_in_dim(pieces, which, 0, keepdims=False)[:, span]


def at_stream(pieces, span=slice(None)):
    stream = lax.axis_index("stream").astype(jnp.uint32)
    zero = jnp.uint32(0)

    def read(which):
        start = (which, stream, zero, zero)
        found = lax.dynamic_slice(pieces, start, (1, 1) + pieces.shape[2:])
        return found.reshape(pieces.shape[2:])[:, span]

    return read


class Scatter:
    def __init__(self, groups, axis, places):
        self.groups, self.axis = groups, axis
        self.count = lax.axis_size("items")
        self.order, self.places = ring_of(self.count), places
        self.hop = self.count // 2
        self.up = self.down = None

    def piece(self, distance):
        which = self.places[distance % self.count]
        parts = [sum(read(which).astype(F32) for read in group) for group in self.groups]
        return jnp.concatenate(parts, axis=self.axis)

    def sends(self):
        own = self.piece(self.hop)
        own = own if self.up is None else own + self.up.astype(F32)
        result = [(own.astype(BF), lambda one: shift_ring(one, self.order, 1))]
        if self.hop <= (self.count - 1) // 2:
            own = self.piece(self.count - self.hop)
            own = own if self.down is None else own + self.down.astype(F32)
            result.append((own.astype(BF), lambda one: shift_ring(one, self.order, -1)))
        return result

    def take(self, arrivals):
        self.up = arrivals[0]
        if len(arrivals) > 1:
            self.down = arrivals[1]
        self.hop -= 1
        return arrivals[0]

    def step(self):
        return self.take(together(self.sends()))

    def result(self):
        return self.piece(0) + self.up.astype(F32) + self.down.astype(F32)


def halves(total):
    count = lax.axis_size("items")
    rows = total.shape[0] // (2 * count)
    parts = total.reshape((count, 2, rows, total.shape[1]))
    stream = lax.axis_index("stream").astype(jnp.uint32)
    away = lax.dynamic_index_in_dim(parts, 1 - stream, 1, keepdims=False)
    return parts, away


def over(axis, distance=0):
    return lambda one: partner(one, axis, distance)


def mul(left, right):
    return jnp.dot(left, right, preferred_element_type=F32)


def mul_t(left, right):
    return lax.dot_general(left, right, (((1,), (1,)), ((), ())), preferred_element_type=F32)


def t_mul(left, right):
    return lax.dot_general(left, right, (((0,), (0,)), ((), ())), preferred_element_type=F32)


def standard(rows):
    center = rows - jnp.mean(rows, axis=-1, keepdims=True)
    scale = lax.rsqrt(jnp.mean(center * center, axis=-1, keepdims=True) + EPS)
    return center * scale, scale


def norm_back(grad, unit, scale, gain):
    inner = grad * gain
    return scale * (
        inner
        - jnp.mean(inner, axis=-1, keepdims=True)
        - unit * jnp.mean(inner * unit, axis=-1, keepdims=True)
    )


def pair_sum(near, away):
    return near[...].astype(F32) + away[...].astype(F32)


def total_rows(rows):
    return jnp.sum(rows, axis=0, keepdims=True)


def head_mask(rows, heads, value, dtype):
    row = lax.broadcasted_iota(jnp.int32, (heads * rows, heads * HEAD_DIM), 0) // rows
    col = lax.broadcasted_iota(jnp.int32, (heads * rows, heads * HEAD_DIM), 1) // HEAD_DIM
    return jnp.where(row == col, value, 0.0).astype(dtype)


def stack_heads(rows, heads, mask):
    return jnp.concatenate([rows] * heads, axis=0) * mask


def fold_heads(stacked, heads, mask):
    rows = stacked.shape[0] // heads
    stacked = stacked * mask
    result = stacked[:rows]
    for head in range(1, heads):
        result = result + stacked[head * rows : (head + 1) * rows]
    return result


def softmax(scores):
    power = jnp.exp(scores - jnp.max(scores, axis=-1, keepdims=True))
    return power * (1.0 / jnp.sum(power, axis=-1, keepdims=True))


def attend(queries, keys, values, hide, heads, scaled_mask, out_mask):
    scores = hide(mul_t(stack_heads(queries, heads, scaled_mask), keys))
    weights = softmax(scores).astype(BF)
    return fold_heads(mul(weights, values), heads, out_mask).astype(BF)


def attend_back(queries, keys, values, grad, hide, heads, scaled_mask, plain_mask, out_mask):
    queries = stack_heads(queries, heads, scaled_mask)
    grad = stack_heads(grad, heads, plain_mask)
    weights = softmax(hide(mul_t(queries, keys)))
    grad_weights = mul_t(grad, values)
    grad_values = t_mul(weights.astype(BF), grad)
    delta = jnp.sum(grad_weights * weights, axis=-1, keepdims=True)
    grad_scores = (weights * (grad_weights - delta)).astype(BF)
    grad_queries = fold_heads(mul(grad_scores, keys), heads, out_mask) * HEAD_DIM ** (-0.5)
    return grad_queries, t_mul(grad_scores, queries), grad_values


def whole(shape):
    return pl.BlockSpec(shape, lambda i: (0,) * len(shape))


def block(shape):
    return pl.BlockSpec(shape, lambda i: (i,) + (0,) * (len(shape) - 1))


def column(shape, first=0):
    return pl.BlockSpec(shape, lambda i: (0, i + first))


def shaped(shape, dtype):
    return jax.ShapeDtypeStruct(shape, dtype)


def call(kernel, grid, in_specs, out_specs, out_shape, scratch=(), flops=0, moved=0):
    return pl.pallas_call(
        kernel,
        grid=(grid,),
        in_specs=in_specs,
        out_specs=out_specs,
        out_shape=out_shape,
        scratch_shapes=list(scratch),
        compiler_params=pltpu.CompilerParams(
            dimension_semantics=("arbitrary",), vmem_limit_bytes=56 << 20
        ),
        cost_estimate=pl.CostEstimate(flops=flops, bytes_accessed=moved, transcendentals=0),
    )


def feature_norm(features, gain, shift, padded, begin, each, prior):
    items, patches, width = features.shape

    def kernel(feat, gain, shift, *refs):
        out, token = refs[-2:]
        unit, _ = standard(feat[0].astype(F32))
        out[0, :patches] = (unit * gain[...] + shift[...]).astype(BF)
        out[0, patches:] = jnp.zeros((padded - patches, width), BF)
        token[...] = jnp.zeros_like(token)

    def at_item(i):
        return (i + begin, 0, 0)

    return pl.pallas_call(
        kernel,
        grid=(each,),
        in_specs=[pl.BlockSpec((1, patches, width), at_item), whole((1, width)), whole((1, width))]
        + [pl.BlockSpec(memory_space=pl.ANY)] * len(prior),
        out_specs=[pl.BlockSpec((1, padded, width), at_item), whole((8, 128))],
        out_shape=[shaped((items, padded, width), BF), shaped((8, 128), F32)],
        input_output_aliases={3: 0} if prior else {},
        compiler_params=pltpu.CompilerParams(
            dimension_semantics=("arbitrary",), vmem_limit_bytes=56 << 20
        ),
        cost_estimate=pl.CostEstimate(
            flops=0, bytes_accessed=4 * each * patches * width, transcendentals=0
        ),
    )(features, gain, shift, *prior)


def project(places, own, far, pieces, bias, each):
    rows, width = own.shape
    count = len(pieces)
    head_cols = pieces[0].shape[1]
    cols = 3 * head_cols
    step = rows // 4
    spots = arrival_order(count)

    def kernel(places, own, far, bias, *refs):
        q, kv, kv_far, weight, laid = refs[count:]

        @pl.when(pl.program_id(0) == 0)
        def _():
            for far_off, one in zip(spots, refs[:count]):
                piece = one[...]
                for side in range(2):
                    for k in range(3):
                        start = (3 * side + k) * each
                        lanes = slice(k * head_cols, (k + 1) * head_cols)
                        laid[places[far_off], side, :, lanes] = piece[start : start + each]
            weight[...] = laid[...].reshape(width, cols)

        near = mul(own[...], weight[...]) + bias[...]
        q[...] = near[:, :head_cols].astype(BF)
        kv[...] = near[:, head_cols:].astype(BF)
        kv_far[...] = (mul(far[...], weight[:, head_cols:]) + bias[:, head_cols:]).astype(BF)

    return call(
        kernel,
        4,
        [pl.BlockSpec(memory_space=pltpu.SMEM)]
        + [block((step, width)), block((step, width)), whole((1, cols))]
        + [whole((6 * each, head_cols))] * count,
        [block((step, head_cols)), block((step, 2 * head_cols)), block((step, 2 * head_cols))]
        + [whole((width, cols))],
        [shaped((rows, head_cols), BF)]
        + [shaped((rows, 2 * head_cols), BF)] * 2
        + [shaped((width, cols), BF)],
        scratch=[pltpu.VMEM((count, 2, each, cols), BF)],
        flops=10 * rows * width * head_cols,
        moved=4 * rows * width + 4 * width * cols,
    )(places, own, far, bias, *pieces)


def assemble(flag, places, pieces, crossed, each, kv_each):
    count = len(pieces)
    cols = pieces[0].shape[1]
    spots = arrival_order(count)
    rows = crossed[0].shape[0]

    def kernel(flag, places, *refs):
        self_out, cross_q, cross_out, kv = refs[2 * count :]
        for number, far_off in enumerate(spots):
            place = places[far_off]
            for side, piece in (
                (flag[0], refs[number][6 * each :]),
                (1 - flag[0], refs[count + number][...]),
            ):
                for k, out in enumerate((self_out, cross_q, cross_out)):
                    out[place, side] = piece[k * each : (k + 1) * each]
                start = 3 * each
                kv[place, side, :, :cols] = piece[start : start + kv_each]
                kv[place, side, :, cols:] = piece[start + kv_each :]

    shapes = [(count, 2, each, cols)] * 3 + [(count, 2, kv_each, 2 * cols)]
    results = call(
        kernel,
        1,
        [pl.BlockSpec(memory_space=pltpu.SMEM)] * 2
        + [whole(pieces[0].shape)] * count
        + [whole((rows, cols))] * count,
        [whole(shape) for shape in shapes],
        [shaped(shape, BF) for shape in shapes],
        moved=8 * count * rows * cols,
    )(flag, places, *pieces, *crossed)
    return [one.reshape(2 * count * one.shape[2], one.shape[3]) for one in results]


def self_attention(q, kv, kv_far, allowed, weight, items, batch):
    rows, cols = q.shape
    heads, each = cols // HEAD_DIM, rows // items
    width = weight.shape[0]

    def kernel(q, kv, kv_far, allowed, weight, attended, out):
        index = pl.program_id(0)
        scaled = head_mask(each, heads, HEAD_DIM ** (-0.5), BF)
        ones = head_mask(each, heads, 1.0, F32)
        for item in range(batch):
            span = slice(item * each, (item + 1) * each)
            keys = jnp.concatenate([kv[span, :cols], kv_far[span, :cols]], axis=0)
            values = jnp.concatenate([kv[span, cols:], kv_far[span, cols:]], axis=0)
            seen = jnp.concatenate([allowed[item]] * heads, axis=0) > 0
            result = attend(
                q[span], keys, values, lambda s: jnp.where(seen, s, NEG), heads, scaled, ones
            )
            start = pl.multiple_of((index * batch + item) * each, each)
            attended[pl.ds(start, each), :] = result

        @pl.when(index == pl.num_programs(0) - 1)
        def _():
            out[...] = mul_t(attended[...], weight[...]).astype(BF)

    part = batch * each
    return call(
        kernel,
        items // batch,
        [
            block((part, cols)),
            block((part, 2 * cols)),
            block((part, 2 * cols)),
            block((batch, each, 2 * each)),
            whole((width, cols)),
        ],
        [whole((rows, cols)), whole((rows, width))],
        [shaped((rows, cols), BF), shaped((rows, width), BF)],
        flops=2 * rows * cols * width * 3,
        moved=rows * cols * 14 + rows * width * 4,
    )(q, kv, kv_far, allowed, weight)


def cross_attention(own, near, away, rows_in, cq, keys_values, weight, items, batch, patches):
    rows, width = own.shape
    cols = weight.shape[1]
    heads, each = cols // HEAD_DIM, rows // items
    padded = keys_values.shape[1]

    def kernel(own, near, away, bias, gain, shift, bias_q, cq, kv, weight, unit, scale, low, qc, attended, out):
        index = pl.program_id(0)

        @pl.when(index == 0)
        def _():
            one, size = standard(own[...].astype(F32) + pair_sum(near, away) + bias[...])
            unit[...] = one
            scale[...] = size
            low[...] = (one * gain[...] + shift[...]).astype(BF)
            qc[...] = (mul(low[...], cq[...]) + bias_q[...]).astype(BF)

        scaled = head_mask(each, heads, HEAD_DIM ** (-0.5), BF)
        ones = head_mask(each, heads, 1.0, F32)
        real = lax.broadcasted_iota(jnp.int32, (heads * each, padded), 1) < patches
        for item in range(batch):
            start = pl.multiple_of((index * batch + item) * each, each)
            attended[pl.ds(start, each), :] = attend(
                qc[pl.ds(start, each), :],
                kv[item, :, :cols],
                kv[item, :, cols:],
                lambda s: jnp.where(real, s, NEG),
                heads,
                scaled,
                ones,
            )

        @pl.when(index == pl.num_programs(0) - 1)
        def _():
            out[...] = mul_t(attended[...], weight[...]).astype(BF)

    bias, gain, shift, bias_q = rows_in
    return call(
        kernel,
        items // batch,
        [whole((rows, width))] * 3
        + [whole((1, width))] * 3
        + [whole((1, cols)), whole((width, cols)), block((batch, padded, 2 * cols)), whole((width, cols))],
        [
            whole((rows, width)),
            whole((rows, 1)),
            whole((rows, width)),
            whole((rows, cols)),
            whole((rows, cols)),
            whole((rows, width)),
        ],
        [
            shaped((rows, width), F32),
            shaped((rows, 1), F32),
            shaped((rows, width), BF),
            shaped((rows, cols), BF),
            shaped((rows, cols), BF),
            shaped((rows, width), BF),
        ],
        flops=2 * rows * cols * padded * heads * 2,
        moved=rows * width * 20 + 4 * items * padded * cols,
    )(own, near, away, bias, gain, shift, bias_q, cq, keys_values, weight)


def lay_pieces(places, spots, refs, laid):
    count, rows, cols = laid.shape[1:]
    for far_off, w_in, w_out in zip(spots, refs[:count], refs[count:]):
        laid[0, places[far_off]] = w_in[...]
        laid[1, places[far_off]] = w_out[...]
    return laid[0].reshape(count * rows, cols), laid[1].reshape(count * rows, cols)


def feed_forward(flag, places, unit, near, away, rows_in, pieces, b_in, chunk):
    rows, width = unit.shape
    hidden = pieces[0].shape[1] // 2
    steps = hidden // chunk
    count = len(pieces)
    spots = arrival_order(count)

    def kernel(flag, places, unit, near, away, gain0, shift0, bias, gain1, shift1, b_in, *refs):
        z, z_low, unit2, scale2, act, slope, part, out, laid = refs[2 * count :]
        w_in, w_out = lay_pieces(places, spots, refs[: 2 * count], laid)

        @pl.when(pl.program_id(0) == 0)
        def _():
            after = unit[...] * gain0[...] + shift0[...]
            one, size = standard(after + pair_sum(near, away) + bias[...])
            unit2[...] = one
            scale2[...] = size
            z[...] = jnp.where(flag[0] == 0, one * gain1[...] + shift1[...], after)
            z_low[...] = z[...].astype(BF)
            out[...] = jnp.zeros_like(out)

        for half in range(2):
            span = slice(half * rows // 2, (half + 1) * rows // 2)
            u = mul(z_low[span], w_in) + b_in[...]
            share = 0.5 + 0.5 * lax.erf(u * math.sqrt(0.5))
            act_half = (u * share).astype(BF)
            act[span] = act_half
            slope[0, span] = share + u * (jnp.exp(-0.5 * u * u) * (1.0 / math.sqrt(2.0 * math.pi)))
            out[span] += mul_t(act_half, w_out)

        @pl.when(pl.program_id(0) == steps - 1)
        def _():
            part[...] = out[...].astype(BF)

    row = whole((1, width))
    return call(
        kernel,
        steps,
        [pl.BlockSpec(memory_space=pltpu.SMEM)] * 2
        + [whole((rows, width))] * 3
        + [row] * 5
        + [column((1, chunk))]
        + [column((width // count, chunk))] * count
        + [column((width // count, chunk), steps)] * count,
        [
            whole((rows, width)),
            whole((rows, width)),
            whole((rows, width)),
            whole((rows, 1)),
            column((rows, chunk)),
            block((1, rows, chunk)),
            whole((rows, width)),
        ],
        [
            shaped((rows, width), F32),
            shaped((rows, width), BF),
            shaped((rows, width), F32),
            shaped((rows, 1), F32),
            shaped((rows, hidden), BF),
            shaped((steps, rows, chunk), F32),
            shaped((rows, width), BF),
        ],
        scratch=[pltpu.VMEM((rows, width), F32), pltpu.VMEM((2, count, width // count, chunk), BF)],
        flops=4 * rows * hidden * width,
        moved=rows * width * 26 + rows * hidden * 6 + width * hidden * 4,
    )(flag, places, unit, near, away, *rows_in, b_in, *pieces, *pieces)


def feed_back(places, z, near, away, cotangent, rows_in, slope, pieces, chunk):
    rows, width = z.shape
    hidden = pieces[0].shape[1] // 2
    steps = hidden // chunk
    count = len(pieces)
    spots = arrival_order(count)

    def kernel(places, z, near, away, cot, bias, gain, shift, slope, *refs):
        result, grad_v, grad_u, grad_pre, part, sums, sum_pre, out, laid = refs[2 * count :]
        w_in, w_out = lay_pieces(places, spots, refs[: 2 * count], laid)

        @pl.when(pl.program_id(0) == 0)
        def _():
            one, size = standard(z[...] + pair_sum(near, away) + bias[...])
            dy = cot[...]
            result[...] = (one * gain[...] + shift[...]).astype(BF)
            grad_v[...] = norm_back(dy, one, size, gain[...])
            grad_u[...] = grad_v[...].astype(BF)
            sums[0:1] = total_rows(dy * one)
            sums[1:2] = total_rows(dy)
            sums[2:3] = total_rows(grad_u[...].astype(F32))
            out[...] = jnp.zeros_like(out)

        for half in range(2):
            span = slice(half * rows // 2, (half + 1) * rows // 2)
            pre = (mul(grad_u[span], w_out) * slope[0, span]).astype(BF)
            grad_pre[span] = pre
            out[span] += mul_t(pre, w_in)
        sum_pre[...] = total_rows(grad_pre[...].astype(F32))

        @pl.when(pl.program_id(0) == steps - 1)
        def _():
            part[...] = out[...].astype(BF)

    row = whole((1, width))
    return call(
        kernel,
        steps,
        [pl.BlockSpec(memory_space=pltpu.SMEM)]
        + [whole((rows, width))] * 4
        + [row] * 3
        + [block((1, rows, chunk))]
        + [column((width // count, chunk))] * count
        + [column((width // count, chunk), steps)] * count,
        [
            whole((rows, width)),
            whole((rows, width)),
            whole((rows, width)),
            column((rows, chunk)),
            whole((rows, width)),
            whole((8, width)),
            column((1, chunk)),
        ],
        [
            shaped((rows, width), BF),
            shaped((rows, width), F32),
            shaped((rows, width), BF),
            shaped((rows, hidden), BF),
            shaped((rows, width), BF),
            shaped((8, width), F32),
            shaped((1, hidden), F32),
        ],
        scratch=[pltpu.VMEM((rows, width), F32), pltpu.VMEM((2, count, width // count, chunk), BF)],
        flops=4 * rows * hidden * width,
        moved=rows * width * 28 + rows * hidden * 6 + width * hidden * 4,
    )(places, z, near, away, cotangent, *rows_in, slope, *pieces, *pieces)


def cross_back(flag, grad_v, near, away, unit2, scale2, gain, qc, keys_values, weight, cq, items, batch, patches):
    rows, width = grad_v.shape
    cols = weight.shape[1]
    heads, each = cols // HEAD_DIM, rows // items
    padded = keys_values.shape[1]

    def kernel(flag, grad_v, near, away, unit2, scale2, gain, qc, kv, weight, cq, after, mix, grad_qc, grad_kv, out, sums, sums_c, grad_att):
        index = pl.program_id(0)

        @pl.when(index == 0)
        def _():
            dz = grad_v[...] + pair_sum(near, away)
            mine = flag[0] == 0
            used = jnp.where(mine, dz, 0.0)
            two = norm_back(used, unit2[...], scale2[...], gain[...])
            after[...] = jnp.where(mine, two, dz)
            mix[...] = two.astype(BF)
            grad_att[...] = mul(mix[...], weight[...]).astype(BF)
            sums[0:1] = total_rows(used * unit2[...])
            sums[1:2] = total_rows(used)
            sums[2:3] = total_rows(mix[...].astype(F32))
            sums_c[...] = jnp.zeros_like(sums_c)

        root = HEAD_DIM ** (-0.5)
        scaled = head_mask(each, heads, root, BF)
        plain = head_mask(each, heads, 1.0, BF)
        ones = head_mask(each, heads, 1.0, F32)
        real = lax.broadcasted_iota(jnp.int32, (heads * each, padded), 1) < patches
        for item in range(batch):
            start = pl.multiple_of((index * batch + item) * each, each)
            dq, dk, dv = attend_back(
                qc[pl.ds(start, each), :],
                kv[item, :, :cols],
                kv[item, :, cols:],
                grad_att[pl.ds(start, each), :],
                lambda s: jnp.where(real, s, NEG),
                heads,
                scaled,
                plain,
                ones,
            )
            grad_qc[pl.ds(start, each), :] = dq.astype(BF)
            dk, dv = dk.astype(BF), dv.astype(BF)
            grad_kv[item, :, :cols] = dk
            grad_kv[item, :, cols:] = dv
            sums_c[1:2] += total_rows(dk.astype(F32))
            sums_c[2:3] += total_rows(dv.astype(F32))

        @pl.when(index == pl.num_programs(0) - 1)
        def _():
            out[...] = mul_t(grad_qc[...], cq[...]).astype(BF)
            sums_c[0:1] = total_rows(grad_qc[...].astype(F32))

    return call(
        kernel,
        items // batch,
        [pl.BlockSpec(memory_space=pltpu.SMEM)]
        + [whole((rows, width))] * 4
        + [
            whole((rows, 1)),
            whole((1, width)),
            whole((rows, cols)),
            block((batch, padded, 2 * cols)),
            whole((width, cols)),
            whole((width, cols)),
        ],
        [
            whole((rows, width)),
            whole((rows, width)),
            whole((rows, cols)),
            block((batch, padded, 2 * cols)),
            whole((rows, width)),
            whole((8, width)),
            whole((8, cols)),
        ],
        [
            shaped((rows, width), F32),
            shaped((rows, width), BF),
            shaped((rows, cols), BF),
            shaped((items, padded, 2 * cols), BF),
            shaped((rows, width), BF),
            shaped((8, width), F32),
            shaped((8, cols), F32),
        ],
        scratch=[pltpu.VMEM((rows, cols), BF)],
        flops=2 * rows * cols * padded * heads * 5,
        moved=rows * width * 26 + 8 * items * padded * cols,
    )(flag, grad_v, near, away, unit2, scale2, gain, qc, keys_values, weight, cq)


def self_back(flag, head, after, near, away, unit, scale, gain, q, kv, kv_far, allowed, weight, w_qkv, own, far, attended, items, batch, shards):
    rows, width = after.shape
    cols = weight.shape[1]
    heads, each = cols // HEAD_DIM, rows // items
    piece = width // shards

    def kernel(flag, head, after, near, away, unit, scale, gain, q, kv, kv_far, allowed, weight, w_qkv, own, far, attended, grad_one, mix, grad_near, grad_away, mine, theirs, sums, sums_c, grad_keep, grad_sent, grad_att):
        index = pl.program_id(0)

        @pl.when(index == 0)
        def _():
            grad = after[...] + pair_sum(near, away)
            grad_one[...] = norm_back(grad, unit[...], scale[...], gain[...])
            mix[...] = grad_one[...].astype(BF)
            grad_att[...] = mul(mix[...], weight[...]).astype(BF)
            sums[0:1] = total_rows(grad * unit[...])
            sums[1:2] = total_rows(grad)
            sums[2:3] = total_rows(mix[...].astype(F32))

        scaled = head_mask(each, heads, HEAD_DIM ** (-0.5), BF)
        plain = head_mask(each, heads, 1.0, BF)
        ones = head_mask(each, heads, 1.0, F32)
        for item in range(batch):
            span = slice(item * each, (item + 1) * each)
            start = pl.multiple_of((index * batch + item) * each, each)
            keys = jnp.concatenate([kv[span, :cols], kv_far[span, :cols]], axis=0)
            values = jnp.concatenate([kv[span, cols:], kv_far[span, cols:]], axis=0)
            seen = jnp.concatenate([allowed[item]] * heads, axis=0) > 0
            dq, dk, dv = attend_back(
                q[span],
                keys,
                values,
                grad_att[pl.ds(start, each), :],
                lambda s: jnp.where(seen, s, NEG),
                heads,
                scaled,
                plain,
                ones,
            )
            grad_near[pl.ds(start, each), :cols] = dq.astype(BF)
            grad_near[pl.ds(start, each), cols : 2 * cols] = dk[:each].astype(BF)
            grad_near[pl.ds(start, each), 2 * cols :] = dv[:each].astype(BF)
            grad_away[pl.ds(start, each), :cols] = dk[each:].astype(BF)
            grad_away[pl.ds(start, each), cols:] = dv[each:].astype(BF)

        @pl.when(index == pl.num_programs(0) - 1)
        def _():
            side = head[0] == 0
            middle = rows // 2
            for part, source, weights in ((0, grad_near, w_qkv), (1, grad_away, w_qkv[:, cols:])):
                lanes = slice(part * width, (part + 1) * width)
                top = mul_t(source[:middle], weights[...]).astype(BF)
                low = mul_t(source[middle:], weights[...]).astype(BF)
                mine[:, lanes] = jnp.where(side, top, low)
                theirs[:, lanes] = jnp.where(side, low, top)
            for place in range(4):
                span = slice(place * cols, (place + 1) * cols)
                if place == 3:
                    total = t_mul(mix[...], attended[...])
                else:
                    total = t_mul(own[...], grad_near[:, span])
                if place in (1, 2):
                    total = total + t_mul(far[...], grad_away[:, (place - 1) * cols : place * cols])
                total = total.astype(BF)
                for side in range(2):
                    pieces = [
                        total[one * piece : (one + 1) * piece] for one in range(side, shards, 2)
                    ]

                    @pl.when(flag[0] == side)
                    def _():
                        for one, value in enumerate(pieces):
                            grad_keep[one, :, span] = value

                    @pl.when(flag[0] != side)
                    def _():
                        for one, value in enumerate(pieces):
                            grad_sent[one, :, span] = value
            sums_c[0:1] = total_rows(grad_near[...].astype(F32))
            sums_c[1:2, cols:] = total_rows(grad_away[...].astype(F32))

    part = batch * each
    return call(
        kernel,
        items // batch,
        [pl.BlockSpec(memory_space=pltpu.SMEM)] * 2
        + [whole((rows, width))] * 4
        + [
            whole((rows, 1)),
            whole((1, width)),
            block((part, cols)),
            block((part, 2 * cols)),
            block((part, 2 * cols)),
            block((batch, each, 2 * each)),
            whole((width, cols)),
            whole((width, 3 * cols)),
            whole((rows, width)),
            whole((rows, width)),
            whole((rows, cols)),
        ],
        [
            whole((rows, width)),
            whole((rows, width)),
            whole((rows, 3 * cols)),
            whole((rows, 2 * cols)),
            whole((rows // 2, 2 * width)),
            whole((rows // 2, 2 * width)),
            whole((8, width)),
            whole((8, 3 * cols)),
            whole((shards // 2, piece, 4 * cols)),
            whole((shards // 2, piece, 4 * cols)),
        ],
        [
            shaped((rows, width), F32),
            shaped((rows, width), BF),
            shaped((rows, 3 * cols), BF),
            shaped((rows, 2 * cols), BF),
            shaped((rows // 2, 2 * width), BF),
            shaped((rows // 2, 2 * width), BF),
            shaped((8, width), F32),
            shaped((8, 3 * cols), F32),
            shaped((shards // 2, piece, 4 * cols), BF),
            shaped((shards // 2, piece, 4 * cols), BF),
        ],
        scratch=[pltpu.VMEM((rows, cols), BF)],
        flops=2 * rows * cols * width * 9,
        moved=rows * width * 32 + rows * cols * 20,
    )(flag, head, after, near, away, unit, scale, gain, q, kv, kv_far, allowed, weight, w_qkv, own, far, attended)


def pack_small(flag, one, two, three, own, cross, pre, kv_grad, kv_all, gain, shift):
    width = one.shape[1]
    cols = cross.shape[1]
    feat_width = kv_all.shape[0]
    pres = pre.shape[1] // width
    folds = (feat_width + width - 1) // width
    rows = (14 + 2 * pres + 2 * folds + 7) // 8 * 8

    def exact(left, right):
        return lax.dot_general(
            left,
            right,
            (((1,), (1,)), ((), ())),
            precision=lax.Precision.HIGHEST,
            preferred_element_type=F32,
        )

    def kernel(flag, one, two, three, own, cross, pre, kv_grad, kv_all, gain, shift, out, line):
        on_text = flag[0].astype(F32)
        on_query = 1.0 - on_text
        out[...] = jnp.zeros_like(out)
        for place in range(3):
            at_row = slice(place, place + 1)
            out[4 * place : 4 * place + 1] = one[at_row]
            out[4 * place + 1 : 4 * place + 2] = two[at_row]
            out[4 * place + 2 : 4 * place + 3] = on_query * three[at_row]
            out[4 * place + 3 : 4 * place + 4] = on_text * three[at_row]
        out[12:13, :cols] = own[0:1, :cols]
        out[12:13, cols:] = own[0:1, 2 * cols :] + own[1:2, 2 * cols :]
        out[13:14, :cols] = cross[0:1]
        out[13:14, cols:] = cross[2:3]
        for k in range(pres):
            part = pre[:, k * width : (k + 1) * width]
            out[14 + k : 15 + k] = on_query * part
            out[14 + pres + k : 15 + pres + k] = on_text * part
        column_sums = jnp.concatenate([cross[1:2], cross[2:3]], axis=1)
        column_sums = jnp.broadcast_to(column_sums, (8, width))
        ones = jnp.ones((8, width), F32)

        def chunk(k, carry):
            span = pl.ds(pl.multiple_of(k * 128, 128), 128)
            weight = kv_all[span, :].astype(F32)
            d_shift = exact(column_sums, weight)[0:1]
            dot = exact(ones, kv_grad[span, :] * weight)[0:1]
            line[0:1, span] = (dot - shift[:, span] * d_shift) / gain[:, span]
            line[1:2, span] = d_shift
            return carry

        lax.fori_loop(0, feat_width // 128, chunk, 0)
        start = 14 + 2 * pres
        for part in range(2):
            for k in range(folds):
                end = min(feat_width, (k + 1) * width)
                spot = start + part * folds + k
                out[spot : spot + 1, : end - k * width] = line[part : part + 1, k * width : end]

    arrays = (one, two, three, own, cross, pre, kv_grad, kv_all, gain, shift)
    return call(
        kernel,
        1,
        [pl.BlockSpec(memory_space=pltpu.SMEM)] + [whole(array.shape) for array in arrays],
        whole((rows, width)),
        shaped((rows, width), F32),
        scratch=[pltpu.VMEM((8, feat_width), F32)],
        moved=6 * feat_width * width,
    )(flag, *arrays)


def unpack_small(head, packed, other, pres, feat_width):
    width = packed.shape[1]
    half = width // 2
    folds = (feat_width + width - 1) // width

    def kernel(head, packed, other, own_bias, cross_bias, gains, shifts, d_gain, d_shift, pre, post):
        first = head[0] == 0
        near, away = packed[12:], other[...]
        low = jnp.where(first, near, away)
        high = jnp.where(first, away, near)
        for place, out in enumerate((own_bias, cross_bias)):
            for part in range(2):
                span = slice(part * half, (part + 1) * half)
                out[part : part + 1, :half] = low[place : place + 1, span]
                out[part : part + 1, half:] = high[place : place + 1, span]
        own_bias[2:3] = packed[8:9]
        cross_bias[2:3] = packed[9:10]
        gains[...] = packed[0:4]
        shifts[...] = packed[4:8]
        post[...] = packed[10:12]
        for side in range(2):
            for k in range(pres):
                line = slice(2 + side * pres + k, 3 + side * pres + k)
                pre[side : side + 1, k * width : (k + 1) * width] = low[line]
                pre[side : side + 1, (pres + k) * width : (pres + k + 1) * width] = high[line]
        both = near + away
        for place, out in enumerate((d_gain, d_shift)):
            for k in range(folds):
                end = min(feat_width, (k + 1) * width)
                line = 2 + 2 * pres + place * folds + k
                for begin in range(k * width, end, 128):
                    spot, left = begin // 128, begin - k * width
                    out[spot : spot + 1] = both[line : line + 1, left : left + 128]

    shapes = [(3, width)] * 2 + [(4, width)] * 2 + [(feat_width // 128, 128)] * 2
    shapes = shapes + [(2, 2 * pres * width), (2, width)]
    return call(
        kernel,
        1,
        [pl.BlockSpec(memory_space=pltpu.SMEM), whole(packed.shape), whole(other.shape)],
        [whole(shape) for shape in shapes],
        [shaped(shape, F32) for shape in shapes],
        moved=200000,
    )(head, packed, other)


def visible(stream, segments, modes):
    same_caption = segments[:, :, None] == segments[:, None, :]
    own = jnp.logical_or(stream == 0, same_caption)
    far = jnp.where(stream == 0, modes == 2, modes >= 1)[:, None, None]
    return jnp.concatenate([own, jnp.broadcast_to(far, own.shape)], axis=2).astype(F32)


def body(
    hidden,
    features,
    segments,
    modes,
    w_qkv,
    self_bias,
    self_out,
    cross_q,
    cross_kv,
    cross_bias,
    cross_out,
    gains,
    shifts,
    feat_gain,
    feat_shift,
    ffn_in,
    ffn_bias_in,
    ffn_out,
    ffn_bias_out,
    cotangent,
):
    stream = lax.axis_index("stream")
    stream_u = stream.astype(jnp.uint32)
    head_index = lax.axis_index("heads")
    items, _, each, width = hidden.shape
    rows = items * each
    half = rows // 2
    cols = w_qkv.shape[2]
    hidden_cols = ffn_in.shape[2]
    patches, feat_width = features.shape[1:]
    padded = (patches + 7) // 8 * 8
    col_start = head_index.astype(jnp.uint32) * cols
    hidden_start = head_index.astype(jnp.uint32) * hidden_cols
    flag = stream.astype(jnp.int32).reshape(1)
    shards = 2 * lax.axis_size("items")
    three = [slice(i * cols, (i + 1) * cols) for i in range(3)]

    ffn_part = jnp.concatenate([ffn_in[0], ffn_out[0].T], axis=1)
    part_qkv = jnp.concatenate([w_qkv[0], w_qkv[1], w_qkv[2]], axis=0)
    pair_qkv = by_stream(part_qkv, partner(part_qkv, "stream", 0), 0)
    places = ring_places()
    spots = ring_row()
    own = hidden.reshape(rows, width)
    heads_u = head_index.astype(jnp.uint32)
    my_half = lax.dynamic_slice_in_dim(own, heads_u * half, half, 0)
    far_half = partner(my_half, "stream", 0)
    piece, kv_piece = cross_q.shape[0], cross_kv.shape[1]
    rest = jnp.concatenate([self_out.T, cross_q, cross_out.T, cross_kv[0], cross_kv[1]], axis=0)

    def row(vector):
        return vector.reshape(1, -1)

    features, pair_qkv = joined(features, pair_qkv)
    ring = Gather(jnp.concatenate([pair_qkv.reshape(6 * piece, cols), rest], axis=0))

    def crossing(one):
        return one[6 * piece :], over("stream")

    kept, chunk = [], items // 4
    crossed = []
    begin = 0
    for number in range(max(4, shards // 4)):
        if ring.left:
            riders = [crossing(one) for one in ring.pieces[begin:]]
            if number == 1:
                riders.append((far_half, over("heads")))
            last_step = ring.hop == shards // 4
            if last_step:
                ffn_part, held = joined(ffn_part, ring.up)
                ring.replace(held, ring.down)
                ffn_gather = Gather(ffn_part)
            fresh = len(ring.pieces) - begin
            begin = len(ring.pieces)
            ridden = gather_step([ring], *riders)
            crossed += ridden[:fresh]
            if number == 1:
                far_other = ridden[-1]
            if last_step:
                gather_step([ffn_gather])
        if number < 4:
            *kept, token = list(
                feature_norm(
                    features, row(feat_gain), row(feat_shift), padded, number * chunk, chunk, kept
                )
            )
            up, down, token = joined(ring.up, ring.down, token)
            ring.replace(up, down)
            kept = [kept[0], token]
    feat_norm = kept[0]
    crossed += [move(one) for one, move in (crossing(one) for one in ring.pieces[begin:])]
    far = jnp.where(
        head_index == 0,
        jnp.concatenate([far_half, far_other], axis=0),
        jnp.concatenate([far_other, far_half], axis=0),
    )
    feat_rows = feat_norm.reshape(items * padded, feat_width)
    early_pieces = list(ring.pieces)
    ends = joined(ffn_gather.up, ffn_gather.down, ring.up, crossed[-2], crossed[-3])
    ffn_gather.replace(*ends[:2])
    ring.replace(ends[2], ends[2])
    crossed[-2], crossed[-3] = ends[3:]
    gather_step([ffn_gather])
    self_out_t, cross_q_all, cross_out_t, kv_all = assemble(
        flag, spots, ring.pieces, crossed, piece, kv_piece
    )

    def ffn_step(value, last=False):
        if ffn_gather.hop - 1 > ffn_gather.count // 2:
            return value
        value, up, down = joined(value, ffn_gather.up, ffn_gather.down)
        ffn_gather.replace(up, down)
        while ffn_gather.left:
            gather_step([ffn_gather])
            if not last:
                break
        return value

    def my_cols(vector):
        return lax.dynamic_slice_in_dim(vector, col_start, cols, 0)

    none = jnp.zeros((cols,), F32)
    bias_qkv = row(jnp.concatenate([my_cols(self_bias[0]), none, my_cols(self_bias[1])]))
    bias_kv = row(jnp.concatenate([none, my_cols(cross_bias[1])]))
    gain_ffn = row(lax.dynamic_index_in_dim(gains, 2 + stream_u, 0, keepdims=False))
    shift_ffn = row(lax.dynamic_index_in_dim(shifts, 2 + stream_u, 0, keepdims=False))
    bias_in = row(
        lax.dynamic_slice_in_dim(
            lax.dynamic_index_in_dim(ffn_bias_in, stream_u, 0, keepdims=False),
            hidden_start,
            hidden_cols,
            0,
        )
    )
    bias_out = row(lax.dynamic_index_in_dim(ffn_bias_out, stream_u, 0, keepdims=False))

    def swap(part):
        return partner(part, "heads", 0)

    q, kv, kv_far, qkv_all = project(spots, own, far, early_pieces, bias_qkv, piece)
    allowed = visible(stream, segments, modes)
    attended, part = self_attention(q, kv, kv_far, allowed, self_out_t, items, 4)
    kv_all = ffn_step(kv_all)
    away_one = swap(part)
    keys_values = (mul(feat_rows, kv_all) + bias_kv).astype(BF).reshape(items, padded, 2 * cols)
    keys_values = ffn_step(keys_values)
    unit_one, scale_one, after_low, qc, attended_c, part_c = cross_attention(
        own,
        part,
        away_one,
        (row(self_bias[2]), row(gains[0]), row(shifts[0]), row(my_cols(cross_bias[0]))),
        cross_q_all,
        keys_values,
        cross_out_t,
        items,
        2,
        patches,
    )
    unit_one, part_c, scale_one, after_low, qc, attended_c = ffn_step(
        (unit_one, part_c, scale_one, after_low, qc, attended_c), True
    )
    ffn_pieces = ffn_gather.pieces
    z, z_low, unit_two, scale_two, activated, slope, part_f = feed_forward(
        flag,
        spots,
        unit_one,
        part_c,
        swap(part_c),
        (row(gains[0]), row(shifts[0]), row(cross_bias[2]), row(gains[1]), row(shifts[1])),
        ffn_pieces,
        bias_in,
        256,
    )

    output, grad_three, grad_u, grad_pre, part_z, sums_three, sum_pre = feed_back(
        spots,
        z,
        part_f,
        swap(part_f),
        cotangent.reshape(rows, width),
        (bias_out, gain_ffn, shift_ffn),
        slope,
        ffn_pieces,
        256,
    )
    away_z = swap(part_z)
    in_grad = t_mul(z_low, grad_pre).astype(BF)
    out_grad = t_mul(grad_u, activated).astype(BF)
    count = shards // 2
    grad_after, mix_c, grad_qc, grad_kv, part_a, sums_two, sums_cross = cross_back(
        flag,
        grad_three,
        part_z,
        away_z,
        unit_two,
        scale_two,
        row(gains[1]),
        qc,
        keys_values,
        cross_out_t,
        cross_q_all,
        items,
        2,
        patches,
    )
    in_grad, out_grad, sums_two = joined(in_grad, out_grad, sums_two)
    ffn_ring = Scatter(
        [
            [at(in_grad.reshape(count, -1, hidden_cols))],
            [at(out_grad.reshape(count, -1, hidden_cols))],
        ],
        1,
        places,
    )
    ffn_ring.step()
    away_a = swap(part_a)
    keep_q, away_q = halves(t_mul(after_low, grad_qc).astype(BF))
    keep_o, away_o = halves(t_mul(mix_c, attended_c).astype(BF))
    away_c = jnp.concatenate([away_q, away_o], axis=2)
    grad_kv, away_c = joined(grad_kv, away_c)
    kv_grad = t_mul(feat_rows, grad_kv.reshape(items * padded, 2 * cols))
    kv_grad_low = kv_grad.astype(BF)
    arrived_c = partner(away_c, "stream", 0)
    kv_grad, kv_grad_low, arrived_c, ffn_ring.up = joined(
        kv_grad, kv_grad_low, arrived_c, ffn_ring.up
    )
    keep_kv, away_kv = halves(kv_grad_low)
    ffn_ring.step()
    away_a, away_kv = joined(away_a, away_kv)
    arrived_kv = partner(away_kv, "stream", 0)
    grad_one, mix, grad_near, grad_away, mine, theirs, sums_one, sums_self, keep_self, away_self = self_back(
        flag,
        head_index.astype(jnp.int32).reshape(1),
        grad_after,
        part_a,
        away_a,
        unit_one,
        scale_one,
        row(gains[0]),
        q,
        kv,
        kv_far,
        allowed,
        self_out_t,
        qkv_all,
        own,
        far,
        attended,
        items,
        4,
        shards,
    )

    results = (grad_one, mine, theirs, sums_one, sums_self, keep_self, away_self, arrived_kv)
    results = lax.optimization_barrier(results + (ffn_ring.up, ffn_ring.down))
    grad_one, mine, theirs, sums_one, sums_self, keep_self, away_self, arrived_kv = results[:-2]
    ffn_ring.up, ffn_ring.down = results[-2:]


    def ring_steps(rings, *riders):
        ridden = [move(value) for value, move in riders]
        sends = [ring.sends() for ring in rings]
        flat = [one for part in sends for one in part]
        arrivals = lax.optimization_barrier(tuple(ridden) + tuple(together(flat)))
        rest = arrivals[len(riders) :]
        for ring, part in zip(rings, sends):
            ring.take(rest[: len(part)])
            rest = rest[len(part) :]
        return arrivals[: len(riders)]

    rest_ring = Scatter(
        [
            [at_stream(keep_q), at(arrived_c, three[0])],
            [at_stream(keep_o), at(arrived_c, three[1])],
            [at_stream(keep_kv, three[0]), at(arrived_kv, three[0])],
            [at_stream(keep_kv, three[1]), at(arrived_kv, three[1])],
        ],
        0,
        places,
    )
    arrived_self, from_swap = ring_steps(
        [ffn_ring, rest_ring], (away_self, over("stream")), (theirs, over("heads"))
    )
    self_ring = Scatter([[at(keep_self), at(arrived_self)]], 0, places)
    total = mine.astype(F32) + from_swap.astype(F32)
    from_far = partner(total[:, width:].astype(BF), "stream", 0)
    packed = pack_small(
        flag,
        sums_one,
        sums_two,
        sums_three,
        sums_self,
        sums_cross,
        sum_pre,
        kv_grad,
        kv_all,
        row(feat_gain),
        row(feat_shift),
    )
    packed = packed + partner(packed, "items", 0)
    moves = [over("stream")] + [over("items", bit) for bit in range(1, (count - 1).bit_length())]

    in_half = (
        lax.dynamic_slice_in_dim(grad_one, heads_u * half, half, 0)
        + total[:, :width]
        + from_far.astype(F32)
    )
    (arrived,) = ring_steps(
        [one for one in (ffn_ring, self_ring) if one.hop], (packed, moves.pop(0))
    )
    packed = packed + arrived
    in_other = swap(in_half)
    while self_ring.hop or ffn_ring.hop or rest_ring.hop:
        rings = [one for one in (ffn_ring, rest_ring, self_ring) if one.hop]
        riders = [(packed, moves.pop(0))] if moves else []
        for arrived in ring_steps(rings, *riders):
            packed = packed + arrived
    while moves:
        packed = packed + moves.pop(0)(packed)
    grad_input = jnp.where(
        head_index == 0,
        jnp.concatenate([in_half, in_other], axis=0),
        jnp.concatenate([in_other, in_half], axis=0),
    )
    ffn_red, rest_red, self_red = ffn_ring.result(), rest_ring.result(), self_ring.result()
    small = unpack_small(
        head_index.astype(jnp.int32).reshape(1),
        packed,
        swap(packed[12:]),
        hidden_cols // width,
        feat_width,
    )
    return (
        output.reshape(items, 1, each, width),
        grad_input.reshape(items, 1, each, width),
        jnp.stack([self_red[:, one] for one in three]),
        small[0],
        self_red[:, 3 * cols :].T,
        rest_red[:piece],
        rest_red[2 * piece :].reshape(2, kv_piece, cols),
        small[1],
        rest_red[piece : 2 * piece].T,
        small[2],
        small[3],
        small[4].reshape(feat_width),
        small[5].reshape(feat_width),
        ffn_red[:, :hidden_cols][None],
        small[6],
        ffn_red[:, hidden_cols:].T[None],
        small[7],
    )


def solution(mesh):
    placed = (
        P("items", "stream", None, None),
        P("items", None, None),
        P("items", None),
        P("items"),
        P(None, ("items", "stream"), "heads"),
        P(),
        P("heads", ("items", "stream")),
        P(("items", "stream"), "heads"),
        P(None, ("items", "stream"), "heads"),
        P(),
        P("heads", ("items", "stream")),
        P(),
        P(),
        P(),
        P(),
        P("stream", "items", "heads"),
        P(),
        P("stream", "heads", "items"),
        P(),
        P("items", "stream", None, None),
    )
    return jax.shard_map(
        body,
        mesh=mesh,
        in_specs=placed,
        out_specs=(
            P("items", "stream", None, None),
            P("items", "stream", None, None),
            P(None, ("items", "stream"), "heads"),
            P(),
            P("heads", ("items", "stream")),
            P(("items", "stream"), "heads"),
            P(None, ("items", "stream"), "heads"),
            P(),
            P("heads", ("items", "stream")),
            P(),
            P(),
            P(),
            P(),
            P("stream", "items", "heads"),
            P(),
            P("stream", "heads", "items"),
            P(),
        ),
        check_vma=False,
    )
```

```python
import math

import jax
import jax.numpy as jnp
import numpy as np
from jax import lax
from jax.experimental import pallas as pl
from jax.experimental.pallas import tpu as pltpu
from jax.sharding import PartitionSpec as P

HEAD_DIM = 64
EPS = 1e-06
NEG = -1e30
BF = jnp.bfloat16
F32 = jnp.float32


def partner(shard, axis, distance):
    return lax.ppermute(shard, axis, [(i, i ^ 1 << distance) for i in range(lax.axis_size(axis))])


def joined(*values):
    return lax.optimization_barrier(values)


def ring_of(count):
    return list(range(0, count, 2)) + list(range(1, count, 2))[::-1]


def ring_table():
    count = lax.axis_size("items")
    order = ring_of(count)
    table = np.zeros((count, count), np.uint32)
    for place, index in enumerate(order):
        table[index] = [order[(place + far) % count] for far in range(count)]
    return table


def ring_row():
    row = lax.axis_index("items").astype(jnp.uint32)
    table = jnp.asarray(ring_table().astype(np.int32))
    found = lax.dynamic_slice(table, (row, jnp.uint32(0)), (1, table.shape[1]))
    return found.reshape(table.shape[1])


def ring_places():
    table = ring_table()
    count = table.shape[0]
    bits = max(1, (count - 1).bit_length())
    per_word = 32 // bits
    index = lax.axis_index("items").astype(jnp.uint32)
    places = []
    for begin in range(0, count, per_word):
        part = table[:, begin : begin + per_word]
        words = [sum(int(one) << (bits * k) for k, one in enumerate(line)) for line in part]
        word = jnp.uint32(words[0])
        for item in range(1, count):
            word = jnp.where(index == jnp.uint32(item), jnp.uint32(words[item]), word)
        for k in range(part.shape[1]):
            places.append((word >> jnp.uint32(bits * k)) & jnp.uint32((1 << bits) - 1))
    return places


def arrival_order(count):
    order = [0]
    for hop in range(1, count // 2 + 1):
        order.append(count - hop)
        if hop <= (count - 1) // 2:
            order.append(hop)
    return order


def shift_ring(shard, order, step):
    count = len(order)
    return lax.ppermute(
        shard, "items", [(order[i], order[(i + step) % count]) for i in range(count)]
    )


def together(sends):
    values = lax.optimization_barrier(tuple(value for value, _ in sends))
    return lax.optimization_barrier(tuple(move(one) for one, (_, move) in zip(values, sends)))


class Gather:
    def __init__(self, shard):
        self.count = lax.axis_size("items")
        self.order = ring_of(self.count)
        self.up = self.down = shard
        self.pieces = [shard]
        self.hop = 1

    def sends(self):
        result = [(self.up, lambda one: shift_ring(one, self.order, 1))]
        if self.hop <= (self.count - 1) // 2:
            result.append((self.down, lambda one: shift_ring(one, self.order, -1)))
        return result

    def take(self, arrivals):
        self.pieces += arrivals
        self.up = arrivals[0]
        self.down = arrivals[-1]
        self.hop += 1

    def replace(self, up, down):
        self.pieces[-1] = down
        if self.hop - 1 <= (self.count - 1) // 2:
            self.pieces[-2] = up
        self.up, self.down = up, down

    @property
    def left(self):
        return self.hop <= self.count // 2


def gather_step(rings, *riders):
    sends = [ring.sends() for ring in rings]
    arrivals = together(list(riders) + [one for part in sends for one in part])
    ridden, arrivals = arrivals[: len(riders)], arrivals[len(riders) :]
    for ring, part in zip(rings, sends):
        ring.take(list(arrivals[: len(part)]))
        arrivals = arrivals[len(part) :]
    return ridden


def place_items(pieces, places):
    whole = jnp.zeros((len(pieces),) + pieces[0].shape, pieces[0].dtype)
    for far, piece in zip(arrival_order(len(pieces)), pieces):
        whole = lax.dynamic_update_index_in_dim(whole, piece, places[far], 0)
    return whole


def by_stream(own, other, axis):
    first = lax.axis_index("stream") == 0
    return jnp.where(
        first, jnp.stack([own, other], axis=axis), jnp.stack([other, own], axis=axis)
    )


def whole_rows(own, other):
    both = by_stream(own, other, 1)
    return both.reshape((both.shape[0] * both.shape[1] * both.shape[2], both.shape[3]))


def at(pieces, span=slice(None)):
    return lambda which: lax.dynamic_index_in_dim(pieces, which, 0, keepdims=False)[:, span]


def at_stream(pieces, span=slice(None)):
    stream = lax.axis_index("stream").astype(jnp.uint32)
    zero = jnp.uint32(0)

    def read(which):
        start = (which, stream, zero, zero)
        found = lax.dynamic_slice(pieces, start, (1, 1) + pieces.shape[2:])
        return found.reshape(pieces.shape[2:])[:, span]

    return read


class Scatter:
    def __init__(self, groups, axis, places):
        self.groups, self.axis = groups, axis
        self.count = lax.axis_size("items")
        self.order, self.places = ring_of(self.count), places
        self.hop = self.count // 2
        self.up = self.down = None

    def piece(self, distance):
        which = self.places[distance % self.count]
        parts = [sum(read(which).astype(F32) for read in group) for group in self.groups]
        return jnp.concatenate(parts, axis=self.axis)

    def sends(self):
        own = self.piece(self.hop)
        own = own if self.up is None else own + self.up.astype(F32)
        result = [(own.astype(BF), lambda one: shift_ring(one, self.order, 1))]
        if self.hop <= (self.count - 1) // 2:
            own = self.piece(self.count - self.hop)
            own = own if self.down is None else own + self.down.astype(F32)
            result.append((own.astype(BF), lambda one: shift_ring(one, self.order, -1)))
        return result

    def take(self, arrivals):
        self.up = arrivals[0]
        if len(arrivals) > 1:
            self.down = arrivals[1]
        self.hop -= 1
        return arrivals[0]

    def step(self):
        return self.take(together(self.sends()))

    def result(self):
        return self.piece(0) + self.up.astype(F32) + self.down.astype(F32)


def halves(total):
    count = lax.axis_size("items")
    rows = total.shape[0] // (2 * count)
    parts = total.reshape((count, 2, rows, total.shape[1]))
    stream = lax.axis_index("stream").astype(jnp.uint32)
    away = lax.dynamic_index_in_dim(parts, 1 - stream, 1, keepdims=False)
    return parts, away


def over(axis, distance=0):
    return lambda one: partner(one, axis, distance)


def mul(left, right):
    return jnp.dot(left, right, preferred_element_type=F32)


def mul_t(left, right):
    return lax.dot_general(left, right, (((1,), (1,)), ((), ())), preferred_element_type=F32)


def t_mul(left, right):
    return lax.dot_general(left, right, (((0,), (0,)), ((), ())), preferred_element_type=F32)


def standard(rows):
    center = rows - jnp.mean(rows, axis=-1, keepdims=True)
    scale = lax.rsqrt(jnp.mean(center * center, axis=-1, keepdims=True) + EPS)
    return center * scale, scale


def norm_back(grad, unit, scale, gain):
    inner = grad * gain
    return scale * (
        inner
        - jnp.mean(inner, axis=-1, keepdims=True)
        - unit * jnp.mean(inner * unit, axis=-1, keepdims=True)
    )


def pair_sum(near, away):
    return near[...].astype(F32) + away[...].astype(F32)


def total_rows(rows):
    return jnp.sum(rows, axis=0, keepdims=True)


def head_mask(rows, heads, value, dtype):
    row = lax.broadcasted_iota(jnp.int32, (heads * rows, heads * HEAD_DIM), 0) // rows
    col = lax.broadcasted_iota(jnp.int32, (heads * rows, heads * HEAD_DIM), 1) // HEAD_DIM
    return jnp.where(row == col, value, 0.0).astype(dtype)


def stack_heads(rows, heads, mask):
    return jnp.concatenate([rows] * heads, axis=0) * mask


def fold_heads(stacked, heads, mask):
    rows = stacked.shape[0] // heads
    stacked = stacked * mask
    result = stacked[:rows]
    for head in range(1, heads):
        result = result + stacked[head * rows : (head + 1) * rows]
    return result


def softmax(scores):
    power = jnp.exp(scores - jnp.max(scores, axis=-1, keepdims=True))
    return power * (1.0 / jnp.sum(power, axis=-1, keepdims=True))


def attend(queries, keys, values, hide, heads, scaled_mask, out_mask):
    scores = hide(mul_t(stack_heads(queries, heads, scaled_mask), keys))
    weights = softmax(scores).astype(BF)
    return fold_heads(mul(weights, values), heads, out_mask).astype(BF)


def attend_back(queries, keys, values, grad, hide, heads, scaled_mask, plain_mask, out_mask):
    queries = stack_heads(queries, heads, scaled_mask)
    grad = stack_heads(grad, heads, plain_mask)
    weights = softmax(hide(mul_t(queries, keys)))
    grad_weights = mul_t(grad, values)
    grad_values = t_mul(weights.astype(BF), grad)
    delta = jnp.sum(grad_weights * weights, axis=-1, keepdims=True)
    grad_scores = (weights * (grad_weights - delta)).astype(BF)
    grad_queries = fold_heads(mul(grad_scores, keys), heads, out_mask) * HEAD_DIM ** (-0.5)
    return grad_queries, t_mul(grad_scores, queries), grad_values


def whole(shape):
    return pl.BlockSpec(shape, lambda i: (0,) * len(shape))


def block(shape):
    return pl.BlockSpec(shape, lambda i: (i,) + (0,) * (len(shape) - 1))


def column(shape, first=0):
    return pl.BlockSpec(shape, lambda i: (0, i + first))


def shaped(shape, dtype):
    return jax.ShapeDtypeStruct(shape, dtype)


def call(kernel, grid, in_specs, out_specs, out_shape, scratch=(), flops=0, moved=0):
    return pl.pallas_call(
        kernel,
        grid=(grid,),
        in_specs=in_specs,
        out_specs=out_specs,
        out_shape=out_shape,
        scratch_shapes=list(scratch),
        compiler_params=pltpu.CompilerParams(
            dimension_semantics=("arbitrary",), vmem_limit_bytes=56 << 20
        ),
        cost_estimate=pl.CostEstimate(flops=flops, bytes_accessed=moved, transcendentals=0),
    )


def feature_norm(features, gain, shift, padded, begin, each, prior):
    items, patches, width = features.shape

    def kernel(feat, gain, shift, *refs):
        out, token = refs[-2:]
        unit, _ = standard(feat[0].astype(F32))
        out[0, :patches] = (unit * gain[...] + shift[...]).astype(BF)
        out[0, patches:] = jnp.zeros((padded - patches, width), BF)
        token[...] = jnp.zeros_like(token)

    def at_item(i):
        return (i + begin, 0, 0)

    return pl.pallas_call(
        kernel,
        grid=(each,),
        in_specs=[pl.BlockSpec((1, patches, width), at_item), whole((1, width)), whole((1, width))]
        + [pl.BlockSpec(memory_space=pl.ANY)] * len(prior),
        out_specs=[pl.BlockSpec((1, padded, width), at_item), whole((8, 128))],
        out_shape=[shaped((items, padded, width), BF), shaped((8, 128), F32)],
        input_output_aliases={3: 0} if prior else {},
        compiler_params=pltpu.CompilerParams(
            dimension_semantics=("arbitrary",), vmem_limit_bytes=56 << 20
        ),
        cost_estimate=pl.CostEstimate(
            flops=0, bytes_accessed=4 * each * patches * width, transcendentals=0
        ),
    )(features, gain, shift, *prior)


def project(places, own, far, pieces, bias, each):
    rows, width = own.shape
    count = len(pieces)
    head_cols = pieces[0].shape[1]
    cols = 3 * head_cols
    step = rows // 4
    spots = arrival_order(count)

    def kernel(places, own, far, bias, *refs):
        q, kv, kv_far, weight, laid = refs[count:]

        @pl.when(pl.program_id(0) == 0)
        def _():
            for far_off, one in zip(spots, refs[:count]):
                piece = one[...]
                for side in range(2):
                    for k in range(3):
                        start = (3 * side + k) * each
                        lanes = slice(k * head_cols, (k + 1) * head_cols)
                        laid[places[far_off], side, :, lanes] = piece[start : start + each]
            weight[...] = laid[...].reshape(width, cols)

        near = mul(own[...], weight[...]) + bias[...]
        q[...] = near[:, :head_cols].astype(BF)
        kv[...] = near[:, head_cols:].astype(BF)
        kv_far[...] = (mul(far[...], weight[:, head_cols:]) + bias[:, head_cols:]).astype(BF)

    return call(
        kernel,
        4,
        [pl.BlockSpec(memory_space=pltpu.SMEM)]
        + [block((step, width)), block((step, width)), whole((1, cols))]
        + [whole((6 * each, head_cols))] * count,
        [block((step, head_cols)), block((step, 2 * head_cols)), block((step, 2 * head_cols))]
        + [whole((width, cols))],
        [shaped((rows, head_cols), BF)]
        + [shaped((rows, 2 * head_cols), BF)] * 2
        + [shaped((width, cols), BF)],
        scratch=[pltpu.VMEM((count, 2, each, cols), BF)],
        flops=10 * rows * width * head_cols,
        moved=4 * rows * width + 4 * width * cols,
    )(places, own, far, bias, *pieces)


def assemble(flag, places, pieces, crossed, each, kv_each):
    count = len(pieces)
    cols = pieces[0].shape[1]
    spots = arrival_order(count)
    rows = crossed[0].shape[0]

    def kernel(flag, places, *refs):
        self_out, cross_q, cross_out, kv = refs[2 * count :]
        for number, far_off in enumerate(spots):
            place = places[far_off]
            for side, piece in (
                (flag[0], refs[number][6 * each :]),
                (1 - flag[0], refs[count + number][...]),
            ):
                for k, out in enumerate((self_out, cross_q, cross_out)):
                    out[place, side] = piece[k * each : (k + 1) * each]
                start = 3 * each
                kv[place, side, :, :cols] = piece[start : start + kv_each]
                kv[place, side, :, cols:] = piece[start + kv_each :]

    shapes = [(count, 2, each, cols)] * 3 + [(count, 2, kv_each, 2 * cols)]
    results = call(
        kernel,
        1,
        [pl.BlockSpec(memory_space=pltpu.SMEM)] * 2
        + [whole(pieces[0].shape)] * count
        + [whole((rows, cols))] * count,
        [whole(shape) for shape in shapes],
        [shaped(shape, BF) for shape in shapes],
        moved=8 * count * rows * cols,
    )(flag, places, *pieces, *crossed)
    return [one.reshape(2 * count * one.shape[2], one.shape[3]) for one in results]


def self_attention(q, kv, kv_far, allowed, weight, items, batch):
    rows, cols = q.shape
    heads, each = cols // HEAD_DIM, rows // items
    width = weight.shape[0]

    def kernel(q, kv, kv_far, allowed, weight, attended, out):
        index = pl.program_id(0)
        scaled = head_mask(each, heads, HEAD_DIM ** (-0.5), BF)
        ones = head_mask(each, heads, 1.0, F32)
        for item in range(batch):
            span = slice(item * each, (item + 1) * each)
            keys = jnp.concatenate([kv[span, :cols], kv_far[span, :cols]], axis=0)
            values = jnp.concatenate([kv[span, cols:], kv_far[span, cols:]], axis=0)
            seen = jnp.concatenate([allowed[item]] * heads, axis=0) > 0
            result = attend(
                q[span], keys, values, lambda s: jnp.where(seen, s, NEG), heads, scaled, ones
            )
            start = pl.multiple_of((index * batch + item) * each, each)
            attended[pl.ds(start, each), :] = result

        @pl.when(index == pl.num_programs(0) - 1)
        def _():
            out[...] = mul_t(attended[...], weight[...]).astype(BF)

    part = batch * each
    return call(
        kernel,
        items // batch,
        [
            block((part, cols)),
            block((part, 2 * cols)),
            block((part, 2 * cols)),
            block((batch, each, 2 * each)),
            whole((width, cols)),
        ],
        [whole((rows, cols)), whole((rows, width))],
        [shaped((rows, cols), BF), shaped((rows, width), BF)],
        flops=2 * rows * cols * width * 3,
        moved=rows * cols * 14 + rows * width * 4,
    )(q, kv, kv_far, allowed, weight)


def cross_attention(own, near, away, rows_in, cq, keys_values, weight, items, batch, patches):
    rows, width = own.shape
    cols = weight.shape[1]
    heads, each = cols // HEAD_DIM, rows // items
    padded = keys_values.shape[1]

    def kernel(own, near, away, bias, gain, shift, bias_q, cq, kv, weight, unit, scale, low, qc, attended, out):
        index = pl.program_id(0)

        @pl.when(index == 0)
        def _():
            one, size = standard(own[...].astype(F32) + pair_sum(near, away) + bias[...])
            unit[...] = one
            scale[...] = size
            low[...] = (one * gain[...] + shift[...]).astype(BF)
            qc[...] = (mul(low[...], cq[...]) + bias_q[...]).astype(BF)

        scaled = head_mask(each, heads, HEAD_DIM ** (-0.5), BF)
        ones = head_mask(each, heads, 1.0, F32)
        real = lax.broadcasted_iota(jnp.int32, (heads * each, padded), 1) < patches
        for item in range(batch):
            start = pl.multiple_of((index * batch + item) * each, each)
            attended[pl.ds(start, each), :] = attend(
                qc[pl.ds(start, each), :],
                kv[item, :, :cols],
                kv[item, :, cols:],
                lambda s: jnp.where(real, s, NEG),
                heads,
                scaled,
                ones,
            )

        @pl.when(index == pl.num_programs(0) - 1)
        def _():
            out[...] = mul_t(attended[...], weight[...]).astype(BF)

    bias, gain, shift, bias_q = rows_in
    return call(
        kernel,
        items // batch,
        [whole((rows, width))] * 3
        + [whole((1, width))] * 3
        + [whole((1, cols)), whole((width, cols)), block((batch, padded, 2 * cols)), whole((width, cols))],
        [
            whole((rows, width)),
            whole((rows, 1)),
            whole((rows, width)),
            whole((rows, cols)),
            whole((rows, cols)),
            whole((rows, width)),
        ],
        [
            shaped((rows, width), F32),
            shaped((rows, 1), F32),
            shaped((rows, width), BF),
            shaped((rows, cols), BF),
            shaped((rows, cols), BF),
            shaped((rows, width), BF),
        ],
        flops=2 * rows * cols * padded * heads * 2,
        moved=rows * width * 20 + 4 * items * padded * cols,
    )(own, near, away, bias, gain, shift, bias_q, cq, keys_values, weight)


def lay_pieces(places, spots, refs, laid):
    count, rows, cols = laid.shape[1:]
    for far_off, w_in, w_out in zip(spots, refs[:count], refs[count:]):
        laid[0, places[far_off]] = w_in[...]
        laid[1, places[far_off]] = w_out[...]
    return laid[0].reshape(count * rows, cols), laid[1].reshape(count * rows, cols)


def feed_forward(flag, places, unit, near, away, rows_in, pieces, b_in, chunk):
    rows, width = unit.shape
    hidden = pieces[0].shape[1] // 2
    steps = hidden // chunk
    count = len(pieces)
    spots = arrival_order(count)

    def kernel(flag, places, unit, near, away, gain0, shift0, bias, gain1, shift1, b_in, *refs):
        z, z_low, unit2, scale2, act, slope, part, out, laid = refs[2 * count :]
        w_in, w_out = lay_pieces(places, spots, refs[: 2 * count], laid)

        @pl.when(pl.program_id(0) == 0)
        def _():
            after = unit[...] * gain0[...] + shift0[...]
            one, size = standard(after + pair_sum(near, away) + bias[...])
            unit2[...] = one
            scale2[...] = size
            z[...] = jnp.where(flag[0] == 0, one * gain1[...] + shift1[...], after)
            z_low[...] = z[...].astype(BF)
            out[...] = jnp.zeros_like(out)

        for half in range(2):
            span = slice(half * rows // 2, (half + 1) * rows // 2)
            u = mul(z_low[span], w_in) + b_in[...]
            share = 0.5 + 0.5 * lax.erf(u * math.sqrt(0.5))
            act_half = (u * share).astype(BF)
            act[span] = act_half
            slope[0, span] = share + u * (jnp.exp(-0.5 * u * u) * (1.0 / math.sqrt(2.0 * math.pi)))
            out[span] += mul_t(act_half, w_out)

        @pl.when(pl.program_id(0) == steps - 1)
        def _():
            part[...] = out[...].astype(BF)

    row = whole((1, width))
    return call(
        kernel,
        steps,
        [pl.BlockSpec(memory_space=pltpu.SMEM)] * 2
        + [whole((rows, width))] * 3
        + [row] * 5
        + [column((1, chunk))]
        + [column((width // count, chunk))] * count
        + [column((width // count, chunk), steps)] * count,
        [
            whole((rows, width)),
            whole((rows, width)),
            whole((rows, width)),
            whole((rows, 1)),
            column((rows, chunk)),
            block((1, rows, chunk)),
            whole((rows, width)),
        ],
        [
            shaped((rows, width), F32),
            shaped((rows, width), BF),
            shaped((rows, width), F32),
            shaped((rows, 1), F32),
            shaped((rows, hidden), BF),
            shaped((steps, rows, chunk), F32),
            shaped((rows, width), BF),
        ],
        scratch=[pltpu.VMEM((rows, width), F32), pltpu.VMEM((2, count, width // count, chunk), BF)],
        flops=4 * rows * hidden * width,
        moved=rows * width * 26 + rows * hidden * 6 + width * hidden * 4,
    )(flag, places, unit, near, away, *rows_in, b_in, *pieces, *pieces)


def feed_back(places, z, near, away, cotangent, rows_in, slope, pieces, chunk):
    rows, width = z.shape
    hidden = pieces[0].shape[1] // 2
    steps = hidden // chunk
    count = len(pieces)
    spots = arrival_order(count)

    def kernel(places, z, near, away, cot, bias, gain, shift, slope, *refs):
        result, grad_v, grad_u, grad_pre, part, sums, sum_pre, out, laid = refs[2 * count :]
        w_in, w_out = lay_pieces(places, spots, refs[: 2 * count], laid)

        @pl.when(pl.program_id(0) == 0)
        def _():
            one, size = standard(z[...] + pair_sum(near, away) + bias[...])
            dy = cot[...]
            result[...] = (one * gain[...] + shift[...]).astype(BF)
            grad_v[...] = norm_back(dy, one, size, gain[...])
            grad_u[...] = grad_v[...].astype(BF)
            sums[0:1] = total_rows(dy * one)
            sums[1:2] = total_rows(dy)
            sums[2:3] = total_rows(grad_u[...].astype(F32))
            out[...] = jnp.zeros_like(out)

        for half in range(2):
            span = slice(half * rows // 2, (half + 1) * rows // 2)
            pre = (mul(grad_u[span], w_out) * slope[0, span]).astype(BF)
            grad_pre[span] = pre
            out[span] += mul_t(pre, w_in)
        sum_pre[...] = total_rows(grad_pre[...].astype(F32))

        @pl.when(pl.program_id(0) == steps - 1)
        def _():
            part[...] = out[...].astype(BF)

    row = whole((1, width))
    return call(
        kernel,
        steps,
        [pl.BlockSpec(memory_space=pltpu.SMEM)]
        + [whole((rows, width))] * 4
        + [row] * 3
        + [block((1, rows, chunk))]
        + [column((width // count, chunk))] * count
        + [column((width // count, chunk), steps)] * count,
        [
            whole((rows, width)),
            whole((rows, width)),
            whole((rows, width)),
            column((rows, chunk)),
            whole((rows, width)),
            whole((8, width)),
            column((1, chunk)),
        ],
        [
            shaped((rows, width), BF),
            shaped((rows, width), F32),
            shaped((rows, width), BF),
            shaped((rows, hidden), BF),
            shaped((rows, width), BF),
            shaped((8, width), F32),
            shaped((1, hidden), F32),
        ],
        scratch=[pltpu.VMEM((rows, width), F32), pltpu.VMEM((2, count, width // count, chunk), BF)],
        flops=4 * rows * hidden * width,
        moved=rows * width * 28 + rows * hidden * 6 + width * hidden * 4,
    )(places, z, near, away, cotangent, *rows_in, slope, *pieces, *pieces)


def cross_back(flag, grad_v, near, away, unit2, scale2, gain, qc, keys_values, weight, cq, items, batch, patches):
    rows, width = grad_v.shape
    cols = weight.shape[1]
    heads, each = cols // HEAD_DIM, rows // items
    padded = keys_values.shape[1]

    def kernel(flag, grad_v, near, away, unit2, scale2, gain, qc, kv, weight, cq, after, mix, grad_qc, grad_kv, out, sums, sums_c, grad_att):
        index = pl.program_id(0)

        @pl.when(index == 0)
        def _():
            dz = grad_v[...] + pair_sum(near, away)
            mine = flag[0] == 0
            used = jnp.where(mine, dz, 0.0)
            two = norm_back(used, unit2[...], scale2[...], gain[...])
            after[...] = jnp.where(mine, two, dz)
            mix[...] = two.astype(BF)
            grad_att[...] = mul(mix[...], weight[...]).astype(BF)
            sums[0:1] = total_rows(used * unit2[...])
            sums[1:2] = total_rows(used)
            sums[2:3] = total_rows(mix[...].astype(F32))
            sums_c[...] = jnp.zeros_like(sums_c)

        root = HEAD_DIM ** (-0.5)
        scaled = head_mask(each, heads, root, BF)
        plain = head_mask(each, heads, 1.0, BF)
        ones = head_mask(each, heads, 1.0, F32)
        real = lax.broadcasted_iota(jnp.int32, (heads * each, padded), 1) < patches
        for item in range(batch):
            start = pl.multiple_of((index * batch + item) * each, each)
            dq, dk, dv = attend_back(
                qc[pl.ds(start, each), :],
                kv[item, :, :cols],
                kv[item, :, cols:],
                grad_att[pl.ds(start, each), :],
                lambda s: jnp.where(real, s, NEG),
                heads,
                scaled,
                plain,
                ones,
            )
            grad_qc[pl.ds(start, each), :] = dq.astype(BF)
            dk, dv = dk.astype(BF), dv.astype(BF)
            grad_kv[item, :, :cols] = dk
            grad_kv[item, :, cols:] = dv
            sums_c[1:2] += total_rows(dk.astype(F32))
            sums_c[2:3] += total_rows(dv.astype(F32))

        @pl.when(index == pl.num_programs(0) - 1)
        def _():
            out[...] = mul_t(grad_qc[...], cq[...]).astype(BF)
            sums_c[0:1] = total_rows(grad_qc[...].astype(F32))

    return call(
        kernel,
        items // batch,
        [pl.BlockSpec(memory_space=pltpu.SMEM)]
        + [whole((rows, width))] * 4
        + [
            whole((rows, 1)),
            whole((1, width)),
            whole((rows, cols)),
            block((batch, padded, 2 * cols)),
            whole((width, cols)),
            whole((width, cols)),
        ],
        [
            whole((rows, width)),
            whole((rows, width)),
            whole((rows, cols)),
            block((batch, padded, 2 * cols)),
            whole((rows, width)),
            whole((8, width)),
            whole((8, cols)),
        ],
        [
            shaped((rows, width), F32),
            shaped((rows, width), BF),
            shaped((rows, cols), BF),
            shaped((items, padded, 2 * cols), BF),
            shaped((rows, width), BF),
            shaped((8, width), F32),
            shaped((8, cols), F32),
        ],
        scratch=[pltpu.VMEM((rows, cols), BF)],
        flops=2 * rows * cols * padded * heads * 5,
        moved=rows * width * 26 + 8 * items * padded * cols,
    )(flag, grad_v, near, away, unit2, scale2, gain, qc, keys_values, weight, cq)


def self_back(flag, head, after, near, away, unit, scale, gain, q, kv, kv_far, allowed, weight, w_qkv, own, far, attended, items, batch, shards):
    rows, width = after.shape
    cols = weight.shape[1]
    heads, each = cols // HEAD_DIM, rows // items
    piece = width // shards

    def kernel(flag, head, after, near, away, unit, scale, gain, q, kv, kv_far, allowed, weight, w_qkv, own, far, attended, grad_one, mix, grad_near, grad_away, mine, theirs, sums, sums_c, grad_keep, grad_sent, grad_att):
        index = pl.program_id(0)

        @pl.when(index == 0)
        def _():
            grad = after[...] + pair_sum(near, away)
            grad_one[...] = norm_back(grad, unit[...], scale[...], gain[...])
            mix[...] = grad_one[...].astype(BF)
            grad_att[...] = mul(mix[...], weight[...]).astype(BF)
            sums[0:1] = total_rows(grad * unit[...])
            sums[1:2] = total_rows(grad)
            sums[2:3] = total_rows(mix[...].astype(F32))

        scaled = head_mask(each, heads, HEAD_DIM ** (-0.5), BF)
        plain = head_mask(each, heads, 1.0, BF)
        ones = head_mask(each, heads, 1.0, F32)
        for item in range(batch):
            span = slice(item * each, (item + 1) * each)
            start = pl.multiple_of((index * batch + item) * each, each)
            keys = jnp.concatenate([kv[span, :cols], kv_far[span, :cols]], axis=0)
            values = jnp.concatenate([kv[span, cols:], kv_far[span, cols:]], axis=0)
            seen = jnp.concatenate([allowed[item]] * heads, axis=0) > 0
            dq, dk, dv = attend_back(
                q[span],
                keys,
                values,
                grad_att[pl.ds(start, each), :],
                lambda s: jnp.where(seen, s, NEG),
                heads,
                scaled,
                plain,
                ones,
            )
            grad_near[pl.ds(start, each), :cols] = dq.astype(BF)
            grad_near[pl.ds(start, each), cols : 2 * cols] = dk[:each].astype(BF)
            grad_near[pl.ds(start, each), 2 * cols :] = dv[:each].astype(BF)
            grad_away[pl.ds(start, each), :cols] = dk[each:].astype(BF)
            grad_away[pl.ds(start, each), cols:] = dv[each:].astype(BF)

        @pl.when(index == pl.num_programs(0) - 1)
        def _():
            side = head[0] == 0
            middle = rows // 2
            for part, source, weights in ((0, grad_near, w_qkv), (1, grad_away, w_qkv[:, cols:])):
                lanes = slice(part * width, (part + 1) * width)
                top = mul_t(source[:middle], weights[...]).astype(BF)
                low = mul_t(source[middle:], weights[...]).astype(BF)
                mine[:, lanes] = jnp.where(side, top, low)
                theirs[:, lanes] = jnp.where(side, low, top)
            for place in range(4):
                span = slice(place * cols, (place + 1) * cols)
                if place == 3:
                    total = t_mul(mix[...], attended[...])
                else:
                    total = t_mul(own[...], grad_near[:, span])
                if place in (1, 2):
                    total = total + t_mul(far[...], grad_away[:, (place - 1) * cols : place * cols])
                total = total.astype(BF)
                for side in range(2):
                    pieces = [
                        total[one * piece : (one + 1) * piece] for one in range(side, shards, 2)
                    ]

                    @pl.when(flag[0] == side)
                    def _():
                        for one, value in enumerate(pieces):
                            grad_keep[one, :, span] = value

                    @pl.when(flag[0] != side)
                    def _():
                        for one, value in enumerate(pieces):
                            grad_sent[one, :, span] = value
            sums_c[0:1] = total_rows(grad_near[...].astype(F32))
            sums_c[1:2, cols:] = total_rows(grad_away[...].astype(F32))

    part = batch * each
    return call(
        kernel,
        items // batch,
        [pl.BlockSpec(memory_space=pltpu.SMEM)] * 2
        + [whole((rows, width))] * 4
        + [
            whole((rows, 1)),
            whole((1, width)),
            block((part, cols)),
            block((part, 2 * cols)),
            block((part, 2 * cols)),
            block((batch, each, 2 * each)),
            whole((width, cols)),
            whole((width, 3 * cols)),
            whole((rows, width)),
            whole((rows, width)),
            whole((rows, cols)),
        ],
        [
            whole((rows, width)),
            whole((rows, width)),
            whole((rows, 3 * cols)),
            whole((rows, 2 * cols)),
            whole((rows // 2, 2 * width)),
            whole((rows // 2, 2 * width)),
            whole((8, width)),
            whole((8, 3 * cols)),
            whole((shards // 2, piece, 4 * cols)),
            whole((shards // 2, piece, 4 * cols)),
        ],
        [
            shaped((rows, width), F32),
            shaped((rows, width), BF),
            shaped((rows, 3 * cols), BF),
            shaped((rows, 2 * cols), BF),
            shaped((rows // 2, 2 * width), BF),
            shaped((rows // 2, 2 * width), BF),
            shaped((8, width), F32),
            shaped((8, 3 * cols), F32),
            shaped((shards // 2, piece, 4 * cols), BF),
            shaped((shards // 2, piece, 4 * cols), BF),
        ],
        scratch=[pltpu.VMEM((rows, cols), BF)],
        flops=2 * rows * cols * width * 9,
        moved=rows * width * 32 + rows * cols * 20,
    )(flag, head, after, near, away, unit, scale, gain, q, kv, kv_far, allowed, weight, w_qkv, own, far, attended)


def pack_small(flag, one, two, three, own, cross, pre, kv_grad, kv_all, gain, shift):
    width = one.shape[1]
    cols = cross.shape[1]
    feat_width = kv_all.shape[0]
    pres = pre.shape[1] // width
    folds = (feat_width + width - 1) // width
    rows = (14 + 2 * pres + 2 * folds + 7) // 8 * 8

    def exact(left, right):
        return lax.dot_general(
            left,
            right,
            (((1,), (1,)), ((), ())),
            precision=lax.Precision.HIGHEST,
            preferred_element_type=F32,
        )

    def kernel(flag, one, two, three, own, cross, pre, kv_grad, kv_all, gain, shift, out, line):
        on_text = flag[0].astype(F32)
        on_query = 1.0 - on_text
        out[...] = jnp.zeros_like(out)
        for place in range(3):
            at_row = slice(place, place + 1)
            out[4 * place : 4 * place + 1] = one[at_row]
            out[4 * place + 1 : 4 * place + 2] = two[at_row]
            out[4 * place + 2 : 4 * place + 3] = on_query * three[at_row]
            out[4 * place + 3 : 4 * place + 4] = on_text * three[at_row]
        out[12:13, :cols] = own[0:1, :cols]
        out[12:13, cols:] = own[0:1, 2 * cols :] + own[1:2, 2 * cols :]
        out[13:14, :cols] = cross[0:1]
        out[13:14, cols:] = cross[2:3]
        for k in range(pres):
            part = pre[:, k * width : (k + 1) * width]
            out[14 + k : 15 + k] = on_query * part
            out[14 + pres + k : 15 + pres + k] = on_text * part
        column_sums = jnp.concatenate([cross[1:2], cross[2:3]], axis=1)
        column_sums = jnp.broadcast_to(column_sums, (8, width))
        ones = jnp.ones((8, width), F32)

        def chunk(k, carry):
            span = pl.ds(pl.multiple_of(k * 128, 128), 128)
            weight = kv_all[span, :].astype(F32)
            d_shift = exact(column_sums, weight)[0:1]
            dot = exact(ones, kv_grad[span, :] * weight)[0:1]
            line[0:1, span] = (dot - shift[:, span] * d_shift) / gain[:, span]
            line[1:2, span] = d_shift
            return carry

        lax.fori_loop(0, feat_width // 128, chunk, 0)
        start = 14 + 2 * pres
        for part in range(2):
            for k in range(folds):
                end = min(feat_width, (k + 1) * width)
                spot = start + part * folds + k
                out[spot : spot + 1, : end - k * width] = line[part : part + 1, k * width : end]

    arrays = (one, two, three, own, cross, pre, kv_grad, kv_all, gain, shift)
    return call(
        kernel,
        1,
        [pl.BlockSpec(memory_space=pltpu.SMEM)] + [whole(array.shape) for array in arrays],
        whole((rows, width)),
        shaped((rows, width), F32),
        scratch=[pltpu.VMEM((8, feat_width), F32)],
        moved=6 * feat_width * width,
    )(flag, *arrays)


def unpack_small(head, packed, other, pres, feat_width):
    width = packed.shape[1]
    half = width // 2
    folds = (feat_width + width - 1) // width

    def kernel(head, packed, other, own_bias, cross_bias, gains, shifts, d_gain, d_shift, pre, post):
        first = head[0] == 0
        near, away = packed[12:], other[...]
        low = jnp.where(first, near, away)
        high = jnp.where(first, away, near)
        for place, out in enumerate((own_bias, cross_bias)):
            for part in range(2):
                span = slice(part * half, (part + 1) * half)
                out[part : part + 1, :half] = low[place : place + 1, span]
                out[part : part + 1, half:] = high[place : place + 1, span]
        own_bias[2:3] = packed[8:9]
        cross_bias[2:3] = packed[9:10]
        gains[...] = packed[0:4]
        shifts[...] = packed[4:8]
        post[...] = packed[10:12]
        for side in range(2):
            for k in range(pres):
                line = slice(2 + side * pres + k, 3 + side * pres + k)
                pre[side : side + 1, k * width : (k + 1) * width] = low[line]
                pre[side : side + 1, (pres + k) * width : (pres + k + 1) * width] = high[line]
        both = near + away
        for place, out in enumerate((d_gain, d_shift)):
            for k in range(folds):
                end = min(feat_width, (k + 1) * width)
                line = 2 + 2 * pres + place * folds + k
                for begin in range(k * width, end, 128):
                    spot, left = begin // 128, begin - k * width
                    out[spot : spot + 1] = both[line : line + 1, left : left + 128]

    shapes = [(3, width)] * 2 + [(4, width)] * 2 + [(feat_width // 128, 128)] * 2
    shapes = shapes + [(2, 2 * pres * width), (2, width)]
    return call(
        kernel,
        1,
        [pl.BlockSpec(memory_space=pltpu.SMEM), whole(packed.shape), whole(other.shape)],
        [whole(shape) for shape in shapes],
        [shaped(shape, F32) for shape in shapes],
        moved=200000,
    )(head, packed, other)


def visible(stream, segments, modes):
    same_caption = segments[:, :, None] == segments[:, None, :]
    own = jnp.logical_or(stream == 0, same_caption)
    far = jnp.where(stream == 0, modes == 2, modes >= 1)[:, None, None]
    return jnp.concatenate([own, jnp.broadcast_to(far, own.shape)], axis=2).astype(F32)


def body(
    hidden,
    features,
    segments,
    modes,
    w_qkv,
    self_bias,
    self_out,
    cross_q,
    cross_kv,
    cross_bias,
    cross_out,
    gains,
    shifts,
    feat_gain,
    feat_shift,
    ffn_in,
    ffn_bias_in,
    ffn_out,
    ffn_bias_out,
    cotangent,
):
    stream = lax.axis_index("stream")
    stream_u = stream.astype(jnp.uint32)
    head_index = lax.axis_index("heads")
    items, _, each, width = hidden.shape
    rows = items * each
    half = rows // 2
    cols = w_qkv.shape[2]
    hidden_cols = ffn_in.shape[2]
    patches, feat_width = features.shape[1:]
    padded = (patches + 7) // 8 * 8
    col_start = head_index.astype(jnp.uint32) * cols
    hidden_start = head_index.astype(jnp.uint32) * hidden_cols
    flag = stream.astype(jnp.int32).reshape(1)
    shards = 2 * lax.axis_size("items")
    three = [slice(i * cols, (i + 1) * cols) for i in range(3)]

    ffn_part = jnp.concatenate([ffn_in[0], ffn_out[0].T], axis=1)
    part_qkv = jnp.concatenate([w_qkv[0], w_qkv[1], w_qkv[2]], axis=0)
    pair_qkv = by_stream(part_qkv, partner(part_qkv, "stream", 0), 0)
    places = ring_places()
    spots = ring_row()
    own = hidden.reshape(rows, width)
    heads_u = head_index.astype(jnp.uint32)
    my_half = lax.dynamic_slice_in_dim(own, heads_u * half, half, 0)
    far_half = partner(my_half, "stream", 0)
    piece, kv_piece = cross_q.shape[0], cross_kv.shape[1]
    rest = jnp.concatenate([self_out.T, cross_q, cross_out.T, cross_kv[0], cross_kv[1]], axis=0)

    def row(vector):
        return vector.reshape(1, -1)

    features, pair_qkv = joined(features, pair_qkv)
    ring = Gather(jnp.concatenate([pair_qkv.reshape(6 * piece, cols), rest], axis=0))

    def crossing(one):
        return one[6 * piece :], over("stream")

    kept, chunk = [], items // 4
    crossed = []
    begin = 0
    for number in range(max(4, shards // 4)):
        if ring.left:
            riders = [crossing(one) for one in ring.pieces[begin:]]
            if number == 1:
                riders.append((far_half, over("heads")))
            last_step = ring.hop == shards // 4
            if last_step:
                ffn_part, held = joined(ffn_part, ring.up)
                ring.replace(held, ring.down)
                ffn_gather = Gather(ffn_part)
            fresh = len(ring.pieces) - begin
            begin = len(ring.pieces)
            ridden = gather_step([ring], *riders)
            crossed += ridden[:fresh]
            if number == 1:
                far_other = ridden[-1]
            if last_step:
                gather_step([ffn_gather])
        if number < 4:
            *kept, token = list(
                feature_norm(
                    features, row(feat_gain), row(feat_shift), padded, number * chunk, chunk, kept
                )
            )
            up, down, token = joined(ring.up, ring.down, token)
            ring.replace(up, down)
            kept = [kept[0], token]
    feat_norm = kept[0]
    crossed += [move(one) for one, move in (crossing(one) for one in ring.pieces[begin:])]
    far = jnp.where(
        head_index == 0,
        jnp.concatenate([far_half, far_other], axis=0),
        jnp.concatenate([far_other, far_half], axis=0),
    )
    def ffn_step(value, last=False):
        if ffn_gather.hop - 1 > ffn_gather.count // 2:
            return value
        value, up, down = joined(value, ffn_gather.up, ffn_gather.down)
        ffn_gather.replace(up, down)
        while ffn_gather.left:
            gather_step([ffn_gather])
            if not last:
                break
        return value

    def my_cols(vector):
        return lax.dynamic_slice_in_dim(vector, col_start, cols, 0)

    none = jnp.zeros((cols,), F32)
    bias_qkv = row(jnp.concatenate([my_cols(self_bias[0]), none, my_cols(self_bias[1])]))
    bias_kv = row(jnp.concatenate([none, my_cols(cross_bias[1])]))
    gain_ffn = row(lax.dynamic_index_in_dim(gains, 2 + stream_u, 0, keepdims=False))
    shift_ffn = row(lax.dynamic_index_in_dim(shifts, 2 + stream_u, 0, keepdims=False))
    bias_in = row(
        lax.dynamic_slice_in_dim(
            lax.dynamic_index_in_dim(ffn_bias_in, stream_u, 0, keepdims=False),
            hidden_start,
            hidden_cols,
            0,
        )
    )
    bias_out = row(lax.dynamic_index_in_dim(ffn_bias_out, stream_u, 0, keepdims=False))

    def swap(part):
        return partner(part, "heads", 0)

    q, kv, kv_far, qkv_all = project(spots, own, far, ring.pieces, bias_qkv, piece)
    ends = joined(ffn_gather.up, ffn_gather.down, ring.up, kv_far, feat_norm, *crossed[-3:])
    ffn_gather.replace(*ends[:2])
    ring.replace(ends[2], ends[2])
    kv_far = ends[3]
    feat_rows = ends[4].reshape(items * padded, feat_width)
    crossed[-3:] = ends[5:]
    gather_step([ffn_gather])
    self_out_t, cross_q_all, cross_out_t, kv_all = assemble(
        flag, spots, ring.pieces, crossed, piece, kv_piece
    )

    allowed = visible(stream, segments, modes)
    attended, part = self_attention(q, kv, kv_far, allowed, self_out_t, items, 4)
    kv_all = ffn_step(kv_all)
    away_one = swap(part)
    keys_values = (mul(feat_rows, kv_all) + bias_kv).astype(BF).reshape(items, padded, 2 * cols)
    keys_values = ffn_step(keys_values)
    unit_one, scale_one, after_low, qc, attended_c, part_c = cross_attention(
        own,
        part,
        away_one,
        (row(self_bias[2]), row(gains[0]), row(shifts[0]), row(my_cols(cross_bias[0]))),
        cross_q_all,
        keys_values,
        cross_out_t,
        items,
        2,
        patches,
    )
    unit_one, part_c, scale_one, after_low, qc, attended_c = ffn_step(
        (unit_one, part_c, scale_one, after_low, qc, attended_c), True
    )
    ffn_pieces = ffn_gather.pieces
    z, z_low, unit_two, scale_two, activated, slope, part_f = feed_forward(
        flag,
        spots,
        unit_one,
        part_c,
        swap(part_c),
        (row(gains[0]), row(shifts[0]), row(cross_bias[2]), row(gains[1]), row(shifts[1])),
        ffn_pieces,
        bias_in,
        256,
    )

    output, grad_three, grad_u, grad_pre, part_z, sums_three, sum_pre = feed_back(
        spots,
        z,
        part_f,
        swap(part_f),
        cotangent.reshape(rows, width),
        (bias_out, gain_ffn, shift_ffn),
        slope,
        ffn_pieces,
        256,
    )
    away_z = swap(part_z)
    in_grad = t_mul(z_low, grad_pre).astype(BF)
    out_grad = t_mul(grad_u, activated).astype(BF)
    count = shards // 2
    grad_after, mix_c, grad_qc, grad_kv, part_a, sums_two, sums_cross = cross_back(
        flag,
        grad_three,
        part_z,
        away_z,
        unit_two,
        scale_two,
        row(gains[1]),
        qc,
        keys_values,
        cross_out_t,
        cross_q_all,
        items,
        2,
        patches,
    )
    in_grad, out_grad, sums_two = joined(in_grad, out_grad, sums_two)
    ffn_ring = Scatter(
        [
            [at(in_grad.reshape(count, -1, hidden_cols))],
            [at(out_grad.reshape(count, -1, hidden_cols))],
        ],
        1,
        places,
    )
    ffn_ring.step()
    away_a = swap(part_a)
    keep_q, away_q = halves(t_mul(after_low, grad_qc).astype(BF))
    keep_o, away_o = halves(t_mul(mix_c, attended_c).astype(BF))
    away_c = jnp.concatenate([away_q, away_o], axis=2)
    grad_kv, away_c = joined(grad_kv, away_c)
    kv_grad = t_mul(feat_rows, grad_kv.reshape(items * padded, 2 * cols))
    kv_grad_low = kv_grad.astype(BF)
    arrived_c = partner(away_c, "stream", 0)
    kv_grad, kv_grad_low, arrived_c, ffn_ring.up = joined(
        kv_grad, kv_grad_low, arrived_c, ffn_ring.up
    )
    keep_kv, away_kv = halves(kv_grad_low)
    ffn_ring.step()
    away_a, away_kv = joined(away_a, away_kv)
    arrived_kv = partner(away_kv, "stream", 0)
    grad_one, mix, grad_near, grad_away, mine, theirs, sums_one, sums_self, keep_self, away_self = self_back(
        flag,
        head_index.astype(jnp.int32).reshape(1),
        grad_after,
        part_a,
        away_a,
        unit_one,
        scale_one,
        row(gains[0]),
        q,
        kv,
        kv_far,
        allowed,
        self_out_t,
        qkv_all,
        own,
        far,
        attended,
        items,
        4,
        shards,
    )

    results = (grad_one, mine, theirs, sums_one, sums_self, keep_self, away_self, arrived_kv)
    results = lax.optimization_barrier(results + (ffn_ring.up, ffn_ring.down))
    grad_one, mine, theirs, sums_one, sums_self, keep_self, away_self, arrived_kv = results[:-2]
    ffn_ring.up, ffn_ring.down = results[-2:]


    def ring_steps(rings, *riders):
        ridden = [move(value) for value, move in riders]
        sends = [ring.sends() for ring in rings]
        flat = [one for part in sends for one in part]
        arrivals = lax.optimization_barrier(tuple(ridden) + tuple(together(flat)))
        rest = arrivals[len(riders) :]
        for ring, part in zip(rings, sends):
            ring.take(rest[: len(part)])
            rest = rest[len(part) :]
        return arrivals[: len(riders)]

    rest_ring = Scatter(
        [
            [at_stream(keep_q), at(arrived_c, three[0])],
            [at_stream(keep_o), at(arrived_c, three[1])],
            [at_stream(keep_kv, three[0]), at(arrived_kv, three[0])],
            [at_stream(keep_kv, three[1]), at(arrived_kv, three[1])],
        ],
        0,
        places,
    )
    arrived_self, from_swap = ring_steps(
        [ffn_ring, rest_ring], (away_self, over("stream")), (theirs, over("heads"))
    )
    self_ring = Scatter([[at(keep_self), at(arrived_self)]], 0, places)
    total = mine.astype(F32) + from_swap.astype(F32)
    from_far = partner(total[:, width:].astype(BF), "stream", 0)
    packed = pack_small(
        flag,
        sums_one,
        sums_two,
        sums_three,
        sums_self,
        sums_cross,
        sum_pre,
        kv_grad,
        kv_all,
        row(feat_gain),
        row(feat_shift),
    )
    packed = packed + partner(packed, "items", 0)
    moves = [over("stream")] + [over("items", bit) for bit in range(1, (count - 1).bit_length())]

    in_half = (
        lax.dynamic_slice_in_dim(grad_one, heads_u * half, half, 0)
        + total[:, :width]
        + from_far.astype(F32)
    )
    (arrived,) = ring_steps(
        [one for one in (ffn_ring, self_ring) if one.hop], (packed, moves.pop(0))
    )
    packed = packed + arrived
    in_other = swap(in_half)
    while self_ring.hop or ffn_ring.hop or rest_ring.hop:
        rings = [one for one in (ffn_ring, rest_ring, self_ring) if one.hop]
        riders = [(packed, moves.pop(0))] if moves else []
        for arrived in ring_steps(rings, *riders):
            packed = packed + arrived
    while moves:
        packed = packed + moves.pop(0)(packed)
    grad_input = jnp.where(
        head_index == 0,
        jnp.concatenate([in_half, in_other], axis=0),
        jnp.concatenate([in_other, in_half], axis=0),
    )
    ffn_red, rest_red, self_red = ffn_ring.result(), rest_ring.result(), self_ring.result()
    small = unpack_small(
        head_index.astype(jnp.int32).reshape(1),
        packed,
        swap(packed[12:]),
        hidden_cols // width,
        feat_width,
    )
    return (
        output.reshape(items, 1, each, width),
        grad_input.reshape(items, 1, each, width),
        jnp.stack([self_red[:, one] for one in three]),
        small[0],
        self_red[:, 3 * cols :].T,
        rest_red[:piece],
        rest_red[2 * piece :].reshape(2, kv_piece, cols),
        small[1],
        rest_red[piece : 2 * piece].T,
        small[2],
        small[3],
        small[4].reshape(feat_width),
        small[5].reshape(feat_width),
        ffn_red[:, :hidden_cols][None],
        small[6],
        ffn_red[:, hidden_cols:].T[None],
        small[7],
    )


def solution(mesh):
    placed = (
        P("items", "stream", None, None),
        P("items", None, None),
        P("items", None),
        P("items"),
        P(None, ("items", "stream"), "heads"),
        P(),
        P("heads", ("items", "stream")),
        P(("items", "stream"), "heads"),
        P(None, ("items", "stream"), "heads"),
        P(),
        P("heads", ("items", "stream")),
        P(),
        P(),
        P(),
        P(),
        P("stream", "items", "heads"),
        P(),
        P("stream", "heads", "items"),
        P(),
        P("items", "stream", None, None),
    )
    return jax.shard_map(
        body,
        mesh=mesh,
        in_specs=placed,
        out_specs=(
            P("items", "stream", None, None),
            P("items", "stream", None, None),
            P(None, ("items", "stream"), "heads"),
            P(),
            P("heads", ("items", "stream")),
            P(("items", "stream"), "heads"),
            P(None, ("items", "stream"), "heads"),
            P(),
            P("heads", ("items", "stream")),
            P(),
            P(),
            P(),
            P(),
            P("stream", "items", "heads"),
            P(),
            P("stream", "heads", "items"),
            P(),
        ),
        check_vma=False,
    )
```

```python
import math

import jax
import jax.numpy as jnp
import numpy as np
from jax import lax
from jax.experimental import pallas as pl
from jax.experimental.pallas import tpu as pltpu
from jax.sharding import PartitionSpec as P

HEAD_DIM = 64
EPS = 1e-06
NEG = -1e30
BF = jnp.bfloat16
F32 = jnp.float32


def partner(shard, axis, distance):
    return lax.ppermute(shard, axis, [(i, i ^ 1 << distance) for i in range(lax.axis_size(axis))])


def joined(*values):
    return lax.optimization_barrier(values)


def ring_of(count):
    return list(range(0, count, 2)) + list(range(1, count, 2))[::-1]


def ring_table():
    count = lax.axis_size("items")
    order = ring_of(count)
    table = np.zeros((count, count), np.uint32)
    for place, index in enumerate(order):
        table[index] = [order[(place + far) % count] for far in range(count)]
    return table


def ring_row():
    row = lax.axis_index("items").astype(jnp.uint32)
    table = jnp.asarray(ring_table().astype(np.int32))
    found = lax.dynamic_slice(table, (row, jnp.uint32(0)), (1, table.shape[1]))
    return found.reshape(table.shape[1])


def ring_places():
    table = ring_table()
    count = table.shape[0]
    bits = max(1, (count - 1).bit_length())
    per_word = 32 // bits
    index = lax.axis_index("items").astype(jnp.uint32)
    places = []
    for begin in range(0, count, per_word):
        part = table[:, begin : begin + per_word]
        words = [sum(int(one) << (bits * k) for k, one in enumerate(line)) for line in part]
        word = jnp.uint32(words[0])
        for item in range(1, count):
            word = jnp.where(index == jnp.uint32(item), jnp.uint32(words[item]), word)
        for k in range(part.shape[1]):
            places.append((word >> jnp.uint32(bits * k)) & jnp.uint32((1 << bits) - 1))
    return places


def arrival_order(count):
    order = [0]
    for hop in range(1, count // 2 + 1):
        order.append(count - hop)
        if hop <= (count - 1) // 2:
            order.append(hop)
    return order


def shift_ring(shard, order, step):
    count = len(order)
    return lax.ppermute(
        shard, "items", [(order[i], order[(i + step) % count]) for i in range(count)]
    )


def together(sends):
    values = lax.optimization_barrier(tuple(value for value, _ in sends))
    return lax.optimization_barrier(tuple(move(one) for one, (_, move) in zip(values, sends)))


class Gather:
    def __init__(self, shard):
        self.count = lax.axis_size("items")
        self.order = ring_of(self.count)
        self.up = self.down = shard
        self.pieces = [shard]
        self.hop = 1

    def sends(self):
        result = [(self.up, lambda one: shift_ring(one, self.order, 1))]
        if self.hop <= (self.count - 1) // 2:
            result.append((self.down, lambda one: shift_ring(one, self.order, -1)))
        return result

    def take(self, arrivals):
        self.pieces += arrivals
        self.up = arrivals[0]
        self.down = arrivals[-1]
        self.hop += 1

    def replace(self, up, down):
        self.pieces[-1] = down
        if self.hop - 1 <= (self.count - 1) // 2:
            self.pieces[-2] = up
        self.up, self.down = up, down

    @property
    def left(self):
        return self.hop <= self.count // 2


def gather_step(rings, *riders):
    sends = [ring.sends() for ring in rings]
    arrivals = together(list(riders) + [one for part in sends for one in part])
    ridden, arrivals = arrivals[: len(riders)], arrivals[len(riders) :]
    for ring, part in zip(rings, sends):
        ring.take(list(arrivals[: len(part)]))
        arrivals = arrivals[len(part) :]
    return ridden


def place_items(pieces, places):
    whole = jnp.zeros((len(pieces),) + pieces[0].shape, pieces[0].dtype)
    for far, piece in zip(arrival_order(len(pieces)), pieces):
        whole = lax.dynamic_update_index_in_dim(whole, piece, places[far], 0)
    return whole


def by_stream(own, other, axis):
    first = lax.axis_index("stream") == 0
    return jnp.where(
        first, jnp.stack([own, other], axis=axis), jnp.stack([other, own], axis=axis)
    )


def whole_rows(own, other):
    both = by_stream(own, other, 1)
    return both.reshape((both.shape[0] * both.shape[1] * both.shape[2], both.shape[3]))


def at(pieces, span=slice(None)):
    return lambda which: lax.dynamic_index_in_dim(pieces, which, 0, keepdims=False)[:, span]


def at_stream(pieces, span=slice(None)):
    stream = lax.axis_index("stream").astype(jnp.uint32)
    zero = jnp.uint32(0)

    def read(which):
        start = (which, stream, zero, zero)
        found = lax.dynamic_slice(pieces, start, (1, 1) + pieces.shape[2:])
        return found.reshape(pieces.shape[2:])[:, span]

    return read


class Scatter:
    def __init__(self, groups, axis, places):
        self.groups, self.axis = groups, axis
        self.count = lax.axis_size("items")
        self.order, self.places = ring_of(self.count), places
        self.hop = self.count // 2
        self.up = self.down = None

    def piece(self, distance):
        which = self.places[distance % self.count]
        parts = [sum(read(which).astype(F32) for read in group) for group in self.groups]
        return jnp.concatenate(parts, axis=self.axis)

    def sends(self):
        own = self.piece(self.hop)
        own = own if self.up is None else own + self.up.astype(F32)
        result = [(own.astype(BF), lambda one: shift_ring(one, self.order, 1))]
        if self.hop <= (self.count - 1) // 2:
            own = self.piece(self.count - self.hop)
            own = own if self.down is None else own + self.down.astype(F32)
            result.append((own.astype(BF), lambda one: shift_ring(one, self.order, -1)))
        return result

    def take(self, arrivals):
        self.up = arrivals[0]
        if len(arrivals) > 1:
            self.down = arrivals[1]
        self.hop -= 1
        return arrivals[0]

    def step(self):
        return self.take(together(self.sends()))

    def result(self):
        return self.piece(0) + self.up.astype(F32) + self.down.astype(F32)


def halves(total):
    count = lax.axis_size("items")
    rows = total.shape[0] // (2 * count)
    parts = total.reshape((count, 2, rows, total.shape[1]))
    stream = lax.axis_index("stream").astype(jnp.uint32)
    away = lax.dynamic_index_in_dim(parts, 1 - stream, 1, keepdims=False)
    return parts, away


def over(axis, distance=0):
    return lambda one: partner(one, axis, distance)


def mul(left, right):
    return jnp.dot(left, right, preferred_element_type=F32)


def mul_t(left, right):
    return lax.dot_general(left, right, (((1,), (1,)), ((), ())), preferred_element_type=F32)


def t_mul(left, right):
    return lax.dot_general(left, right, (((0,), (0,)), ((), ())), preferred_element_type=F32)


def standard(rows):
    center = rows - jnp.mean(rows, axis=-1, keepdims=True)
    scale = lax.rsqrt(jnp.mean(center * center, axis=-1, keepdims=True) + EPS)
    return center * scale, scale


def norm_back(grad, unit, scale, gain):
    inner = grad * gain
    return scale * (
        inner
        - jnp.mean(inner, axis=-1, keepdims=True)
        - unit * jnp.mean(inner * unit, axis=-1, keepdims=True)
    )


def pair_sum(near, away):
    return near[...].astype(F32) + away[...].astype(F32)


def total_rows(rows):
    return jnp.sum(rows, axis=0, keepdims=True)


def head_mask(rows, heads, value, dtype):
    row = lax.broadcasted_iota(jnp.int32, (heads * rows, heads * HEAD_DIM), 0) // rows
    col = lax.broadcasted_iota(jnp.int32, (heads * rows, heads * HEAD_DIM), 1) // HEAD_DIM
    return jnp.where(row == col, value, 0.0).astype(dtype)


def stack_heads(rows, heads, mask):
    return jnp.concatenate([rows] * heads, axis=0) * mask


def fold_heads(stacked, heads, mask):
    rows = stacked.shape[0] // heads
    stacked = stacked * mask
    result = stacked[:rows]
    for head in range(1, heads):
        result = result + stacked[head * rows : (head + 1) * rows]
    return result


def softmax(scores):
    power = jnp.exp(scores - jnp.max(scores, axis=-1, keepdims=True))
    return power * (1.0 / jnp.sum(power, axis=-1, keepdims=True))


def attend(queries, keys, values, hide, heads, scaled_mask, out_mask):
    scores = hide(mul_t(stack_heads(queries, heads, scaled_mask), keys))
    weights = softmax(scores).astype(BF)
    return fold_heads(mul(weights, values), heads, out_mask).astype(BF)


def attend_back(queries, keys, values, grad, hide, heads, scaled_mask, plain_mask, out_mask):
    queries = stack_heads(queries, heads, scaled_mask)
    grad = stack_heads(grad, heads, plain_mask)
    weights = softmax(hide(mul_t(queries, keys)))
    grad_weights = mul_t(grad, values)
    grad_values = t_mul(weights.astype(BF), grad)
    delta = jnp.sum(grad_weights * weights, axis=-1, keepdims=True)
    grad_scores = (weights * (grad_weights - delta)).astype(BF)
    grad_queries = fold_heads(mul(grad_scores, keys), heads, out_mask) * HEAD_DIM ** (-0.5)
    return grad_queries, t_mul(grad_scores, queries), grad_values


def whole(shape):
    return pl.BlockSpec(shape, lambda i: (0,) * len(shape))


def block(shape):
    return pl.BlockSpec(shape, lambda i: (i,) + (0,) * (len(shape) - 1))


def column(shape, first=0):
    return pl.BlockSpec(shape, lambda i: (0, i + first))


def shaped(shape, dtype):
    return jax.ShapeDtypeStruct(shape, dtype)


def call(kernel, grid, in_specs, out_specs, out_shape, scratch=(), flops=0, moved=0):
    return pl.pallas_call(
        kernel,
        grid=(grid,),
        in_specs=in_specs,
        out_specs=out_specs,
        out_shape=out_shape,
        scratch_shapes=list(scratch),
        compiler_params=pltpu.CompilerParams(
            dimension_semantics=("arbitrary",), vmem_limit_bytes=56 << 20
        ),
        cost_estimate=pl.CostEstimate(flops=flops, bytes_accessed=moved, transcendentals=0),
    )


def feature_norm(features, gain, shift, padded, begin, each, prior):
    items, patches, width = features.shape

    def kernel(feat, gain, shift, *refs):
        out, token = refs[-2:]
        unit, _ = standard(feat[0].astype(F32))
        out[0, :patches] = (unit * gain[...] + shift[...]).astype(BF)
        out[0, patches:] = jnp.zeros((padded - patches, width), BF)
        token[...] = jnp.zeros_like(token)

    def at_item(i):
        return (i + begin, 0, 0)

    return pl.pallas_call(
        kernel,
        grid=(each,),
        in_specs=[pl.BlockSpec((1, patches, width), at_item), whole((1, width)), whole((1, width))]
        + [pl.BlockSpec(memory_space=pl.ANY)] * len(prior),
        out_specs=[pl.BlockSpec((1, padded, width), at_item), whole((8, 128))],
        out_shape=[shaped((items, padded, width), BF), shaped((8, 128), F32)],
        input_output_aliases={3: 0} if prior else {},
        compiler_params=pltpu.CompilerParams(
            dimension_semantics=("arbitrary",), vmem_limit_bytes=56 << 20
        ),
        cost_estimate=pl.CostEstimate(
            flops=0, bytes_accessed=4 * each * patches * width, transcendentals=0
        ),
    )(features, gain, shift, *prior)


def project(places, own, far, pieces, bias, each):
    rows, width = own.shape
    count = len(pieces)
    head_cols = pieces[0].shape[1]
    cols = 3 * head_cols
    step = rows // 4
    spots = arrival_order(count)

    def kernel(places, own, far, bias, *refs):
        q, kv, kv_far, weight, laid = refs[count:]

        @pl.when(pl.program_id(0) == 0)
        def _():
            for far_off, one in zip(spots, refs[:count]):
                piece = one[...]
                for side in range(2):
                    for k in range(3):
                        start = (3 * side + k) * each
                        lanes = slice(k * head_cols, (k + 1) * head_cols)
                        laid[places[far_off], side, :, lanes] = piece[start : start + each]
            weight[...] = laid[...].reshape(width, cols)

        near = mul(own[...], weight[...]) + bias[...]
        q[...] = near[:, :head_cols].astype(BF)
        kv[...] = near[:, head_cols:].astype(BF)
        kv_far[...] = (mul(far[...], weight[:, head_cols:]) + bias[:, head_cols:]).astype(BF)

    return call(
        kernel,
        4,
        [pl.BlockSpec(memory_space=pltpu.SMEM)]
        + [block((step, width)), block((step, width)), whole((1, cols))]
        + [whole((6 * each, head_cols))] * count,
        [block((step, head_cols)), block((step, 2 * head_cols)), block((step, 2 * head_cols))]
        + [whole((width, cols))],
        [shaped((rows, head_cols), BF)]
        + [shaped((rows, 2 * head_cols), BF)] * 2
        + [shaped((width, cols), BF)],
        scratch=[pltpu.VMEM((count, 2, each, cols), BF)],
        flops=10 * rows * width * head_cols,
        moved=4 * rows * width + 4 * width * cols,
    )(places, own, far, bias, *pieces)


def assemble(flag, places, pieces, crossed, each, kv_each):
    count = len(pieces)
    cols = pieces[0].shape[1]
    spots = arrival_order(count)
    rows = crossed[0].shape[0]

    def kernel(flag, places, *refs):
        self_out, cross_q, cross_out, kv = refs[2 * count :]
        for number, far_off in enumerate(spots):
            place = places[far_off]
            for side, piece in (
                (flag[0], refs[number][6 * each :]),
                (1 - flag[0], refs[count + number][...]),
            ):
                for k, out in enumerate((self_out, cross_q, cross_out)):
                    out[place, side] = piece[k * each : (k + 1) * each]
                start = 3 * each
                kv[place, side, :, :cols] = piece[start : start + kv_each]
                kv[place, side, :, cols:] = piece[start + kv_each :]

    shapes = [(count, 2, each, cols)] * 3 + [(count, 2, kv_each, 2 * cols)]
    results = call(
        kernel,
        1,
        [pl.BlockSpec(memory_space=pltpu.SMEM)] * 2
        + [whole(pieces[0].shape)] * count
        + [whole((rows, cols))] * count,
        [whole(shape) for shape in shapes],
        [shaped(shape, BF) for shape in shapes],
        moved=8 * count * rows * cols,
    )(flag, places, *pieces, *crossed)
    return [one.reshape(2 * count * one.shape[2], one.shape[3]) for one in results]


def self_attention(q, kv, kv_far, allowed, weight, items, batch):
    rows, cols = q.shape
    heads, each = cols // HEAD_DIM, rows // items
    width = weight.shape[0]

    def kernel(q, kv, kv_far, allowed, weight, attended, out):
        index = pl.program_id(0)
        scaled = head_mask(each, heads, HEAD_DIM ** (-0.5), BF)
        ones = head_mask(each, heads, 1.0, F32)
        for item in range(batch):
            span = slice(item * each, (item + 1) * each)
            keys = jnp.concatenate([kv[span, :cols], kv_far[span, :cols]], axis=0)
            values = jnp.concatenate([kv[span, cols:], kv_far[span, cols:]], axis=0)
            seen = jnp.concatenate([allowed[item]] * heads, axis=0) > 0
            result = attend(
                q[span], keys, values, lambda s: jnp.where(seen, s, NEG), heads, scaled, ones
            )
            start = pl.multiple_of((index * batch + item) * each, each)
            attended[pl.ds(start, each), :] = result

        @pl.when(index == pl.num_programs(0) - 1)
        def _():
            out[...] = mul_t(attended[...], weight[...]).astype(BF)

    part = batch * each
    return call(
        kernel,
        items // batch,
        [
            block((part, cols)),
            block((part, 2 * cols)),
            block((part, 2 * cols)),
            block((batch, each, 2 * each)),
            whole((width, cols)),
        ],
        [whole((rows, cols)), whole((rows, width))],
        [shaped((rows, cols), BF), shaped((rows, width), BF)],
        flops=2 * rows * cols * width * 3,
        moved=rows * cols * 14 + rows * width * 4,
    )(q, kv, kv_far, allowed, weight)


def cross_attention(own, near, away, rows_in, cq, keys_values, weight, items, batch, patches):
    rows, width = own.shape
    cols = weight.shape[1]
    heads, each = cols // HEAD_DIM, rows // items
    padded = keys_values.shape[1]

    def kernel(own, near, away, bias, gain, shift, bias_q, cq, kv, weight, unit, scale, low, qc, attended, out):
        index = pl.program_id(0)

        @pl.when(index == 0)
        def _():
            one, size = standard(own[...].astype(F32) + pair_sum(near, away) + bias[...])
            unit[...] = one
            scale[...] = size
            low[...] = (one * gain[...] + shift[...]).astype(BF)
            qc[...] = (mul(low[...], cq[...]) + bias_q[...]).astype(BF)

        scaled = head_mask(each, heads, HEAD_DIM ** (-0.5), BF)
        ones = head_mask(each, heads, 1.0, F32)
        real = lax.broadcasted_iota(jnp.int32, (heads * each, padded), 1) < patches
        for item in range(batch):
            start = pl.multiple_of((index * batch + item) * each, each)
            attended[pl.ds(start, each), :] = attend(
                qc[pl.ds(start, each), :],
                kv[item, :, :cols],
                kv[item, :, cols:],
                lambda s: jnp.where(real, s, NEG),
                heads,
                scaled,
                ones,
            )

        @pl.when(index == pl.num_programs(0) - 1)
        def _():
            out[...] = mul_t(attended[...], weight[...]).astype(BF)

    bias, gain, shift, bias_q = rows_in
    return call(
        kernel,
        items // batch,
        [whole((rows, width))] * 3
        + [whole((1, width))] * 3
        + [whole((1, cols)), whole((width, cols)), block((batch, padded, 2 * cols)), whole((width, cols))],
        [
            whole((rows, width)),
            whole((rows, 1)),
            whole((rows, width)),
            whole((rows, cols)),
            whole((rows, cols)),
            whole((rows, width)),
        ],
        [
            shaped((rows, width), F32),
            shaped((rows, 1), F32),
            shaped((rows, width), BF),
            shaped((rows, cols), BF),
            shaped((rows, cols), BF),
            shaped((rows, width), BF),
        ],
        flops=2 * rows * cols * padded * heads * 2,
        moved=rows * width * 20 + 4 * items * padded * cols,
    )(own, near, away, bias, gain, shift, bias_q, cq, keys_values, weight)


def lay_pieces(places, spots, refs, laid):
    count, rows, cols = laid.shape[1:]
    for far_off, w_in, w_out in zip(spots, refs[:count], refs[count:]):
        laid[0, places[far_off]] = w_in[...]
        laid[1, places[far_off]] = w_out[...]
    return laid[0].reshape(count * rows, cols), laid[1].reshape(count * rows, cols)


def feed_forward(flag, places, unit, near, away, rows_in, pieces, b_in, chunk):
    rows, width = unit.shape
    hidden = pieces[0].shape[1] // 2
    steps = hidden // chunk
    count = len(pieces)
    spots = arrival_order(count)

    def kernel(flag, places, unit, near, away, gain0, shift0, bias, gain1, shift1, b_in, *refs):
        z, z_low, unit2, scale2, act, slope, part, out, laid = refs[2 * count :]
        w_in, w_out = lay_pieces(places, spots, refs[: 2 * count], laid)

        @pl.when(pl.program_id(0) == 0)
        def _():
            after = unit[...] * gain0[...] + shift0[...]
            one, size = standard(after + pair_sum(near, away) + bias[...])
            unit2[...] = one
            scale2[...] = size
            z[...] = jnp.where(flag[0] == 0, one * gain1[...] + shift1[...], after)
            z_low[...] = z[...].astype(BF)
            out[...] = jnp.zeros_like(out)

        for half in range(2):
            span = slice(half * rows // 2, (half + 1) * rows // 2)
            u = mul(z_low[span], w_in) + b_in[...]
            share = 0.5 + 0.5 * lax.erf(u * math.sqrt(0.5))
            act_half = (u * share).astype(BF)
            act[span] = act_half
            slope[0, span] = share + u * (jnp.exp(-0.5 * u * u) * (1.0 / math.sqrt(2.0 * math.pi)))
            out[span] += mul_t(act_half, w_out)

        @pl.when(pl.program_id(0) == steps - 1)
        def _():
            part[...] = out[...].astype(BF)

    row = whole((1, width))
    return call(
        kernel,
        steps,
        [pl.BlockSpec(memory_space=pltpu.SMEM)] * 2
        + [whole((rows, width))] * 3
        + [row] * 5
        + [column((1, chunk))]
        + [column((width // count, chunk))] * count
        + [column((width // count, chunk), steps)] * count,
        [
            whole((rows, width)),
            whole((rows, width)),
            whole((rows, width)),
            whole((rows, 1)),
            column((rows, chunk)),
            block((1, rows, chunk)),
            whole((rows, width)),
        ],
        [
            shaped((rows, width), F32),
            shaped((rows, width), BF),
            shaped((rows, width), F32),
            shaped((rows, 1), F32),
            shaped((rows, hidden), BF),
            shaped((steps, rows, chunk), F32),
            shaped((rows, width), BF),
        ],
        scratch=[pltpu.VMEM((rows, width), F32), pltpu.VMEM((2, count, width // count, chunk), BF)],
        flops=4 * rows * hidden * width,
        moved=rows * width * 26 + rows * hidden * 6 + width * hidden * 4,
    )(flag, places, unit, near, away, *rows_in, b_in, *pieces, *pieces)


def feed_back(places, z, near, away, cotangent, rows_in, slope, pieces, chunk):
    rows, width = z.shape
    hidden = pieces[0].shape[1] // 2
    steps = hidden // chunk
    count = len(pieces)
    spots = arrival_order(count)

    def kernel(places, z, near, away, cot, bias, gain, shift, slope, *refs):
        result, grad_v, grad_u, grad_pre, part, sums, sum_pre, out, laid = refs[2 * count :]
        w_in, w_out = lay_pieces(places, spots, refs[: 2 * count], laid)

        @pl.when(pl.program_id(0) == 0)
        def _():
            one, size = standard(z[...] + pair_sum(near, away) + bias[...])
            dy = cot[...]
            result[...] = (one * gain[...] + shift[...]).astype(BF)
            grad_v[...] = norm_back(dy, one, size, gain[...])
            grad_u[...] = grad_v[...].astype(BF)
            sums[0:1] = total_rows(dy * one)
            sums[1:2] = total_rows(dy)
            sums[2:3] = total_rows(grad_u[...].astype(F32))
            out[...] = jnp.zeros_like(out)

        for half in range(2):
            span = slice(half * rows // 2, (half + 1) * rows // 2)
            pre = (mul(grad_u[span], w_out) * slope[0, span]).astype(BF)
            grad_pre[span] = pre
            out[span] += mul_t(pre, w_in)
        sum_pre[...] = total_rows(grad_pre[...].astype(F32))

        @pl.when(pl.program_id(0) == steps - 1)
        def _():
            part[...] = out[...].astype(BF)

    row = whole((1, width))
    return call(
        kernel,
        steps,
        [pl.BlockSpec(memory_space=pltpu.SMEM)]
        + [whole((rows, width))] * 4
        + [row] * 3
        + [block((1, rows, chunk))]
        + [column((width // count, chunk))] * count
        + [column((width // count, chunk), steps)] * count,
        [
            whole((rows, width)),
            whole((rows, width)),
            whole((rows, width)),
            column((rows, chunk)),
            whole((rows, width)),
            whole((8, width)),
            column((1, chunk)),
        ],
        [
            shaped((rows, width), BF),
            shaped((rows, width), F32),
            shaped((rows, width), BF),
            shaped((rows, hidden), BF),
            shaped((rows, width), BF),
            shaped((8, width), F32),
            shaped((1, hidden), F32),
        ],
        scratch=[pltpu.VMEM((rows, width), F32), pltpu.VMEM((2, count, width // count, chunk), BF)],
        flops=4 * rows * hidden * width,
        moved=rows * width * 28 + rows * hidden * 6 + width * hidden * 4,
    )(places, z, near, away, cotangent, *rows_in, slope, *pieces, *pieces)


def cross_back(flag, grad_v, near, away, unit2, scale2, gain, qc, keys_values, weight, cq, items, batch, patches):
    rows, width = grad_v.shape
    cols = weight.shape[1]
    heads, each = cols // HEAD_DIM, rows // items
    padded = keys_values.shape[1]

    def kernel(flag, grad_v, near, away, unit2, scale2, gain, qc, kv, weight, cq, after, mix, grad_qc, grad_kv, out, sums, sums_c, grad_att):
        index = pl.program_id(0)

        @pl.when(index == 0)
        def _():
            dz = grad_v[...] + pair_sum(near, away)
            mine = flag[0] == 0
            used = jnp.where(mine, dz, 0.0)
            two = norm_back(used, unit2[...], scale2[...], gain[...])
            after[...] = jnp.where(mine, two, dz)
            mix[...] = two.astype(BF)
            grad_att[...] = mul(mix[...], weight[...]).astype(BF)
            sums[0:1] = total_rows(used * unit2[...])
            sums[1:2] = total_rows(used)
            sums[2:3] = total_rows(mix[...].astype(F32))
            sums_c[...] = jnp.zeros_like(sums_c)

        root = HEAD_DIM ** (-0.5)
        scaled = head_mask(each, heads, root, BF)
        plain = head_mask(each, heads, 1.0, BF)
        ones = head_mask(each, heads, 1.0, F32)
        real = lax.broadcasted_iota(jnp.int32, (heads * each, padded), 1) < patches
        for item in range(batch):
            start = pl.multiple_of((index * batch + item) * each, each)
            dq, dk, dv = attend_back(
                qc[pl.ds(start, each), :],
                kv[item, :, :cols],
                kv[item, :, cols:],
                grad_att[pl.ds(start, each), :],
                lambda s: jnp.where(real, s, NEG),
                heads,
                scaled,
                plain,
                ones,
            )
            grad_qc[pl.ds(start, each), :] = dq.astype(BF)
            dk, dv = dk.astype(BF), dv.astype(BF)
            grad_kv[item, :, :cols] = dk
            grad_kv[item, :, cols:] = dv
            sums_c[1:2] += total_rows(dk.astype(F32))
            sums_c[2:3] += total_rows(dv.astype(F32))

        @pl.when(index == pl.num_programs(0) - 1)
        def _():
            out[...] = mul_t(grad_qc[...], cq[...]).astype(BF)
            sums_c[0:1] = total_rows(grad_qc[...].astype(F32))

    return call(
        kernel,
        items // batch,
        [pl.BlockSpec(memory_space=pltpu.SMEM)]
        + [whole((rows, width))] * 4
        + [
            whole((rows, 1)),
            whole((1, width)),
            whole((rows, cols)),
            block((batch, padded, 2 * cols)),
            whole((width, cols)),
            whole((width, cols)),
        ],
        [
            whole((rows, width)),
            whole((rows, width)),
            whole((rows, cols)),
            block((batch, padded, 2 * cols)),
            whole((rows, width)),
            whole((8, width)),
            whole((8, cols)),
        ],
        [
            shaped((rows, width), F32),
            shaped((rows, width), BF),
            shaped((rows, cols), BF),
            shaped((items, padded, 2 * cols), BF),
            shaped((rows, width), BF),
            shaped((8, width), F32),
            shaped((8, cols), F32),
        ],
        scratch=[pltpu.VMEM((rows, cols), BF)],
        flops=2 * rows * cols * padded * heads * 5,
        moved=rows * width * 26 + 8 * items * padded * cols,
    )(flag, grad_v, near, away, unit2, scale2, gain, qc, keys_values, weight, cq)


def self_back(flag, head, after, near, away, unit, scale, gain, q, kv, kv_far, allowed, weight, w_qkv, own, far, attended, items, batch, shards):
    rows, width = after.shape
    cols = weight.shape[1]
    heads, each = cols // HEAD_DIM, rows // items
    piece = width // shards

    def kernel(flag, head, after, near, away, unit, scale, gain, q, kv, kv_far, allowed, weight, w_qkv, own, far, attended, grad_one, mix, grad_near, grad_away, mine, theirs, sums, sums_c, grad_keep, grad_sent, grad_att):
        index = pl.program_id(0)

        @pl.when(index == 0)
        def _():
            grad = after[...] + pair_sum(near, away)
            grad_one[...] = norm_back(grad, unit[...], scale[...], gain[...])
            mix[...] = grad_one[...].astype(BF)
            grad_att[...] = mul(mix[...], weight[...]).astype(BF)
            sums[0:1] = total_rows(grad * unit[...])
            sums[1:2] = total_rows(grad)
            sums[2:3] = total_rows(mix[...].astype(F32))

        scaled = head_mask(each, heads, HEAD_DIM ** (-0.5), BF)
        plain = head_mask(each, heads, 1.0, BF)
        ones = head_mask(each, heads, 1.0, F32)
        for item in range(batch):
            span = slice(item * each, (item + 1) * each)
            start = pl.multiple_of((index * batch + item) * each, each)
            keys = jnp.concatenate([kv[span, :cols], kv_far[span, :cols]], axis=0)
            values = jnp.concatenate([kv[span, cols:], kv_far[span, cols:]], axis=0)
            seen = jnp.concatenate([allowed[item]] * heads, axis=0) > 0
            dq, dk, dv = attend_back(
                q[span],
                keys,
                values,
                grad_att[pl.ds(start, each), :],
                lambda s: jnp.where(seen, s, NEG),
                heads,
                scaled,
                plain,
                ones,
            )
            grad_near[pl.ds(start, each), :cols] = dq.astype(BF)
            grad_near[pl.ds(start, each), cols : 2 * cols] = dk[:each].astype(BF)
            grad_near[pl.ds(start, each), 2 * cols :] = dv[:each].astype(BF)
            grad_away[pl.ds(start, each), :cols] = dk[each:].astype(BF)
            grad_away[pl.ds(start, each), cols:] = dv[each:].astype(BF)

        @pl.when(index == pl.num_programs(0) - 1)
        def _():
            side = head[0] == 0
            middle = rows // 2
            for part, source, weights in ((0, grad_near, w_qkv), (1, grad_away, w_qkv[:, cols:])):
                lanes = slice(part * width, (part + 1) * width)
                top = mul_t(source[:middle], weights[...]).astype(BF)
                low = mul_t(source[middle:], weights[...]).astype(BF)
                mine[:, lanes] = jnp.where(side, top, low)
                theirs[:, lanes] = jnp.where(side, low, top)
            for place in range(4):
                span = slice(place * cols, (place + 1) * cols)
                if place == 3:
                    total = t_mul(mix[...], attended[...])
                else:
                    total = t_mul(own[...], grad_near[:, span])
                if place in (1, 2):
                    total = total + t_mul(far[...], grad_away[:, (place - 1) * cols : place * cols])
                total = total.astype(BF)
                for side in range(2):
                    pieces = [
                        total[one * piece : (one + 1) * piece] for one in range(side, shards, 2)
                    ]

                    @pl.when(flag[0] == side)
                    def _():
                        for one, value in enumerate(pieces):
                            grad_keep[one, :, span] = value

                    @pl.when(flag[0] != side)
                    def _():
                        for one, value in enumerate(pieces):
                            grad_sent[one, :, span] = value
            sums_c[0:1] = total_rows(grad_near[...].astype(F32))
            sums_c[1:2, cols:] = total_rows(grad_away[...].astype(F32))

    part = batch * each
    return call(
        kernel,
        items // batch,
        [pl.BlockSpec(memory_space=pltpu.SMEM)] * 2
        + [whole((rows, width))] * 4
        + [
            whole((rows, 1)),
            whole((1, width)),
            block((part, cols)),
            block((part, 2 * cols)),
            block((part, 2 * cols)),
            block((batch, each, 2 * each)),
            whole((width, cols)),
            whole((width, 3 * cols)),
            whole((rows, width)),
            whole((rows, width)),
            whole((rows, cols)),
        ],
        [
            whole((rows, width)),
            whole((rows, width)),
            whole((rows, 3 * cols)),
            whole((rows, 2 * cols)),
            whole((rows // 2, 2 * width)),
            whole((rows // 2, 2 * width)),
            whole((8, width)),
            whole((8, 3 * cols)),
            whole((shards // 2, piece, 4 * cols)),
            whole((shards // 2, piece, 4 * cols)),
        ],
        [
            shaped((rows, width), F32),
            shaped((rows, width), BF),
            shaped((rows, 3 * cols), BF),
            shaped((rows, 2 * cols), BF),
            shaped((rows // 2, 2 * width), BF),
            shaped((rows // 2, 2 * width), BF),
            shaped((8, width), F32),
            shaped((8, 3 * cols), F32),
            shaped((shards // 2, piece, 4 * cols), BF),
            shaped((shards // 2, piece, 4 * cols), BF),
        ],
        scratch=[pltpu.VMEM((rows, cols), BF)],
        flops=2 * rows * cols * width * 9,
        moved=rows * width * 32 + rows * cols * 20,
    )(flag, head, after, near, away, unit, scale, gain, q, kv, kv_far, allowed, weight, w_qkv, own, far, attended)


def pack_small(flag, one, two, three, own, cross, pre, kv_grad, kv_all, gain, shift):
    width = one.shape[1]
    cols = cross.shape[1]
    feat_width = kv_all.shape[0]
    pres = pre.shape[1] // width
    folds = (feat_width + width - 1) // width
    rows = (14 + 2 * pres + 2 * folds + 7) // 8 * 8

    def exact(left, right):
        return lax.dot_general(
            left,
            right,
            (((1,), (1,)), ((), ())),
            precision=lax.Precision.HIGHEST,
            preferred_element_type=F32,
        )

    def kernel(flag, one, two, three, own, cross, pre, kv_grad, kv_all, gain, shift, out, line):
        on_text = flag[0].astype(F32)
        on_query = 1.0 - on_text
        out[...] = jnp.zeros_like(out)
        for place in range(3):
            at_row = slice(place, place + 1)
            out[4 * place : 4 * place + 1] = one[at_row]
            out[4 * place + 1 : 4 * place + 2] = two[at_row]
            out[4 * place + 2 : 4 * place + 3] = on_query * three[at_row]
            out[4 * place + 3 : 4 * place + 4] = on_text * three[at_row]
        out[12:13, :cols] = own[0:1, :cols]
        out[12:13, cols:] = own[0:1, 2 * cols :] + own[1:2, 2 * cols :]
        out[13:14, :cols] = cross[0:1]
        out[13:14, cols:] = cross[2:3]
        for k in range(pres):
            part = pre[:, k * width : (k + 1) * width]
            out[14 + k : 15 + k] = on_query * part
            out[14 + pres + k : 15 + pres + k] = on_text * part
        column_sums = jnp.concatenate([cross[1:2], cross[2:3]], axis=1)
        column_sums = jnp.broadcast_to(column_sums, (8, width))
        ones = jnp.ones((8, width), F32)

        def chunk(k, carry):
            span = pl.ds(pl.multiple_of(k * 128, 128), 128)
            weight = kv_all[span, :].astype(F32)
            d_shift = exact(column_sums, weight)[0:1]
            dot = exact(ones, kv_grad[span, :] * weight)[0:1]
            line[0:1, span] = (dot - shift[:, span] * d_shift) / gain[:, span]
            line[1:2, span] = d_shift
            return carry

        lax.fori_loop(0, feat_width // 128, chunk, 0)
        start = 14 + 2 * pres
        for part in range(2):
            for k in range(folds):
                end = min(feat_width, (k + 1) * width)
                spot = start + part * folds + k
                out[spot : spot + 1, : end - k * width] = line[part : part + 1, k * width : end]

    arrays = (one, two, three, own, cross, pre, kv_grad, kv_all, gain, shift)
    return call(
        kernel,
        1,
        [pl.BlockSpec(memory_space=pltpu.SMEM)] + [whole(array.shape) for array in arrays],
        whole((rows, width)),
        shaped((rows, width), F32),
        scratch=[pltpu.VMEM((8, feat_width), F32)],
        moved=6 * feat_width * width,
    )(flag, *arrays)


def unpack_small(head, packed, other, pres, feat_width):
    width = packed.shape[1]
    half = width // 2
    folds = (feat_width + width - 1) // width

    def kernel(head, packed, other, own_bias, cross_bias, gains, shifts, d_gain, d_shift, pre, post):
        first = head[0] == 0
        near, away = packed[12:], other[...]
        low = jnp.where(first, near, away)
        high = jnp.where(first, away, near)
        for place, out in enumerate((own_bias, cross_bias)):
            for part in range(2):
                span = slice(part * half, (part + 1) * half)
                out[part : part + 1, :half] = low[place : place + 1, span]
                out[part : part + 1, half:] = high[place : place + 1, span]
        own_bias[2:3] = packed[8:9]
        cross_bias[2:3] = packed[9:10]
        gains[...] = packed[0:4]
        shifts[...] = packed[4:8]
        post[...] = packed[10:12]
        for side in range(2):
            for k in range(pres):
                line = slice(2 + side * pres + k, 3 + side * pres + k)
                pre[side : side + 1, k * width : (k + 1) * width] = low[line]
                pre[side : side + 1, (pres + k) * width : (pres + k + 1) * width] = high[line]
        both = near + away
        for place, out in enumerate((d_gain, d_shift)):
            for k in range(folds):
                end = min(feat_width, (k + 1) * width)
                line = 2 + 2 * pres + place * folds + k
                for begin in range(k * width, end, 128):
                    spot, left = begin // 128, begin - k * width
                    out[spot : spot + 1] = both[line : line + 1, left : left + 128]

    shapes = [(3, width)] * 2 + [(4, width)] * 2 + [(feat_width // 128, 128)] * 2
    shapes = shapes + [(2, 2 * pres * width), (2, width)]
    return call(
        kernel,
        1,
        [pl.BlockSpec(memory_space=pltpu.SMEM), whole(packed.shape), whole(other.shape)],
        [whole(shape) for shape in shapes],
        [shaped(shape, F32) for shape in shapes],
        moved=200000,
    )(head, packed, other)


def visible(stream, segments, modes):
    same_caption = segments[:, :, None] == segments[:, None, :]
    own = jnp.logical_or(stream == 0, same_caption)
    far = jnp.where(stream == 0, modes == 2, modes >= 1)[:, None, None]
    return jnp.concatenate([own, jnp.broadcast_to(far, own.shape)], axis=2).astype(F32)


def body(
    hidden,
    features,
    segments,
    modes,
    w_qkv,
    self_bias,
    self_out,
    cross_q,
    cross_kv,
    cross_bias,
    cross_out,
    gains,
    shifts,
    feat_gain,
    feat_shift,
    ffn_in,
    ffn_bias_in,
    ffn_out,
    ffn_bias_out,
    cotangent,
):
    stream = lax.axis_index("stream")
    stream_u = stream.astype(jnp.uint32)
    head_index = lax.axis_index("heads")
    items, _, each, width = hidden.shape
    rows = items * each
    half = rows // 2
    cols = w_qkv.shape[2]
    hidden_cols = ffn_in.shape[2]
    patches, feat_width = features.shape[1:]
    padded = (patches + 7) // 8 * 8
    col_start = head_index.astype(jnp.uint32) * cols
    hidden_start = head_index.astype(jnp.uint32) * hidden_cols
    flag = stream.astype(jnp.int32).reshape(1)
    shards = 2 * lax.axis_size("items")
    three = [slice(i * cols, (i + 1) * cols) for i in range(3)]

    ffn_part = jnp.concatenate([ffn_in[0], ffn_out[0].T], axis=1)
    part_qkv = jnp.concatenate([w_qkv[0], w_qkv[1], w_qkv[2]], axis=0)
    pair_qkv = by_stream(part_qkv, partner(part_qkv, "stream", 0), 0)
    places = ring_places()
    spots = ring_row()
    own = hidden.reshape(rows, width)
    heads_u = head_index.astype(jnp.uint32)
    my_half = lax.dynamic_slice_in_dim(own, heads_u * half, half, 0)
    far_half = partner(my_half, "stream", 0)
    piece, kv_piece = cross_q.shape[0], cross_kv.shape[1]
    rest = jnp.concatenate([self_out.T, cross_q, cross_out.T, cross_kv[0], cross_kv[1]], axis=0)

    def row(vector):
        return vector.reshape(1, -1)

    features, pair_qkv = joined(features, pair_qkv)
    ring = Gather(jnp.concatenate([pair_qkv.reshape(6 * piece, cols), rest], axis=0))

    def crossing(one):
        return one[6 * piece :], over("stream")

    kept, chunk = [], items // 4
    crossed = []
    begin = 0
    for number in range(max(4, shards // 4)):
        if ring.left:
            riders = [crossing(one) for one in ring.pieces[begin:]]
            if number == 1:
                riders.append((far_half, over("heads")))
            last_step = ring.hop == shards // 4
            if last_step:
                ffn_part, held = joined(ffn_part, ring.up)
                ring.replace(held, ring.down)
                ffn_gather = Gather(ffn_part)
            fresh = len(ring.pieces) - begin
            begin = len(ring.pieces)
            ridden = gather_step([ring], *riders)
            crossed += ridden[:fresh]
            if number == 1:
                far_other = ridden[-1]
            if last_step:
                gather_step([ffn_gather])
        if number < 4:
            *kept, token = list(
                feature_norm(
                    features, row(feat_gain), row(feat_shift), padded, number * chunk, chunk, kept
                )
            )
            up, down, token = joined(ring.up, ring.down, token)
            ring.replace(up, down)
            kept = [kept[0], token]
    feat_norm = kept[0]
    crossed += [move(one) for one, move in (crossing(one) for one in ring.pieces[begin:])]
    far = jnp.where(
        head_index == 0,
        jnp.concatenate([far_half, far_other], axis=0),
        jnp.concatenate([far_other, far_half], axis=0),
    )
    def ffn_step(value, last=False):
        if ffn_gather.hop - 1 > ffn_gather.count // 2:
            return value
        value, up, down = joined(value, ffn_gather.up, ffn_gather.down)
        ffn_gather.replace(up, down)
        while ffn_gather.left:
            gather_step([ffn_gather])
            if not last:
                break
        return value

    def my_cols(vector):
        return lax.dynamic_slice_in_dim(vector, col_start, cols, 0)

    none = jnp.zeros((cols,), F32)
    bias_qkv = row(jnp.concatenate([my_cols(self_bias[0]), none, my_cols(self_bias[1])]))
    bias_kv = row(jnp.concatenate([none, my_cols(cross_bias[1])]))
    gain_ffn = row(lax.dynamic_index_in_dim(gains, 2 + stream_u, 0, keepdims=False))
    shift_ffn = row(lax.dynamic_index_in_dim(shifts, 2 + stream_u, 0, keepdims=False))
    bias_in = row(
        lax.dynamic_slice_in_dim(
            lax.dynamic_index_in_dim(ffn_bias_in, stream_u, 0, keepdims=False),
            hidden_start,
            hidden_cols,
            0,
        )
    )
    bias_out = row(lax.dynamic_index_in_dim(ffn_bias_out, stream_u, 0, keepdims=False))

    def swap(part):
        return partner(part, "heads", 0)

    q, kv, kv_far, qkv_all = project(spots, own, far, ring.pieces, bias_qkv, piece)
    ends = joined(ffn_gather.up, ffn_gather.down, ring.up, kv_far, feat_norm, *crossed[-3:])
    ffn_gather.replace(*ends[:2])
    ring.replace(ends[2], ends[2])
    kv_far = ends[3]
    feat_rows = ends[4].reshape(items * padded, feat_width)
    crossed[-3:] = ends[5:]
    gather_step([ffn_gather])
    self_out_t, cross_q_all, cross_out_t, kv_all = assemble(
        flag, spots, ring.pieces, crossed, piece, kv_piece
    )

    allowed = visible(stream, segments, modes)
    attended, part = self_attention(q, kv, kv_far, allowed, self_out_t, items, 4)
    kv_all = ffn_step(kv_all)
    away_one = swap(part)
    keys_values = (mul(feat_rows, kv_all) + bias_kv).astype(BF).reshape(items, padded, 2 * cols)
    keys_values = ffn_step(keys_values)
    unit_one, scale_one, after_low, qc, attended_c, part_c = cross_attention(
        own,
        part,
        away_one,
        (row(self_bias[2]), row(gains[0]), row(shifts[0]), row(my_cols(cross_bias[0]))),
        cross_q_all,
        keys_values,
        cross_out_t,
        items,
        2,
        patches,
    )
    unit_one, part_c, scale_one, after_low, qc, attended_c = ffn_step(
        (unit_one, part_c, scale_one, after_low, qc, attended_c), True
    )
    ffn_pieces = ffn_gather.pieces
    z, z_low, unit_two, scale_two, activated, slope, part_f = feed_forward(
        flag,
        spots,
        unit_one,
        part_c,
        swap(part_c),
        (row(gains[0]), row(shifts[0]), row(cross_bias[2]), row(gains[1]), row(shifts[1])),
        ffn_pieces,
        bias_in,
        256,
    )

    output, grad_three, grad_u, grad_pre, part_z, sums_three, sum_pre = feed_back(
        spots,
        z,
        part_f,
        swap(part_f),
        cotangent.reshape(rows, width),
        (bias_out, gain_ffn, shift_ffn),
        slope,
        ffn_pieces,
        256,
    )
    away_z = swap(part_z)
    in_grad = t_mul(z_low, grad_pre).astype(BF)
    out_grad = t_mul(grad_u, activated).astype(BF)
    count = shards // 2
    grad_after, mix_c, grad_qc, grad_kv, part_a, sums_two, sums_cross = cross_back(
        flag,
        grad_three,
        part_z,
        away_z,
        unit_two,
        scale_two,
        row(gains[1]),
        qc,
        keys_values,
        cross_out_t,
        cross_q_all,
        items,
        2,
        patches,
    )
    in_grad, out_grad, sums_two = joined(in_grad, out_grad, sums_two)
    ffn_ring = Scatter(
        [
            [at(in_grad.reshape(count, -1, hidden_cols))],
            [at(out_grad.reshape(count, -1, hidden_cols))],
        ],
        1,
        places,
    )
    ffn_ring.step()
    away_a = swap(part_a)
    keep_q, away_q = halves(t_mul(after_low, grad_qc).astype(BF))
    keep_o, away_o = halves(t_mul(mix_c, attended_c).astype(BF))
    away_c = jnp.concatenate([away_q, away_o], axis=2)
    grad_kv, away_c = joined(grad_kv, away_c)
    kv_grad = t_mul(feat_rows, grad_kv.reshape(items * padded, 2 * cols))
    kv_grad_low = kv_grad.astype(BF)
    arrived_c = partner(away_c, "stream", 0)
    kv_grad, kv_grad_low, arrived_c, ffn_ring.up = joined(
        kv_grad, kv_grad_low, arrived_c, ffn_ring.up
    )
    keep_kv, away_kv = halves(kv_grad_low)
    ffn_ring.step()
    away_a, away_kv = joined(away_a, away_kv)
    arrived_kv = partner(away_kv, "stream", 0)
    grad_one, mix, grad_near, grad_away, mine, theirs, sums_one, sums_self, keep_self, away_self = self_back(
        flag,
        head_index.astype(jnp.int32).reshape(1),
        grad_after,
        part_a,
        away_a,
        unit_one,
        scale_one,
        row(gains[0]),
        q,
        kv,
        kv_far,
        allowed,
        self_out_t,
        qkv_all,
        own,
        far,
        attended,
        items,
        4,
        shards,
    )

    results = (grad_one, mine, theirs, sums_one, sums_self, keep_self, away_self, arrived_kv)
    results = lax.optimization_barrier(results + (ffn_ring.up, ffn_ring.down))
    grad_one, mine, theirs, sums_one, sums_self, keep_self, away_self, arrived_kv = results[:-2]
    ffn_ring.up, ffn_ring.down = results[-2:]


    def ring_steps(rings, *riders):
        ridden = [move(value) for value, move in riders]
        sends = [ring.sends() for ring in rings]
        flat = [one for part in sends for one in part]
        arrivals = lax.optimization_barrier(tuple(ridden) + tuple(together(flat)))
        rest = arrivals[len(riders) :]
        for ring, part in zip(rings, sends):
            ring.take(rest[: len(part)])
            rest = rest[len(part) :]
        return arrivals[: len(riders)]

    rest_ring = Scatter(
        [
            [at_stream(keep_q), at(arrived_c, three[0])],
            [at_stream(keep_o), at(arrived_c, three[1])],
            [at_stream(keep_kv, three[0]), at(arrived_kv, three[0])],
            [at_stream(keep_kv, three[1]), at(arrived_kv, three[1])],
        ],
        0,
        places,
    )
    arrived_self, from_swap = partner(away_self, "stream", 0), swap(theirs)
    ffn_ring.step()
    ring_steps([rest_ring])
    while ffn_ring.hop:
        ffn_ring.step()
    ends = joined(arrived_self, ffn_ring.up, ffn_ring.down, rest_ring.up)
    arrived_self, ffn_ring.up, ffn_ring.down, rest_ring.up = ends
    self_ring = Scatter([[at(keep_self), at(arrived_self)]], 0, places)
    total = mine.astype(F32) + from_swap.astype(F32)
    from_far = partner(total[:, width:].astype(BF), "stream", 0)
    packed = pack_small(
        flag,
        sums_one,
        sums_two,
        sums_three,
        sums_self,
        sums_cross,
        sum_pre,
        kv_grad,
        kv_all,
        row(feat_gain),
        row(feat_shift),
    )
    packed = packed + partner(packed, "items", 0)
    moves = [over("stream")] + [over("items", bit) for bit in range(1, (count - 1).bit_length())]

    in_half = (
        lax.dynamic_slice_in_dim(grad_one, heads_u * half, half, 0)
        + total[:, :width]
        + from_far.astype(F32)
    )
    (arrived,) = ring_steps(
        [one for one in (rest_ring, self_ring) if one.hop], (packed, moves.pop(0))
    )
    packed = packed + arrived
    in_other = swap(in_half)
    while self_ring.hop or ffn_ring.hop or rest_ring.hop:
        rings = [one for one in (ffn_ring, rest_ring, self_ring) if one.hop]
        riders = [(packed, moves.pop(0))] if moves else []
        for arrived in ring_steps(rings, *riders):
            packed = packed + arrived
    while moves:
        packed = packed + moves.pop(0)(packed)
    grad_input = jnp.where(
        head_index == 0,
        jnp.concatenate([in_half, in_other], axis=0),
        jnp.concatenate([in_other, in_half], axis=0),
    )
    ffn_red, rest_red, self_red = ffn_ring.result(), rest_ring.result(), self_ring.result()
    small = unpack_small(
        head_index.astype(jnp.int32).reshape(1),
        packed,
        swap(packed[12:]),
        hidden_cols // width,
        feat_width,
    )
    return (
        output.reshape(items, 1, each, width),
        grad_input.reshape(items, 1, each, width),
        jnp.stack([self_red[:, one] for one in three]),
        small[0],
        self_red[:, 3 * cols :].T,
        rest_red[:piece],
        rest_red[2 * piece :].reshape(2, kv_piece, cols),
        small[1],
        rest_red[piece : 2 * piece].T,
        small[2],
        small[3],
        small[4].reshape(feat_width),
        small[5].reshape(feat_width),
        ffn_red[:, :hidden_cols][None],
        small[6],
        ffn_red[:, hidden_cols:].T[None],
        small[7],
    )


def solution(mesh):
    placed = (
        P("items", "stream", None, None),
        P("items", None, None),
        P("items", None),
        P("items"),
        P(None, ("items", "stream"), "heads"),
        P(),
        P("heads", ("items", "stream")),
        P(("items", "stream"), "heads"),
        P(None, ("items", "stream"), "heads"),
        P(),
        P("heads", ("items", "stream")),
        P(),
        P(),
        P(),
        P(),
        P("stream", "items", "heads"),
        P(),
        P("stream", "heads", "items"),
        P(),
        P("items", "stream", None, None),
    )
    return jax.shard_map(
        body,
        mesh=mesh,
        in_specs=placed,
        out_specs=(
            P("items", "stream", None, None),
            P("items", "stream", None, None),
            P(None, ("items", "stream"), "heads"),
            P(),
            P("heads", ("items", "stream")),
            P(("items", "stream"), "heads"),
            P(None, ("items", "stream"), "heads"),
            P(),
            P("heads", ("items", "stream")),
            P(),
            P(),
            P(),
            P(),
            P("stream", "items", "heads"),
            P(),
            P("stream", "heads", "items"),
            P(),
        ),
        check_vma=False,
    )
```

```python
import math

import jax
import jax.numpy as jnp
import numpy as np
from jax import lax
from jax.experimental import pallas as pl
from jax.experimental.pallas import tpu as pltpu
from jax.sharding import PartitionSpec as P

HEAD_DIM = 64
EPS = 1e-06
NEG = -1e30
BF = jnp.bfloat16
F32 = jnp.float32


def partner(shard, axis, distance):
    return lax.ppermute(shard, axis, [(i, i ^ 1 << distance) for i in range(lax.axis_size(axis))])


def joined(*values):
    return lax.optimization_barrier(values)


def ring_of(count):
    return list(range(0, count, 2)) + list(range(1, count, 2))[::-1]


def ring_table():
    count = lax.axis_size("items")
    order = ring_of(count)
    table = np.zeros((count, count), np.uint32)
    for place, index in enumerate(order):
        table[index] = [order[(place + far) % count] for far in range(count)]
    return table


def ring_row():
    row = lax.axis_index("items").astype(jnp.uint32)
    table = jnp.asarray(ring_table().astype(np.int32))
    found = lax.dynamic_slice(table, (row, jnp.uint32(0)), (1, table.shape[1]))
    return found.reshape(table.shape[1])


def ring_places():
    table = ring_table()
    count = table.shape[0]
    bits = max(1, (count - 1).bit_length())
    per_word = 32 // bits
    index = lax.axis_index("items").astype(jnp.uint32)
    places = []
    for begin in range(0, count, per_word):
        part = table[:, begin : begin + per_word]
        words = [sum(int(one) << (bits * k) for k, one in enumerate(line)) for line in part]
        word = jnp.uint32(words[0])
        for item in range(1, count):
            word = jnp.where(index == jnp.uint32(item), jnp.uint32(words[item]), word)
        for k in range(part.shape[1]):
            places.append((word >> jnp.uint32(bits * k)) & jnp.uint32((1 << bits) - 1))
    return places


def arrival_order(count):
    order = [0]
    for hop in range(1, count // 2 + 1):
        order.append(count - hop)
        if hop <= (count - 1) // 2:
            order.append(hop)
    return order


def shift_ring(shard, order, step):
    count = len(order)
    return lax.ppermute(
        shard, "items", [(order[i], order[(i + step) % count]) for i in range(count)]
    )


def together(sends):
    values = lax.optimization_barrier(tuple(value for value, _ in sends))
    return lax.optimization_barrier(tuple(move(one) for one, (_, move) in zip(values, sends)))


class Gather:
    def __init__(self, shard):
        self.count = lax.axis_size("items")
        self.order = ring_of(self.count)
        self.up = self.down = shard
        self.pieces = [shard]
        self.hop = 1

    def sends(self):
        result = [(self.up, lambda one: shift_ring(one, self.order, 1))]
        if self.hop <= (self.count - 1) // 2:
            result.append((self.down, lambda one: shift_ring(one, self.order, -1)))
        return result

    def take(self, arrivals):
        self.pieces += arrivals
        self.up = arrivals[0]
        self.down = arrivals[-1]
        self.hop += 1

    def replace(self, up, down):
        self.pieces[-1] = down
        if self.hop - 1 <= (self.count - 1) // 2:
            self.pieces[-2] = up
        self.up, self.down = up, down

    @property
    def left(self):
        return self.hop <= self.count // 2


def gather_step(rings, *riders):
    sends = [ring.sends() for ring in rings]
    arrivals = together(list(riders) + [one for part in sends for one in part])
    ridden, arrivals = arrivals[: len(riders)], arrivals[len(riders) :]
    for ring, part in zip(rings, sends):
        ring.take(list(arrivals[: len(part)]))
        arrivals = arrivals[len(part) :]
    return ridden


def place_items(pieces, places):
    whole = jnp.zeros((len(pieces),) + pieces[0].shape, pieces[0].dtype)
    for far, piece in zip(arrival_order(len(pieces)), pieces):
        whole = lax.dynamic_update_index_in_dim(whole, piece, places[far], 0)
    return whole


def by_stream(own, other, axis):
    first = lax.axis_index("stream") == 0
    return jnp.where(
        first, jnp.stack([own, other], axis=axis), jnp.stack([other, own], axis=axis)
    )


def whole_rows(own, other):
    both = by_stream(own, other, 1)
    return both.reshape((both.shape[0] * both.shape[1] * both.shape[2], both.shape[3]))


def at(pieces, span=slice(None)):
    return lambda which: lax.dynamic_index_in_dim(pieces, which, 0, keepdims=False)[:, span]


def at_stream(pieces, span=slice(None)):
    stream = lax.axis_index("stream").astype(jnp.uint32)
    zero = jnp.uint32(0)

    def read(which):
        start = (which, stream, zero, zero)
        found = lax.dynamic_slice(pieces, start, (1, 1) + pieces.shape[2:])
        return found.reshape(pieces.shape[2:])[:, span]

    return read


class Scatter:
    def __init__(self, groups, axis, places):
        self.groups, self.axis = groups, axis
        self.count = lax.axis_size("items")
        self.order, self.places = ring_of(self.count), places
        self.hop = self.count // 2
        self.up = self.down = None

    def piece(self, distance):
        which = self.places[distance % self.count]
        parts = [sum(read(which).astype(F32) for read in group) for group in self.groups]
        return jnp.concatenate(parts, axis=self.axis)

    def sends(self):
        own = self.piece(self.hop)
        own = own if self.up is None else own + self.up.astype(F32)
        result = [(own.astype(BF), lambda one: shift_ring(one, self.order, 1))]
        if self.hop <= (self.count - 1) // 2:
            own = self.piece(self.count - self.hop)
            own = own if self.down is None else own + self.down.astype(F32)
            result.append((own.astype(BF), lambda one: shift_ring(one, self.order, -1)))
        return result

    def take(self, arrivals):
        self.up = arrivals[0]
        if len(arrivals) > 1:
            self.down = arrivals[1]
        self.hop -= 1
        return arrivals[0]

    def step(self):
        return self.take(together(self.sends()))

    def result(self):
        return self.piece(0) + self.up.astype(F32) + self.down.astype(F32)


def halves(total):
    count = lax.axis_size("items")
    rows = total.shape[0] // (2 * count)
    parts = total.reshape((count, 2, rows, total.shape[1]))
    stream = lax.axis_index("stream").astype(jnp.uint32)
    away = lax.dynamic_index_in_dim(parts, 1 - stream, 1, keepdims=False)
    return parts, away


def over(axis, distance=0):
    return lambda one: partner(one, axis, distance)


def mul(left, right):
    return jnp.dot(left, right, preferred_element_type=F32)


def mul_t(left, right):
    return lax.dot_general(left, right, (((1,), (1,)), ((), ())), preferred_element_type=F32)


def t_mul(left, right):
    return lax.dot_general(left, right, (((0,), (0,)), ((), ())), preferred_element_type=F32)


def standard(rows):
    center = rows - jnp.mean(rows, axis=-1, keepdims=True)
    scale = lax.rsqrt(jnp.mean(center * center, axis=-1, keepdims=True) + EPS)
    return center * scale, scale


def norm_back(grad, unit, scale, gain):
    inner = grad * gain
    return scale * (
        inner
        - jnp.mean(inner, axis=-1, keepdims=True)
        - unit * jnp.mean(inner * unit, axis=-1, keepdims=True)
    )


def pair_sum(near, away):
    return near[...].astype(F32) + away[...].astype(F32)


def total_rows(rows):
    return jnp.sum(rows, axis=0, keepdims=True)


def head_mask(rows, heads, value, dtype):
    row = lax.broadcasted_iota(jnp.int32, (heads * rows, heads * HEAD_DIM), 0) // rows
    col = lax.broadcasted_iota(jnp.int32, (heads * rows, heads * HEAD_DIM), 1) // HEAD_DIM
    return jnp.where(row == col, value, 0.0).astype(dtype)


def stack_heads(rows, heads, mask):
    return jnp.concatenate([rows] * heads, axis=0) * mask


def fold_heads(stacked, heads, mask):
    rows = stacked.shape[0] // heads
    stacked = stacked * mask
    result = stacked[:rows]
    for head in range(1, heads):
        result = result + stacked[head * rows : (head + 1) * rows]
    return result


def softmax(scores):
    power = jnp.exp(scores - jnp.max(scores, axis=-1, keepdims=True))
    return power * (1.0 / jnp.sum(power, axis=-1, keepdims=True))


def attend(queries, keys, values, hide, heads, scaled_mask, out_mask):
    scores = hide(mul_t(stack_heads(queries, heads, scaled_mask), keys))
    weights = softmax(scores).astype(BF)
    return fold_heads(mul(weights, values), heads, out_mask).astype(BF)


def attend_back(queries, keys, values, grad, hide, heads, scaled_mask, plain_mask, out_mask):
    queries = stack_heads(queries, heads, scaled_mask)
    grad = stack_heads(grad, heads, plain_mask)
    weights = softmax(hide(mul_t(queries, keys)))
    grad_weights = mul_t(grad, values)
    grad_values = t_mul(weights.astype(BF), grad)
    delta = jnp.sum(grad_weights * weights, axis=-1, keepdims=True)
    grad_scores = (weights * (grad_weights - delta)).astype(BF)
    grad_queries = fold_heads(mul(grad_scores, keys), heads, out_mask) * HEAD_DIM ** (-0.5)
    return grad_queries, t_mul(grad_scores, queries), grad_values


def whole(shape):
    return pl.BlockSpec(shape, lambda i: (0,) * len(shape))


def block(shape):
    return pl.BlockSpec(shape, lambda i: (i,) + (0,) * (len(shape) - 1))


def column(shape, first=0):
    return pl.BlockSpec(shape, lambda i: (0, i + first))


def shaped(shape, dtype):
    return jax.ShapeDtypeStruct(shape, dtype)


def call(kernel, grid, in_specs, out_specs, out_shape, scratch=(), flops=0, moved=0):
    return pl.pallas_call(
        kernel,
        grid=(grid,),
        in_specs=in_specs,
        out_specs=out_specs,
        out_shape=out_shape,
        scratch_shapes=list(scratch),
        compiler_params=pltpu.CompilerParams(
            dimension_semantics=("arbitrary",), vmem_limit_bytes=28 << 20
        ),
        cost_estimate=pl.CostEstimate(flops=flops, bytes_accessed=moved, transcendentals=0),
    )


def feature_norm(features, gain, shift, padded, begin, each, prior):
    items, patches, width = features.shape

    def kernel(feat, gain, shift, *refs):
        out, token = refs[-2:]
        unit, _ = standard(feat[0].astype(F32))
        out[0, :patches] = (unit * gain[...] + shift[...]).astype(BF)
        out[0, patches:] = jnp.zeros((padded - patches, width), BF)
        token[...] = jnp.zeros_like(token)

    def at_item(i):
        return (i + begin, 0, 0)

    return pl.pallas_call(
        kernel,
        grid=(each,),
        in_specs=[pl.BlockSpec((1, patches, width), at_item), whole((1, width)), whole((1, width))]
        + [pl.BlockSpec(memory_space=pl.ANY)] * len(prior),
        out_specs=[pl.BlockSpec((1, padded, width), at_item), whole((8, 128))],
        out_shape=[shaped((items, padded, width), BF), shaped((8, 128), F32)],
        input_output_aliases={3: 0} if prior else {},
        compiler_params=pltpu.CompilerParams(
            dimension_semantics=("arbitrary",), vmem_limit_bytes=28 << 20
        ),
        cost_estimate=pl.CostEstimate(
            flops=0, bytes_accessed=4 * each * patches * width, transcendentals=0
        ),
    )(features, gain, shift, *prior)


def project(places, own, far, pieces, bias, each):
    rows, width = own.shape
    count = len(pieces)
    head_cols = pieces[0].shape[1]
    cols = 3 * head_cols
    step = rows // 4
    spots = arrival_order(count)

    def kernel(places, own, far, bias, *refs):
        q, kv, kv_far, weight, laid = refs[count:]

        @pl.when(pl.program_id(0) == 0)
        def _():
            for far_off, one in zip(spots, refs[:count]):
                piece = one[...]
                for side in range(2):
                    for k in range(3):
                        start = (3 * side + k) * each
                        lanes = slice(k * head_cols, (k + 1) * head_cols)
                        laid[places[far_off], side, :, lanes] = piece[start : start + each]
            weight[...] = laid[...].reshape(width, cols)

        near = mul(own[...], weight[...]) + bias[...]
        q[...] = near[:, :head_cols].astype(BF)
        kv[...] = near[:, head_cols:].astype(BF)
        kv_far[...] = (mul(far[...], weight[:, head_cols:]) + bias[:, head_cols:]).astype(BF)

    return call(
        kernel,
        4,
        [pl.BlockSpec(memory_space=pltpu.SMEM)]
        + [block((step, width)), block((step, width)), whole((1, cols))]
        + [whole((6 * each, head_cols))] * count,
        [block((step, head_cols)), block((step, 2 * head_cols)), block((step, 2 * head_cols))]
        + [whole((width, cols))],
        [shaped((rows, head_cols), BF)]
        + [shaped((rows, 2 * head_cols), BF)] * 2
        + [shaped((width, cols), BF)],
        scratch=[pltpu.VMEM((count, 2, each, cols), BF)],
        flops=10 * rows * width * head_cols,
        moved=4 * rows * width + 4 * width * cols,
    )(places, own, far, bias, *pieces)


def assemble(flag, places, pieces, crossed, each, kv_each):
    count = len(pieces)
    cols = pieces[0].shape[1]
    spots = arrival_order(count)
    rows = crossed[0].shape[0]

    def kernel(flag, places, *refs):
        self_out, cross_q, cross_out, kv = refs[2 * count :]
        for number, far_off in enumerate(spots):
            place = places[far_off]
            for side, piece in (
                (flag[0], refs[number][6 * each :]),
                (1 - flag[0], refs[count + number][...]),
            ):
                for k, out in enumerate((self_out, cross_q, cross_out)):
                    out[place, side] = piece[k * each : (k + 1) * each]
                start = 3 * each
                kv[place, side, :, :cols] = piece[start : start + kv_each]
                kv[place, side, :, cols:] = piece[start + kv_each :]

    shapes = [(count, 2, each, cols)] * 3 + [(count, 2, kv_each, 2 * cols)]
    results = call(
        kernel,
        1,
        [pl.BlockSpec(memory_space=pltpu.SMEM)] * 2
        + [whole(pieces[0].shape)] * count
        + [whole((rows, cols))] * count,
        [whole(shape) for shape in shapes],
        [shaped(shape, BF) for shape in shapes],
        moved=8 * count * rows * cols,
    )(flag, places, *pieces, *crossed)
    return [one.reshape(2 * count * one.shape[2], one.shape[3]) for one in results]


def self_attention(q, kv, kv_far, allowed, weight, items, batch):
    rows, cols = q.shape
    heads, each = cols // HEAD_DIM, rows // items
    width = weight.shape[0]

    def kernel(q, kv, kv_far, allowed, weight, attended, out):
        index = pl.program_id(0)
        scaled = head_mask(each, heads, HEAD_DIM ** (-0.5), BF)
        ones = head_mask(each, heads, 1.0, F32)
        for item in range(batch):
            span = slice(item * each, (item + 1) * each)
            keys = jnp.concatenate([kv[span, :cols], kv_far[span, :cols]], axis=0)
            values = jnp.concatenate([kv[span, cols:], kv_far[span, cols:]], axis=0)
            seen = jnp.concatenate([allowed[item]] * heads, axis=0) > 0
            result = attend(
                q[span], keys, values, lambda s: jnp.where(seen, s, NEG), heads, scaled, ones
            )
            start = pl.multiple_of((index * batch + item) * each, each)
            attended[pl.ds(start, each), :] = result

        @pl.when(index == pl.num_programs(0) - 1)
        def _():
            out[...] = mul_t(attended[...], weight[...]).astype(BF)

    part = batch * each
    return call(
        kernel,
        items // batch,
        [
            block((part, cols)),
            block((part, 2 * cols)),
            block((part, 2 * cols)),
            block((batch, each, 2 * each)),
            whole((width, cols)),
        ],
        [whole((rows, cols)), whole((rows, width))],
        [shaped((rows, cols), BF), shaped((rows, width), BF)],
        flops=2 * rows * cols * width * 3,
        moved=rows * cols * 14 + rows * width * 4,
    )(q, kv, kv_far, allowed, weight)


def cross_attention(own, near, away, rows_in, cq, keys_values, weight, items, batch, patches):
    rows, width = own.shape
    cols = weight.shape[1]
    heads, each = cols // HEAD_DIM, rows // items
    padded = keys_values.shape[1]

    def kernel(own, near, away, bias, gain, shift, bias_q, cq, kv, weight, unit, scale, low, qc, attended, out):
        index = pl.program_id(0)

        @pl.when(index == 0)
        def _():
            one, size = standard(own[...].astype(F32) + pair_sum(near, away) + bias[...])
            unit[...] = one
            scale[...] = size
            low[...] = (one * gain[...] + shift[...]).astype(BF)
            qc[...] = (mul(low[...], cq[...]) + bias_q[...]).astype(BF)

        scaled = head_mask(each, heads, HEAD_DIM ** (-0.5), BF)
        ones = head_mask(each, heads, 1.0, F32)
        real = lax.broadcasted_iota(jnp.int32, (heads * each, padded), 1) < patches
        for item in range(batch):
            start = pl.multiple_of((index * batch + item) * each, each)
            attended[pl.ds(start, each), :] = attend(
                qc[pl.ds(start, each), :],
                kv[item, :, :cols],
                kv[item, :, cols:],
                lambda s: jnp.where(real, s, NEG),
                heads,
                scaled,
                ones,
            )

        @pl.when(index == pl.num_programs(0) - 1)
        def _():
            out[...] = mul_t(attended[...], weight[...]).astype(BF)

    bias, gain, shift, bias_q = rows_in
    return call(
        kernel,
        items // batch,
        [whole((rows, width))] * 3
        + [whole((1, width))] * 3
        + [whole((1, cols)), whole((width, cols)), block((batch, padded, 2 * cols)), whole((width, cols))],
        [
            whole((rows, width)),
            whole((rows, 1)),
            whole((rows, width)),
            whole((rows, cols)),
            whole((rows, cols)),
            whole((rows, width)),
        ],
        [
            shaped((rows, width), F32),
            shaped((rows, 1), F32),
            shaped((rows, width), BF),
            shaped((rows, cols), BF),
            shaped((rows, cols), BF),
            shaped((rows, width), BF),
        ],
        flops=2 * rows * cols * padded * heads * 2,
        moved=rows * width * 20 + 4 * items * padded * cols,
    )(own, near, away, bias, gain, shift, bias_q, cq, keys_values, weight)


def lay_pieces(places, spots, refs, laid):
    count, rows, cols = laid.shape[1:]
    for far_off, w_in, w_out in zip(spots, refs[:count], refs[count:]):
        laid[0, places[far_off]] = w_in[...]
        laid[1, places[far_off]] = w_out[...]
    return laid[0].reshape(count * rows, cols), laid[1].reshape(count * rows, cols)


def feed_forward(flag, places, unit, near, away, rows_in, pieces, b_in, chunk):
    rows, width = unit.shape
    hidden = pieces[0].shape[1] // 2
    steps = hidden // chunk
    count = len(pieces)
    spots = arrival_order(count)

    def kernel(flag, places, unit, near, away, gain0, shift0, bias, gain1, shift1, b_in, *refs):
        z, z_low, unit2, scale2, act, slope, part, out, laid = refs[2 * count :]
        w_in, w_out = lay_pieces(places, spots, refs[: 2 * count], laid)

        @pl.when(pl.program_id(0) == 0)
        def _():
            after = unit[...] * gain0[...] + shift0[...]
            one, size = standard(after + pair_sum(near, away) + bias[...])
            unit2[...] = one
            scale2[...] = size
            z[...] = jnp.where(flag[0] == 0, one * gain1[...] + shift1[...], after)
            z_low[...] = z[...].astype(BF)
            out[...] = jnp.zeros_like(out)

        for half in range(2):
            span = slice(half * rows // 2, (half + 1) * rows // 2)
            u = mul(z_low[span], w_in) + b_in[...]
            share = 0.5 + 0.5 * lax.erf(u * math.sqrt(0.5))
            act_half = (u * share).astype(BF)
            act[span] = act_half
            slope[0, span] = share + u * (jnp.exp(-0.5 * u * u) * (1.0 / math.sqrt(2.0 * math.pi)))
            out[span] += mul_t(act_half, w_out)

        @pl.when(pl.program_id(0) == steps - 1)
        def _():
            part[...] = out[...].astype(BF)

    row = whole((1, width))
    return call(
        kernel,
        steps,
        [pl.BlockSpec(memory_space=pltpu.SMEM)] * 2
        + [whole((rows, width))] * 3
        + [row] * 5
        + [column((1, chunk))]
        + [column((width // count, chunk))] * count
        + [column((width // count, chunk), steps)] * count,
        [
            whole((rows, width)),
            whole((rows, width)),
            whole((rows, width)),
            whole((rows, 1)),
            column((rows, chunk)),
            block((1, rows, chunk)),
            whole((rows, width)),
        ],
        [
            shaped((rows, width), F32),
            shaped((rows, width), BF),
            shaped((rows, width), F32),
            shaped((rows, 1), F32),
            shaped((rows, hidden), BF),
            shaped((steps, rows, chunk), F32),
            shaped((rows, width), BF),
        ],
        scratch=[pltpu.VMEM((rows, width), F32), pltpu.VMEM((2, count, width // count, chunk), BF)],
        flops=4 * rows * hidden * width,
        moved=rows * width * 26 + rows * hidden * 6 + width * hidden * 4,
    )(flag, places, unit, near, away, *rows_in, b_in, *pieces, *pieces)


def feed_back(places, z, near, away, cotangent, rows_in, slope, pieces, chunk):
    rows, width = z.shape
    hidden = pieces[0].shape[1] // 2
    steps = hidden // chunk
    count = len(pieces)
    spots = arrival_order(count)

    def kernel(places, z, near, away, cot, bias, gain, shift, slope, *refs):
        result, grad_v, grad_u, grad_pre, part, sums, sum_pre, out, laid = refs[2 * count :]
        w_in, w_out = lay_pieces(places, spots, refs[: 2 * count], laid)

        @pl.when(pl.program_id(0) == 0)
        def _():
            one, size = standard(z[...] + pair_sum(near, away) + bias[...])
            dy = cot[...]
            result[...] = (one * gain[...] + shift[...]).astype(BF)
            grad_v[...] = norm_back(dy, one, size, gain[...])
            grad_u[...] = grad_v[...].astype(BF)
            sums[0:1] = total_rows(dy * one)
            sums[1:2] = total_rows(dy)
            sums[2:3] = total_rows(grad_u[...].astype(F32))
            out[...] = jnp.zeros_like(out)

        for half in range(2):
            span = slice(half * rows // 2, (half + 1) * rows // 2)
            pre = (mul(grad_u[span], w_out) * slope[0, span]).astype(BF)
            grad_pre[span] = pre
            out[span] += mul_t(pre, w_in)
        sum_pre[...] = total_rows(grad_pre[...].astype(F32))

        @pl.when(pl.program_id(0) == steps - 1)
        def _():
            part[...] = out[...].astype(BF)

    row = whole((1, width))
    return call(
        kernel,
        steps,
        [pl.BlockSpec(memory_space=pltpu.SMEM)]
        + [whole((rows, width))] * 4
        + [row] * 3
        + [block((1, rows, chunk))]
        + [column((width // count, chunk))] * count
        + [column((width // count, chunk), steps)] * count,
        [
            whole((rows, width)),
            whole((rows, width)),
            whole((rows, width)),
            column((rows, chunk)),
            whole((rows, width)),
            whole((8, width)),
            column((1, chunk)),
        ],
        [
            shaped((rows, width), BF),
            shaped((rows, width), F32),
            shaped((rows, width), BF),
            shaped((rows, hidden), BF),
            shaped((rows, width), BF),
            shaped((8, width), F32),
            shaped((1, hidden), F32),
        ],
        scratch=[pltpu.VMEM((rows, width), F32), pltpu.VMEM((2, count, width // count, chunk), BF)],
        flops=4 * rows * hidden * width,
        moved=rows * width * 28 + rows * hidden * 6 + width * hidden * 4,
    )(places, z, near, away, cotangent, *rows_in, slope, *pieces, *pieces)


def cross_back(flag, grad_v, near, away, unit2, scale2, gain, qc, keys_values, weight, cq, items, batch, patches):
    rows, width = grad_v.shape
    cols = weight.shape[1]
    heads, each = cols // HEAD_DIM, rows // items
    padded = keys_values.shape[1]

    def kernel(flag, grad_v, near, away, unit2, scale2, gain, qc, kv, weight, cq, after, mix, grad_qc, grad_kv, out, sums, sums_c, grad_att):
        index = pl.program_id(0)

        @pl.when(index == 0)
        def _():
            dz = grad_v[...] + pair_sum(near, away)
            mine = flag[0] == 0
            used = jnp.where(mine, dz, 0.0)
            two = norm_back(used, unit2[...], scale2[...], gain[...])
            after[...] = jnp.where(mine, two, dz)
            mix[...] = two.astype(BF)
            grad_att[...] = mul(mix[...], weight[...]).astype(BF)
            sums[0:1] = total_rows(used * unit2[...])
            sums[1:2] = total_rows(used)
            sums[2:3] = total_rows(mix[...].astype(F32))
            sums_c[...] = jnp.zeros_like(sums_c)

        root = HEAD_DIM ** (-0.5)
        scaled = head_mask(each, heads, root, BF)
        plain = head_mask(each, heads, 1.0, BF)
        ones = head_mask(each, heads, 1.0, F32)
        real = lax.broadcasted_iota(jnp.int32, (heads * each, padded), 1) < patches
        for item in range(batch):
            start = pl.multiple_of((index * batch + item) * each, each)
            dq, dk, dv = attend_back(
                qc[pl.ds(start, each), :],
                kv[item, :, :cols],
                kv[item, :, cols:],
                grad_att[pl.ds(start, each), :],
                lambda s: jnp.where(real, s, NEG),
                heads,
                scaled,
                plain,
                ones,
            )
            grad_qc[pl.ds(start, each), :] = dq.astype(BF)
            dk, dv = dk.astype(BF), dv.astype(BF)
            grad_kv[item, :, :cols] = dk
            grad_kv[item, :, cols:] = dv
            sums_c[1:2] += total_rows(dk.astype(F32))
            sums_c[2:3] += total_rows(dv.astype(F32))

        @pl.when(index == pl.num_programs(0) - 1)
        def _():
            out[...] = mul_t(grad_qc[...], cq[...]).astype(BF)
            sums_c[0:1] = total_rows(grad_qc[...].astype(F32))

    return call(
        kernel,
        items // batch,
        [pl.BlockSpec(memory_space=pltpu.SMEM)]
        + [whole((rows, width))] * 4
        + [
            whole((rows, 1)),
            whole((1, width)),
            whole((rows, cols)),
            block((batch, padded, 2 * cols)),
            whole((width, cols)),
            whole((width, cols)),
        ],
        [
            whole((rows, width)),
            whole((rows, width)),
            whole((rows, cols)),
            block((batch, padded, 2 * cols)),
            whole((rows, width)),
            whole((8, width)),
            whole((8, cols)),
        ],
        [
            shaped((rows, width), F32),
            shaped((rows, width), BF),
            shaped((rows, cols), BF),
            shaped((items, padded, 2 * cols), BF),
            shaped((rows, width), BF),
            shaped((8, width), F32),
            shaped((8, cols), F32),
        ],
        scratch=[pltpu.VMEM((rows, cols), BF)],
        flops=2 * rows * cols * padded * heads * 5,
        moved=rows * width * 26 + 8 * items * padded * cols,
    )(flag, grad_v, near, away, unit2, scale2, gain, qc, keys_values, weight, cq)


def self_back(flag, head, after, near, away, unit, scale, gain, q, kv, kv_far, allowed, weight, w_qkv, own, far, attended, items, batch, shards):
    rows, width = after.shape
    cols = weight.shape[1]
    heads, each = cols // HEAD_DIM, rows // items
    piece = width // shards

    def kernel(flag, head, after, near, away, unit, scale, gain, q, kv, kv_far, allowed, weight, w_qkv, own, far, attended, grad_one, mix, grad_near, grad_away, mine, theirs, sums, sums_c, grad_keep, grad_sent, grad_att):
        index = pl.program_id(0)

        @pl.when(index == 0)
        def _():
            grad = after[...] + pair_sum(near, away)
            grad_one[...] = norm_back(grad, unit[...], scale[...], gain[...])
            mix[...] = grad_one[...].astype(BF)
            grad_att[...] = mul(mix[...], weight[...]).astype(BF)
            sums[0:1] = total_rows(grad * unit[...])
            sums[1:2] = total_rows(grad)
            sums[2:3] = total_rows(mix[...].astype(F32))

        scaled = head_mask(each, heads, HEAD_DIM ** (-0.5), BF)
        plain = head_mask(each, heads, 1.0, BF)
        ones = head_mask(each, heads, 1.0, F32)
        for item in range(batch):
            span = slice(item * each, (item + 1) * each)
            start = pl.multiple_of((index * batch + item) * each, each)
            keys = jnp.concatenate([kv[span, :cols], kv_far[span, :cols]], axis=0)
            values = jnp.concatenate([kv[span, cols:], kv_far[span, cols:]], axis=0)
            seen = jnp.concatenate([allowed[item]] * heads, axis=0) > 0
            dq, dk, dv = attend_back(
                q[span],
                keys,
                values,
                grad_att[pl.ds(start, each), :],
                lambda s: jnp.where(seen, s, NEG),
                heads,
                scaled,
                plain,
                ones,
            )
            grad_near[pl.ds(start, each), :cols] = dq.astype(BF)
            grad_near[pl.ds(start, each), cols : 2 * cols] = dk[:each].astype(BF)
            grad_near[pl.ds(start, each), 2 * cols :] = dv[:each].astype(BF)
            grad_away[pl.ds(start, each), :cols] = dk[each:].astype(BF)
            grad_away[pl.ds(start, each), cols:] = dv[each:].astype(BF)

        @pl.when(index == pl.num_programs(0) - 1)
        def _():
            side = head[0] == 0
            middle = rows // 2
            for part, source, weights in ((0, grad_near, w_qkv), (1, grad_away, w_qkv[:, cols:])):
                lanes = slice(part * width, (part + 1) * width)
                top = mul_t(source[:middle], weights[...]).astype(BF)
                low = mul_t(source[middle:], weights[...]).astype(BF)
                mine[:, lanes] = jnp.where(side, top, low)
                theirs[:, lanes] = jnp.where(side, low, top)
            for place in range(4):
                span = slice(place * cols, (place + 1) * cols)
                if place == 3:
                    total = t_mul(mix[...], attended[...])
                else:
                    total = t_mul(own[...], grad_near[:, span])
                if place in (1, 2):
                    total = total + t_mul(far[...], grad_away[:, (place - 1) * cols : place * cols])
                total = total.astype(BF)
                for side in range(2):
                    pieces = [
                        total[one * piece : (one + 1) * piece] for one in range(side, shards, 2)
                    ]

                    @pl.when(flag[0] == side)
                    def _():
                        for one, value in enumerate(pieces):
                            grad_keep[one, :, span] = value

                    @pl.when(flag[0] != side)
                    def _():
                        for one, value in enumerate(pieces):
                            grad_sent[one, :, span] = value
            sums_c[0:1] = total_rows(grad_near[...].astype(F32))
            sums_c[1:2, cols:] = total_rows(grad_away[...].astype(F32))

    part = batch * each
    return call(
        kernel,
        items // batch,
        [pl.BlockSpec(memory_space=pltpu.SMEM)] * 2
        + [whole((rows, width))] * 4
        + [
            whole((rows, 1)),
            whole((1, width)),
            block((part, cols)),
            block((part, 2 * cols)),
            block((part, 2 * cols)),
            block((batch, each, 2 * each)),
            whole((width, cols)),
            whole((width, 3 * cols)),
            whole((rows, width)),
            whole((rows, width)),
            whole((rows, cols)),
        ],
        [
            whole((rows, width)),
            whole((rows, width)),
            whole((rows, 3 * cols)),
            whole((rows, 2 * cols)),
            whole((rows // 2, 2 * width)),
            whole((rows // 2, 2 * width)),
            whole((8, width)),
            whole((8, 3 * cols)),
            whole((shards // 2, piece, 4 * cols)),
            whole((shards // 2, piece, 4 * cols)),
        ],
        [
            shaped((rows, width), F32),
            shaped((rows, width), BF),
            shaped((rows, 3 * cols), BF),
            shaped((rows, 2 * cols), BF),
            shaped((rows // 2, 2 * width), BF),
            shaped((rows // 2, 2 * width), BF),
            shaped((8, width), F32),
            shaped((8, 3 * cols), F32),
            shaped((shards // 2, piece, 4 * cols), BF),
            shaped((shards // 2, piece, 4 * cols), BF),
        ],
        scratch=[pltpu.VMEM((rows, cols), BF)],
        flops=2 * rows * cols * width * 9,
        moved=rows * width * 32 + rows * cols * 20,
    )(flag, head, after, near, away, unit, scale, gain, q, kv, kv_far, allowed, weight, w_qkv, own, far, attended)


def pack_small(flag, one, two, three, own, cross, pre, kv_grad, kv_all, gain, shift):
    width = one.shape[1]
    cols = cross.shape[1]
    feat_width = kv_all.shape[0]
    pres = pre.shape[1] // width
    folds = (feat_width + width - 1) // width
    rows = (14 + 2 * pres + 2 * folds + 7) // 8 * 8

    def exact(left, right):
        return lax.dot_general(
            left,
            right,
            (((1,), (1,)), ((), ())),
            precision=lax.Precision.HIGHEST,
            preferred_element_type=F32,
        )

    def kernel(flag, one, two, three, own, cross, pre, kv_grad, kv_all, gain, shift, out, line):
        on_text = flag[0].astype(F32)
        on_query = 1.0 - on_text
        out[...] = jnp.zeros_like(out)
        for place in range(3):
            at_row = slice(place, place + 1)
            out[4 * place : 4 * place + 1] = one[at_row]
            out[4 * place + 1 : 4 * place + 2] = two[at_row]
            out[4 * place + 2 : 4 * place + 3] = on_query * three[at_row]
            out[4 * place + 3 : 4 * place + 4] = on_text * three[at_row]
        out[12:13, :cols] = own[0:1, :cols]
        out[12:13, cols:] = own[0:1, 2 * cols :] + own[1:2, 2 * cols :]
        out[13:14, :cols] = cross[0:1]
        out[13:14, cols:] = cross[2:3]
        for k in range(pres):
            part = pre[:, k * width : (k + 1) * width]
            out[14 + k : 15 + k] = on_query * part
            out[14 + pres + k : 15 + pres + k] = on_text * part
        column_sums = jnp.concatenate([cross[1:2], cross[2:3]], axis=1)
        column_sums = jnp.broadcast_to(column_sums, (8, width))
        ones = jnp.ones((8, width), F32)

        def chunk(k, carry):
            span = pl.ds(pl.multiple_of(k * 128, 128), 128)
            weight = kv_all[span, :].astype(F32)
            d_shift = exact(column_sums, weight)[0:1]
            dot = exact(ones, kv_grad[span, :] * weight)[0:1]
            line[0:1, span] = (dot - shift[:, span] * d_shift) / gain[:, span]
            line[1:2, span] = d_shift
            return carry

        lax.fori_loop(0, feat_width // 128, chunk, 0)
        start = 14 + 2 * pres
        for part in range(2):
            for k in range(folds):
                end = min(feat_width, (k + 1) * width)
                spot = start + part * folds + k
                out[spot : spot + 1, : end - k * width] = line[part : part + 1, k * width : end]

    arrays = (one, two, three, own, cross, pre, kv_grad, kv_all, gain, shift)
    return call(
        kernel,
        1,
        [pl.BlockSpec(memory_space=pltpu.SMEM)] + [whole(array.shape) for array in arrays],
        whole((rows, width)),
        shaped((rows, width), F32),
        scratch=[pltpu.VMEM((8, feat_width), F32)],
        moved=6 * feat_width * width,
    )(flag, *arrays)


def unpack_small(head, packed, other, pres, feat_width):
    width = packed.shape[1]
    half = width // 2
    folds = (feat_width + width - 1) // width

    def kernel(head, packed, other, own_bias, cross_bias, gains, shifts, d_gain, d_shift, pre, post):
        first = head[0] == 0
        near, away = packed[12:], other[...]
        low = jnp.where(first, near, away)
        high = jnp.where(first, away, near)
        for place, out in enumerate((own_bias, cross_bias)):
            for part in range(2):
                span = slice(part * half, (part + 1) * half)
                out[part : part + 1, :half] = low[place : place + 1, span]
                out[part : part + 1, half:] = high[place : place + 1, span]
        own_bias[2:3] = packed[8:9]
        cross_bias[2:3] = packed[9:10]
        gains[...] = packed[0:4]
        shifts[...] = packed[4:8]
        post[...] = packed[10:12]
        for side in range(2):
            for k in range(pres):
                line = slice(2 + side * pres + k, 3 + side * pres + k)
                pre[side : side + 1, k * width : (k + 1) * width] = low[line]
                pre[side : side + 1, (pres + k) * width : (pres + k + 1) * width] = high[line]
        both = near + away
        for place, out in enumerate((d_gain, d_shift)):
            for k in range(folds):
                end = min(feat_width, (k + 1) * width)
                line = 2 + 2 * pres + place * folds + k
                for begin in range(k * width, end, 128):
                    spot, left = begin // 128, begin - k * width
                    out[spot : spot + 1] = both[line : line + 1, left : left + 128]

    shapes = [(3, width)] * 2 + [(4, width)] * 2 + [(feat_width // 128, 128)] * 2
    shapes = shapes + [(2, 2 * pres * width), (2, width)]
    return call(
        kernel,
        1,
        [pl.BlockSpec(memory_space=pltpu.SMEM), whole(packed.shape), whole(other.shape)],
        [whole(shape) for shape in shapes],
        [shaped(shape, F32) for shape in shapes],
        moved=200000,
    )(head, packed, other)


def visible(stream, segments, modes):
    same_caption = segments[:, :, None] == segments[:, None, :]
    own = jnp.logical_or(stream == 0, same_caption)
    far = jnp.where(stream == 0, modes == 2, modes >= 1)[:, None, None]
    return jnp.concatenate([own, jnp.broadcast_to(far, own.shape)], axis=2).astype(F32)


def body(
    hidden,
    features,
    segments,
    modes,
    w_qkv,
    self_bias,
    self_out,
    cross_q,
    cross_kv,
    cross_bias,
    cross_out,
    gains,
    shifts,
    feat_gain,
    feat_shift,
    ffn_in,
    ffn_bias_in,
    ffn_out,
    ffn_bias_out,
    cotangent,
):
    stream = lax.axis_index("stream")
    stream_u = stream.astype(jnp.uint32)
    head_index = lax.axis_index("heads")
    items, _, each, width = hidden.shape
    rows = items * each
    half = rows // 2
    cols = w_qkv.shape[2]
    hidden_cols = ffn_in.shape[2]
    patches, feat_width = features.shape[1:]
    padded = (patches + 7) // 8 * 8
    col_start = head_index.astype(jnp.uint32) * cols
    hidden_start = head_index.astype(jnp.uint32) * hidden_cols
    flag = stream.astype(jnp.int32).reshape(1)
    shards = 2 * lax.axis_size("items")
    three = [slice(i * cols, (i + 1) * cols) for i in range(3)]

    ffn_part = jnp.concatenate([ffn_in[0], ffn_out[0].T], axis=1)
    part_qkv = jnp.concatenate([w_qkv[0], w_qkv[1], w_qkv[2]], axis=0)
    pair_qkv = by_stream(part_qkv, partner(part_qkv, "stream", 0), 0)
    places = ring_places()
    spots = ring_row()
    own = hidden.reshape(rows, width)
    heads_u = head_index.astype(jnp.uint32)
    my_half = lax.dynamic_slice_in_dim(own, heads_u * half, half, 0)
    far_half = partner(my_half, "stream", 0)
    piece, kv_piece = cross_q.shape[0], cross_kv.shape[1]
    rest = jnp.concatenate([self_out.T, cross_q, cross_out.T, cross_kv[0], cross_kv[1]], axis=0)

    def row(vector):
        return vector.reshape(1, -1)

    features, pair_qkv = joined(features, pair_qkv)
    ring = Gather(jnp.concatenate([pair_qkv.reshape(6 * piece, cols), rest], axis=0))

    def crossing(one):
        return one[6 * piece :], over("stream")

    kept, chunk = [], items // 4
    crossed = []
    begin = 0
    for number in range(max(4, shards // 4)):
        if ring.left:
            riders = [crossing(one) for one in ring.pieces[begin:]]
            if number == 1:
                riders.append((far_half, over("heads")))
            last_step = ring.hop == shards // 4
            if last_step:
                ffn_part, held = joined(ffn_part, ring.up)
                ring.replace(held, ring.down)
                ffn_gather = Gather(ffn_part)
            fresh = len(ring.pieces) - begin
            begin = len(ring.pieces)
            ridden = gather_step([ring], *riders)
            crossed += ridden[:fresh]
            if number == 1:
                far_other = ridden[-1]
            if last_step:
                gather_step([ffn_gather])
        if number < 4:
            *kept, token = list(
                feature_norm(
                    features, row(feat_gain), row(feat_shift), padded, number * chunk, chunk, kept
                )
            )
            up, down, token = joined(ring.up, ring.down, token)
            ring.replace(up, down)
            kept = [kept[0], token]
    feat_norm = kept[0]
    crossed += [move(one) for one, move in (crossing(one) for one in ring.pieces[begin:])]
    far = jnp.where(
        head_index == 0,
        jnp.concatenate([far_half, far_other], axis=0),
        jnp.concatenate([far_other, far_half], axis=0),
    )
    def ffn_step(value, last=False):
        if ffn_gather.hop - 1 > ffn_gather.count // 2:
            return value
        value, up, down = joined(value, ffn_gather.up, ffn_gather.down)
        ffn_gather.replace(up, down)
        while ffn_gather.left:
            gather_step([ffn_gather])
            if not last:
                break
        return value

    def my_cols(vector):
        return lax.dynamic_slice_in_dim(vector, col_start, cols, 0)

    none = jnp.zeros((cols,), F32)
    bias_qkv = row(jnp.concatenate([my_cols(self_bias[0]), none, my_cols(self_bias[1])]))
    bias_kv = row(jnp.concatenate([none, my_cols(cross_bias[1])]))
    gain_ffn = row(lax.dynamic_index_in_dim(gains, 2 + stream_u, 0, keepdims=False))
    shift_ffn = row(lax.dynamic_index_in_dim(shifts, 2 + stream_u, 0, keepdims=False))
    bias_in = row(
        lax.dynamic_slice_in_dim(
            lax.dynamic_index_in_dim(ffn_bias_in, stream_u, 0, keepdims=False),
            hidden_start,
            hidden_cols,
            0,
        )
    )
    bias_out = row(lax.dynamic_index_in_dim(ffn_bias_out, stream_u, 0, keepdims=False))

    def swap(part):
        return partner(part, "heads", 0)

    q, kv, kv_far, qkv_all = project(spots, own, far, ring.pieces, bias_qkv, piece)
    ends = joined(ffn_gather.up, ffn_gather.down, ring.up, kv_far, feat_norm, *crossed[-3:])
    ffn_gather.replace(*ends[:2])
    ring.replace(ends[2], ends[2])
    kv_far = ends[3]
    feat_rows = ends[4].reshape(items * padded, feat_width)
    crossed[-3:] = ends[5:]
    gather_step([ffn_gather])
    self_out_t, cross_q_all, cross_out_t, kv_all = assemble(
        flag, spots, ring.pieces, crossed, piece, kv_piece
    )

    allowed = visible(stream, segments, modes)
    attended, part = self_attention(q, kv, kv_far, allowed, self_out_t, items, 4)
    kv_all = ffn_step(kv_all)
    away_one = swap(part)
    keys_values = (mul(feat_rows, kv_all) + bias_kv).astype(BF).reshape(items, padded, 2 * cols)
    keys_values = ffn_step(keys_values)
    unit_one, scale_one, after_low, qc, attended_c, part_c = cross_attention(
        own,
        part,
        away_one,
        (row(self_bias[2]), row(gains[0]), row(shifts[0]), row(my_cols(cross_bias[0]))),
        cross_q_all,
        keys_values,
        cross_out_t,
        items,
        2,
        patches,
    )
    unit_one, part_c, scale_one, after_low, qc, attended_c = ffn_step(
        (unit_one, part_c, scale_one, after_low, qc, attended_c), True
    )
    ffn_pieces = ffn_gather.pieces
    z, z_low, unit_two, scale_two, activated, slope, part_f = feed_forward(
        flag,
        spots,
        unit_one,
        part_c,
        swap(part_c),
        (row(gains[0]), row(shifts[0]), row(cross_bias[2]), row(gains[1]), row(shifts[1])),
        ffn_pieces,
        bias_in,
        256,
    )

    output, grad_three, grad_u, grad_pre, part_z, sums_three, sum_pre = feed_back(
        spots,
        z,
        part_f,
        swap(part_f),
        cotangent.reshape(rows, width),
        (bias_out, gain_ffn, shift_ffn),
        slope,
        ffn_pieces,
        256,
    )
    away_z = swap(part_z)
    in_grad = t_mul(z_low, grad_pre).astype(BF)
    out_grad = t_mul(grad_u, activated).astype(BF)
    count = shards // 2
    grad_after, mix_c, grad_qc, grad_kv, part_a, sums_two, sums_cross = cross_back(
        flag,
        grad_three,
        part_z,
        away_z,
        unit_two,
        scale_two,
        row(gains[1]),
        qc,
        keys_values,
        cross_out_t,
        cross_q_all,
        items,
        2,
        patches,
    )
    in_grad, out_grad, sums_two = joined(in_grad, out_grad, sums_two)
    ffn_ring = Scatter(
        [
            [at(in_grad.reshape(count, -1, hidden_cols))],
            [at(out_grad.reshape(count, -1, hidden_cols))],
        ],
        1,
        places,
    )
    ffn_ring.step()
    away_a = swap(part_a)
    keep_q, away_q = halves(t_mul(after_low, grad_qc).astype(BF))
    keep_o, away_o = halves(t_mul(mix_c, attended_c).astype(BF))
    away_c = jnp.concatenate([away_q, away_o], axis=2)
    grad_kv, away_c = joined(grad_kv, away_c)
    kv_grad = t_mul(feat_rows, grad_kv.reshape(items * padded, 2 * cols))
    kv_grad_low = kv_grad.astype(BF)
    arrived_c = partner(away_c, "stream", 0)
    kv_grad, kv_grad_low, arrived_c, ffn_ring.up = joined(
        kv_grad, kv_grad_low, arrived_c, ffn_ring.up
    )
    keep_kv, away_kv = halves(kv_grad_low)
    ffn_ring.step()
    away_a, away_kv = joined(away_a, away_kv)
    arrived_kv = partner(away_kv, "stream", 0)
    grad_one, mix, grad_near, grad_away, mine, theirs, sums_one, sums_self, keep_self, away_self = self_back(
        flag,
        head_index.astype(jnp.int32).reshape(1),
        grad_after,
        part_a,
        away_a,
        unit_one,
        scale_one,
        row(gains[0]),
        q,
        kv,
        kv_far,
        allowed,
        self_out_t,
        qkv_all,
        own,
        far,
        attended,
        items,
        4,
        shards,
    )

    results = (grad_one, mine, theirs, sums_one, sums_self, keep_self, away_self, arrived_kv)
    results = lax.optimization_barrier(results + (ffn_ring.up, ffn_ring.down))
    grad_one, mine, theirs, sums_one, sums_self, keep_self, away_self, arrived_kv = results[:-2]
    ffn_ring.up, ffn_ring.down = results[-2:]


    def ring_steps(rings, *riders):
        ridden = [move(value) for value, move in riders]
        sends = [ring.sends() for ring in rings]
        flat = [one for part in sends for one in part]
        arrivals = lax.optimization_barrier(tuple(ridden) + tuple(together(flat)))
        rest = arrivals[len(riders) :]
        for ring, part in zip(rings, sends):
            ring.take(rest[: len(part)])
            rest = rest[len(part) :]
        return arrivals[: len(riders)]

    rest_ring = Scatter(
        [
            [at_stream(keep_q), at(arrived_c, three[0])],
            [at_stream(keep_o), at(arrived_c, three[1])],
            [at_stream(keep_kv, three[0]), at(arrived_kv, three[0])],
            [at_stream(keep_kv, three[1]), at(arrived_kv, three[1])],
        ],
        0,
        places,
    )
    arrived_self, from_swap = partner(away_self, "stream", 0), swap(theirs)
    ffn_ring.step()
    ring_steps([rest_ring])
    while ffn_ring.hop:
        ffn_ring.step()
    ends = joined(arrived_self, ffn_ring.up, ffn_ring.down, rest_ring.up)
    arrived_self, ffn_ring.up, ffn_ring.down, rest_ring.up = ends
    self_ring = Scatter([[at(keep_self), at(arrived_self)]], 0, places)
    total = mine.astype(F32) + from_swap.astype(F32)
    from_far = partner(total[:, width:].astype(BF), "stream", 0)
    packed = pack_small(
        flag,
        sums_one,
        sums_two,
        sums_three,
        sums_self,
        sums_cross,
        sum_pre,
        kv_grad,
        kv_all,
        row(feat_gain),
        row(feat_shift),
    )
    packed = packed + partner(packed, "items", 0)
    moves = [over("stream")] + [over("items", bit) for bit in range(1, (count - 1).bit_length())]

    in_half = (
        lax.dynamic_slice_in_dim(grad_one, heads_u * half, half, 0)
        + total[:, :width]
        + from_far.astype(F32)
    )
    (arrived,) = ring_steps(
        [one for one in (rest_ring, self_ring) if one.hop], (packed, moves.pop(0))
    )
    packed = packed + arrived
    in_other = swap(in_half)
    while self_ring.hop or ffn_ring.hop or rest_ring.hop:
        rings = [one for one in (ffn_ring, rest_ring, self_ring) if one.hop]
        riders = [(packed, moves.pop(0))] if moves else []
        for arrived in ring_steps(rings, *riders):
            packed = packed + arrived
    while moves:
        packed = packed + moves.pop(0)(packed)
    grad_input = jnp.where(
        head_index == 0,
        jnp.concatenate([in_half, in_other], axis=0),
        jnp.concatenate([in_other, in_half], axis=0),
    )
    ffn_red, rest_red, self_red = ffn_ring.result(), rest_ring.result(), self_ring.result()
    small = unpack_small(
        head_index.astype(jnp.int32).reshape(1),
        packed,
        swap(packed[12:]),
        hidden_cols // width,
        feat_width,
    )
    return (
        output.reshape(items, 1, each, width),
        grad_input.reshape(items, 1, each, width),
        jnp.stack([self_red[:, one] for one in three]),
        small[0],
        self_red[:, 3 * cols :].T,
        rest_red[:piece],
        rest_red[2 * piece :].reshape(2, kv_piece, cols),
        small[1],
        rest_red[piece : 2 * piece].T,
        small[2],
        small[3],
        small[4].reshape(feat_width),
        small[5].reshape(feat_width),
        ffn_red[:, :hidden_cols][None],
        small[6],
        ffn_red[:, hidden_cols:].T[None],
        small[7],
    )


def solution(mesh):
    placed = (
        P("items", "stream", None, None),
        P("items", None, None),
        P("items", None),
        P("items"),
        P(None, ("items", "stream"), "heads"),
        P(),
        P("heads", ("items", "stream")),
        P(("items", "stream"), "heads"),
        P(None, ("items", "stream"), "heads"),
        P(),
        P("heads", ("items", "stream")),
        P(),
        P(),
        P(),
        P(),
        P("stream", "items", "heads"),
        P(),
        P("stream", "heads", "items"),
        P(),
        P("items", "stream", None, None),
    )
    return jax.shard_map(
        body,
        mesh=mesh,
        in_specs=placed,
        out_specs=(
            P("items", "stream", None, None),
            P("items", "stream", None, None),
            P(None, ("items", "stream"), "heads"),
            P(),
            P("heads", ("items", "stream")),
            P(("items", "stream"), "heads"),
            P(None, ("items", "stream"), "heads"),
            P(),
            P("heads", ("items", "stream")),
            P(),
            P(),
            P(),
            P(),
            P("stream", "items", "heads"),
            P(),
            P("stream", "heads", "items"),
            P(),
        ),
        check_vma=False,
    )
```

```python
import math

import jax
import jax.numpy as jnp
import numpy as np
from jax import lax
from jax.experimental import pallas as pl
from jax.experimental.pallas import tpu as pltpu
from jax.sharding import PartitionSpec as P

HEAD_DIM = 64
EPS = 1e-06
NEG = -1e30
BF = jnp.bfloat16
F32 = jnp.float32


def partner(shard, axis, distance):
    return lax.ppermute(shard, axis, [(i, i ^ 1 << distance) for i in range(lax.axis_size(axis))])


def joined(*values):
    return lax.optimization_barrier(values)


def ring_of(count):
    return list(range(0, count, 2)) + list(range(1, count, 2))[::-1]


def ring_table():
    count = lax.axis_size("items")
    order = ring_of(count)
    table = np.zeros((count, count), np.uint32)
    for place, index in enumerate(order):
        table[index] = [order[(place + far) % count] for far in range(count)]
    return table


def ring_row():
    row = lax.axis_index("items").astype(jnp.uint32)
    table = jnp.asarray(ring_table().astype(np.int32))
    found = lax.dynamic_slice(table, (row, jnp.uint32(0)), (1, table.shape[1]))
    return found.reshape(table.shape[1])


def ring_places():
    table = ring_table()
    count = table.shape[0]
    bits = max(1, (count - 1).bit_length())
    per_word = 32 // bits
    index = lax.axis_index("items").astype(jnp.uint32)
    places = []
    for begin in range(0, count, per_word):
        part = table[:, begin : begin + per_word]
        words = [sum(int(one) << (bits * k) for k, one in enumerate(line)) for line in part]
        word = jnp.uint32(words[0])
        for item in range(1, count):
            word = jnp.where(index == jnp.uint32(item), jnp.uint32(words[item]), word)
        for k in range(part.shape[1]):
            places.append((word >> jnp.uint32(bits * k)) & jnp.uint32((1 << bits) - 1))
    return places


def arrival_order(count):
    order = [0]
    for hop in range(1, count // 2 + 1):
        order.append(count - hop)
        if hop <= (count - 1) // 2:
            order.append(hop)
    return order


def shift_ring(shard, order, step):
    count = len(order)
    return lax.ppermute(
        shard, "items", [(order[i], order[(i + step) % count]) for i in range(count)]
    )


def together(sends):
    values = lax.optimization_barrier(tuple(value for value, _ in sends))
    return lax.optimization_barrier(tuple(move(one) for one, (_, move) in zip(values, sends)))


class Gather:
    def __init__(self, shard):
        self.count = lax.axis_size("items")
        self.order = ring_of(self.count)
        self.up = self.down = shard
        self.pieces = [shard]
        self.hop = 1

    def sends(self):
        result = [(self.up, lambda one: shift_ring(one, self.order, 1))]
        if self.hop <= (self.count - 1) // 2:
            result.append((self.down, lambda one: shift_ring(one, self.order, -1)))
        return result

    def take(self, arrivals):
        self.pieces += arrivals
        self.up = arrivals[0]
        self.down = arrivals[-1]
        self.hop += 1

    def replace(self, up, down):
        self.pieces[-1] = down
        if self.hop - 1 <= (self.count - 1) // 2:
            self.pieces[-2] = up
        self.up, self.down = up, down

    @property
    def left(self):
        return self.hop <= self.count // 2


def gather_step(rings, *riders):
    sends = [ring.sends() for ring in rings]
    arrivals = together(list(riders) + [one for part in sends for one in part])
    ridden, arrivals = arrivals[: len(riders)], arrivals[len(riders) :]
    for ring, part in zip(rings, sends):
        ring.take(list(arrivals[: len(part)]))
        arrivals = arrivals[len(part) :]
    return ridden


def place_items(pieces, places):
    whole = jnp.zeros((len(pieces),) + pieces[0].shape, pieces[0].dtype)
    for far, piece in zip(arrival_order(len(pieces)), pieces):
        whole = lax.dynamic_update_index_in_dim(whole, piece, places[far], 0)
    return whole


def by_stream(own, other, axis):
    first = lax.axis_index("stream") == 0
    return jnp.where(
        first, jnp.stack([own, other], axis=axis), jnp.stack([other, own], axis=axis)
    )


def whole_rows(own, other):
    both = by_stream(own, other, 1)
    return both.reshape((both.shape[0] * both.shape[1] * both.shape[2], both.shape[3]))


def at(pieces, span=slice(None)):
    return lambda which: lax.dynamic_index_in_dim(pieces, which, 0, keepdims=False)[:, span]


def at_stream(pieces, span=slice(None)):
    stream = lax.axis_index("stream").astype(jnp.uint32)
    zero = jnp.uint32(0)

    def read(which):
        start = (which, stream, zero, zero)
        found = lax.dynamic_slice(pieces, start, (1, 1) + pieces.shape[2:])
        return found.reshape(pieces.shape[2:])[:, span]

    return read


class Scatter:
    def __init__(self, groups, axis, places):
        self.groups, self.axis = groups, axis
        self.count = lax.axis_size("items")
        self.order, self.places = ring_of(self.count), places
        self.hop = self.count // 2
        self.up = self.down = None

    def piece(self, distance):
        which = self.places[distance % self.count]
        parts = [sum(read(which).astype(F32) for read in group) for group in self.groups]
        return jnp.concatenate(parts, axis=self.axis)

    def sends(self):
        own = self.piece(self.hop)
        own = own if self.up is None else own + self.up.astype(F32)
        result = [(own.astype(BF), lambda one: shift_ring(one, self.order, 1))]
        if self.hop <= (self.count - 1) // 2:
            own = self.piece(self.count - self.hop)
            own = own if self.down is None else own + self.down.astype(F32)
            result.append((own.astype(BF), lambda one: shift_ring(one, self.order, -1)))
        return result

    def take(self, arrivals):
        self.up = arrivals[0]
        if len(arrivals) > 1:
            self.down = arrivals[1]
        self.hop -= 1
        return arrivals[0]

    def step(self):
        return self.take(together(self.sends()))

    def result(self):
        return self.piece(0) + self.up.astype(F32) + self.down.astype(F32)


def halves(total):
    count = lax.axis_size("items")
    rows = total.shape[0] // (2 * count)
    parts = total.reshape((count, 2, rows, total.shape[1]))
    stream = lax.axis_index("stream").astype(jnp.uint32)
    away = lax.dynamic_index_in_dim(parts, 1 - stream, 1, keepdims=False)
    return parts, away


def over(axis, distance=0):
    return lambda one: partner(one, axis, distance)


def mul(left, right):
    return jnp.dot(left, right, preferred_element_type=F32)


def mul_t(left, right):
    return lax.dot_general(left, right, (((1,), (1,)), ((), ())), preferred_element_type=F32)


def t_mul(left, right):
    return lax.dot_general(left, right, (((0,), (0,)), ((), ())), preferred_element_type=F32)


def standard(rows):
    center = rows - jnp.mean(rows, axis=-1, keepdims=True)
    scale = lax.rsqrt(jnp.mean(center * center, axis=-1, keepdims=True) + EPS)
    return center * scale, scale


def norm_back(grad, unit, scale, gain):
    inner = grad * gain
    return scale * (
        inner
        - jnp.mean(inner, axis=-1, keepdims=True)
        - unit * jnp.mean(inner * unit, axis=-1, keepdims=True)
    )


def pair_sum(near, away):
    return near[...].astype(F32) + away[...].astype(F32)


def total_rows(rows):
    return jnp.sum(rows, axis=0, keepdims=True)


def head_mask(rows, heads, value, dtype):
    row = lax.broadcasted_iota(jnp.int32, (heads * rows, heads * HEAD_DIM), 0) // rows
    col = lax.broadcasted_iota(jnp.int32, (heads * rows, heads * HEAD_DIM), 1) // HEAD_DIM
    return jnp.where(row == col, value, 0.0).astype(dtype)


def stack_heads(rows, heads, mask):
    return jnp.concatenate([rows] * heads, axis=0) * mask


def fold_heads(stacked, heads, mask):
    rows = stacked.shape[0] // heads
    stacked = stacked * mask
    result = stacked[:rows]
    for head in range(1, heads):
        result = result + stacked[head * rows : (head + 1) * rows]
    return result


def softmax(scores):
    power = jnp.exp(scores - jnp.max(scores, axis=-1, keepdims=True))
    return power * (1.0 / jnp.sum(power, axis=-1, keepdims=True))


def attend(queries, keys, values, hide, heads, scaled_mask, out_mask):
    scores = hide(mul_t(stack_heads(queries, heads, scaled_mask), keys))
    weights = softmax(scores).astype(BF)
    return fold_heads(mul(weights, values), heads, out_mask).astype(BF)


def attend_back(queries, keys, values, grad, hide, heads, scaled_mask, plain_mask, out_mask):
    queries = stack_heads(queries, heads, scaled_mask)
    grad = stack_heads(grad, heads, plain_mask)
    weights = softmax(hide(mul_t(queries, keys)))
    grad_weights = mul_t(grad, values)
    grad_values = t_mul(weights.astype(BF), grad)
    delta = jnp.sum(grad_weights * weights, axis=-1, keepdims=True)
    grad_scores = (weights * (grad_weights - delta)).astype(BF)
    grad_queries = fold_heads(mul(grad_scores, keys), heads, out_mask) * HEAD_DIM ** (-0.5)
    return grad_queries, t_mul(grad_scores, queries), grad_values


def whole(shape):
    return pl.BlockSpec(shape, lambda i: (0,) * len(shape))


def block(shape):
    return pl.BlockSpec(shape, lambda i: (i,) + (0,) * (len(shape) - 1))


def column(shape, first=0):
    return pl.BlockSpec(shape, lambda i: (0, i + first))


def shaped(shape, dtype):
    return jax.ShapeDtypeStruct(shape, dtype)


def call(kernel, grid, in_specs, out_specs, out_shape, scratch=(), flops=0, moved=0, limit=56):
    return pl.pallas_call(
        kernel,
        grid=(grid,),
        in_specs=in_specs,
        out_specs=out_specs,
        out_shape=out_shape,
        scratch_shapes=list(scratch),
        compiler_params=pltpu.CompilerParams(
            dimension_semantics=("arbitrary",), vmem_limit_bytes=limit << 20
        ),
        cost_estimate=pl.CostEstimate(flops=flops, bytes_accessed=moved, transcendentals=0),
    )


def feature_norm(features, gain, shift, padded, begin, each, prior):
    items, patches, width = features.shape

    def kernel(feat, gain, shift, *refs):
        out, token = refs[-2:]
        unit, _ = standard(feat[0].astype(F32))
        out[0, :patches] = (unit * gain[...] + shift[...]).astype(BF)
        out[0, patches:] = jnp.zeros((padded - patches, width), BF)
        token[...] = jnp.zeros_like(token)

    def at_item(i):
        return (i + begin, 0, 0)

    return pl.pallas_call(
        kernel,
        grid=(each,),
        in_specs=[pl.BlockSpec((1, patches, width), at_item), whole((1, width)), whole((1, width))]
        + [pl.BlockSpec(memory_space=pl.ANY)] * len(prior),
        out_specs=[pl.BlockSpec((1, padded, width), at_item), whole((8, 128))],
        out_shape=[shaped((items, padded, width), BF), shaped((8, 128), F32)],
        input_output_aliases={3: 0} if prior else {},
        compiler_params=pltpu.CompilerParams(
            dimension_semantics=("arbitrary",), vmem_limit_bytes=56 << 20
        ),
        cost_estimate=pl.CostEstimate(
            flops=0, bytes_accessed=4 * each * patches * width, transcendentals=0
        ),
    )(features, gain, shift, *prior)


def project(places, own, far, pieces, bias, each):
    rows, width = own.shape
    count = len(pieces)
    head_cols = pieces[0].shape[1]
    cols = 3 * head_cols
    step = rows // 4
    spots = arrival_order(count)

    def kernel(places, own, far, bias, *refs):
        q, kv, kv_far, weight, laid = refs[count:]

        @pl.when(pl.program_id(0) == 0)
        def _():
            for far_off, one in zip(spots, refs[:count]):
                piece = one[...]
                for side in range(2):
                    for k in range(3):
                        start = (3 * side + k) * each
                        lanes = slice(k * head_cols, (k + 1) * head_cols)
                        laid[places[far_off], side, :, lanes] = piece[start : start + each]
            weight[...] = laid[...].reshape(width, cols)

        near = mul(own[...], weight[...]) + bias[...]
        q[...] = near[:, :head_cols].astype(BF)
        kv[...] = near[:, head_cols:].astype(BF)
        kv_far[...] = (mul(far[...], weight[:, head_cols:]) + bias[:, head_cols:]).astype(BF)

    return call(
        kernel,
        4,
        [pl.BlockSpec(memory_space=pltpu.SMEM)]
        + [block((step, width)), block((step, width)), whole((1, cols))]
        + [whole((6 * each, head_cols))] * count,
        [block((step, head_cols)), block((step, 2 * head_cols)), block((step, 2 * head_cols))]
        + [whole((width, cols))],
        [shaped((rows, head_cols), BF)]
        + [shaped((rows, 2 * head_cols), BF)] * 2
        + [shaped((width, cols), BF)],
        scratch=[pltpu.VMEM((count, 2, each, cols), BF)],
        flops=10 * rows * width * head_cols,
        moved=4 * rows * width + 4 * width * cols,
    )(places, own, far, bias, *pieces)


def assemble(flag, places, pieces, crossed, each, kv_each):
    count = len(pieces)
    cols = pieces[0].shape[1]
    spots = arrival_order(count)
    rows = crossed[0].shape[0]

    def kernel(flag, places, *refs):
        self_out, cross_q, cross_out, kv = refs[2 * count :]
        for number, far_off in enumerate(spots):
            place = places[far_off]
            for side, piece in (
                (flag[0], refs[number][6 * each :]),
                (1 - flag[0], refs[count + number][...]),
            ):
                for k, out in enumerate((self_out, cross_q, cross_out)):
                    out[place, side] = piece[k * each : (k + 1) * each]
                start = 3 * each
                kv[place, side, :, :cols] = piece[start : start + kv_each]
                kv[place, side, :, cols:] = piece[start + kv_each :]

    shapes = [(count, 2, each, cols)] * 3 + [(count, 2, kv_each, 2 * cols)]
    results = call(
        kernel,
        1,
        [pl.BlockSpec(memory_space=pltpu.SMEM)] * 2
        + [whole(pieces[0].shape)] * count
        + [whole((rows, cols))] * count,
        [whole(shape) for shape in shapes],
        [shaped(shape, BF) for shape in shapes],
        moved=8 * count * rows * cols,
    )(flag, places, *pieces, *crossed)
    return [one.reshape(2 * count * one.shape[2], one.shape[3]) for one in results]


def self_attention(q, kv, kv_far, allowed, weight, items, batch):
    rows, cols = q.shape
    heads, each = cols // HEAD_DIM, rows // items
    width = weight.shape[0]

    def kernel(q, kv, kv_far, allowed, weight, attended, out):
        index = pl.program_id(0)
        scaled = head_mask(each, heads, HEAD_DIM ** (-0.5), BF)
        ones = head_mask(each, heads, 1.0, F32)
        for item in range(batch):
            span = slice(item * each, (item + 1) * each)
            keys = jnp.concatenate([kv[span, :cols], kv_far[span, :cols]], axis=0)
            values = jnp.concatenate([kv[span, cols:], kv_far[span, cols:]], axis=0)
            seen = jnp.concatenate([allowed[item]] * heads, axis=0) > 0
            result = attend(
                q[span], keys, values, lambda s: jnp.where(seen, s, NEG), heads, scaled, ones
            )
            start = pl.multiple_of((index * batch + item) * each, each)
            attended[pl.ds(start, each), :] = result

        @pl.when(index == pl.num_programs(0) - 1)
        def _():
            out[...] = mul_t(attended[...], weight[...]).astype(BF)

    part = batch * each
    return call(
        kernel,
        items // batch,
        [
            block((part, cols)),
            block((part, 2 * cols)),
            block((part, 2 * cols)),
            block((batch, each, 2 * each)),
            whole((width, cols)),
        ],
        [whole((rows, cols)), whole((rows, width))],
        [shaped((rows, cols), BF), shaped((rows, width), BF)],
        flops=2 * rows * cols * width * 3,
        moved=rows * cols * 14 + rows * width * 4,
    )(q, kv, kv_far, allowed, weight)


def cross_attention(own, near, away, rows_in, cq, keys_values, weight, items, batch, patches):
    rows, width = own.shape
    cols = weight.shape[1]
    heads, each = cols // HEAD_DIM, rows // items
    padded = keys_values.shape[1]

    def kernel(own, near, away, bias, gain, shift, bias_q, cq, kv, weight, unit, scale, low, qc, attended, out):
        index = pl.program_id(0)

        @pl.when(index == 0)
        def _():
            one, size = standard(own[...].astype(F32) + pair_sum(near, away) + bias[...])
            unit[...] = one
            scale[...] = size
            low[...] = (one * gain[...] + shift[...]).astype(BF)
            qc[...] = (mul(low[...], cq[...]) + bias_q[...]).astype(BF)

        scaled = head_mask(each, heads, HEAD_DIM ** (-0.5), BF)
        ones = head_mask(each, heads, 1.0, F32)
        real = lax.broadcasted_iota(jnp.int32, (heads * each, padded), 1) < patches
        for item in range(batch):
            start = pl.multiple_of((index * batch + item) * each, each)
            attended[pl.ds(start, each), :] = attend(
                qc[pl.ds(start, each), :],
                kv[item, :, :cols],
                kv[item, :, cols:],
                lambda s: jnp.where(real, s, NEG),
                heads,
                scaled,
                ones,
            )

        @pl.when(index == pl.num_programs(0) - 1)
        def _():
            out[...] = mul_t(attended[...], weight[...]).astype(BF)

    bias, gain, shift, bias_q = rows_in
    return call(
        kernel,
        items // batch,
        [whole((rows, width))] * 3
        + [whole((1, width))] * 3
        + [whole((1, cols)), whole((width, cols)), block((batch, padded, 2 * cols)), whole((width, cols))],
        [
            whole((rows, width)),
            whole((rows, 1)),
            whole((rows, width)),
            whole((rows, cols)),
            whole((rows, cols)),
            whole((rows, width)),
        ],
        [
            shaped((rows, width), F32),
            shaped((rows, 1), F32),
            shaped((rows, width), BF),
            shaped((rows, cols), BF),
            shaped((rows, cols), BF),
            shaped((rows, width), BF),
        ],
        flops=2 * rows * cols * padded * heads * 2,
        moved=rows * width * 20 + 4 * items * padded * cols,
    )(own, near, away, bias, gain, shift, bias_q, cq, keys_values, weight)


def lay_pieces(places, spots, refs, laid):
    count, rows, cols = laid.shape[1:]
    for far_off, w_in, w_out in zip(spots, refs[:count], refs[count:]):
        laid[0, places[far_off]] = w_in[...]
        laid[1, places[far_off]] = w_out[...]
    return laid[0].reshape(count * rows, cols), laid[1].reshape(count * rows, cols)


def feed_forward(flag, places, unit, near, away, rows_in, pieces, b_in, chunk):
    rows, width = unit.shape
    hidden = pieces[0].shape[1] // 2
    steps = hidden // chunk
    count = len(pieces)
    spots = arrival_order(count)

    def kernel(flag, places, unit, near, away, gain0, shift0, bias, gain1, shift1, b_in, *refs):
        z, z_low, unit2, scale2, act, slope, part, out, laid = refs[2 * count :]
        w_in, w_out = lay_pieces(places, spots, refs[: 2 * count], laid)

        @pl.when(pl.program_id(0) == 0)
        def _():
            after = unit[...] * gain0[...] + shift0[...]
            one, size = standard(after + pair_sum(near, away) + bias[...])
            unit2[...] = one
            scale2[...] = size
            z[...] = jnp.where(flag[0] == 0, one * gain1[...] + shift1[...], after)
            z_low[...] = z[...].astype(BF)
            out[...] = jnp.zeros_like(out)

        for half in range(2):
            span = slice(half * rows // 2, (half + 1) * rows // 2)
            u = mul(z_low[span], w_in) + b_in[...]
            share = 0.5 + 0.5 * lax.erf(u * math.sqrt(0.5))
            act_half = (u * share).astype(BF)
            act[span] = act_half
            slope[0, span] = share + u * (jnp.exp(-0.5 * u * u) * (1.0 / math.sqrt(2.0 * math.pi)))
            out[span] += mul_t(act_half, w_out)

        @pl.when(pl.program_id(0) == steps - 1)
        def _():
            part[...] = out[...].astype(BF)

    row = whole((1, width))
    return call(
        kernel,
        steps,
        [pl.BlockSpec(memory_space=pltpu.SMEM)] * 2
        + [whole((rows, width))] * 3
        + [row] * 5
        + [column((1, chunk))]
        + [column((width // count, chunk))] * count
        + [column((width // count, chunk), steps)] * count,
        [
            whole((rows, width)),
            whole((rows, width)),
            whole((rows, width)),
            whole((rows, 1)),
            column((rows, chunk)),
            block((1, rows, chunk)),
            whole((rows, width)),
        ],
        [
            shaped((rows, width), F32),
            shaped((rows, width), BF),
            shaped((rows, width), F32),
            shaped((rows, 1), F32),
            shaped((rows, hidden), BF),
            shaped((steps, rows, chunk), F32),
            shaped((rows, width), BF),
        ],
        scratch=[pltpu.VMEM((rows, width), F32), pltpu.VMEM((2, count, width // count, chunk), BF)],
        flops=4 * rows * hidden * width,
        moved=rows * width * 26 + rows * hidden * 6 + width * hidden * 4,
    )(flag, places, unit, near, away, *rows_in, b_in, *pieces, *pieces)


def feed_back(places, z, near, away, cotangent, rows_in, slope, pieces, chunk):
    rows, width = z.shape
    hidden = pieces[0].shape[1] // 2
    steps = hidden // chunk
    count = len(pieces)
    spots = arrival_order(count)

    def kernel(places, z, near, away, cot, bias, gain, shift, slope, *refs):
        result, grad_v, grad_u, grad_pre, part, sums, sum_pre, out, laid = refs[2 * count :]
        w_in, w_out = lay_pieces(places, spots, refs[: 2 * count], laid)

        @pl.when(pl.program_id(0) == 0)
        def _():
            one, size = standard(z[...] + pair_sum(near, away) + bias[...])
            dy = cot[...]
            result[...] = (one * gain[...] + shift[...]).astype(BF)
            grad_v[...] = norm_back(dy, one, size, gain[...])
            grad_u[...] = grad_v[...].astype(BF)
            sums[0:1] = total_rows(dy * one)
            sums[1:2] = total_rows(dy)
            sums[2:3] = total_rows(grad_u[...].astype(F32))
            out[...] = jnp.zeros_like(out)

        for half in range(2):
            span = slice(half * rows // 2, (half + 1) * rows // 2)
            pre = (mul(grad_u[span], w_out) * slope[0, span]).astype(BF)
            grad_pre[span] = pre
            out[span] += mul_t(pre, w_in)
        sum_pre[...] = total_rows(grad_pre[...].astype(F32))

        @pl.when(pl.program_id(0) == steps - 1)
        def _():
            part[...] = out[...].astype(BF)

    row = whole((1, width))
    return call(
        kernel,
        steps,
        [pl.BlockSpec(memory_space=pltpu.SMEM)]
        + [whole((rows, width))] * 4
        + [row] * 3
        + [block((1, rows, chunk))]
        + [column((width // count, chunk))] * count
        + [column((width // count, chunk), steps)] * count,
        [
            whole((rows, width)),
            whole((rows, width)),
            whole((rows, width)),
            column((rows, chunk)),
            whole((rows, width)),
            whole((8, width)),
            column((1, chunk)),
        ],
        [
            shaped((rows, width), BF),
            shaped((rows, width), F32),
            shaped((rows, width), BF),
            shaped((rows, hidden), BF),
            shaped((rows, width), BF),
            shaped((8, width), F32),
            shaped((1, hidden), F32),
        ],
        scratch=[pltpu.VMEM((rows, width), F32), pltpu.VMEM((2, count, width // count, chunk), BF)],
        flops=4 * rows * hidden * width,
        moved=rows * width * 28 + rows * hidden * 6 + width * hidden * 4,
    )(places, z, near, away, cotangent, *rows_in, slope, *pieces, *pieces)


def cross_back(flag, grad_v, near, away, unit2, scale2, gain, qc, keys_values, weight, cq, items, batch, patches):
    rows, width = grad_v.shape
    cols = weight.shape[1]
    heads, each = cols // HEAD_DIM, rows // items
    padded = keys_values.shape[1]

    def kernel(flag, grad_v, near, away, unit2, scale2, gain, qc, kv, weight, cq, after, mix, grad_qc, grad_kv, out, sums, sums_c, grad_att):
        index = pl.program_id(0)

        @pl.when(index == 0)
        def _():
            dz = grad_v[...] + pair_sum(near, away)
            mine = flag[0] == 0
            used = jnp.where(mine, dz, 0.0)
            two = norm_back(used, unit2[...], scale2[...], gain[...])
            after[...] = jnp.where(mine, two, dz)
            mix[...] = two.astype(BF)
            grad_att[...] = mul(mix[...], weight[...]).astype(BF)
            sums[0:1] = total_rows(used * unit2[...])
            sums[1:2] = total_rows(used)
            sums[2:3] = total_rows(mix[...].astype(F32))
            sums_c[...] = jnp.zeros_like(sums_c)

        root = HEAD_DIM ** (-0.5)
        scaled = head_mask(each, heads, root, BF)
        plain = head_mask(each, heads, 1.0, BF)
        ones = head_mask(each, heads, 1.0, F32)
        real = lax.broadcasted_iota(jnp.int32, (heads * each, padded), 1) < patches
        for item in range(batch):
            start = pl.multiple_of((index * batch + item) * each, each)
            dq, dk, dv = attend_back(
                qc[pl.ds(start, each), :],
                kv[item, :, :cols],
                kv[item, :, cols:],
                grad_att[pl.ds(start, each), :],
                lambda s: jnp.where(real, s, NEG),
                heads,
                scaled,
                plain,
                ones,
            )
            grad_qc[pl.ds(start, each), :] = dq.astype(BF)
            dk, dv = dk.astype(BF), dv.astype(BF)
            grad_kv[item, :, :cols] = dk
            grad_kv[item, :, cols:] = dv
            sums_c[1:2] += total_rows(dk.astype(F32))
            sums_c[2:3] += total_rows(dv.astype(F32))

        @pl.when(index == pl.num_programs(0) - 1)
        def _():
            out[...] = mul_t(grad_qc[...], cq[...]).astype(BF)
            sums_c[0:1] = total_rows(grad_qc[...].astype(F32))

    return call(
        kernel,
        items // batch,
        [pl.BlockSpec(memory_space=pltpu.SMEM)]
        + [whole((rows, width))] * 4
        + [
            whole((rows, 1)),
            whole((1, width)),
            whole((rows, cols)),
            block((batch, padded, 2 * cols)),
            whole((width, cols)),
            whole((width, cols)),
        ],
        [
            whole((rows, width)),
            whole((rows, width)),
            whole((rows, cols)),
            block((batch, padded, 2 * cols)),
            whole((rows, width)),
            whole((8, width)),
            whole((8, cols)),
        ],
        [
            shaped((rows, width), F32),
            shaped((rows, width), BF),
            shaped((rows, cols), BF),
            shaped((items, padded, 2 * cols), BF),
            shaped((rows, width), BF),
            shaped((8, width), F32),
            shaped((8, cols), F32),
        ],
        scratch=[pltpu.VMEM((rows, cols), BF)],
        flops=2 * rows * cols * padded * heads * 5,
        moved=rows * width * 26 + 8 * items * padded * cols,
    )(flag, grad_v, near, away, unit2, scale2, gain, qc, keys_values, weight, cq)


def self_back(flag, head, after, near, away, unit, scale, gain, q, kv, kv_far, allowed, weight, w_qkv, own, far, attended, items, batch, shards):
    rows, width = after.shape
    cols = weight.shape[1]
    heads, each = cols // HEAD_DIM, rows // items
    piece = width // shards

    def kernel(flag, head, after, near, away, unit, scale, gain, q, kv, kv_far, allowed, weight, w_qkv, own, far, attended, grad_one, mix, grad_near, grad_away, mine, theirs, sums, sums_c, grad_keep, grad_sent, grad_att):
        index = pl.program_id(0)

        @pl.when(index == 0)
        def _():
            grad = after[...] + pair_sum(near, away)
            grad_one[...] = norm_back(grad, unit[...], scale[...], gain[...])
            mix[...] = grad_one[...].astype(BF)
            grad_att[...] = mul(mix[...], weight[...]).astype(BF)
            sums[0:1] = total_rows(grad * unit[...])
            sums[1:2] = total_rows(grad)
            sums[2:3] = total_rows(mix[...].astype(F32))

        scaled = head_mask(each, heads, HEAD_DIM ** (-0.5), BF)
        plain = head_mask(each, heads, 1.0, BF)
        ones = head_mask(each, heads, 1.0, F32)
        for item in range(batch):
            span = slice(item * each, (item + 1) * each)
            start = pl.multiple_of((index * batch + item) * each, each)
            keys = jnp.concatenate([kv[span, :cols], kv_far[span, :cols]], axis=0)
            values = jnp.concatenate([kv[span, cols:], kv_far[span, cols:]], axis=0)
            seen = jnp.concatenate([allowed[item]] * heads, axis=0) > 0
            dq, dk, dv = attend_back(
                q[span],
                keys,
                values,
                grad_att[pl.ds(start, each), :],
                lambda s: jnp.where(seen, s, NEG),
                heads,
                scaled,
                plain,
                ones,
            )
            grad_near[pl.ds(start, each), :cols] = dq.astype(BF)
            grad_near[pl.ds(start, each), cols : 2 * cols] = dk[:each].astype(BF)
            grad_near[pl.ds(start, each), 2 * cols :] = dv[:each].astype(BF)
            grad_away[pl.ds(start, each), :cols] = dk[each:].astype(BF)
            grad_away[pl.ds(start, each), cols:] = dv[each:].astype(BF)

        @pl.when(index == pl.num_programs(0) - 1)
        def _():
            side = head[0] == 0
            middle = rows // 2
            for part, source, weights in ((0, grad_near, w_qkv), (1, grad_away, w_qkv[:, cols:])):
                lanes = slice(part * width, (part + 1) * width)
                top = mul_t(source[:middle], weights[...]).astype(BF)
                low = mul_t(source[middle:], weights[...]).astype(BF)
                mine[:, lanes] = jnp.where(side, top, low)
                theirs[:, lanes] = jnp.where(side, low, top)
            for place in range(4):
                span = slice(place * cols, (place + 1) * cols)
                if place == 3:
                    total = t_mul(mix[...], attended[...])
                else:
                    total = t_mul(own[...], grad_near[:, span])
                if place in (1, 2):
                    total = total + t_mul(far[...], grad_away[:, (place - 1) * cols : place * cols])
                total = total.astype(BF)
                for side in range(2):
                    pieces = [
                        total[one * piece : (one + 1) * piece] for one in range(side, shards, 2)
                    ]

                    @pl.when(flag[0] == side)
                    def _():
                        for one, value in enumerate(pieces):
                            grad_keep[one, :, span] = value

                    @pl.when(flag[0] != side)
                    def _():
                        for one, value in enumerate(pieces):
                            grad_sent[one, :, span] = value
            sums_c[0:1] = total_rows(grad_near[...].astype(F32))
            sums_c[1:2, cols:] = total_rows(grad_away[...].astype(F32))

    part = batch * each
    return call(
        kernel,
        items // batch,
        [pl.BlockSpec(memory_space=pltpu.SMEM)] * 2
        + [whole((rows, width))] * 4
        + [
            whole((rows, 1)),
            whole((1, width)),
            block((part, cols)),
            block((part, 2 * cols)),
            block((part, 2 * cols)),
            block((batch, each, 2 * each)),
            whole((width, cols)),
            whole((width, 3 * cols)),
            whole((rows, width)),
            whole((rows, width)),
            whole((rows, cols)),
        ],
        [
            whole((rows, width)),
            whole((rows, width)),
            whole((rows, 3 * cols)),
            whole((rows, 2 * cols)),
            whole((rows // 2, 2 * width)),
            whole((rows // 2, 2 * width)),
            whole((8, width)),
            whole((8, 3 * cols)),
            whole((shards // 2, piece, 4 * cols)),
            whole((shards // 2, piece, 4 * cols)),
        ],
        [
            shaped((rows, width), F32),
            shaped((rows, width), BF),
            shaped((rows, 3 * cols), BF),
            shaped((rows, 2 * cols), BF),
            shaped((rows // 2, 2 * width), BF),
            shaped((rows // 2, 2 * width), BF),
            shaped((8, width), F32),
            shaped((8, 3 * cols), F32),
            shaped((shards // 2, piece, 4 * cols), BF),
            shaped((shards // 2, piece, 4 * cols), BF),
        ],
        scratch=[pltpu.VMEM((rows, cols), BF)],
        flops=2 * rows * cols * width * 9,
        limit=28,
        moved=rows * width * 32 + rows * cols * 20,
    )(flag, head, after, near, away, unit, scale, gain, q, kv, kv_far, allowed, weight, w_qkv, own, far, attended)


def pack_small(flag, one, two, three, own, cross, pre, kv_grad, kv_all, gain, shift):
    width = one.shape[1]
    cols = cross.shape[1]
    feat_width = kv_all.shape[0]
    pres = pre.shape[1] // width
    folds = (feat_width + width - 1) // width
    rows = (14 + 2 * pres + 2 * folds + 7) // 8 * 8

    def exact(left, right):
        return lax.dot_general(
            left,
            right,
            (((1,), (1,)), ((), ())),
            precision=lax.Precision.HIGHEST,
            preferred_element_type=F32,
        )

    def kernel(flag, one, two, three, own, cross, pre, kv_grad, kv_all, gain, shift, out, line):
        on_text = flag[0].astype(F32)
        on_query = 1.0 - on_text
        out[...] = jnp.zeros_like(out)
        for place in range(3):
            at_row = slice(place, place + 1)
            out[4 * place : 4 * place + 1] = one[at_row]
            out[4 * place + 1 : 4 * place + 2] = two[at_row]
            out[4 * place + 2 : 4 * place + 3] = on_query * three[at_row]
            out[4 * place + 3 : 4 * place + 4] = on_text * three[at_row]
        out[12:13, :cols] = own[0:1, :cols]
        out[12:13, cols:] = own[0:1, 2 * cols :] + own[1:2, 2 * cols :]
        out[13:14, :cols] = cross[0:1]
        out[13:14, cols:] = cross[2:3]
        for k in range(pres):
            part = pre[:, k * width : (k + 1) * width]
            out[14 + k : 15 + k] = on_query * part
            out[14 + pres + k : 15 + pres + k] = on_text * part
        column_sums = jnp.concatenate([cross[1:2], cross[2:3]], axis=1)
        column_sums = jnp.broadcast_to(column_sums, (8, width))
        ones = jnp.ones((8, width), F32)

        def chunk(k, carry):
            span = pl.ds(pl.multiple_of(k * 128, 128), 128)
            weight = kv_all[span, :].astype(F32)
            d_shift = exact(column_sums, weight)[0:1]
            dot = exact(ones, kv_grad[span, :] * weight)[0:1]
            line[0:1, span] = (dot - shift[:, span] * d_shift) / gain[:, span]
            line[1:2, span] = d_shift
            return carry

        lax.fori_loop(0, feat_width // 128, chunk, 0)
        start = 14 + 2 * pres
        for part in range(2):
            for k in range(folds):
                end = min(feat_width, (k + 1) * width)
                spot = start + part * folds + k
                out[spot : spot + 1, : end - k * width] = line[part : part + 1, k * width : end]

    arrays = (one, two, three, own, cross, pre, kv_grad, kv_all, gain, shift)
    return call(
        kernel,
        1,
        [pl.BlockSpec(memory_space=pltpu.SMEM)] + [whole(array.shape) for array in arrays],
        whole((rows, width)),
        shaped((rows, width), F32),
        scratch=[pltpu.VMEM((8, feat_width), F32)],
        limit=28,
        moved=6 * feat_width * width,
    )(flag, *arrays)


def unpack_small(head, packed, other, pres, feat_width):
    width = packed.shape[1]
    half = width // 2
    folds = (feat_width + width - 1) // width

    def kernel(head, packed, other, own_bias, cross_bias, gains, shifts, d_gain, d_shift, pre, post):
        first = head[0] == 0
        near, away = packed[12:], other[...]
        low = jnp.where(first, near, away)
        high = jnp.where(first, away, near)
        for place, out in enumerate((own_bias, cross_bias)):
            for part in range(2):
                span = slice(part * half, (part + 1) * half)
                out[part : part + 1, :half] = low[place : place + 1, span]
                out[part : part + 1, half:] = high[place : place + 1, span]
        own_bias[2:3] = packed[8:9]
        cross_bias[2:3] = packed[9:10]
        gains[...] = packed[0:4]
        shifts[...] = packed[4:8]
        post[...] = packed[10:12]
        for side in range(2):
            for k in range(pres):
                line = slice(2 + side * pres + k, 3 + side * pres + k)
                pre[side : side + 1, k * width : (k + 1) * width] = low[line]
                pre[side : side + 1, (pres + k) * width : (pres + k + 1) * width] = high[line]
        both = near + away
        for place, out in enumerate((d_gain, d_shift)):
            for k in range(folds):
                end = min(feat_width, (k + 1) * width)
                line = 2 + 2 * pres + place * folds + k
                for begin in range(k * width, end, 128):
                    spot, left = begin // 128, begin - k * width
                    out[spot : spot + 1] = both[line : line + 1, left : left + 128]

    shapes = [(3, width)] * 2 + [(4, width)] * 2 + [(feat_width // 128, 128)] * 2
    shapes = shapes + [(2, 2 * pres * width), (2, width)]
    return call(
        kernel,
        1,
        [pl.BlockSpec(memory_space=pltpu.SMEM), whole(packed.shape), whole(other.shape)],
        [whole(shape) for shape in shapes],
        [shaped(shape, F32) for shape in shapes],
        moved=200000,
    )(head, packed, other)


def visible(stream, segments, modes):
    same_caption = segments[:, :, None] == segments[:, None, :]
    own = jnp.logical_or(stream == 0, same_caption)
    far = jnp.where(stream == 0, modes == 2, modes >= 1)[:, None, None]
    return jnp.concatenate([own, jnp.broadcast_to(far, own.shape)], axis=2).astype(F32)


def body(
    hidden,
    features,
    segments,
    modes,
    w_qkv,
    self_bias,
    self_out,
    cross_q,
    cross_kv,
    cross_bias,
    cross_out,
    gains,
    shifts,
    feat_gain,
    feat_shift,
    ffn_in,
    ffn_bias_in,
    ffn_out,
    ffn_bias_out,
    cotangent,
):
    stream = lax.axis_index("stream")
    stream_u = stream.astype(jnp.uint32)
    head_index = lax.axis_index("heads")
    items, _, each, width = hidden.shape
    rows = items * each
    half = rows // 2
    cols = w_qkv.shape[2]
    hidden_cols = ffn_in.shape[2]
    patches, feat_width = features.shape[1:]
    padded = (patches + 7) // 8 * 8
    col_start = head_index.astype(jnp.uint32) * cols
    hidden_start = head_index.astype(jnp.uint32) * hidden_cols
    flag = stream.astype(jnp.int32).reshape(1)
    shards = 2 * lax.axis_size("items")
    three = [slice(i * cols, (i + 1) * cols) for i in range(3)]

    ffn_part = jnp.concatenate([ffn_in[0], ffn_out[0].T], axis=1)
    part_qkv = jnp.concatenate([w_qkv[0], w_qkv[1], w_qkv[2]], axis=0)
    pair_qkv = by_stream(part_qkv, partner(part_qkv, "stream", 0), 0)
    places = ring_places()
    spots = ring_row()
    own = hidden.reshape(rows, width)
    heads_u = head_index.astype(jnp.uint32)
    my_half = lax.dynamic_slice_in_dim(own, heads_u * half, half, 0)
    far_half = partner(my_half, "stream", 0)
    piece, kv_piece = cross_q.shape[0], cross_kv.shape[1]
    rest = jnp.concatenate([self_out.T, cross_q, cross_out.T, cross_kv[0], cross_kv[1]], axis=0)

    def row(vector):
        return vector.reshape(1, -1)

    features, pair_qkv = joined(features, pair_qkv)
    ring = Gather(jnp.concatenate([pair_qkv.reshape(6 * piece, cols), rest], axis=0))

    def crossing(one):
        return one[6 * piece :], over("stream")

    kept, chunk = [], items // 4
    crossed = []
    begin = 0
    for number in range(max(4, shards // 4)):
        if ring.left:
            riders = [crossing(one) for one in ring.pieces[begin:]]
            if number == 1:
                riders.append((far_half, over("heads")))
            last_step = ring.hop == shards // 4
            if last_step:
                ffn_part, held = joined(ffn_part, ring.up)
                ring.replace(held, ring.down)
                ffn_gather = Gather(ffn_part)
            fresh = len(ring.pieces) - begin
            begin = len(ring.pieces)
            ridden = gather_step([ring], *riders)
            crossed += ridden[:fresh]
            if number == 1:
                far_other = ridden[-1]
            if last_step:
                gather_step([ffn_gather])
        if number < 4:
            *kept, token = list(
                feature_norm(
                    features, row(feat_gain), row(feat_shift), padded, number * chunk, chunk, kept
                )
            )
            up, down, token = joined(ring.up, ring.down, token)
            ring.replace(up, down)
            kept = [kept[0], token]
    feat_norm = kept[0]
    crossed += [move(one) for one, move in (crossing(one) for one in ring.pieces[begin:])]
    far = jnp.where(
        head_index == 0,
        jnp.concatenate([far_half, far_other], axis=0),
        jnp.concatenate([far_other, far_half], axis=0),
    )
    def ffn_step(value, last=False):
        if ffn_gather.hop - 1 > ffn_gather.count // 2:
            return value
        value, up, down = joined(value, ffn_gather.up, ffn_gather.down)
        ffn_gather.replace(up, down)
        while ffn_gather.left:
            gather_step([ffn_gather])
            if not last:
                break
        return value

    def my_cols(vector):
        return lax.dynamic_slice_in_dim(vector, col_start, cols, 0)

    none = jnp.zeros((cols,), F32)
    bias_qkv = row(jnp.concatenate([my_cols(self_bias[0]), none, my_cols(self_bias[1])]))
    bias_kv = row(jnp.concatenate([none, my_cols(cross_bias[1])]))
    gain_ffn = row(lax.dynamic_index_in_dim(gains, 2 + stream_u, 0, keepdims=False))
    shift_ffn = row(lax.dynamic_index_in_dim(shifts, 2 + stream_u, 0, keepdims=False))
    bias_in = row(
        lax.dynamic_slice_in_dim(
            lax.dynamic_index_in_dim(ffn_bias_in, stream_u, 0, keepdims=False),
            hidden_start,
            hidden_cols,
            0,
        )
    )
    bias_out = row(lax.dynamic_index_in_dim(ffn_bias_out, stream_u, 0, keepdims=False))

    def swap(part):
        return partner(part, "heads", 0)

    q, kv, kv_far, qkv_all = project(spots, own, far, ring.pieces, bias_qkv, piece)
    ends = joined(ffn_gather.up, ffn_gather.down, ring.up, kv_far, feat_norm, *crossed[-3:])
    ffn_gather.replace(*ends[:2])
    ring.replace(ends[2], ends[2])
    kv_far = ends[3]
    feat_rows = ends[4].reshape(items * padded, feat_width)
    crossed[-3:] = ends[5:]
    gather_step([ffn_gather])
    self_out_t, cross_q_all, cross_out_t, kv_all = assemble(
        flag, spots, ring.pieces, crossed, piece, kv_piece
    )

    allowed = visible(stream, segments, modes)
    attended, part = self_attention(q, kv, kv_far, allowed, self_out_t, items, 4)
    kv_all = ffn_step(kv_all)
    away_one = swap(part)
    keys_values = (mul(feat_rows, kv_all) + bias_kv).astype(BF).reshape(items, padded, 2 * cols)
    keys_values = ffn_step(keys_values)
    unit_one, scale_one, after_low, qc, attended_c, part_c = cross_attention(
        own,
        part,
        away_one,
        (row(self_bias[2]), row(gains[0]), row(shifts[0]), row(my_cols(cross_bias[0]))),
        cross_q_all,
        keys_values,
        cross_out_t,
        items,
        2,
        patches,
    )
    unit_one, part_c, scale_one, after_low, qc, attended_c = ffn_step(
        (unit_one, part_c, scale_one, after_low, qc, attended_c), True
    )
    ffn_pieces = ffn_gather.pieces
    z, z_low, unit_two, scale_two, activated, slope, part_f = feed_forward(
        flag,
        spots,
        unit_one,
        part_c,
        swap(part_c),
        (row(gains[0]), row(shifts[0]), row(cross_bias[2]), row(gains[1]), row(shifts[1])),
        ffn_pieces,
        bias_in,
        256,
    )

    output, grad_three, grad_u, grad_pre, part_z, sums_three, sum_pre = feed_back(
        spots,
        z,
        part_f,
        swap(part_f),
        cotangent.reshape(rows, width),
        (bias_out, gain_ffn, shift_ffn),
        slope,
        ffn_pieces,
        256,
    )
    away_z = swap(part_z)
    in_grad = t_mul(z_low, grad_pre).astype(BF)
    out_grad = t_mul(grad_u, activated).astype(BF)
    count = shards // 2
    grad_after, mix_c, grad_qc, grad_kv, part_a, sums_two, sums_cross = cross_back(
        flag,
        grad_three,
        part_z,
        away_z,
        unit_two,
        scale_two,
        row(gains[1]),
        qc,
        keys_values,
        cross_out_t,
        cross_q_all,
        items,
        2,
        patches,
    )
    in_grad, out_grad, sums_two = joined(in_grad, out_grad, sums_two)
    ffn_ring = Scatter(
        [
            [at(in_grad.reshape(count, -1, hidden_cols))],
            [at(out_grad.reshape(count, -1, hidden_cols))],
        ],
        1,
        places,
    )
    ffn_ring.step()
    away_a = swap(part_a)
    keep_q, away_q = halves(t_mul(after_low, grad_qc).astype(BF))
    keep_o, away_o = halves(t_mul(mix_c, attended_c).astype(BF))
    away_c = jnp.concatenate([away_q, away_o], axis=2)
    grad_kv, away_c = joined(grad_kv, away_c)
    kv_grad = t_mul(feat_rows, grad_kv.reshape(items * padded, 2 * cols))
    kv_grad_low = kv_grad.astype(BF)
    arrived_c = partner(away_c, "stream", 0)
    kv_grad, kv_grad_low, arrived_c, ffn_ring.up = joined(
        kv_grad, kv_grad_low, arrived_c, ffn_ring.up
    )
    keep_kv, away_kv = halves(kv_grad_low)
    ffn_ring.step()
    away_a, away_kv = joined(away_a, away_kv)
    arrived_kv = partner(away_kv, "stream", 0)
    grad_one, mix, grad_near, grad_away, mine, theirs, sums_one, sums_self, keep_self, away_self = self_back(
        flag,
        head_index.astype(jnp.int32).reshape(1),
        grad_after,
        part_a,
        away_a,
        unit_one,
        scale_one,
        row(gains[0]),
        q,
        kv,
        kv_far,
        allowed,
        self_out_t,
        qkv_all,
        own,
        far,
        attended,
        items,
        4,
        shards,
    )

    results = (grad_one, mine, theirs, sums_one, sums_self, keep_self, away_self, arrived_kv)
    results = lax.optimization_barrier(results + (ffn_ring.up, ffn_ring.down))
    grad_one, mine, theirs, sums_one, sums_self, keep_self, away_self, arrived_kv = results[:-2]
    ffn_ring.up, ffn_ring.down = results[-2:]


    def ring_steps(rings, *riders):
        ridden = [move(value) for value, move in riders]
        sends = [ring.sends() for ring in rings]
        flat = [one for part in sends for one in part]
        arrivals = lax.optimization_barrier(tuple(ridden) + tuple(together(flat)))
        rest = arrivals[len(riders) :]
        for ring, part in zip(rings, sends):
            ring.take(rest[: len(part)])
            rest = rest[len(part) :]
        return arrivals[: len(riders)]

    rest_ring = Scatter(
        [
            [at_stream(keep_q), at(arrived_c, three[0])],
            [at_stream(keep_o), at(arrived_c, three[1])],
            [at_stream(keep_kv, three[0]), at(arrived_kv, three[0])],
            [at_stream(keep_kv, three[1]), at(arrived_kv, three[1])],
        ],
        0,
        places,
    )
    arrived_self, from_swap = partner(away_self, "stream", 0), swap(theirs)
    ffn_ring.step()
    ring_steps([rest_ring])
    while ffn_ring.hop:
        ffn_ring.step()
    ends = joined(arrived_self, ffn_ring.up, ffn_ring.down, rest_ring.up)
    arrived_self, ffn_ring.up, ffn_ring.down, rest_ring.up = ends
    self_ring = Scatter([[at(keep_self), at(arrived_self)]], 0, places)
    total = mine.astype(F32) + from_swap.astype(F32)
    from_far = partner(total[:, width:].astype(BF), "stream", 0)
    packed = pack_small(
        flag,
        sums_one,
        sums_two,
        sums_three,
        sums_self,
        sums_cross,
        sum_pre,
        kv_grad,
        kv_all,
        row(feat_gain),
        row(feat_shift),
    )
    packed = packed + partner(packed, "items", 0)
    moves = [over("stream")] + [over("items", bit) for bit in range(1, (count - 1).bit_length())]

    in_half = (
        lax.dynamic_slice_in_dim(grad_one, heads_u * half, half, 0)
        + total[:, :width]
        + from_far.astype(F32)
    )
    (arrived,) = ring_steps(
        [one for one in (rest_ring, self_ring) if one.hop], (packed, moves.pop(0))
    )
    packed = packed + arrived
    in_other = swap(in_half)
    while self_ring.hop or ffn_ring.hop or rest_ring.hop:
        rings = [one for one in (ffn_ring, rest_ring, self_ring) if one.hop]
        riders = [(packed, moves.pop(0))] if moves else []
        for arrived in ring_steps(rings, *riders):
            packed = packed + arrived
    while moves:
        packed = packed + moves.pop(0)(packed)
    grad_input = jnp.where(
        head_index == 0,
        jnp.concatenate([in_half, in_other], axis=0),
        jnp.concatenate([in_other, in_half], axis=0),
    )
    ffn_red, rest_red, self_red = ffn_ring.result(), rest_ring.result(), self_ring.result()
    small = unpack_small(
        head_index.astype(jnp.int32).reshape(1),
        packed,
        swap(packed[12:]),
        hidden_cols // width,
        feat_width,
    )
    return (
        output.reshape(items, 1, each, width),
        grad_input.reshape(items, 1, each, width),
        jnp.stack([self_red[:, one] for one in three]),
        small[0],
        self_red[:, 3 * cols :].T,
        rest_red[:piece],
        rest_red[2 * piece :].reshape(2, kv_piece, cols),
        small[1],
        rest_red[piece : 2 * piece].T,
        small[2],
        small[3],
        small[4].reshape(feat_width),
        small[5].reshape(feat_width),
        ffn_red[:, :hidden_cols][None],
        small[6],
        ffn_red[:, hidden_cols:].T[None],
        small[7],
    )


def solution(mesh):
    placed = (
        P("items", "stream", None, None),
        P("items", None, None),
        P("items", None),
        P("items"),
        P(None, ("items", "stream"), "heads"),
        P(),
        P("heads", ("items", "stream")),
        P(("items", "stream"), "heads"),
        P(None, ("items", "stream"), "heads"),
        P(),
        P("heads", ("items", "stream")),
        P(),
        P(),
        P(),
        P(),
        P("stream", "items", "heads"),
        P(),
        P("stream", "heads", "items"),
        P(),
        P("items", "stream", None, None),
    )
    return jax.shard_map(
        body,
        mesh=mesh,
        in_specs=placed,
        out_specs=(
            P("items", "stream", None, None),
            P("items", "stream", None, None),
            P(None, ("items", "stream"), "heads"),
            P(),
            P("heads", ("items", "stream")),
            P(("items", "stream"), "heads"),
            P(None, ("items", "stream"), "heads"),
            P(),
            P("heads", ("items", "stream")),
            P(),
            P(),
            P(),
            P(),
            P("stream", "items", "heads"),
            P(),
            P("stream", "heads", "items"),
            P(),
        ),
        check_vma=False,
    )
```
